32 devices in a mesh: dp: 4 (over y, x), fs: 8 (over z, core).
Axes of the slice: x: 2, y: 2, z: 4, core: 2. Of those that a mesh axis runs over, the one named last changes fastest.
Arguments:
- tokens: bfloat16 [32, 320, 1024], P(('dp', 'fs')), may hold values from -6 to 6
- image_side: int32 [32], P(('dp', 'fs')), may hold values from 16 to 32, as said below
- cotangent: bfloat16 [32, 512, 256], P(('dp', 'fs')), may hold values from -26 to 26
- query_weight: bfloat16 [102400], P(('dp', 'fs')), may hold values from -0.3125 to 0.3125
- keyval_weight: bfloat16 [204800], P(('dp', 'fs')), may hold values from -0.3125 to 0.3125
- reduce_weight: bfloat16 [409600], P(('dp', 'fs')), may hold values from -0.15625 to 0.15625
- output_weight: bfloat16 [102400], P(('dp', 'fs')), may hold values from -2.5 to 2.5
- expand_weight: bfloat16 [409600], P(('dp', 'fs')), may hold values from -0.3125 to 0.3125
- depth_weight: bfloat16 [11520], P(('dp', 'fs')), may hold values from -2 to 2
- contract_weight: bfloat16 [409600], P(('dp', 'fs')), may hold values from -0.15625 to 0.15625
- merge_weight: bfloat16 [1474560], P(('dp', 'fs')), may hold values from -0.109375 to 0.109375
- norm_gains: bfloat16 [1792], P(('dp', 'fs')), may hold values from 0.25 to 1.75
- all_biases: bfloat16 [6144], P(('dp', 'fs')), may hold values from -3 to 3
Outputs:
- section_four: bfloat16 [32, 512, 256], P(('dp', 'fs'))
- token_grad: float32 [32, 320, 1024], P(('dp', 'fs'))
- query_grad: float32 [102400], P(('dp', 'fs'))
- keyval_grad: float32 [204800], P(('dp', 'fs'))
- reduce_grad: float32 [409600], P(('dp', 'fs'))
- output_grad: float32 [102400], P(('dp', 'fs'))
- expand_grad: float32 [409600], P(('dp', 'fs'))
- depth_grad: float32 [11520], P(('dp', 'fs'))
- contract_grad: float32 [409600], P(('dp', 'fs'))
- merge_grad: float32 [1474560], P(('dp', 'fs'))
- gains_grad: float32 [1792], P(('dp', 'fs'))
- biases_grad: float32 [6144], P(('dp', 'fs'))
The draws below stay inside these ranges and needn't reach their ends.
Inputs may be any that keep to these rules, and one draw needn't show every extreme that they name: `image_side`: each frame holds one square image in its top left corner with side 32, 16, or 0 for an empty frame; the first of each device's 1 frames always holds an image.
All inputs are finite; a program needn't handle non-finite values.
Results may differ from the reference program's by a relative error of at most 0.014.
Values may be sent and summed in bfloat16 or wider, within the bound.
No kernel may reach another device: no remote copies, remote signals or barrier semaphores. Data moves between devices by JAX's collectives and lax.ppermute only.
A program may use at most 256 MiB of HBM per device.

```python
import jax
import jax.numpy as jnp
from jax import lax

D = 320
HEADS = 5
FF = 1280
OUT_D = 512
SIDE = 32
SLOTS = 1
HEAD_DIM = 64
QUARTER = 256
IMAGES = 32


def draw_image_side(key, part):
    position = jnp.arange(IMAGES, dtype=jnp.int32)
    first_pick = jax.random.randint(jax.random.fold_in(key, 1), (IMAGES,), 0, 2)
    other_pick = jax.random.randint(jax.random.fold_in(key, 2), (IMAGES,), 0, 4)
    first_side = jnp.where(first_pick == 1, SIDE, SIDE // 2)
    other_side = jnp.where(other_pick >= 2, SIDE, jnp.where(other_pick == 1, SIDE // 2, 0))
    side_values = jnp.where(position % SLOTS == 0, first_side, other_side)
    second_value = 0 if SLOTS > 1 else SIDE // 2
    side_values = jnp.where(position == 0, SIDE, jnp.where(position == 1, second_value, side_values))
    return side_values.astype(jnp.int32)


def draw_cotangent(key, part):
    position = jnp.arange(IMAGES, dtype=jnp.float32)
    rising = jnp.exp(jnp.log(3.0) * position / max(IMAGES - 1, 1))
    jitter = jnp.exp(jax.random.uniform(jax.random.fold_in(key, 1), (IMAGES,), minval=-0.35, maxval=0.35))
    base_values = jnp.clip(jax.random.normal(jax.random.fold_in(key, 2), (IMAGES, OUT_D, QUARTER)), -6.0, 6.0)
    return (base_values * (rising * jitter)[:, None, None]).astype(jnp.bfloat16)


def steps_of(key, dims, cuts, least, top_value):
    def one(axis_at, parts):
        steps = jax.random.uniform(jax.random.fold_in(jax.random.fold_in(key, 6), axis_at), (parts,), jnp.float32, least / len(cuts), top_value / len(cuts))
        return jnp.repeat(jnp.exp(steps), dims[axis_at] // parts).reshape((-1,) + (1,) * (len(dims) - axis_at - 1))

    level = one(*cuts[0])
    for cut in cuts[1:]:
        level = level * one(*cut)
    return level


def normal_values(key, extent, width, reach, shards=(), kind=jnp.bfloat16):
    drawn = jax.random.normal(key, extent, jnp.float32) * width
    if len(shards) > 0:
        drawn = steps_of(key, extent, shards, -0.22, 0.18) * drawn
    return jnp.clip(drawn, min=-reach, max=reach).astype(kind)


def setup_inputs(seed: int = 0) -> dict:
    keys = jax.random.split(jax.random.key(seed), 14)
    tokens = normal_values(keys[0], (IMAGES, D, SIDE * SIDE), 1.0, 6.0, ((0, 32),))
    image_side = draw_image_side(jax.random.fold_in(keys[13], 71), 0)
    cotangent = draw_cotangent(jax.random.fold_in(keys[13], 71), 0)
    query_weight = normal_values(keys[3], (D * D,), D ** -0.5, 0.3125, ((0, 32),))
    keyval_weight = normal_values(keys[4], (2 * D * D,), D ** -0.5, 0.3125, ((0, 32),))
    reduce_weight = normal_values(keys[5], (4 * D * D,), (4 * D) ** -0.5, 0.15625, ((0, 32),))
    output_weight = normal_values(keys[6], (D * D,), (4 * D // QUARTER) ** -0.5, 2.5, ((0, 32),))
    expand_weight = normal_values(keys[7], (FF * D,), D ** -0.5, 0.3125, ((0, 32),))
    depth_weight = normal_values(keys[8], (9 * FF,), 9 ** -0.5, 2.0, ((0, 32),))
    contract_weight = normal_values(keys[9], (D * FF,), FF ** -0.5, 0.15625, ((0, 32),))
    merge_weight = normal_values(keys[10], (9 * D * OUT_D,), (9 * D) ** -0.5, 0.109375, ((0, 32),))
    norm_gains = jnp.clip(1.0 + 0.15 * jax.random.normal(keys[11], (4 * D + OUT_D,), jnp.float32), 0.25, 1.75).astype(jnp.bfloat16)
    all_biases = normal_values(keys[12], (8 * D + 2 * FF + 2 * OUT_D,), 0.5, 3.0, ((0, 32),))
    return dict(tokens=tokens, image_side=image_side, cotangent=cotangent, query_weight=query_weight, keyval_weight=keyval_weight, reduce_weight=reduce_weight, output_weight=output_weight, expand_weight=expand_weight, depth_weight=depth_weight, contract_weight=contract_weight, merge_weight=merge_weight, norm_gains=norm_gains, all_biases=all_biases)


norm_eps = 1e-06

@jax.custom_vjp
def low(v):
    return lax.optimization_barrier(v.astype(jnp.bfloat16)).astype(jnp.float32)

@jax.custom_vjp
def low_back(v):
    return v

def low_keep(v):
    return (low(v), None)

def low_pass(kept, grad):
    return (grad,)

def back_keep(v):
    return (v, None)

def back_low(kept, grad):
    return (low(grad),)
low.defvjp(low_keep, low_pass)
low_back.defvjp(back_keep, back_low)

def layer_norm(values_in, norm_gain, norm_shift):
    average = lax.optimization_barrier(jnp.mean(values_in, axis=1, keepdims=True))
    centred = values_in - average
    variance = lax.optimization_barrier(jnp.mean(centred * centred, axis=1, keepdims=True))
    return centred * lax.rsqrt(variance + norm_eps) * norm_gain[None, :, None] + norm_shift[None, :, None]

def frame_masks(side_values):
    places = jnp.arange(SIDE, dtype=jnp.int32)
    inside = (places[None, :] < side_values[:, None]).astype(jnp.float32)
    token_mask = (inside[:, :, None] * inside[:, None, :]).reshape(-1, 1, SIDE * SIDE)
    halves = jnp.arange(SIDE // 2, dtype=jnp.int32)
    inside_half = (halves[None, :] < (side_values // 2)[:, None]).astype(jnp.float32)
    key_mask = (inside_half[:, :, None] * inside_half[:, None, :]).reshape(-1, 1, QUARTER)
    return (token_mask, key_mask)

def cut_pieces(packed, lengths):
    pieces = []
    offset = 0
    for length in lengths:
        pieces.append(packed[offset:offset + length])
        offset = offset + length
    return pieces

def reduce_patches(channels):
    images = channels.shape[0]
    blocks = channels.reshape(images, D, SIDE // 2, 2, SIDE // 2, 2)
    return blocks.transpose(0, 3, 5, 1, 2, 4).reshape(images, 4 * D, QUARTER)

def merge_patches(channels):
    images = channels.shape[0]
    square = channels.reshape(images, D, SIDE, SIDE)
    padded = jnp.pad(square, ((0, 0), (0, 0), (1, 1), (1, 1)))
    pieces = [padded[:, :, row_off:row_off + SIDE:2, col_off:col_off + SIDE:2] for row_off in range(3) for col_off in range(3)]
    return jnp.stack(pieces, axis=1).reshape(images, 9 * D, QUARTER)

def depthwise(hidden, kernel):
    images = hidden.shape[0]
    square = hidden.reshape(images, FF, SIDE, SIDE)
    padded = jnp.pad(square, ((0, 0), (0, 0), (1, 1), (1, 1)))
    summed = jnp.zeros_like(square)
    for row_off in range(3):
        for col_off in range(3):
            summed = summed + kernel[:, row_off, col_off][None, :, None, None] * padded[:, :, row_off:row_off + SIDE, col_off:col_off + SIDE]
    return summed.reshape(images, FF, SIDE * SIDE)

def product(matrix, inputs):
    return jnp.einsum('oi,bit->bot', matrix, inputs, precision=lax.Precision.HIGHEST)

def attention(queries, keys_in, values_in, key_mask):
    images = queries.shape[0]
    query_heads = queries.reshape(images, HEADS, HEAD_DIM, -1)
    key_heads = keys_in.reshape(images, HEADS, HEAD_DIM, -1)
    value_heads = values_in.reshape(images, HEADS, HEAD_DIM, -1)
    scores = jnp.einsum('bhdq,bhdk->bhqk', query_heads, key_heads, precision=lax.Precision.HIGHEST)
    scores = low_back(scores * HEAD_DIM ** (-0.5) + jnp.where(key_mask[:, :, None, :] > 0, 0.0, -10000.0))
    softmax_weights = low(jax.nn.softmax(scores, axis=-1))
    attended = jnp.einsum('bhqk,bhdk->bhdq', softmax_weights, value_heads, precision=lax.Precision.HIGHEST)
    return low(low_back(attended.reshape(images, D, -1)))

def forward(weights, tokens_in, side_values):
    query_matrix, keyval_matrix, reduce_matrix, output_matrix, expand_matrix, depth_matrix, contract_matrix, merge_matrix, gain_pack, bias_pack = weights
    token_mask, key_mask = frame_masks(side_values)
    reduce_gain, first_gain, second_gain, section_gain, merge_gain = cut_pieces(gain_pack, [D, D, D, D, OUT_D])
    query_bias, reduce_bias, reduce_shift, output_bias, first_shift, second_shift, expand_bias, depth_bias, contract_bias, section_shift, merge_bias, merge_shift = cut_pieces(bias_pack, [D, D, D, D, D, D, FF, FF, D, D, OUT_D, OUT_D])
    entry_tokens = tokens_in * token_mask
    first_norm = low(layer_norm(entry_tokens, first_gain, first_shift))
    queries = low(low_back(product(query_matrix.reshape(D, D), first_norm) + query_bias[None, :, None]))
    reduced = low_back(product(reduce_matrix.reshape(D, 4 * D), reduce_patches(first_norm)) + reduce_bias[None, :, None])
    reduced = low(layer_norm(reduced, reduce_gain, reduce_shift))
    keyval = low(low_back(product(keyval_matrix.reshape(2 * D, D), reduced)))
    attended = attention(queries, keyval[:, :D], keyval[:, D:], key_mask)
    branch = low_back(product(output_matrix.reshape(D, D), attended) + output_bias[None, :, None])
    middle = entry_tokens + token_mask * branch
    second_norm = low(layer_norm(middle, second_gain, second_shift))
    hidden = low_back(product(expand_matrix.reshape(FF, D), second_norm) + expand_bias[None, :, None]) * token_mask
    convolved = depthwise(hidden, depth_matrix.reshape(FF, 3, 3)) + depth_bias[None, :, None]
    active = low(jax.nn.gelu(convolved, approximate=False))
    branch_two = low_back(product(contract_matrix.reshape(D, FF), active) + contract_bias[None, :, None])
    ending = middle + token_mask * branch_two
    sectioned = low(layer_norm(ending, section_gain, section_shift)) * token_mask
    merged = low_back(product(merge_matrix.reshape(OUT_D, 9 * D), merge_patches(sectioned)) + merge_bias[None, :, None])
    return layer_norm(merged, merge_gain, merge_shift) * key_mask

def reference(tokens, image_side, cotangent, query_weight, keyval_weight, reduce_weight, output_weight, expand_weight, depth_weight, contract_weight, merge_weight, norm_gains, all_biases):
    weights = tuple((member.astype(jnp.float32) for member in (query_weight, keyval_weight, reduce_weight, output_weight, expand_weight, depth_weight, contract_weight, merge_weight, norm_gains, all_biases)))
    groups = IMAGES // 4
    token_groups = tokens.astype(jnp.float32).reshape(groups, 4, D, SIDE * SIDE)
    side_groups = image_side.reshape(groups, 4)
    cot_groups = cotangent.astype(jnp.float32).reshape(groups, 4, OUT_D, QUARTER)

    def one_group(totals, inputs):
        token_block, side_block, cot_block = inputs

        def local_forward(params, token_part):
            return forward(params, token_part, side_block)
        outputs, pullback = jax.vjp(local_forward, weights, token_block)
        weight_grads, token_grads = pullback(cot_block)
        totals = tuple((total_now + grad_now for total_now, grad_now in zip(totals, weight_grads)))
        return (totals, (outputs.astype(jnp.bfloat16), token_grads))
    initial = tuple((jnp.zeros_like(member) for member in weights))
    totals, (outputs, token_grads) = lax.scan(one_group, initial, (token_groups, side_groups, cot_groups))
    return (outputs.reshape(IMAGES, OUT_D, QUARTER), token_grads.reshape(IMAGES, D, SIDE * SIDE), totals[0], totals[1], totals[2], totals[3], totals[4], totals[5], totals[6], totals[7], totals[8], totals[9])
```

```python
import functools

import jax
import jax.numpy as jnp
import numpy as np
from jax import lax
from jax.experimental import pallas as pl
from jax.experimental.pallas import tpu as pltpu
from jax.sharding import PartitionSpec as P

D = 320
HEADS = 5
FF = 1280
OUT_D = 512
SIDE = 32
HEAD_DIM = 64
QUARTER = 256
TOKENS = SIDE * SIDE
MERGE_PAD = 2944
SUPER = 32
FLIPS = (2, 4, 8, 16)
EPS = 1e-06
F32, BF16, I32 = jnp.float32, jnp.bfloat16, jnp.int32

B_Q, B_R, C_R, B_O, C_1, C_2, B_1, B_DW, B_2, C_S, B_M, C_M = 0, 5, 10, 15, 20, 25, 30, 50, 70, 75, 80, 88
G_R, G_1, G_2, G_S, G_M = 96, 101, 106, 111, 116

A_ROWS, B_ROWS, C_ROWS = 248, 208, 368
VMEM_LIMIT = 56 * 1024 * 1024

ERFC = (
    0.22567586600780487,
    0.22566913068294525,
    0.20784910023212433,
    0.16850189864635468,
    0.14156633615493774,
    -0.005866652354598045,
    0.1693696677684784,
    -0.18306706845760345,
    0.05030185356736183,
)


def slot_of(xor):
    return (xor >> 1) | ((xor & 1) << 4)


def xor_of(slot):
    return ((slot & 15) << 1) | (slot >> 4)


def dot(a, b):
    return jnp.dot(a, b, preferred_element_type=F32)


def dot_nt(a, b):
    return lax.dot_general(a, b, (((1,), (1,)), ((), ())), preferred_element_type=F32)


def dot_tn(a, b):
    return lax.dot_general(a, b, (((0,), (0,)), ((), ())), preferred_element_type=F32)


def iota(shape, axis):
    return lax.broadcasted_iota(I32, shape, axis)


def one_hot(test):
    return jnp.where(test, 1.0, 0.0).astype(BF16)


def lanes(index, width=128):
    return pl.ds(pl.multiple_of(index * width, width), width)


def loop(count, body):
    def step(index, carry):
        body(index)
        return carry

    lax.fori_loop(0, count, step, 0)


def column(table, start, count):
    return jnp.concatenate(
        [jnp.broadcast_to(table[:, h : h + 1], (64, 128)) for h in range(start, start + count)], axis=0
    )


def put_column(table, start, values):
    for h in range(values.shape[0] // 64):
        table[:, start + h : start + h + 1] = values[64 * h : 64 * h + 64, 0:1]


def token_place(lane):
    quad = lane >> 8
    row = 2 * ((lane >> 4) & 15) + (quad >> 1)
    col = 2 * (lane & 15) + (quad & 1)
    return row, col


def token_mask(tile, side, width=128):
    row, col = token_place(iota((1, width), 1) + tile * width)
    return jnp.where((row < side) & (col < side), 1.0, 0.0)


def key_place(index):
    return index >> 4, index & 15


def select_kernel(count, bases, exact, *refs):
    sources, (low_ref, high_ref), outs, (rows_ref,) = (
        refs[:count],
        refs[count : count + 2],
        refs[count + 2 : -1],
        refs[-1:],
    )
    half = rows_ref.shape[0] // 2
    rows_ref[...] = jnp.zeros_like(rows_ref)
    for source, base in zip(sources, bases):
        rows = source.shape[0]
        rows_ref[base : base + rows, :] = source[...].astype(F32)
    rows_ref[half:, :] = pltpu.roll(rows_ref[0:half, :], 64, 1)
    total = rows_ref[...]
    high = total.astype(BF16)
    pieces = [high]
    if exact:
        pieces.append((total - high.astype(F32)).astype(BF16))
    total_rows = low_ref.shape[0]
    place = iota((total_rows, 2 * half), 1)
    pick_low = one_hot(place == low_ref[...])
    pick_high = one_hot(place == high_ref[...])
    low = sum(dot(pick_low, piece) for piece in pieces)
    upper = sum(dot(pick_high, piece) for piece in pieces)
    chosen = jnp.where(iota((total_rows, 128), 1) < 64, low, upper)
    at = 0
    for out in outs:
        rows = out.shape[0]
        out[...] = chosen[at : at + rows, :].astype(out.dtype)
        at += -(-rows // 16) * 16


def select(sources, table, out_rows, dtype, exact, name):
    bases, at = [], 0
    for source in sources:
        bases.append(at)
        at += -(-source.shape[0] // 16) * 16
    half = at
    low, high = table(bases, half)
    total = sum(-(-rows // 16) * 16 for rows in out_rows)
    low = np.concatenate([low, np.full(total - len(low), -1)]).astype(np.int32)[:, None]
    high = np.concatenate([high, np.full(total - len(high), -1)]).astype(np.int32)[:, None]
    return pl.pallas_call(
        functools.partial(select_kernel, len(sources), tuple(bases), exact),
        out_shape=[jax.ShapeDtypeStruct((rows, 128), dtype) for rows in out_rows],
        scratch_shapes=[pltpu.VMEM((2 * half, 128), F32)],
        compiler_params=pltpu.CompilerParams(vmem_limit_bytes=VMEM_LIMIT),
        name=name,
    )(*sources, low, high)


def pair(half, low_src, high_src):
    low = -1 if low_src is None else low_src[0] + low_src[1] // 2 + half * (low_src[1] % 2)
    high = -1 if high_src is None else high_src[0] + high_src[1] // 2 + half * (1 - high_src[1] % 2)
    return low, high


def table_a(bases, half):
    q, o, kv, r, w2, small = bases
    rows = []
    for c in range(10):
        for row in range(24):
            if row < 10 and c < 8:
                base, first = ((q, 0), (o, 0), (kv, 0), (kv, 10))[c // 2]
                at = 5 * (first + row) + 2 * (c % 2)
                rows.append(pair(half, (base, at), (base, at + 1)))
            elif row < 10:
                if c == 8:
                    rows.append(pair(half, (q, 5 * row + 4), (o, 5 * row + 4)))
                else:
                    rows.append(pair(half, (kv, 5 * row + 4), (kv, 5 * (10 + row) + 4)))
            else:
                base, o_row = (r, row - 10) if row < 20 else (w2, row - 20)
                at = 20 * o_row + 2 * c
                rows.append(pair(half, (base, at), (base, at + 1)))
    for row in range(8):
        rows.append(pair(half, (small, 2 * row), (small, 2 * row + 1)) if row < 3 else (-1, -1))
    return np.array(rows).T


def table_b(bases, half):
    w2, w1, dw = bases
    rows = []
    for c in range(10):
        for row in range(8):
            at = 20 * (row + 4) + 2 * c
            rows.append(pair(half, (w2, at), (w2, at + 1)) if row < 6 else (-1, -1))
    for c in range(3):
        for row in range(40):
            at = 5 * row + 2 * c
            rows.append(pair(half, (w1, at), (w1, at + 1) if c < 2 else (dw, 2 * row + 1)))
    rows += [(-1, -1)] * 8
    return np.array(rows).T


def table_c(bases, half):
    (m,) = bases
    rows = []
    for c in range(23):
        for row in range(16):
            at = 45 * row + 2 * c
            rows.append(pair(half, (m, at), (m, at + 1) if c < 22 else None))
    return np.array(rows).T


def padded(rows):
    return rows + [(-1, -1)] * (-len(rows) % 16)


def table_out_a(bases, half):
    (a,) = bases

    def square(w, k):
        def source(at):
            row, piece = divmod(at, 5)
            first = w + (row // 10 if w == 2 else 0)
            row = row % 10
            if piece < 4:
                return (a + (2 * first + piece // 2) * 24 + row, piece % 2)
            return (a + (8 + first // 2) * 24 + row, first % 2)

        return [source(at) for at in range(k)]

    def wide(at):
        row, piece = divmod(at, 20)
        return (a + piece // 2 * 24 + 10 + row, piece % 2)

    def emit(sources):
        rows = [pair(half, s, t) for s, t in zip(sources[0::2], sources[1::2])]
        return padded(rows)

    rows = emit(square(0, 50)) + emit(square(1, 50)) + emit(square(2, 100)) + emit([wide(at) for at in range(200)])
    return np.array(rows).T


def table_out_b(bases, half):
    a, b = bases

    def w2(at):
        row, piece = divmod(at, 20)
        if row < 4:
            return (a + piece // 2 * 24 + 20 + row, piece % 2)
        return (b + piece // 2 * 8 + row - 4, piece % 2)

    def w1(at):
        row, piece = divmod(at, 5)
        return (b + 80 + piece // 2 * 40 + row, piece % 2)

    rows = []
    for source in (w2, w1):
        sources = [source(at) for at in range(200)]
        rows += padded([pair(half, s, t) for s, t in zip(sources[0::2], sources[1::2])])
    return np.array(rows).T


def table_out_c(bases, half):
    (c,) = bases

    def source(at):
        row, piece = divmod(at, 45)
        return (c + piece // 2 * 16 + row, piece % 2)

    sources = [source(at) for at in range(720)]
    return np.array(padded([pair(half, s, t) for s, t in zip(sources[0::2], sources[1::2])])).T


def split_ten(row, per, magic):
    owner = (row * magic) >> 16
    return owner, row - per * owner


def place_ten(row, me, stride, shift):
    owner, rest = split_ten(row, 10, 6554)
    return slot_of(owner ^ me) * stride + shift + rest


def place_kv(row, me, upper):
    owner, rest = split_ten(row, 20, 3277)
    inside = (rest >= 10) if upper else (rest < 10)
    return jnp.where(inside, slot_of(owner ^ me) * 24 + rest - (10 if upper else 0), -1)


def place_forty(row, me):
    owner, rest = split_ten(row, 40, 1639)
    return slot_of(owner ^ me) * 40 + rest


def norm(values, gain, shift):
    mean = jnp.mean(values, axis=0, keepdims=True)
    centred = values - mean
    rstd = lax.rsqrt(jnp.mean(centred * centred, axis=0, keepdims=True) + EPS)
    return centred * rstd * gain + shift, mean, rstd


def norm_back(grad, hat, rstd, gain):
    scaled = grad * gain
    return rstd * (
        scaled
        - jnp.mean(scaled, axis=0, keepdims=True)
        - hat * jnp.mean(scaled * hat, axis=0, keepdims=True)
    )


def stat_rows(mean, rstd):
    row = iota((8, mean.shape[1]), 0)
    return jnp.where(row == 0, mean, jnp.where(row == 1, rstd, 0.0))


def entry_kernel(scal, tokens, entry, stats):
    side = scal[1]
    for quad in range(4):
        lane = iota((1, 256), 1) + quad * 256
        row, col = token_place(lane)
        natural = row * SIDE + col
        pick = one_hot(iota((TOKENS, 256), 0) == natural)
        mask = jnp.where((row < side) & (col < side), 1.0, 0.0)
        entry[:, quad * 256 : quad * 256 + 256] = (dot(tokens[...], pick) * mask).astype(BF16)

    def body(tile):
        values = entry[:, lanes(tile)].astype(F32)
        mean = jnp.mean(values, axis=0, keepdims=True)
        centred = values - mean
        rstd = lax.rsqrt(jnp.mean(centred * centred, axis=0, keepdims=True) + EPS)
        stats[:, lanes(tile)] = stat_rows(mean, rstd)

    loop(8, body)


def small_table(me, low, high):
    gathered = jnp.concatenate(
        [half[:, 240:248, :].astype(F32).reshape(128, 128) for half in (low, high)], axis=0
    ).astype(BF16)
    vector = iota((128, 256), 0)
    place = iota((128, 256), 1)
    row = place & 7
    owner = xor_of(place >> 3) ^ me
    first = (7 * owner) >> 3
    straight = (
        ((row == 0) & (vector == 3 * owner))
        | ((row == 1) & (vector == 3 * owner + 2))
        | ((row == 2) & (vector == 96 + first))
    )
    turned = ((row == 0) & (vector == 3 * owner + 1)) | ((row == 2) & (vector == 97 + first))
    rows = dot(one_hot(straight), gathered) + pltpu.roll(dot(one_hot(turned), gathered), 64, 1)
    return jnp.transpose(rows)[0:64, :]


def project_kernel(scal, low, high, entry, stats, wq, wkv, wr, wo, first, qs, raw, stat_r, red, kv, kt, vt, bt, gath, redin):
    me = scal[0]
    bt[...] = small_table(me, low, high)
    for half, source in enumerate((low, high)):
        for p in range(5):
            block = source[:, 48 * p : 48 * p + 48, :].astype(F32).reshape(16, 2, 24, 128)
            for e in range(2):
                c = 2 * p + e
                gath[384 * half : 384 * half + 384, 128 * c : 128 * c + 128] = (
                    block[:, e].reshape(384, 128).astype(BF16)
                )
    row = iota((D, 1), 0)
    place = iota((D, 768), 1)
    wr[...] = dot(one_hot(place == place_ten(row, me, 24, 10)), gath[...]).astype(BF16)
    pick = one_hot(place == place_ten(row, me, 24, 0))
    both = dot(pick, gath[:, 0:512])
    wq[:, 0:256] = both[:, 0:256].astype(BF16)
    wo[:, 0:256] = both[:, 256:512].astype(BF16)
    tail = dot(pick, gath[:, 1024:1152])
    wq[:, 256:320] = tail[:, 0:64].astype(BF16)
    wo[:, 256:320] = pltpu.roll(tail, 64, 1)[:, 0:64].astype(BF16)
    row = iota((2 * D, 1), 0)
    place = iota((2 * D, 768), 1)
    lower = one_hot(place == place_kv(row, me, False))
    upper = one_hot(place == place_kv(row, me, True))
    wkv[:, 0:256] = (dot(lower, gath[:, 512:768]) + dot(upper, gath[:, 768:1024])).astype(BF16)
    tail = dot(lower, gath[:, 1152:1280])[:, 0:64] + pltpu.roll(dot(upper, gath[:, 1152:1280]), 64, 1)[:, 0:64]
    wkv[:, 256:320] = tail.astype(BF16)

    gain, shift = column(bt, G_1, 5), column(bt, C_1, 5)

    def body(tile):
        centred = entry[:, lanes(tile)].astype(F32) - stats[0:1, lanes(tile)]
        first[:, lanes(tile)] = (centred * stats[1:2, lanes(tile)] * gain + shift).astype(BF16)

    loop(8, body)
    for quad in range(4):
        redin[D * quad : D * quad + D, :] = first[:, 256 * quad : 256 * quad + 256]
    bias = column(bt, B_R, 5)
    bias = jnp.concatenate([bias, bias], axis=1)
    raw[...] = dot(wr[...], redin[...]) + bias
    gain, shift = column(bt, G_R, 5), column(bt, C_R, 5)
    for tile in range(2):
        at = slice(128 * tile, 128 * tile + 128)
        values, mean, rstd = norm(raw[:, at], gain, shift)
        red[:, at] = values.astype(BF16)
        stat_r[:, at] = stat_rows(mean, rstd)
    keyval = dot(wkv[...], red[...])
    kv[...] = keyval.astype(BF16)
    turned = jnp.transpose(keyval)
    for h in range(HEADS):
        kt[h] = turned[:, 64 * h : 64 * h + 64].astype(BF16)
        vt[h] = turned[:, D + 64 * h : D + 64 * h + 64].astype(BF16)
    bias = column(bt, B_Q, 5)
    bias = jnp.concatenate([bias, bias], axis=1)
    for quad in range(4):
        at = slice(256 * quad, 256 * quad + 256)
        qs[:, at] = (dot(wq[...], first[:, at]) + bias).astype(BF16) * BF16(0.125)


def key_bias(side):
    i, j = key_place(iota((QUARTER, 1), 0))
    return jnp.where((i < (side >> 1)) & (j < (side >> 1)), 0.0, -10000.0)


def attend_kernel(scal, kt, qs, kv, att, lse):
    bias = key_bias(scal[1])
    lse[...] = jnp.zeros_like(lse)
    for h in range(HEADS):
        rows = slice(64 * h, 64 * h + 64)
        for quad in range(4):
            at = slice(256 * quad, 256 * quad + 256)
            scores = dot(kt[h], qs[rows, at]) + bias
            top = jnp.max(scores, axis=0, keepdims=True)
            weights = jnp.exp(scores - top)
            total = jnp.sum(weights, axis=0, keepdims=True)
            lse[h : h + 1, at] = top + jnp.log(total)
            probs = (weights * (1.0 / total)).astype(BF16)
            att[rows, at] = dot(kv[D + 64 * h : D + 64 * h + 64, :], probs).astype(BF16)


def middle_kernel(scal, bt, wo, att, entry, mid, sec, stats, work):
    side = scal[1]
    work[...] = dot(wo[...], att[...])
    bias, gain, shift = column(bt, B_O, 5), column(bt, G_2, 5), column(bt, C_2, 5)

    def body(tile):
        at = lanes(tile)
        mask = token_mask(tile, side)
        values = entry[:, at].astype(F32) + mask * (work[:, at] + bias)
        mid[:, at] = values
        normed, mean, rstd = norm(values, gain, shift)
        stats[:, at] = stat_rows(mean, rstd)
        sec[0:D, at] = (normed.astype(BF16).astype(F32) * mask).astype(BF16)
        sec[D : D + 64, at] = jnp.where(iota((64, 128), 0) == 9, mask, 0.0).astype(BF16)

    loop(8, body)


def ffn_weights_kernel(scal, bt, a_low, a_high, b_low, b_high, w1, w1t, w2, w2t, kd, ga, gb, g1):
    me = scal[0]
    for half, (a, b) in enumerate(((a_low, b_low), (a_high, b_high))):
        for p in range(5):
            block = a[:, 48 * p : 48 * p + 48, :].astype(F32).reshape(16, 2, 24, 128)
            other = b[:, 16 * p : 16 * p + 16, :].astype(F32).reshape(16, 2, 8, 128)
            for e in range(2):
                c = 2 * p + e
                at = slice(128 * c, 128 * c + 128)
                ga[128 * half : 128 * half + 128, at] = block[:, e, 16:24].reshape(128, 128).astype(BF16)
                gb[128 * half : 128 * half + 128, at] = other[:, e].reshape(128, 128).astype(BF16)
        rest = b[:, 80:208, :].astype(F32)
        for c in range(3):
            g1[640 * half : 640 * half + 640, 128 * c : 128 * c + 128] = (
                rest[:, 40 * c : 40 * c + 40].reshape(640, 128).astype(BF16)
            )
    row = iota((D, 1), 0)
    place = iota((D, 256), 1)
    owner, rest = split_ten(row, 10, 6554)
    at = slot_of(owner ^ me) * 8
    in_a = one_hot(place == jnp.where(rest < 4, at + 4 + rest, -1))
    in_b = one_hot(place == jnp.where(rest >= 4, at + rest - 4, -1))
    full = dot(in_a, ga[...]) + dot(in_b, gb[...])
    w2[...] = full.astype(BF16)
    w2t[...] = jnp.transpose(full).astype(BF16)
    row = iota((FF, 1), 0)
    full = dot(one_hot(iota((FF, FF), 1) == place_forty(row, me)), g1[...])
    w1t[...] = jnp.transpose(full[:, 0:D]).astype(BF16)
    w1[:, 0:256] = full[:, 0:256].astype(BF16)
    tail = full[:, 256:384]
    lane = iota((FF, 128), 1)
    kd[...] = jnp.where(lane < 9, pltpu.roll(tail, 64, 1), jnp.where(lane == 9, column(bt, B_DW, 20), 0.0))
    w1[:, 256:384] = jnp.where(lane < 64, tail, jnp.where(lane == 73, column(bt, B_1, 20), 0.0)).astype(BF16)


def edge_masks():
    i, j = key_place(iota((1, 256), 1))
    return tuple(
        jnp.where(test, 1.0, 0.0) for test in (i != 0, i != 15, j != 0, j != 15)
    )


def from_before(values, step, mask):
    return pltpu.roll(values, step, 1) * mask


def from_after(values, step, mask):
    return pltpu.roll(values, 256 - step, 1) * mask


def gelu_parts(x):
    z = jnp.abs(x) * np.float32(0.4 * 0.5**0.5) + 1.0
    t = 1.0 / z
    poly = jnp.full_like(t, np.float32(0.5 * ERFC[8]))
    for coefficient in ERFC[7::-1]:
        poly = poly * t + np.float32(0.5 * coefficient)
    bell = jnp.exp(x * x * -0.5)
    tail = poly * t * bell
    cdf = jnp.where(x < 0, tail, 1.0 - tail)
    return x * cdf, cdf + x * bell * np.float32(1.0 / np.sqrt(2.0 * np.pi))


def ffn_kernel(scal, bt, w1, kd, sec, w2, mid, act, slope, end, sect, stats, hid, acc):
    side = scal[1]
    step = pl.program_id(0)
    hid[...] = dot(w1[...], sec[...])
    i_first, i_last, j_first, j_last = edge_masks()

    def conv(group):
        rows = pl.ds(pl.multiple_of(group * 8, 8), 8)
        taps = kd[rows, :]
        k = [jnp.broadcast_to(taps[:, n : n + 1], (8, 256)) for n in range(10)]
        quad = [[hid[rows, 256 * (2 * a + e) : 256 * (2 * a + e) + 256] for e in range(2)] for a in range(2)]
        cols = []
        for a in range(2):
            left = from_before(quad[a][1], 1, j_first)
            right = from_after(quad[a][0], 1, j_last)
            cols.append(((left, quad[a][0], quad[a][1]), (quad[a][0], quad[a][1], right)))

        def across(a, e, row):
            c = cols[a][e]
            return k[3 * row] * c[0] + k[3 * row + 1] * c[1] + k[3 * row + 2] * c[2]

        for e in range(2):
            top = across(0, e, 1) + across(1, e, 2) + k[9] + from_before(across(1, e, 0), 16, i_first)
            low = across(0, e, 0) + across(1, e, 1) + k[9] + from_after(across(0, e, 2), 16, i_last)
            hid[rows, 256 * e : 256 * e + 256] = top
            hid[rows, 512 + 256 * e : 512 + 256 * e + 256] = low

    loop(32, conv)

    def gelu(group):
        rows = pl.ds(pl.multiple_of(group * 16, 16), 16)
        for part in range(4):
            at = slice(256 * part, 256 * part + 256)
            value, grad = gelu_parts(hid[rows, at])
            act[rows, at] = value.astype(BF16)
            slope[rows, at] = grad.astype(BF16)

    loop(16, gelu)
    product = dot(w2[...], act[...])

    @pl.when(step == 0)
    def _():
        acc[...] = product

    @pl.when(step > 0)
    def _():
        acc[...] += product

    @pl.when(step == 4)
    def _():
        bias, gain, shift = column(bt, B_2, 5), column(bt, G_S, 5), column(bt, C_S, 5)

        def body(tile):
            at = lanes(tile)
            mask = token_mask(tile, side)
            values = mid[:, at] + mask * (acc[:, at] + bias)
            end[:, at] = values
            normed, mean, rstd = norm(values, gain, shift)
            stats[:, at] = stat_rows(mean, rstd)
            sect[:, at] = (normed.astype(BF16).astype(F32) * mask).astype(BF16)

        loop(8, body)


def lane_sum(values):
    return jnp.sum(values, axis=1, keepdims=True)


def merge_kernel(scal, bt, c_low, c_high, sect, end, stats, cot, four, keep, send, end_grad, branch, grads, wm, patch, mg, back, work):
    me, side = scal[0], scal[1]
    grads[...] = jnp.zeros_like(grads)
    for half, source in enumerate((c_low, c_high)):

        def place_at(slot, half=half, source=source):
            owner = ((slot << 1) | half) ^ me
            at = pl.ds(pl.multiple_of(owner * 16, 16), 16)
            for c in range(23):
                wm[at, 128 * c : 128 * c + 128] = source[slot, 16 * c : 16 * c + 16, :]

        loop(16, place_at)
    i_first, i_last, j_first, j_last = edge_masks()
    quad = [[sect[:, 256 * (2 * a + e) : 256 * (2 * a + e) + 256] for e in range(2)] for a in range(2)]
    left = [from_before(quad[a][1].astype(F32), 1, j_first) for a in range(2)]
    pieces = (
        from_before(left[1], 16, i_first).astype(BF16),
        from_before(quad[1][0].astype(F32), 16, i_first).astype(BF16),
        from_before(quad[1][1].astype(F32), 16, i_first).astype(BF16),
        left[0].astype(BF16),
        quad[0][0],
        quad[0][1],
        left[1].astype(BF16),
        quad[1][0],
        quad[1][1],
    )
    for n, piece in enumerate(pieces):
        patch[D * n : D * n + D, :] = piece
    patch[9 * D :, :] = jnp.zeros((MERGE_PAD - 9 * D, 256), BF16)
    bias, gain, shift = column(bt, B_M, 8), column(bt, G_M, 8), column(bt, C_M, 8)
    work[...] = dot(wm[...], patch[...])
    half_side = side >> 1
    for tile in range(2):
        at = slice(128 * tile, 128 * tile + 128)
        i, j = key_place(iota((1, 128), 1) + 128 * tile)
        mask = jnp.where((i < half_side) & (j < half_side), 1.0, 0.0)
        values = work[:, at] + bias
        mean = jnp.mean(values, axis=0, keepdims=True)
        centred = values - mean
        rstd = lax.rsqrt(jnp.mean(centred * centred, axis=0, keepdims=True) + EPS)
        hat = centred * rstd
        four[:, at] = ((hat * gain + shift) * mask).astype(BF16)
        grad = cot[:, at].astype(F32) * mask
        low = norm_back(grad, hat, rstd, gain).astype(BF16)
        mg[:, at] = low
        if tile == 0:
            sums = [grad * hat, grad, low.astype(F32)]
        else:
            sums = [s + v for s, v in zip(sums, (grad * hat, grad, low.astype(F32)))]
    put_column(grads, G_M, lane_sum(sums[0]))
    put_column(grads, C_M, lane_sum(sums[1]))
    put_column(grads, B_M, lane_sum(sums[2]))
    back[...] = dot_tn(wm[...], mg[...])

    def piece(n):
        return back[D * n : D * n + D, :]

    work_quads = (
        piece(4),
        piece(5) + from_after(piece(3), 1, j_last),
        piece(7) + from_after(piece(1), 16, i_last),
        piece(8)
        + from_after(piece(6), 1, j_last)
        + from_after(piece(2) + from_after(piece(0), 1, j_last), 16, i_last),
    )
    for n, values in enumerate(work_quads):
        end_grad[:, 256 * n : 256 * n + 256] = values
    gain = column(bt, G_S, 5)
    zeros = jnp.zeros((D, 128), F32)

    def body(tile, carry):
        at = lanes(tile)
        mask = token_mask(tile, side)
        grad = end_grad[:, at] * mask
        hat = (end[:, at] - stats[0:1, at]) * stats[1:2, at]
        result = norm_back(grad, hat, stats[1:2, at], gain)
        end_grad[:, at] = result
        low = (result * mask).astype(BF16)
        branch[:, at] = low
        return carry[0] + grad * hat, carry[1] + grad, carry[2] + low.astype(F32)

    sums = lax.fori_loop(0, 8, body, (zeros, zeros, zeros))
    put_column(grads, G_S, lane_sum(sums[0]))
    put_column(grads, C_S, lane_sum(sums[1]))
    put_column(grads, B_2, lane_sum(sums[2]))
    for c in range(23):
        work2 = dot_nt(mg[...], patch[128 * c : 128 * c + 128, :])
        back[0:512, 0:128] = work2

        def give(slot, c=c):
            for half, out in enumerate((keep, send)):
                owner = ((slot << 1) | half) ^ me
                at = pl.ds(pl.multiple_of(owner * 16, 16), 16)
                out[slot, 16 * c : 16 * c + 16, :] = back[at, 0:128].astype(BF16)

        loop(16, give)


def ffn_back_kernel(scal, bt, w1, w1t, w2t, kd, sec, act, slope, branch, end_grad, mid, stats, dw1, dw2, dkx, mid_grad, low_grad, grads, hid, cg, hg, acc):
    side = scal[1]
    step = pl.program_id(0)
    cg[...] = dot(w2t[...], branch[...])
    dw2[...] = dot_nt(branch[...], act[...]).astype(BF16)
    hid[...] = dot(w1[...], sec[...])
    i_first, i_last, j_first, j_last = edge_masks()

    def scale(group):
        rows = pl.ds(pl.multiple_of(group * 16, 16), 16)
        cg[rows, :] = cg[rows, :] * slope[rows, :].astype(F32)

    loop(16, scale)
    lane = iota((8, 128), 1)

    def conv(group):
        rows = pl.ds(pl.multiple_of(group * 8, 8), 8)
        taps = kd[rows, :]
        k = [jnp.broadcast_to(taps[:, n : n + 1], (8, 256)) for n in range(9)]
        quad = [[cg[rows, 256 * (2 * a + e) : 256 * (2 * a + e) + 256] for e in range(2)] for a in range(2)]
        bias = lane_sum(quad[0][0] + quad[0][1] + quad[1][0] + quad[1][1])
        across = [
            (
                (from_before(quad[a][1], 1, j_first), quad[a][0], quad[a][1]),
                (quad[a][0], quad[a][1], from_after(quad[a][0], 1, j_last)),
            )
            for a in range(2)
        ]
        sums = [None] * 9
        for e in range(2):
            lower = [from_before(v, 16, i_first) for v in across[1][e]]
            upper = [from_after(v, 16, i_last) for v in across[0][e]]
            for a, near in ((0, (lower, across[0][e], across[1][e])), (1, (across[0][e], across[1][e], upper))):
                at = slice(256 * (2 * a + e), 256 * (2 * a + e) + 256)
                value = hid[rows, at]
                total = None
                for r in range(3):
                    for c in range(3):
                        tap = 3 * (2 - r) + (2 - c)
                        part = k[tap] * near[r][c]
                        total = part if total is None else total + part
                        part = value * near[r][c]
                        sums[tap] = part if sums[tap] is None else sums[tap] + part
                hid[rows, at] = total
        block = jnp.where(lane == 9, bias, 0.0)
        for tap in range(9):
            block = jnp.where(lane == tap, lane_sum(sums[tap]), block)
        dkx[rows, :] = block

    loop(32, conv)
    mask = [token_mask(quad, side, 256) for quad in range(4)]

    def finish(group):
        rows = pl.ds(pl.multiple_of(group * 16, 16), 16)
        total = None
        for quad in range(4):
            at = slice(256 * quad, 256 * quad + 256)
            low = (hid[rows, at] * mask[quad]).astype(BF16)
            hg[rows, at] = low
            total = low.astype(F32) if total is None else total + low.astype(F32)
        block = dkx[rows, :]
        dkx[rows, :] = jnp.where(iota((16, 128), 1) == 10, lane_sum(total), block)

    loop(16, finish)
    dw1[:, 0:256] = dot_nt(hg[...], sec[0:256, :]).astype(BF16)
    tail = dot_nt(hg[...], sec[256:384, :])
    lane_all = iota((256, 128), 1)
    turned = pltpu.roll(dkx[...], 64, 1)
    dw1[:, 256:384] = jnp.where(lane_all < 64, tail, jnp.where(lane_all < 73, turned, 0.0)).astype(BF16)
    product = dot(w1t[...], hg[...])

    @pl.when(step == 0)
    def _():
        acc[...] = product

    @pl.when(step > 0)
    def _():
        acc[...] += product

    @pl.when(step == 4)
    def _():
        grads[...] = jnp.zeros_like(grads)
        gain = column(bt, G_2, 5)
        zeros = jnp.zeros((D, 128), F32)

        def body(tile, carry):
            at = lanes(tile)
            mask = token_mask(tile, side)
            grad = acc[:, at]
            hat = (mid[:, at] - stats[0:1, at]) * stats[1:2, at]
            result = end_grad[:, at] + norm_back(grad, hat, stats[1:2, at], gain)
            mid_grad[:, at] = result
            low = (result * mask).astype(BF16)
            low_grad[:, at] = low
            return carry[0] + grad * hat, carry[1] + grad, carry[2] + low.astype(F32)

        sums = lax.fori_loop(0, 8, body, (zeros, zeros, zeros))
        put_column(grads, G_2, lane_sum(sums[0]))
        put_column(grads, C_2, lane_sum(sums[1]))
        put_column(grads, B_O, lane_sum(sums[2]))


def store_pairs(values, height, keep, send):
    for p in range(5):
        both = [values[:, 128 * (2 * p + e) : 128 * (2 * p + e) + 128].reshape(32, 1, height, 128) for e in range(2)]
        block = jnp.concatenate(both, axis=1).reshape(32, 2 * height, 128).astype(BF16)
        at = slice(2 * height * p, 2 * height * p + 2 * height)
        keep[:, at, :] = block[0:16]
        send[:, at, :] = block[16:32]


def pack_b_kernel(scal, dw1, dw2, keep, send):
    me = scal[0]
    owner, rest = split_ten(iota((1, D), 1), 10, 6554)
    at = jnp.where(rest >= 4, slot_of(owner ^ me) * 8 + rest - 4, -1)
    store_pairs(dot(one_hot(iota((256, D), 0) == at), dw2[...]), 8, keep, send)
    at = place_forty(iota((1, FF), 1), me)
    blocks = dot(one_hot(iota((FF, FF), 0) == at), dw1[...])
    parts = [blocks[:, 128 * c : 128 * c + 128].reshape(32, 40, 128) for c in range(3)]
    parts.append(jnp.zeros((32, 8, 128), F32))
    block = jnp.concatenate(parts, axis=1).astype(BF16)
    keep[:, 80:208, :] = block[0:16]
    send[:, 80:208, :] = block[16:32]


def attend_back_kernel(scal, kt, vt, qs, kv, wo, low_grad, att, lse, dwo, dq, dkv, og):
    bias = key_bias(scal[1])
    dwo[...] = dot_nt(low_grad[...], att[...]).astype(BF16)
    og[...] = dot_tn(wo[...], low_grad[...]).astype(BF16)
    for h in range(HEADS):
        rows = slice(64 * h, 64 * h + 64)
        dk = jnp.zeros((64, 256), F32)
        dv = jnp.zeros((64, 256), F32)
        for quad in range(4):
            at = slice(256 * quad, 256 * quad + 256)
            probs = jnp.exp(dot(kt[h], qs[rows, at]) + bias - lse[h : h + 1, at])
            grad = dot(vt[h], og[rows, at])
            mean = jnp.sum(probs * grad, axis=0, keepdims=True)
            score = (probs * (grad - mean)).astype(BF16)
            dq[rows, at] = (dot(kv[rows, :], score) * 0.125).astype(BF16)
            dk += dot_nt(qs[rows, at], score)
            dv += dot_nt(og[rows, at], probs.astype(BF16))
        dkv[rows, :] = dk.astype(BF16)
        dkv[D + 64 * h : D + 64 * h + 64, :] = dv.astype(BF16)


def first_kernel(scal, bt, wq, wkv, wr, first, red, raw, stat_r, dq, dkv, dwo, dw2, dkx, mid_grad, entry, stats, g_one, g_two, tok, keep, send, grads, work, wide, redin):
    me, side = scal[0], scal[1]
    grads[...] = g_one[...] + g_two[...]
    for m in range(20):
        block = dkx[64 * m : 64 * m + 64, :]
        grads[:, B_1 + m : B_1 + m + 1] = block[:, 10:11]
        grads[:, B_DW + m : B_DW + m + 1] = block[:, 9:10]
    for quad in range(4):
        redin[D * quad : D * quad + D, :] = first[:, 256 * quad : 256 * quad + 256]
    dred = dot_tn(wkv[...], dkv[...])
    gain = column(bt, G_R, 5)
    lows = []
    for tile in range(2):
        at = slice(128 * tile, 128 * tile + 128)
        grad = dred[:, at]
        hat = (raw[:, at] - stat_r[0:1, at]) * stat_r[1:2, at]
        low = norm_back(grad, hat, stat_r[1:2, at], gain).astype(BF16)
        lows.append(low)
        parts = (grad * hat, grad, low.astype(F32))
        sums = parts if tile == 0 else [s + v for s, v in zip(sums, parts)]
    put_column(grads, G_R, lane_sum(sums[0]))
    put_column(grads, C_R, lane_sum(sums[1]))
    put_column(grads, B_R, lane_sum(sums[2]))
    low = jnp.concatenate(lows, axis=1)
    wide[...] = dot_tn(wr[...], low)
    for quad in range(4):
        at = slice(256 * quad, 256 * quad + 256)
        work[:, at] = dot_tn(wq[...], dq[:, at]) + wide[D * quad : D * quad + D, :]
    gain = column(bt, G_1, 5)
    zeros = jnp.zeros((D, 128), F32)

    def body(tile, carry):
        at = lanes(tile)
        grad = work[:, at]
        hat = (entry[:, at].astype(F32) - stats[0:1, at]) * stats[1:2, at]
        result = mid_grad[:, at] + norm_back(grad, hat, stats[1:2, at], gain)
        work[:, at] = result * token_mask(tile, side)
        return carry[0] + grad * hat, carry[1] + grad, carry[2] + dq[:, at].astype(F32)

    sums = lax.fori_loop(0, 8, body, (zeros, zeros, zeros))
    put_column(grads, G_1, lane_sum(sums[0]))
    put_column(grads, C_1, lane_sum(sums[1]))
    put_column(grads, B_Q, lane_sum(sums[2]))
    high = work[...].astype(BF16)
    rest = (work[...] - high.astype(F32)).astype(BF16)
    row, col = token_place(iota((TOKENS, 1), 0))
    natural = row * SIDE + col
    for quad in range(4):
        pick = one_hot(iota((TOKENS, 256), 1) + 256 * quad == natural)
        tok[:, 256 * quad : 256 * quad + 256] = dot(high, pick) + dot(rest, pick)
    dwq = dot_nt(dq[...], first[...]).astype(BF16)
    dwkv = dot_nt(dkv[...], red[...]).astype(BF16)
    dwr = dot_nt(low, redin[...]).astype(BF16)
    lane = iota((1, D), 1)
    height = iota((768, D), 0)
    at_o = one_hot(height == place_ten(lane, me, 24, 0))
    at_r = one_hot(height == place_ten(lane, me, 24, 10))
    owner, rest = split_ten(lane, 10, 6554)
    at_w = one_hot(height == jnp.where(rest < 4, slot_of(owner ^ me) * 24 + 20 + rest, -1))
    lane = iota((1, 2 * D), 1)
    height = iota((768, 2 * D), 0)
    at_low = one_hot(height == place_kv(lane, me, False))
    at_high = one_hot(height == place_kv(lane, me, True))
    dwo_all = dwo[...]
    zq = dot(at_o, dwq)
    zo = dot(at_o, dwo_all)
    zl = dot(at_low, dwkv)
    zh = dot(at_high, dwkv)
    tails = jnp.concatenate(
        [
            jnp.concatenate([zq[:, 256:320], zo[:, 256:320]], axis=1),
            jnp.concatenate([zl[:, 256:320], zh[:, 256:320]], axis=1),
        ],
        axis=1,
    )
    ten = jnp.concatenate([zq[:, 0:256], zo[:, 0:256], zl[:, 0:256], zh[:, 0:256], tails], axis=1)
    store_pairs(ten + dot(at_r, dwr) + dot(at_w, dw2[...]), 24, keep, send)
    rows = jnp.transpose(jnp.concatenate([grads[...], jnp.zeros((64, 128), F32)], axis=0)).astype(BF16)
    place = iota((256, 128), 0)
    vector = iota((256, 128), 1)
    line = place & 7
    owner = xor_of(place >> 3) ^ me
    start = (7 * owner) >> 3
    straight = (
        ((line == 0) & (vector == 3 * owner))
        | ((line == 1) & (vector == 3 * owner + 2))
        | ((line == 2) & (vector == 96 + start))
    )
    turned = ((line == 0) & (vector == 3 * owner + 1)) | ((line == 2) & (vector == 97 + start))
    small = dot(one_hot(straight), rows) + pltpu.roll(dot(one_hot(turned), rows), 64, 1)
    small = small.reshape(32, 8, 128).astype(BF16)
    keep[:, 240:248, :] = small[0:16]
    send[:, 240:248, :] = small[16:32]


def call(kernel, args, outs, scratch=(), grid=None, in_specs=None, out_specs=None, name=None):
    specs = {}
    if in_specs is None:
        in_specs = [pl.BlockSpec(memory_space=pltpu.SMEM)] + [pl.BlockSpec(memory_space=pltpu.VMEM)] * (len(args) - 1)
    specs["in_specs"] = in_specs
    if out_specs is not None:
        specs["out_specs"] = out_specs
    if grid is not None:
        specs["grid"] = grid
    return pl.pallas_call(
        kernel,
        out_shape=[jax.ShapeDtypeStruct(shape, dtype) for shape, dtype in outs],
        scratch_shapes=[pltpu.VMEM(shape, dtype) for shape, dtype in scratch],
        compiler_params=pltpu.CompilerParams(vmem_limit_bytes=VMEM_LIMIT),
        name=name,
        **specs,
    )(*args)


def whole(shape):
    return pl.BlockSpec(shape, lambda *_: (0,) * len(shape))


def local(group, axes, tokens, image_side, cotangent, *shards):
    index = lax.axis_index(axes[0]) * lax.axis_size(axes[1]) + lax.axis_index(axes[1])
    me = index // group
    devices = SUPER * group

    def flip(values, mask):
        pairs = [(i, ((i // group) ^ mask) * group + i % group) for i in range(devices)]
        return lax.ppermute(values, axes, pairs)

    def gather(block):
        held = block[None]
        for mask in FLIPS:
            held = jnp.concatenate([held, flip(held, mask)], axis=0)
        return held, flip(held, 1)

    def scatter(keep, send):
        held = keep.astype(F32) + flip(send, 1).astype(F32)
        for mask in FLIPS[::-1]:
            held = held.astype(BF16)
            half = held.shape[0] // 2
            held = held[:half].astype(F32) + flip(held[half:], mask).astype(F32)
        return held[0]

    if group > 1:
        per = lax.axis_size(axes[1])
        start = (index % per) // group * group

        def join(shard):
            full = lax.all_gather(shard, axes[1], axis=0)
            return lax.dynamic_slice_in_dim(full, start, group, axis=0).reshape(-1)

        shards = [join(shard) for shard in shards]
    query, keyval, reduce_w, output, expand, depth, contract, merge, gains, biases = shards

    def rows(flat):
        return flat.reshape(-1, 128)

    spot = (56 * me) % 64
    placed = lax.dynamic_update_slice(jnp.zeros((128,), BF16), gains, (spot,))
    small = rows(jnp.concatenate([biases, jnp.zeros((64,), BF16), placed]))
    taps = jnp.pad(depth.reshape(40, 9), ((0, 0), (64, 55)))
    (block_a,) = select(
        [rows(query), rows(output), rows(keyval), rows(reduce_w), rows(contract), small],
        table_a, [A_ROWS], BF16, False, "pack_a",
    )
    (block_b,) = select([rows(contract), rows(expand), taps], table_b, [B_ROWS], BF16, False, "pack_b")
    (block_c,) = select([rows(merge)], table_c, [C_ROWS], BF16, False, "pack_c")
    a_low, a_high = gather(block_a)
    b_low, b_high = gather(block_b)
    c_low, c_high = gather(block_c)

    scal = jnp.stack([me.astype(I32), image_side[0].astype(I32)])
    big, narrow = (D, TOKENS), (D, QUARTER)
    entry, stats_1 = call(entry_kernel, (scal, tokens[0]), [(big, BF16), ((8, TOKENS), F32)], name="entry")
    wq, wkv, wr, wo, first, qs, raw, stat_r, red, kv, kt, vt, bt = call(
        project_kernel,
        (scal, a_low, a_high, entry, stats_1),
        [
            ((D, D), BF16), ((2 * D, D), BF16), ((D, 4 * D), BF16), ((D, D), BF16), (big, BF16), (big, BF16),
            (narrow, F32), ((8, QUARTER), F32), (narrow, BF16), ((2 * D, QUARTER), BF16),
            ((HEADS, QUARTER, 64), BF16), ((HEADS, QUARTER, 64), BF16), ((64, 128), F32),
        ],
        [((768, 1280), BF16), ((4 * D, QUARTER), BF16)],
        name="project",
    )
    att, lse = call(attend_kernel, (scal, kt, qs, kv), [(big, BF16), ((8, TOKENS), F32)], name="attend")
    mid, sec, stats_2 = call(
        middle_kernel, (scal, bt, wo, att, entry), [(big, F32), ((384, TOKENS), BF16), ((8, TOKENS), F32)], [(big, F32)],
        name="middle",
    )
    w1, w1t, w2, w2t, kd = call(
        ffn_weights_kernel,
        (scal, bt, a_low, a_high, b_low, b_high),
        [((FF, 384), BF16), ((D, FF), BF16), ((D, FF), BF16), ((FF, D), BF16), ((FF, 128), F32)],
        [((256, FF), BF16), ((256, FF), BF16), ((FF, 384), BF16)],
        name="ffn_weights",
    )
    smem = pl.BlockSpec(memory_space=pltpu.SMEM)

    def down(width):
        return pl.BlockSpec((256, width), lambda s: (s, 0))

    def along(height):
        return pl.BlockSpec((height, 256), lambda s: (0, s))

    act, slope, end, sect, stats_s = call(
        ffn_kernel,
        (scal, bt, w1, kd, sec, w2, mid),
        [((FF, TOKENS), BF16), ((FF, TOKENS), BF16), (big, F32), (big, BF16), ((8, TOKENS), F32)],
        [((256, TOKENS), F32), (big, F32)],
        grid=(5,),
        in_specs=[smem, whole((64, 128)), down(384), down(128), whole((384, TOKENS)), along(D), whole(big)],
        out_specs=[down(TOKENS), down(TOKENS), whole(big), whole(big), whole((8, TOKENS))],
        name="ffn",
    )
    four, c_keep, c_send, end_grad, branch, g_one = call(
        merge_kernel,
        (scal, bt, c_low, c_high, sect, end, stats_s, cotangent[0]),
        [
            ((OUT_D, QUARTER), BF16), ((16, C_ROWS, 128), BF16), ((16, C_ROWS, 128), BF16), (big, F32), (big, BF16),
            ((64, 128), F32),
        ],
        [
            ((OUT_D, MERGE_PAD), BF16), ((MERGE_PAD, QUARTER), BF16), ((OUT_D, QUARTER), BF16),
            ((MERGE_PAD, QUARTER), F32), ((OUT_D, QUARTER), F32),
        ],
        name="merge",
    )
    dw1, dw2, dkx, mid_grad, low_grad, g_two = call(
        ffn_back_kernel,
        (scal, bt, w1, w1t, w2t, kd, sec, act, slope, branch, end_grad, mid, stats_2),
        [
            ((FF, 384), BF16), ((D, FF), BF16), ((FF, 128), F32), (big, F32), (big, BF16), ((64, 128), F32),
        ],
        [((256, TOKENS), F32), ((256, TOKENS), F32), ((256, TOKENS), BF16), (big, F32)],
        grid=(5,),
        in_specs=[
            smem, whole((64, 128)), down(384), along(D), down(D), down(128), whole((384, TOKENS)), down(TOKENS),
            down(TOKENS), whole(big), whole(big), whole(big), whole((8, TOKENS)),
        ],
        out_specs=[down(384), along(D), down(128), whole(big), whole(big), whole((64, 128))],
        name="ffn_back",
    )
    b_keep, b_send = call(
        pack_b_kernel, (scal, dw1, dw2), [((16, B_ROWS, 128), BF16), ((16, B_ROWS, 128), BF16)], name="give_b"
    )
    dwo, dq, dkv = call(
        attend_back_kernel,
        (scal, kt, vt, qs, kv, wo, low_grad, att, lse),
        [((D, D), BF16), (big, BF16), ((2 * D, QUARTER), BF16)],
        [(big, BF16)],
        name="attend_back",
    )
    token_grad, a_keep, a_send, _ = call(
        first_kernel,
        (scal, bt, wq, wkv, wr, first, red, raw, stat_r, dq, dkv, dwo, dw2, dkx, mid_grad, entry, stats_1, g_one, g_two),
        [(big, F32), ((16, A_ROWS, 128), BF16), ((16, A_ROWS, 128), BF16), ((64, 128), F32)],
        [(big, F32), ((4 * D, QUARTER), F32), ((4 * D, QUARTER), BF16)],
        name="first",
    )
    sum_c = scatter(c_keep, c_send)
    sum_b = scatter(b_keep, b_send)
    sum_a = scatter(a_keep, a_send)
    if group > 1:

        def total(part):
            full = lax.all_gather(part, axes[1], axis=0)
            return jnp.sum(lax.dynamic_slice_in_dim(full, start, group, axis=0), axis=0)

        sum_a, sum_b, sum_c = total(sum_a), total(sum_b), total(sum_c)
    query_g, output_g, keyval_g, reduce_g = select([sum_a], table_out_a, [25, 25, 50, 100], F32, True, "out_a")
    contract_g, expand_g = select([sum_a, sum_b], table_out_b, [100, 100], F32, True, "out_b")
    (merge_g,) = select([sum_c], table_out_c, [360], F32, True, "out_c")
    depth_g = sum_b[160:200, 64:73]
    biases_g = sum_a[240:242].reshape(-1)[:192]
    gains_g = lax.dynamic_slice(sum_a[242], (spot,), (56,))
    grads = [query_g, keyval_g, reduce_g, output_g, expand_g, depth_g, contract_g, merge_g, gains_g, biases_g]
    grads = [grad.reshape(-1) for grad in grads]
    if group > 1:
        mine = index % group
        grads = [lax.dynamic_index_in_dim(grad.reshape(group, -1), mine, keepdims=False) for grad in grads]
    return (four[None], token_grad[None], *grads)


def solution(mesh):
    axes = ("dp", "fs")
    devices = mesh.shape["dp"] * mesh.shape["fs"]
    group = devices // SUPER
    if devices != SUPER * group or mesh.shape["fs"] % group:
        raise ValueError("unsupported mesh")
    one, three = P(axes), P(axes, None, None)
    return jax.shard_map(
        functools.partial(local, group, axes),
        mesh=mesh,
        in_specs=(three, one, three) + (one,) * 10,
        out_specs=(three, three) + (one,) * 10,
        check_vma=False,
    )
```

```python
import functools

import jax
import jax.numpy as jnp
import numpy as np
from jax import lax
from jax.experimental import pallas as pl
from jax.experimental.pallas import tpu as pltpu
from jax.sharding import PartitionSpec as P


D = 320
HEADS = 5
FF = 1280
OUT_D = 512
SIDE = 32
QUARTER = 256
TOKENS = SIDE * SIDE
MERGE_PAD = 2944
SUPER = 32
FLIPS = (2, 4, 8, 16)
EPS = 1e-06
F32, BF16, I32 = jnp.float32, jnp.bfloat16, jnp.int32

B_Q, B_R, C_R, B_O, C_1, C_2, B_1, B_DW, B_2, C_S, B_M, C_M = 0, 5, 10, 15, 20, 25, 30, 50, 70, 75, 80, 88
G_R, G_1, G_2, G_S, G_M = 96, 101, 106, 111, 116

A_ROWS, B_ROWS, C_ROWS = 248, 208, 368
VMEM_LIMIT = 24 * 1024 * 1024


def slot_of(xor):
    return (xor >> 1) | ((xor & 1) << 4)


def xor_of(slot):
    return ((slot & 15) << 1) | (slot >> 4)


def dot(a, b):
    return jnp.dot(a, b, preferred_element_type=F32)


def dot_nt(a, b):
    return lax.dot_general(a, b, (((1,), (1,)), ((), ())), preferred_element_type=F32)


def dot_tn(a, b):
    return lax.dot_general(a, b, (((0,), (0,)), ((), ())), preferred_element_type=F32)


def iota(shape, axis):
    return lax.broadcasted_iota(I32, shape, axis)


def one_hot(test):
    return jnp.where(test, 1.0, 0.0).astype(BF16)


def lanes(index, width=128):
    return pl.ds(pl.multiple_of(index * width, width), width)


def loop(count, body):
    def step(index, carry):
        body(index)
        return carry

    lax.fori_loop(0, count, step, 0)


def column(table, start, count):
    return jnp.concatenate(
        [jnp.broadcast_to(table[:, h : h + 1], (64, 128)) for h in range(start, start + count)], axis=0
    )


def put_column(table, start, values):
    for h in range(values.shape[0] // 64):
        table[:, start + h : start + h + 1] = values[64 * h : 64 * h + 64, 0:1]


def token_place(lane):
    quad = lane >> 8
    row = 2 * ((lane >> 4) & 15) + (quad >> 1)
    col = 2 * (lane & 15) + (quad & 1)
    return row, col


def token_mask(tile, side, width=128):
    row, col = token_place(iota((1, width), 1) + tile * width)
    return jnp.where((row < side) & (col < side), 1.0, 0.0)


def key_place(index):
    return index >> 4, index & 15


def select_kernel(count, bases, exact, *refs):
    sources, (low_ref, high_ref), outs, (rows_ref,) = (
        refs[:count],
        refs[count : count + 2],
        refs[count + 2 : -1],
        refs[-1:],
    )
    half = rows_ref.shape[0] // 2
    rows_ref[...] = jnp.zeros_like(rows_ref)
    for source, base in zip(sources, bases):
        rows = source.shape[0]
        rows_ref[base : base + rows, :] = source[...].astype(F32)
    rows_ref[half:, :] = pltpu.roll(rows_ref[0:half, :], 64, 1)
    total = rows_ref[...]
    high = total.astype(BF16)
    pieces = [high]
    if exact:
        pieces.append((total - high.astype(F32)).astype(BF16))
    total_rows = low_ref.shape[0]
    place = iota((total_rows, 2 * half), 1)
    pick_low = one_hot(place == low_ref[...])
    pick_high = one_hot(place == high_ref[...])
    low = sum(dot(pick_low, piece) for piece in pieces)
    upper = sum(dot(pick_high, piece) for piece in pieces)
    chosen = jnp.where(iota((total_rows, 128), 1) < 64, low, upper)
    at = 0
    for out in outs:
        rows = out.shape[0]
        out[...] = chosen[at : at + rows, :].astype(out.dtype)
        at += -(-rows // 16) * 16


def select(sources, table, out_rows, dtype, exact):
    bases, at = [], 0
    for source in sources:
        bases.append(at)
        at += -(-source.shape[0] // 16) * 16
    half = at
    low, high = table(bases, half)
    total = sum(-(-rows // 16) * 16 for rows in out_rows)
    low = np.concatenate([low, np.full(total - len(low), -1)]).astype(np.int32)[:, None]
    high = np.concatenate([high, np.full(total - len(high), -1)]).astype(np.int32)[:, None]
    return select_call(sources, bases, half, low, high, out_rows, dtype, exact)


def select_call(sources, bases, half, low, high, out_rows, dtype, exact):
    return pl.pallas_call(
        functools.partial(select_kernel, len(sources), tuple(bases), exact),
        out_shape=[jax.ShapeDtypeStruct((rows, 128), dtype) for rows in out_rows],
        scratch_shapes=[pltpu.VMEM((2 * half, 128), F32)],
        compiler_params=pltpu.CompilerParams(vmem_limit_bytes=VMEM_LIMIT),
        cost_estimate=cost(2),
    )(*sources, low, high)


def pair(half, low_src, high_src):
    low = -1 if low_src is None else low_src[0] + low_src[1] // 2 + half * (low_src[1] % 2)
    high = -1 if high_src is None else high_src[0] + high_src[1] // 2 + half * (1 - high_src[1] % 2)
    return low, high


def table_a(bases, half):
    q, o, kv, r, w2, small = bases
    rows = []
    for c in range(10):
        for row in range(24):
            if row < 10 and c < 8:
                base, first = ((q, 0), (o, 0), (kv, 0), (kv, 10))[c // 2]
                at = 5 * (first + row) + 2 * (c % 2)
                rows.append(pair(half, (base, at), (base, at + 1)))
            elif row < 10:
                if c == 8:
                    rows.append(pair(half, (q, 5 * row + 4), (o, 5 * row + 4)))
                else:
                    rows.append(pair(half, (kv, 5 * row + 4), (kv, 5 * (10 + row) + 4)))
            else:
                base, o_row = (r, row - 10) if row < 20 else (w2, row - 20)
                at = 20 * o_row + 2 * c
                rows.append(pair(half, (base, at), (base, at + 1)))
    for row in range(8):
        rows.append(pair(half, (small, 2 * row), (small, 2 * row + 1)) if row < 3 else (-1, -1))
    return np.array(rows).T


def table_b(bases, half):
    w2, w1, dw = bases
    rows = []
    for c in range(10):
        for row in range(8):
            at = 20 * (row + 4) + 2 * c
            rows.append(pair(half, (w2, at), (w2, at + 1)) if row < 6 else (-1, -1))
    for c in range(3):
        for row in range(40):
            at = 5 * row + 2 * c
            rows.append(pair(half, (w1, at), (w1, at + 1) if c < 2 else (dw, 2 * row + 1)))
    rows += [(-1, -1)] * 8
    return np.array(rows).T


def table_c(bases, half):
    (m,) = bases
    rows = []
    for c in range(23):
        for row in range(16):
            at = 45 * row + 2 * c
            rows.append(pair(half, (m, at), (m, at + 1) if c < 22 else None))
    return np.array(rows).T


def padded(rows):
    return rows + [(-1, -1)] * (-len(rows) % 16)


def table_out_a(bases, half):
    (a,) = bases

    def square(w, k):
        def source(at):
            row, piece = divmod(at, 5)
            first = w + (row // 10 if w == 2 else 0)
            row = row % 10
            if piece < 4:
                return (a + (2 * first + piece // 2) * 24 + row, piece % 2)
            return (a + (8 + first // 2) * 24 + row, first % 2)

        return [source(at) for at in range(k)]

    def wide(at):
        row, piece = divmod(at, 20)
        return (a + piece // 2 * 24 + 10 + row, piece % 2)

    def emit(sources):
        rows = [pair(half, s, t) for s, t in zip(sources[0::2], sources[1::2])]
        return padded(rows)

    rows = emit(square(0, 50)) + emit(square(1, 50)) + emit(square(2, 100)) + emit([wide(at) for at in range(200)])
    return np.array(rows).T


def table_out_b(bases, half):
    a, b = bases

    def w2(at):
        row, piece = divmod(at, 20)
        if row < 4:
            return (a + piece // 2 * 24 + 20 + row, piece % 2)
        return (b + piece // 2 * 8 + row - 4, piece % 2)

    def w1(at):
        row, piece = divmod(at, 5)
        return (b + 80 + piece // 2 * 40 + row, piece % 2)

    rows = []
    for source in (w2, w1):
        sources = [source(at) for at in range(200)]
        rows += padded([pair(half, s, t) for s, t in zip(sources[0::2], sources[1::2])])
    return np.array(rows).T


def table_out_c(bases, half):
    (c,) = bases

    def source(at):
        row, piece = divmod(at, 45)
        return (c + piece // 2 * 16 + row, piece % 2)

    sources = [source(at) for at in range(720)]
    return np.array(padded([pair(half, s, t) for s, t in zip(sources[0::2], sources[1::2])])).T


def split_ten(row, per, magic):
    owner = (row * magic) >> 16
    return owner, row - per * owner


def place_ten(row, me, stride, shift):
    owner, rest = split_ten(row, 10, 6554)
    return slot_of(owner ^ me) * stride + shift + rest


def place_kv(row, me, upper):
    owner, rest = split_ten(row, 20, 3277)
    inside = (rest >= 10) if upper else (rest < 10)
    return jnp.where(inside, slot_of(owner ^ me) * 24 + rest - (10 if upper else 0), -1)


def place_forty(row, me):
    owner, rest = split_ten(row, 40, 1639)
    return slot_of(owner ^ me) * 40 + rest


def norm(values, gain, shift):
    mean = jnp.mean(values, axis=0, keepdims=True)
    centred = values - mean
    rstd = lax.rsqrt(jnp.mean(centred * centred, axis=0, keepdims=True) + EPS)
    return centred * rstd * gain + shift, mean, rstd


def norm_back(grad, hat, rstd, gain):
    scaled = grad * gain
    return rstd * (
        scaled
        - jnp.mean(scaled, axis=0, keepdims=True)
        - hat * jnp.mean(scaled * hat, axis=0, keepdims=True)
    )


def stat_rows(mean, rstd):
    row = iota((8, mean.shape[1]), 0)
    return jnp.where(row == 0, mean, jnp.where(row == 1, rstd, 0.0))


def entry_kernel(scal, tokens, entry, stats):
    side = scal[1]
    for quad in range(4):
        lane = iota((1, 256), 1) + quad * 256
        row, col = token_place(lane)
        natural = row * SIDE + col
        pick = one_hot(iota((TOKENS, 256), 0) == natural)
        mask = jnp.where((row < side) & (col < side), 1.0, 0.0)
        entry[:, quad * 256 : quad * 256 + 256] = (dot(tokens[...], pick) * mask).astype(BF16)

    def body(tile):
        values = entry[:, lanes(tile)].astype(F32)
        mean = jnp.mean(values, axis=0, keepdims=True)
        centred = values - mean
        rstd = lax.rsqrt(jnp.mean(centred * centred, axis=0, keepdims=True) + EPS)
        stats[:, lanes(tile)] = stat_rows(mean, rstd)

    loop(8, body)


def small_table(me, low, high):
    gathered = jnp.concatenate(
        [half[:, 240:248, :].astype(F32).reshape(128, 128) for half in (low, high)], axis=0
    ).astype(BF16)
    vector = iota((128, 256), 0)
    place = iota((128, 256), 1)
    row = place & 7
    owner = xor_of(place >> 3) ^ me
    first = (7 * owner) >> 3
    straight = (
        ((row == 0) & (vector == 3 * owner))
        | ((row == 1) & (vector == 3 * owner + 2))
        | ((row == 2) & (vector == 96 + first))
    )
    turned = ((row == 0) & (vector == 3 * owner + 1)) | ((row == 2) & (vector == 97 + first))
    rows = dot(one_hot(straight), gathered) + pltpu.roll(dot(one_hot(turned), gathered), 64, 1)
    return jnp.transpose(rows)[0:64, :]


def project_kernel(scal, low, high, entry, stats, wq, wkv, wr, wo, first, qs, raw, stat_r, red, kv, kt, vt, bt, gath, redin):
    me = scal[0]
    bt[...] = small_table(me, low, high)
    for half, source in enumerate((low, high)):
        for p in range(5):
            block = source[:, 48 * p : 48 * p + 48, :].astype(F32).reshape(16, 2, 24, 128)
            for e in range(2):
                c = 2 * p + e
                gath[384 * half : 384 * half + 384, 128 * c : 128 * c + 128] = (
                    block[:, e].reshape(384, 128).astype(BF16)
                )
    row = iota((D, 1), 0)
    place = iota((D, 768), 1)
    wr[...] = dot(one_hot(place == place_ten(row, me, 24, 10)), gath[...]).astype(BF16)
    pick = one_hot(place == place_ten(row, me, 24, 0))
    both = dot(pick, gath[:, 0:512])
    wq[:, 0:256] = both[:, 0:256].astype(BF16)
    wo[:, 0:256] = both[:, 256:512].astype(BF16)
    tail = dot(pick, gath[:, 1024:1152])
    wq[:, 256:320] = tail[:, 0:64].astype(BF16)
    wo[:, 256:320] = pltpu.roll(tail, 64, 1)[:, 0:64].astype(BF16)
    row = iota((2 * D, 1), 0)
    place = iota((2 * D, 768), 1)
    lower = one_hot(place == place_kv(row, me, False))
    upper = one_hot(place == place_kv(row, me, True))
    wkv[:, 0:256] = (dot(lower, gath[:, 512:768]) + dot(upper, gath[:, 768:1024])).astype(BF16)
    tail = dot(lower, gath[:, 1152:1280])[:, 0:64] + pltpu.roll(dot(upper, gath[:, 1152:1280]), 64, 1)[:, 0:64]
    wkv[:, 256:320] = tail.astype(BF16)

    gain, shift = column(bt, G_1, 5), column(bt, C_1, 5)

    def body(tile):
        centred = entry[:, lanes(tile)].astype(F32) - stats[0:1, lanes(tile)]
        first[:, lanes(tile)] = (centred * stats[1:2, lanes(tile)] * gain + shift).astype(BF16)

    loop(8, body)
    for quad in range(4):
        redin[D * quad : D * quad + D, :] = first[:, 256 * quad : 256 * quad + 256]
    bias = column(bt, B_R, 5)
    bias = jnp.concatenate([bias, bias], axis=1)
    raw[...] = dot(wr[...], redin[...]) + bias
    gain, shift = column(bt, G_R, 5), column(bt, C_R, 5)
    for tile in range(2):
        at = slice(128 * tile, 128 * tile + 128)
        values, mean, rstd = norm(raw[:, at], gain, shift)
        red[:, at] = values.astype(BF16)
        stat_r[:, at] = stat_rows(mean, rstd)
    keyval = dot(wkv[...], red[...])
    kv[...] = keyval.astype(BF16)
    turned = jnp.transpose(keyval)
    for h in range(HEADS):
        kt[h] = turned[:, 64 * h : 64 * h + 64].astype(BF16)
        vt[h] = turned[:, D + 64 * h : D + 64 * h + 64].astype(BF16)
    bias = column(bt, B_Q, 5)
    bias = jnp.concatenate([bias, bias], axis=1)
    for quad in range(4):
        at = slice(256 * quad, 256 * quad + 256)
        qs[:, at] = (dot(wq[...], first[:, at]) + bias).astype(BF16) * BF16(0.125)


def key_bias(side):
    i, j = key_place(iota((QUARTER, 1), 0))
    return jnp.where((i < (side >> 1)) & (j < (side >> 1)), 0.0, -10000.0)


def attend_kernel(scal, kt, qs, kv, att, lse):
    bias = key_bias(scal[1])

    def head(h):
        rows = pl.ds(pl.multiple_of(64 * h, 64), 64)
        values = kv[pl.ds(pl.multiple_of(D + 64 * h, 64), 64), :]
        for quad in range(4):
            at = slice(256 * quad, 256 * quad + 256)
            scores = dot(kt[h], qs[rows, at]) + bias
            top = jnp.max(scores, axis=0, keepdims=True)
            weights = jnp.exp(scores - top)
            total = jnp.sum(weights, axis=0, keepdims=True)
            lse[h, :, at] = top + jnp.log(total)
            probs = (weights * (1.0 / total)).astype(BF16)
            att[rows, at] = dot(values, probs).astype(BF16)

    loop(HEADS, head)


def middle_kernel(scal, bt, wo, att, entry, mid, sec, stats, work):
    side = scal[1]
    work[...] = dot(wo[...], att[...])
    bias, gain, shift = column(bt, B_O, 5), column(bt, G_2, 5), column(bt, C_2, 5)

    def body(tile):
        at = lanes(tile)
        mask = token_mask(tile, side)
        values = entry[:, at].astype(F32) + mask * (work[:, at] + bias)
        mid[:, at] = values
        normed, mean, rstd = norm(values, gain, shift)
        stats[:, at] = stat_rows(mean, rstd)
        sec[0:D, at] = (normed.astype(BF16).astype(F32) * mask).astype(BF16)
        sec[D : D + 64, at] = jnp.where(iota((64, 128), 0) == 9, mask, 0.0).astype(BF16)

    loop(8, body)


def ffn_weights_kernel(scal, bt, a_low, a_high, b_low, b_high, w1, w1t, w2, w2t, taps, ga, gb, g1):
    me = scal[0]
    for half, (a, b) in enumerate(((a_low, b_low), (a_high, b_high))):
        for p in range(5):
            block = a[:, 48 * p : 48 * p + 48, :].astype(F32).reshape(16, 2, 24, 128)
            other = b[:, 16 * p : 16 * p + 16, :].astype(F32).reshape(16, 2, 8, 128)
            for e in range(2):
                c = 2 * p + e
                at = slice(128 * c, 128 * c + 128)
                ga[128 * half : 128 * half + 128, at] = block[:, e, 16:24].reshape(128, 128).astype(BF16)
                gb[128 * half : 128 * half + 128, at] = other[:, e].reshape(128, 128).astype(BF16)
        rest = b[:, 80:208, :].astype(F32)
        for c in range(3):
            g1[640 * half : 640 * half + 640, 128 * c : 128 * c + 128] = (
                rest[:, 40 * c : 40 * c + 40].reshape(640, 128).astype(BF16)
            )
    row = iota((D, 1), 0)
    place = iota((D, 256), 1)
    owner, rest = split_ten(row, 10, 6554)
    at = slot_of(owner ^ me) * 8
    in_a = one_hot(place == jnp.where(rest < 4, at + 4 + rest, -1))
    in_b = one_hot(place == jnp.where(rest >= 4, at + rest - 4, -1))
    full = dot(in_a, ga[...]) + dot(in_b, gb[...])
    w2[...] = full.astype(BF16)
    w2t[...] = jnp.transpose(full).astype(BF16)
    row = iota((FF, 1), 0)
    full = dot(one_hot(iota((FF, FF), 1) == place_forty(row, me)), g1[...])
    w1t[...] = jnp.transpose(full[:, 0:D]).astype(BF16)
    w1[:, 0:256] = full[:, 0:256].astype(BF16)
    tail = full[:, 256:384]
    lane = iota((FF, 128), 1)
    spread = tail.astype(BF16)
    for tap in range(9):
        taps[tap] = dot(spread, one_hot(iota((128, 128), 0) == 64 + tap))
    taps[9] = column(bt, B_DW, 20)
    w1[:, 256:384] = jnp.where(lane < 64, tail, jnp.where(lane == 73, column(bt, B_1, 20), 0.0)).astype(BF16)


def edge_masks():
    lane = iota((1, 128), 1)
    j = lane & 15
    return jnp.where(j != 0, 1.0, 0.0), jnp.where(j != 15, 1.0, 0.0), lane >= 16, lane < 112


def left_of(tiles):
    return [pltpu.roll(tile, 1, 1) for tile in tiles]


def right_of(tiles):
    return [pltpu.roll(tile, 127, 1) for tile in tiles]


def above(tiles, inside):
    turned = [pltpu.roll(tile, 16, 1) for tile in tiles]
    return [jnp.where(inside, turned[0], 0.0), jnp.where(inside, turned[1], turned[0])]


def below(tiles, inside):
    turned = [pltpu.roll(tile, 112, 1) for tile in tiles]
    return [jnp.where(inside, turned[0], turned[1]), jnp.where(inside, turned[1], 0.0)]


def times(tiles, factor):
    return [tile * factor for tile in tiles]


def plus(*many):
    return [functools.reduce(lambda a, b: a + b, tiles) for tiles in zip(*many)]


def tile_at(a, e, half):
    start = 256 * (2 * a + e) + 128 * half
    return slice(start, start + 128)


def quads(ref, rows):
    return [[[ref[rows, tile_at(a, e, half)] for half in range(2)] for e in range(2)] for a in range(2)]


LOG2E = float(np.log2(np.e))


def gelu_parts(x):
    y = x * np.float32(0.5**0.5)
    cdf = lax.erf(y) * 0.5 + 0.5
    bell = jnp.exp2(y * y * np.float32(-LOG2E) + np.float32(-0.5 * np.log2(2.0 * np.pi)))
    return x * cdf, cdf + x * bell


def ffn_kernel(scal, w1, taps, sec, act, slope, hid):
    j_first, j_last, i_first, i_last = edge_masks()

    def block(step):
        start = pl.multiple_of(step * 256, 256)
        hid[...] = dot(w1[pl.ds(start, 256), :], sec[...])

        def group(index):
            rows = pl.ds(pl.multiple_of(index * 16, 16), 16)
            out_rows = pl.ds(pl.multiple_of(start + index * 16, 16), 16)
            k = [taps[n, out_rows, :] for n in range(10)]
            first = [k[3 * r] * j_first for r in range(3)]
            last = [k[3 * r + 2] * j_last for r in range(3)]
            quad = quads(hid, rows)
            left = [left_of(quad[a][1]) for a in range(2)]
            right = [right_of(quad[a][0]) for a in range(2)]

            def across(a, e, r):
                if e == 0:
                    parts = zip(left[a], quad[a][0], quad[a][1])
                    return [first[r] * x + k[3 * r + 1] * y + k[3 * r + 2] * z for x, y, z in parts]
                parts = zip(quad[a][0], quad[a][1], right[a])
                return [k[3 * r] * x + k[3 * r + 1] * y + last[r] * z for x, y, z in parts]

            for e in range(2):
                up = above(across(1, e, 0), i_first)
                down = below(across(0, e, 2), i_last)
                outs = (plus(across(0, e, 1), across(1, e, 2), up), plus(across(0, e, 0), across(1, e, 1), down))
                for a in range(2):
                    for half in range(2):
                        value, grad = gelu_parts(outs[a][half] + k[9])
                        act[out_rows, tile_at(a, e, half)] = value.astype(BF16)
                        slope[out_rows, tile_at(a, e, half)] = grad.astype(BF16)

        loop(16, group)

    loop(5, block)


def ending_kernel(scal, bt, w2, act, mid, end, sect, stats, work):
    side = scal[1]
    work[...] = dot(w2[...], act[...])
    bias, gain, shift = column(bt, B_2, 5), column(bt, G_S, 5), column(bt, C_S, 5)

    def body(tile):
        at = lanes(tile)
        mask = token_mask(tile, side)
        values = mid[:, at] + mask * (work[:, at] + bias)
        end[:, at] = values
        normed, mean, rstd = norm(values, gain, shift)
        stats[:, at] = stat_rows(mean, rstd)
        sect[:, at] = (normed.astype(BF16).astype(F32) * mask).astype(BF16)

    loop(8, body)


def lane_sum(values):
    return jnp.sum(values, axis=1, keepdims=True)


def merge_kernel(scal, bt, c_low, c_high, sect, end, stats, cot, four, keep, send, end_grad, branch, grads, wm, patch, mg, back, work):
    me, side = scal[0], scal[1]
    grads[...] = jnp.zeros_like(grads)
    for half, source in enumerate((c_low, c_high)):

        def place(slot, half=half, source=source):
            owner = ((slot << 1) | half) ^ me
            at = pl.ds(pl.multiple_of(owner * 16, 16), 16)
            for c in range(23):
                wm[at, 128 * c : 128 * c + 128] = source[slot, 16 * c : 16 * c + 16, :]

        loop(16, place)
    j_first, j_last, i_first, i_last = edge_masks()
    quad = [[[t.astype(F32) for t in pair] for pair in row] for row in quads(sect, slice(None))]
    left = [times(left_of(quad[a][1]), j_first) for a in range(2)]
    pieces = (
        above(left[1], i_first),
        above(quad[1][0], i_first),
        above(quad[1][1], i_first),
        left[0],
        quad[0][0],
        quad[0][1],
        left[1],
        quad[1][0],
        quad[1][1],
    )
    for n, piece in enumerate(pieces):
        for half in range(2):
            patch[D * n : D * n + D, 128 * half : 128 * half + 128] = piece[half].astype(BF16)
    patch[9 * D :, :] = jnp.zeros((MERGE_PAD - 9 * D, 256), BF16)
    bias, gain, shift = column(bt, B_M, 8), column(bt, G_M, 8), column(bt, C_M, 8)
    work[...] = dot(wm[...], patch[...])
    half_side = side >> 1
    for tile in range(2):
        at = slice(128 * tile, 128 * tile + 128)
        i, j = key_place(iota((1, 128), 1) + 128 * tile)
        mask = jnp.where((i < half_side) & (j < half_side), 1.0, 0.0)
        values = work[:, at] + bias
        mean = jnp.mean(values, axis=0, keepdims=True)
        centred = values - mean
        rstd = lax.rsqrt(jnp.mean(centred * centred, axis=0, keepdims=True) + EPS)
        hat = centred * rstd
        four[:, at] = ((hat * gain + shift) * mask).astype(BF16)
        grad = cot[:, at].astype(F32) * mask
        low = norm_back(grad, hat, rstd, gain).astype(BF16)
        mg[:, at] = low
        parts = (grad * hat, grad, low.astype(F32))
        sums = parts if tile == 0 else [s + v for s, v in zip(sums, parts)]
    put_column(grads, G_M, lane_sum(sums[0]))
    put_column(grads, C_M, lane_sum(sums[1]))
    put_column(grads, B_M, lane_sum(sums[2]))

    def widths(body):
        loop(11, lambda c: body(pl.multiple_of(c * 256, 256), 256))
        body(11 * 256, 128)

    def patch_grad(start, width):
        back[pl.ds(start, width), :] = dot_tn(wm[:, pl.ds(start, width)], mg[...])

    widths(patch_grad)

    def piece(n):
        return [back[D * n : D * n + D, 128 * half : 128 * half + 128] for half in range(2)]

    results = (
        piece(4),
        plus(piece(5), times(right_of(piece(3)), j_last)),
        plus(piece(7), below(piece(1), i_last)),
        plus(
            piece(8),
            times(right_of(piece(6)), j_last),
            below(plus(piece(2), times(right_of(piece(0)), j_last)), i_last),
        ),
    )
    for n, values in enumerate(results):
        for half in range(2):
            end_grad[:, 256 * n + 128 * half : 256 * n + 128 * half + 128] = values[half]
    gain = column(bt, G_S, 5)
    zeros = jnp.zeros((D, 128), F32)

    def body(tile, carry):
        at = lanes(tile)
        mask = token_mask(tile, side)
        grad = end_grad[:, at] * mask
        hat = (end[:, at] - stats[0:1, at]) * stats[1:2, at]
        result = norm_back(grad, hat, stats[1:2, at], gain)
        end_grad[:, at] = result
        low = (result * mask).astype(BF16)
        branch[:, at] = low
        return carry[0] + grad * hat, carry[1] + grad, carry[2] + low.astype(F32)

    sums = lax.fori_loop(0, 8, body, (zeros, zeros, zeros))
    put_column(grads, G_S, lane_sum(sums[0]))
    put_column(grads, C_S, lane_sum(sums[1]))
    put_column(grads, B_2, lane_sum(sums[2]))

    def give(start, width):
        work[:, 0:width] = dot_nt(mg[...], patch[pl.ds(start, width), :])

        def one(slot):
            for half, out in enumerate((keep, send)):
                owner = ((slot << 1) | half) ^ me
                at = pl.ds(pl.multiple_of(owner * 16, 16), 16)
                for c in range(width // 128):
                    to = pl.ds(pl.multiple_of((start >> 3) + 16 * c, 16), 16)
                    out[slot, to, :] = work[at, 128 * c : 128 * c + 128].astype(BF16)

        loop(16, one)

    widths(give)


def ffn_back_kernel(part, scal, w1, w2t, taps, sec, slope, branch, hg, dkx, hid, cg):
    side = scal[1]
    block = slice(256 * part, 256 * part + 256)
    cg[...] = dot(w2t[block, :], branch[...])
    hid[...] = dot(w1[block, :], sec[...])
    j_first, j_last, i_first, i_last = edge_masks()
    masks = [token_mask(tile, side) for tile in range(8)]
    lane = iota((16, 128), 1)

    def group(index):
        rows = pl.ds(pl.multiple_of(index * 16, 16), 16)
        from_rows = pl.ds(pl.multiple_of(256 * part + index * 16, 16), 16)
        k = [taps[n, from_rows, :] for n in range(9)]
        quad = quads(cg, rows)
        weight = quads(slope, from_rows)
        quad = [
            [[quad[a][e][h] * weight[a][e][h].astype(F32) for h in range(2)] for e in range(2)] for a in range(2)
        ]
        bias = functools.reduce(lambda x, y: x + y, [t for row in quad for pair in row for t in pair])
        across = [
            (
                (times(left_of(quad[a][1]), j_first), quad[a][0], quad[a][1]),
                (quad[a][0], quad[a][1], times(right_of(quad[a][0]), j_last)),
            )
            for a in range(2)
        ]
        sums = [None] * 10
        for e in range(2):
            upper = [above(tiles, i_first) for tiles in across[1][e]]
            lower = [below(tiles, i_last) for tiles in across[0][e]]
            for a, near in ((0, (upper, across[0][e], across[1][e])), (1, (across[0][e], across[1][e], lower))):
                for half in range(2):
                    value = hid[rows, tile_at(a, e, half)]
                    total = None
                    for r in range(3):
                        for c in range(3):
                            tap = 3 * (2 - r) + (2 - c)
                            term = k[tap] * near[r][c][half]
                            total = term if total is None else total + term
                            term = value * near[r][c][half]
                            sums[tap] = term if sums[tap] is None else sums[tap] + term
                    low = (total * masks[2 * (2 * a + e) + half]).astype(BF16)
                    hg[rows, tile_at(a, e, half)] = low
                    low = low.astype(F32)
                    sums[9] = low if sums[9] is None else sums[9] + low
        table = jnp.where(lane == 9, lane_sum(bias), 0.0)
        for n in range(10):
            table = jnp.where(lane == (n if n < 9 else 10), lane_sum(sums[n]), table)
        dkx[rows, :] = table

    loop(16, group)


def middle_back_kernel(scal, bt, w1t, hg0, hg1, hg2, hg3, hg4, end_grad, mid, stats, mid_grad, low_grad, grads, work):
    side = scal[1]
    total = None
    for n, hg in enumerate((hg0, hg1, hg2, hg3, hg4)):
        part = dot(w1t[:, 256 * n : 256 * n + 256], hg[...])
        total = part if total is None else total + part
    work[...] = total
    grads[...] = jnp.zeros_like(grads)
    gain = column(bt, G_2, 5)
    zeros = jnp.zeros((D, 128), F32)

    def body(tile, carry):
        at = lanes(tile)
        mask = token_mask(tile, side)
        grad = work[:, at]
        hat = (mid[:, at] - stats[0:1, at]) * stats[1:2, at]
        result = end_grad[:, at] + norm_back(grad, hat, stats[1:2, at], gain)
        mid_grad[:, at] = result
        low = (result * mask).astype(BF16)
        low_grad[:, at] = low
        return carry[0] + grad * hat, carry[1] + grad, carry[2] + low.astype(F32)

    sums = lax.fori_loop(0, 8, body, (zeros, zeros, zeros))
    put_column(grads, G_2, lane_sum(sums[0]))
    put_column(grads, C_2, lane_sum(sums[1]))
    put_column(grads, B_O, lane_sum(sums[2]))


def store_pairs(values, height, keep, send):
    for p in range(5):
        both = [values[:, 128 * (2 * p + e) : 128 * (2 * p + e) + 128].reshape(32, 1, height, 128) for e in range(2)]
        block = jnp.concatenate(both, axis=1).reshape(32, 2 * height, 128).astype(BF16)
        at = slice(2 * height * p, 2 * height * p + 2 * height)
        keep[:, at, :] = block[0:16]
        send[:, at, :] = block[16:32]


def pack_b_kernel(scal, hg0, hg1, hg2, hg3, hg4, dk0, dk1, dk2, dk3, dk4, sec, branch, act, keep, send, dw2, dw1):
    me = scal[0]
    dw2[...] = dot_nt(branch[...], act[...]).astype(BF16)
    lane = iota((256, 128), 1)
    for n, (hg, dkx) in enumerate(zip((hg0, hg1, hg2, hg3, hg4), (dk0, dk1, dk2, dk3, dk4))):
        rows = slice(256 * n, 256 * n + 256)
        part = dot_nt(hg[...], sec[...])
        dw1[rows, 0:256] = part[:, 0:256].astype(BF16)
        turned = pltpu.roll(dkx[...], 64, 1)
        tail = jnp.where(lane < 64, part[:, 256:384], jnp.where(lane < 73, turned, 0.0))
        dw1[rows, 256:384] = tail.astype(BF16)
    owner, rest = split_ten(iota((1, D), 1), 10, 6554)
    at = jnp.where(rest >= 4, slot_of(owner ^ me) * 8 + rest - 4, -1)
    store_pairs(dot(one_hot(iota((256, D), 0) == at), dw2[...]), 8, keep, send)
    at = place_forty(iota((1, FF), 1), me)
    blocks = dot(one_hot(iota((FF, FF), 0) == at), dw1[...])
    parts = [blocks[:, 128 * c : 128 * c + 128].reshape(32, 40, 128) for c in range(3)]
    parts.append(jnp.zeros((32, 8, 128), F32))
    block = jnp.concatenate(parts, axis=1).astype(BF16)
    keep[:, 80:208, :] = block[0:16]
    send[:, 80:208, :] = block[16:32]


def attend_back_kernel(scal, kt, vt, qs, kv, wo, low_grad, att, lse, dwo, dq, dkv, og):
    bias = key_bias(scal[1])
    dwo[...] = dot_nt(low_grad[...], att[...]).astype(BF16)
    og[...] = dot_tn(wo[...], low_grad[...]).astype(BF16)

    def head(h):
        rows = pl.ds(pl.multiple_of(64 * h, 64), 64)
        more = pl.ds(pl.multiple_of(D + 64 * h, 64), 64)
        dk = jnp.zeros((64, 256), F32)
        dv = jnp.zeros((64, 256), F32)
        for quad in range(4):
            at = slice(256 * quad, 256 * quad + 256)
            probs = jnp.exp(dot(kt[h], qs[rows, at]) + bias - lse[h, :, at])
            grad = dot(vt[h], og[rows, at])
            mean = jnp.sum(probs * grad, axis=0, keepdims=True)
            score = (probs * (grad - mean)).astype(BF16)
            dq[rows, at] = (dot(kv[rows, :], score) * 0.125).astype(BF16)
            dk += dot_nt(qs[rows, at], score)
            dv += dot_nt(og[rows, at], probs.astype(BF16))
        dkv[rows, :] = dk.astype(BF16)
        dkv[more, :] = dv.astype(BF16)

    loop(HEADS, head)


def first_kernel(scal, bt, wq, wkv, wr, first, red, raw, stat_r, dq, dkv, dwo, dw2, dk0, dk1, dk2, dk3, dk4, entry, stats, g_one, g_two, keep, send, work, grads, wide, redin):
    me = scal[0]
    grads[...] = g_one[...] + g_two[...]
    for m in range(20):
        block = (dk0, dk1, dk2, dk3, dk4)[m // 4][64 * (m % 4) : 64 * (m % 4) + 64, :]
        grads[:, B_1 + m : B_1 + m + 1] = block[:, 10:11]
        grads[:, B_DW + m : B_DW + m + 1] = block[:, 9:10]
    for quad in range(4):
        redin[D * quad : D * quad + D, :] = first[:, 256 * quad : 256 * quad + 256]
    dred = dot_tn(wkv[...], dkv[...])
    gain = column(bt, G_R, 5)
    lows = []
    for tile in range(2):
        at = slice(128 * tile, 128 * tile + 128)
        grad = dred[:, at]
        hat = (raw[:, at] - stat_r[0:1, at]) * stat_r[1:2, at]
        low = norm_back(grad, hat, stat_r[1:2, at], gain).astype(BF16)
        lows.append(low)
        parts = (grad * hat, grad, low.astype(F32))
        sums = parts if tile == 0 else [s + v for s, v in zip(sums, parts)]
    put_column(grads, G_R, lane_sum(sums[0]))
    put_column(grads, C_R, lane_sum(sums[1]))
    put_column(grads, B_R, lane_sum(sums[2]))
    low = jnp.concatenate(lows, axis=1)
    wide[...] = dot_tn(wr[...], low)
    straight = dot_tn(wq[...], dq[...])
    for quad in range(4):
        at = slice(256 * quad, 256 * quad + 256)
        work[:, at] = straight[:, at] + wide[D * quad : D * quad + D, :]
    zeros = jnp.zeros((D, 128), F32)

    def body(tile, carry):
        at = lanes(tile)
        grad = work[:, at]
        hat = (entry[:, at].astype(F32) - stats[0:1, at]) * stats[1:2, at]
        return carry[0] + grad * hat, carry[1] + grad, carry[2] + dq[:, at].astype(F32)

    sums = lax.fori_loop(0, 8, body, (zeros, zeros, zeros))
    put_column(grads, G_1, lane_sum(sums[0]))
    put_column(grads, C_1, lane_sum(sums[1]))
    put_column(grads, B_Q, lane_sum(sums[2]))
    dwq = dot_nt(dq[...], first[...]).astype(BF16)
    dwkv = dot_nt(dkv[...], red[...]).astype(BF16)
    dwr = dot_nt(low, redin[...]).astype(BF16)
    lane = iota((1, D), 1)
    height = iota((768, D), 0)
    at_o = one_hot(height == place_ten(lane, me, 24, 0))
    at_r = one_hot(height == place_ten(lane, me, 24, 10))
    owner, rest = split_ten(lane, 10, 6554)
    at_w = one_hot(height == jnp.where(rest < 4, slot_of(owner ^ me) * 24 + 20 + rest, -1))
    lane = iota((1, 2 * D), 1)
    height = iota((768, 2 * D), 0)
    at_low = one_hot(height == place_kv(lane, me, False))
    at_high = one_hot(height == place_kv(lane, me, True))
    dwo_all = dwo[...]
    zq = dot(at_o, dwq)
    zo = dot(at_o, dwo_all)
    zl = dot(at_low, dwkv)
    zh = dot(at_high, dwkv)
    tails = jnp.concatenate(
        [
            jnp.concatenate([zq[:, 256:320], zo[:, 256:320]], axis=1),
            jnp.concatenate([zl[:, 256:320], zh[:, 256:320]], axis=1),
        ],
        axis=1,
    )
    ten = jnp.concatenate([zq[:, 0:256], zo[:, 0:256], zl[:, 0:256], zh[:, 0:256], tails], axis=1)
    store_pairs(ten + dot(at_r, dwr) + dot(at_w, dw2[...]), 24, keep, send)
    rows = jnp.transpose(jnp.concatenate([grads[...], jnp.zeros((64, 128), F32)], axis=0)).astype(BF16)
    place = iota((256, 128), 0)
    vector = iota((256, 128), 1)
    line = place & 7
    owner = xor_of(place >> 3) ^ me
    start = (7 * owner) >> 3
    straight = (
        ((line == 0) & (vector == 3 * owner))
        | ((line == 1) & (vector == 3 * owner + 2))
        | ((line == 2) & (vector == 96 + start))
    )
    turned = ((line == 0) & (vector == 3 * owner + 1)) | ((line == 2) & (vector == 97 + start))
    small = dot(one_hot(straight), rows) + pltpu.roll(dot(one_hot(turned), rows), 64, 1)
    small = small.reshape(32, 8, 128).astype(BF16)
    keep[:, 240:248, :] = small[0:16]
    send[:, 240:248, :] = small[16:32]


def token_kernel(scal, bt, grad_in, mid_grad, entry, stats, tok, high, rest):
    side = scal[1]
    gain = column(bt, G_1, 5)

    def body(tile):
        at = lanes(tile)
        hat = (entry[:, at].astype(F32) - stats[0:1, at]) * stats[1:2, at]
        result = mid_grad[:, at] + norm_back(grad_in[:, at], hat, stats[1:2, at], gain)
        result = result * token_mask(tile, side)
        upper = result.astype(BF16)
        high[:, at] = upper
        rest[:, at] = (result - upper.astype(F32)).astype(BF16)

    loop(8, body)
    row, col = token_place(iota((TOKENS, 1), 0))
    natural = row * SIDE + col

    def quad(index):
        at = lanes(index, 256)
        pick = one_hot(iota((TOKENS, 256), 1) + 256 * index == natural)
        tok[:, at] = dot(high[...], pick) + dot(rest[...], pick)

    loop(4, quad)


def cost(micros):
    return pl.CostEstimate(flops=int(micros * 1e9), bytes_accessed=1000, transcendentals=0)


def call(kernel, args, outs, scratch=(), micros=5):
    return pl.pallas_call(
        kernel,
        in_specs=[pl.BlockSpec(memory_space=pltpu.SMEM)] + [pl.BlockSpec(memory_space=pltpu.VMEM)] * (len(args) - 1),
        out_shape=[jax.ShapeDtypeStruct(shape, dtype) for shape, dtype in outs],
        scratch_shapes=[pltpu.VMEM(shape, dtype) for shape, dtype in scratch],
        compiler_params=pltpu.CompilerParams(vmem_limit_bytes=VMEM_LIMIT),
        cost_estimate=cost(micros),
    )(*args)


def local(group, axes, *arrays):
    return step_of(group, axes, *arrays)


def step_of(group, axes, tokens, image_side, cotangent, *shards):
    index = lax.axis_index(axes[0]) * lax.axis_size(axes[1]) + lax.axis_index(axes[1])
    me = index // group
    devices = SUPER * group

    def flip(values, mask):
        pairs = [(i, ((i // group) ^ mask) * group + i % group) for i in range(devices)]
        return lax.ppermute(values, axes, pairs)

    def gather(block):
        held = block[None]
        for mask in FLIPS:
            other = flip(held, mask)
            held = jnp.concatenate([held, other], axis=0)
        return held, flip(held, 1)

    def scatter(keep, send):
        other = flip(send, 1)
        held = keep.astype(F32) + other.astype(F32)
        for mask in FLIPS[::-1]:
            held = held.astype(BF16)
            half = held.shape[0] // 2
            other = flip(held[half:], mask)
            held = held[:half].astype(F32) + other.astype(F32)
        return held[0]

    if group > 1:
        per = lax.axis_size(axes[1])
        start = (index % per) // group * group

        def join(shard):
            full = lax.all_gather(shard, axes[1], axis=0)
            return lax.dynamic_slice_in_dim(full, start, group, axis=0).reshape(-1)

        shards = [join(shard) for shard in shards]
    query, keyval, reduce_w, output, expand, depth, contract, merge, gains, biases = shards

    def rows(flat):
        return flat.reshape(-1, 128)

    spot = (56 * me) % 64
    placed = lax.dynamic_update_slice(jnp.zeros((128,), BF16), gains, (spot,))
    small = rows(jnp.concatenate([biases, jnp.zeros((64,), BF16), placed]))
    taps = jnp.pad(depth.reshape(40, 9), ((0, 0), (64, 55)))
    (block_a,) = select(
        [rows(query), rows(output), rows(keyval), rows(reduce_w), rows(contract), small],
        table_a, [A_ROWS], BF16, False,
    )
    (block_b,) = select([rows(contract), rows(expand), taps], table_b, [B_ROWS], BF16, False)
    (block_c,) = select([rows(merge)], table_c, [C_ROWS], BF16, False)
    a_low, a_high = gather(block_a)
    b_low, b_high = gather(block_b)
    c_low, c_high = gather(block_c)

    scal = jnp.stack([me.astype(I32), image_side[0].astype(I32)])
    big, narrow = (D, TOKENS), (D, QUARTER)
    entry, stats_1 = call(entry_kernel, (scal, tokens[0]), [(big, BF16), ((8, TOKENS), F32)], micros=3.5)
    wq, wkv, wr, wo, first, qs, raw, stat_r, red, kv, kt, vt, bt = call(
        project_kernel,
        (scal, a_low, a_high, entry, stats_1),
        [
            ((D, D), BF16), ((2 * D, D), BF16), ((D, 4 * D), BF16), ((D, D), BF16), (big, BF16), (big, BF16),
            (narrow, F32), ((8, QUARTER), F32), (narrow, BF16), ((2 * D, QUARTER), BF16),
            ((HEADS, QUARTER, 64), BF16), ((HEADS, QUARTER, 64), BF16), ((64, 128), F32),
        ],
        [((768, 1280), BF16), ((4 * D, QUARTER), BF16)],
        micros=8,
    )
    att, lse = call(attend_kernel, (scal, kt, qs, kv), [(big, BF16), ((HEADS, 1, TOKENS), F32)], micros=8.5)
    mid, sec, stats_2 = call(
        middle_kernel, (scal, bt, wo, att, entry), [(big, F32), ((384, TOKENS), BF16), ((8, TOKENS), F32)], [(big, F32)],
        micros=5,
    )
    w1, w1t, w2, w2t, taps = call(
        ffn_weights_kernel,
        (scal, bt, a_low, a_high, b_low, b_high),
        [((FF, 384), BF16), ((D, FF), BF16), ((D, FF), BF16), ((FF, D), BF16), ((10, FF, 128), F32)],
        [((256, FF), BF16), ((256, FF), BF16), ((FF, 384), BF16)],
        micros=8,
    )
    act, slope = call(
        ffn_kernel,
        (scal, w1, taps, sec),
        [((FF, TOKENS), BF16), ((FF, TOKENS), BF16)],
        [((256, TOKENS), F32)],
        micros=20,
    )
    end, sect, stats_s = call(
        ending_kernel, (scal, bt, w2, act, mid), [(big, F32), (big, BF16), ((8, TOKENS), F32)], [(big, F32)], micros=5
    )
    four, c_keep, c_send, end_grad, branch, g_one = call(
        merge_kernel,
        (scal, bt, c_low, c_high, sect, end, stats_s, cotangent[0]),
        [
            ((OUT_D, QUARTER), BF16), ((16, C_ROWS, 128), BF16), ((16, C_ROWS, 128), BF16), (big, F32), (big, BF16),
            ((64, 128), F32),
        ],
        [
            ((OUT_D, MERGE_PAD), BF16), ((MERGE_PAD, QUARTER), BF16), ((OUT_D, QUARTER), BF16),
            ((MERGE_PAD, QUARTER), F32), ((OUT_D, QUARTER), F32),
        ],
        micros=20,
    )
    sum_c = scatter(c_keep, c_send)
    hgs, dks = [], []
    for part in range(5):
        hg, dk = call(
            functools.partial(ffn_back_kernel, part),
            (scal, w1, w2t, taps, sec, slope, branch),
            [((256, TOKENS), BF16), ((256, 128), F32)],
            [((256, TOKENS), F32), ((256, TOKENS), F32)],
            micros=7,
        )
        hgs.append(hg)
        dks.append(dk)
    b_keep, b_send, dw2 = call(
        pack_b_kernel,
        (scal, *hgs, *dks, sec, branch, act),
        [((16, B_ROWS, 128), BF16), ((16, B_ROWS, 128), BF16), ((D, FF), BF16)],
        [((FF, 384), BF16)],
        micros=9,
    )
    sum_b = scatter(b_keep, b_send)
    mid_grad, low_grad, g_two = call(
        middle_back_kernel,
        (scal, bt, w1t, *hgs, end_grad, mid, stats_2),
        [(big, F32), (big, BF16), ((64, 128), F32)],
        [(big, F32)],
        micros=6,
    )
    dwo, dq, dkv = call(
        attend_back_kernel,
        (scal, kt, vt, qs, kv, wo, low_grad, att, lse),
        [((D, D), BF16), (big, BF16), ((2 * D, QUARTER), BF16)],
        [(big, BF16)],
        micros=10,
    )
    a_keep, a_send, first_grad = call(
        first_kernel,
        (
            scal, bt, wq, wkv, wr, first, red, raw, stat_r, dq, dkv, dwo, dw2, *dks, entry, stats_1, g_one, g_two,
        ),
        [((16, A_ROWS, 128), BF16), ((16, A_ROWS, 128), BF16), (big, F32)],
        [((64, 128), F32), ((4 * D, QUARTER), F32), ((4 * D, QUARTER), BF16)],
        micros=11,
    )
    sum_a = scatter(a_keep, a_send)
    (token_grad,) = call(
        token_kernel,
        (scal, bt, first_grad, mid_grad, entry, stats_1),
        [(big, F32)],
        [(big, BF16), (big, BF16)],
        micros=5,
    )
    if group > 1:

        def total(part):
            full = lax.all_gather(part, axes[1], axis=0)
            return jnp.sum(lax.dynamic_slice_in_dim(full, start, group, axis=0), axis=0)

        sum_a, sum_b, sum_c = total(sum_a), total(sum_b), total(sum_c)
    query_g, output_g, keyval_g, reduce_g = select([sum_a], table_out_a, [25, 25, 50, 100], F32, True)
    contract_g, expand_g = select([sum_a, sum_b], table_out_b, [100, 100], F32, True)
    (merge_g,) = select([sum_c], table_out_c, [360], F32, True)
    depth_g = sum_b[160:200, 64:73]
    biases_g = sum_a[240:242].reshape(-1)[:192]
    gains_g = lax.dynamic_slice(sum_a[242], (spot,), (56,))
    grads = [query_g, keyval_g, reduce_g, output_g, expand_g, depth_g, contract_g, merge_g, gains_g, biases_g]
    grads = [grad.reshape(-1) for grad in grads]
    if group > 1:
        mine = index % group
        grads = [lax.dynamic_index_in_dim(grad.reshape(group, -1), mine, keepdims=False) for grad in grads]
    return (four[None], token_grad[None], *grads)


def solution(mesh):
    axes = ("dp", "fs")
    devices = mesh.shape["dp"] * mesh.shape["fs"]
    group = devices // SUPER
    if devices != SUPER * group or mesh.shape["fs"] % group:
        raise ValueError("unsupported mesh")
    one, three = P(axes), P(axes, None, None)
    return jax.shard_map(
        functools.partial(local, group, axes),
        mesh=mesh,
        in_specs=(three, one, three) + (one,) * 10,
        out_specs=(three, three) + (one,) * 10,
        check_vma=False,
    )
```

```python
import functools

import jax
import jax.numpy as jnp
import numpy as np
from jax import lax
from jax.experimental import pallas as pl
from jax.experimental.pallas import tpu as pltpu
from jax.sharding import PartitionSpec as P


D = 320
HEADS = 5
FF = 1280
OUT_D = 512
SIDE = 32
QUARTER = 256
TOKENS = SIDE * SIDE
MERGE_PAD = 2944
SUPER = 32
FLIPS = (2, 4, 8, 16)
EPS = 1e-06
F32, BF16, I32 = jnp.float32, jnp.bfloat16, jnp.int32

B_Q, B_R, C_R, B_O, C_1, C_2, B_1, B_DW, B_2, C_S, B_M, C_M = 0, 5, 10, 15, 20, 25, 30, 50, 70, 75, 80, 88
G_R, G_1, G_2, G_S, G_M = 96, 101, 106, 111, 116

PARTS = ((0, 1), (1, 3), (4, 1))
A_ROWS, B_ROWS, C_ROWS = 208, 224, 368
SMALL_ROW = 200
A_SPLIT = 104
VMEM_LIMIT = 24 * 1024 * 1024
VMEM_ALL = 60 * 1024 * 1024


def slot_of(xor):
    return (xor >> 1) | ((xor & 1) << 4)


def xor_of(slot):
    return ((slot & 15) << 1) | (slot >> 4)


def dot(a, b):
    return jnp.dot(a, b, preferred_element_type=F32)


def dot_nt(a, b):
    return lax.dot_general(a, b, (((1,), (1,)), ((), ())), preferred_element_type=F32)


def dot_tn(a, b):
    return lax.dot_general(a, b, (((0,), (0,)), ((), ())), preferred_element_type=F32)


def iota(shape, axis):
    return lax.broadcasted_iota(I32, shape, axis)


def one_hot(test):
    return jnp.where(test, 1.0, 0.0).astype(BF16)


def lanes(index, width=128):
    return pl.ds(pl.multiple_of(index * width, width), width)


def loop(count, body):
    def step(index, carry):
        body(index)
        return carry

    lax.fori_loop(0, count, step, 0)


def column(table, start, count):
    return jnp.concatenate(
        [jnp.broadcast_to(table[:, h : h + 1], (64, 128)) for h in range(start, start + count)], axis=0
    )


def put_column(table, start, values):
    for h in range(values.shape[0] // 64):
        table[:, start + h : start + h + 1] = values[64 * h : 64 * h + 64, 0:1]


def token_place(lane):
    quad = lane >> 8
    row = 2 * ((lane >> 4) & 15) + (quad >> 1)
    col = 2 * (lane & 15) + (quad & 1)
    return row, col


def token_mask(tile, side, width=128):
    row, col = token_place(iota((1, width), 1) + tile * width)
    return jnp.where((row < side) & (col < side), 1.0, 0.0)


def key_place(index):
    return index >> 4, index & 15


def select_kernel(count, bases, exact, small, me_at, *refs):
    sources, refs = refs[:count], refs[count:]
    if small:
        scal, biases, gains = refs[:3]
        refs = refs[3:]
    low_ref, high_ref = refs[:2]
    rows_ref, sems, held = refs[-count - 2], refs[-count - 1], refs[-count:]
    outs = refs[2 : -count - 2]
    copies = [
        pltpu.make_async_copy(source, place, sems.at[n]) for n, (source, place) in enumerate(zip(sources, held))
    ]
    for copy in copies:
        copy.start()
    half = rows_ref.shape[0] // 2
    rows_ref[...] = jnp.zeros_like(rows_ref)
    total_rows = low_ref.shape[0]
    place = iota((total_rows, 2 * half), 1)
    pick_low = one_hot(place == low_ref[...])
    pick_high = one_hot(place == high_ref[...])
    for copy in copies:
        copy.wait()
    for source, base in zip(held, bases):
        rows_ref[base : base + source.shape[0], :] = source[...].astype(F32)
    if small == "in":
        rows_ref[me_at : me_at + 1, :] = biases[:, 0:128].astype(F32)
        rows_ref[me_at + 1 : me_at + 2, 0:64] = biases[:, 128:192].astype(F32)
        wide = jnp.concatenate([gains[...].astype(F32), jnp.zeros((1, 72), F32)], axis=1)
        wide = jnp.broadcast_to(wide, (8, 128))
        rows_ref[me_at + 2 : me_at + 3, :] = pltpu.roll(wide, (56 * scal[0]) & 63, 1)[0:1, :]
    rows_ref[half:, :] = pltpu.roll(rows_ref[0:half, :], 64, 1)
    total = rows_ref[...]
    high = total.astype(BF16)
    pieces = [high]
    if exact:
        pieces.append((total - high.astype(F32)).astype(BF16))
    low = sum(dot(pick_low, piece) for piece in pieces)
    upper = sum(dot(pick_high, piece) for piece in pieces)
    chosen = jnp.where(iota((total_rows, 128), 1) < 64, low, upper)
    at = 0
    for out in outs:
        rows = out.shape[0]
        if rows == 1:
            continue
        out[...] = chosen[at : at + rows, :].astype(out.dtype)
        at += -(-rows // 16) * 16
    if small == "out":
        bias_out, gain_out = outs[-2:]
        bias_out[:, 0:128] = held[0][me_at : me_at + 1, :]
        bias_out[:, 128:192] = held[0][me_at + 1 : me_at + 2, 0:64]
        wide = jnp.broadcast_to(held[0][me_at + 2 : me_at + 3, :], (8, 128))
        gain_out[...] = pltpu.roll(wide, (128 - ((56 * scal[0]) & 63)) & 127, 1)[0:1, 0:56]


def select(sources, table, out_rows, dtype, exact, small="", vectors=()):
    bases, at = [], 0
    for source in sources:
        bases.append(at)
        at += -(-source.shape[0] // 16) * 16
    half = at + (16 if small == "in" else 0)
    low, high = table(bases + [at], half)
    total = sum(-(-rows // 16) * 16 for rows in out_rows)
    low = np.concatenate([low, np.full(total - len(low), -1)]).astype(np.int32)[:, None]
    high = np.concatenate([high, np.full(total - len(high), -1)]).astype(np.int32)[:, None]
    outs = [jax.ShapeDtypeStruct((rows, 128), dtype) for rows in out_rows]
    specs = [pl.BlockSpec(memory_space=pltpu.VMEM if exact else pltpu.HBM)] * len(sources)
    if small:
        specs += [pl.BlockSpec(memory_space=pltpu.SMEM)] + [pl.BlockSpec(memory_space=pltpu.VMEM)] * 2
    specs += [pl.BlockSpec(memory_space=pltpu.VMEM)] * 2
    if small == "out":
        outs += [jax.ShapeDtypeStruct((1, 192), F32), jax.ShapeDtypeStruct((1, 56), F32)]
    return pl.pallas_call(
        functools.partial(select_kernel, len(sources), tuple(bases), exact, small, at if small == "in" else SMALL_ROW),
        in_specs=specs,
        out_shape=outs,
        scratch_shapes=[pltpu.VMEM((2 * half, 128), F32), pltpu.SemaphoreType.DMA((len(sources),))]
        + [pltpu.VMEM(source.shape, source.dtype) for source in sources],
        compiler_params=pltpu.CompilerParams(vmem_limit_bytes=VMEM_ALL if small == "in" else VMEM_LIMIT),
        cost_estimate=cost(2),
    )(*sources, *vectors, low, high)


def pair(half, low_src, high_src):
    low = -1 if low_src is None else low_src[0] + low_src[1] // 2 + half * (low_src[1] % 2)
    high = -1 if high_src is None else high_src[0] + high_src[1] // 2 + half * (1 - high_src[1] % 2)
    return low, high


def chunk_sources(bases, row, c):
    q, o, kv = bases
    if c < 6 or c >= 8:
        base, first = ((q, 0), (kv, 0), (kv, 10), None, (o, 0))[c // 2]
        at = 5 * (first + row) + 2 * (c % 2)
        return (base, at), (base, at + 1)
    if c == 6:
        return (q, 5 * row + 4), (kv, 5 * row + 4)
    return (kv, 5 * (10 + row) + 4), (o, 5 * row + 4)


def a_place(kind, row, c):
    if row < 8:
        return 16 * c + 8 * kind + row
    return 160 + 8 * (c // 2) + 4 * kind + 2 * (c % 2) + row - 8


def b_place(row, c):
    if row < 8:
        return 8 * c + row
    return 80 + 8 * (c // 4) + 2 * (c % 4) + row - 8


def table_a(bases, half):
    q, o, kv, r, small = bases
    rows = [(-1, -1)] * A_ROWS
    for c in range(10):
        for row in range(10):
            at = 20 * row + 2 * c
            rows[a_place(0, row, c)] = pair(half, (r, at), (r, at + 1))
            rows[a_place(1, row, c)] = pair(half, *chunk_sources((q, o, kv), row, c))
    for row in range(3):
        rows[SMALL_ROW + row] = pair(half, (small, 2 * row), (small, 2 * row + 1))
    return np.array(rows).T


def table_b(bases, half):
    w2, w1, dw, _ = bases
    rows = [(-1, -1)] * B_ROWS
    for c in range(10):
        for row in range(10):
            at = 20 * row + 2 * c
            rows[b_place(row, c)] = pair(half, (w2, at), (w2, at + 1))
    for c in range(3):
        for row in range(40):
            at = 5 * row + 2 * c
            rows[104 + 40 * c + row] = pair(half, (w1, at), (w1, at + 1) if c < 2 else (dw, 2 * row + 1))
    return np.array(rows).T


def table_c(bases, half):
    m, _ = bases
    rows = []
    for c in range(23):
        for row in range(16):
            at = 45 * row + 2 * c
            rows.append(pair(half, (m, at), (m, at + 1) if c < 22 else None))
    return np.array(rows).T


def padded(rows):
    return rows + [(-1, -1)] * (-len(rows) % 16)


def table_out_a(bases, half):
    a, _ = bases

    def square(first, tail, count):
        def source(at):
            row, piece = divmod(at, 5)
            pick = row // 10
            if piece < 4:
                return (a + a_place(1, row % 10, first[pick] + piece // 2), piece % 2)
            chunk, side = tail[pick]
            return (a + a_place(1, row % 10, chunk), side)

        return [source(at) for at in range(count)]

    wide = [(a + a_place(0, at // 20, at % 20 // 2), at % 2) for at in range(200)]

    def emit(sources):
        rows = [pair(half, s, t) for s, t in zip(sources[0::2], sources[1::2])]
        return padded(rows)

    rows = emit(square((0,), ((6, 0),), 50))
    rows += emit(square((8,), ((7, 1),), 50))
    rows += emit(square((2, 4), ((6, 1), (7, 0)), 100))
    rows += emit(wide)
    return np.array(rows).T


def table_out_b(bases, half):
    b, _ = bases

    def w1(at):
        row, piece = divmod(at, 5)
        return (b + 104 + piece // 2 * 40 + row, piece % 2)

    rows = []
    wide = [(b + b_place(at // 20, at % 20 // 2), at % 2) for at in range(200)]
    for sources in (wide, [w1(at) for at in range(200)]):
        rows += padded([pair(half, s, t) for s, t in zip(sources[0::2], sources[1::2])])
    return np.array(rows).T


def table_out_c(bases, half):
    c, _ = bases

    def source(at):
        row, piece = divmod(at, 45)
        return (c + piece // 2 * 16 + row, piece % 2)

    sources = [source(at) for at in range(720)]
    return np.array(padded([pair(half, s, t) for s, t in zip(sources[0::2], sources[1::2])])).T


def split_ten(row, per, magic):
    owner = (row * magic) >> 16
    return owner, row - per * owner


def place_a(row, me, rest_of):
    kind = jnp.where(row >= D, 1, 0)
    owner, rest = split_ten(row - D * kind, 10, 6554)
    slot = slot_of(owner ^ me)
    if rest_of is None:
        return jnp.where(rest < 8, slot * 16 + 8 * kind + rest, -1)
    return jnp.where(rest >= 8, slot * 8 + 4 * kind + 2 * rest_of + rest - 8, -1)


def place_b(row, me, group):
    odd = jnp.where(row >= D, 1, 0)
    owner, rest = split_ten(row - D * odd, 10, 6554)
    slot = slot_of(owner ^ me)
    if group is None:
        return jnp.where(rest < 8, slot * 16 + 8 * odd + rest, -1)
    return jnp.where(rest >= 8, slot * 8 + 4 * group + 2 * odd + rest - 8, -1)


def keyval_rows(shape, ten_axis, upper):
    ten = iota(shape, ten_axis)
    owner, rest = split_ten(ten, 10, 6554)
    return one_hot(iota(shape, 1 - ten_axis) == 20 * owner + rest + (10 if upper else 0))


def norm(values, gain, shift):
    mean = jnp.mean(values, axis=0, keepdims=True)
    centred = values - mean
    rstd = lax.rsqrt(jnp.mean(centred * centred, axis=0, keepdims=True) + EPS)
    return centred * rstd * gain + shift, mean, rstd


def norm_back(grad, hat, rstd, gain):
    scaled = grad * gain
    return rstd * (
        scaled
        - jnp.mean(scaled, axis=0, keepdims=True)
        - hat * jnp.mean(scaled * hat, axis=0, keepdims=True)
    )


def stat_rows(mean, rstd):
    row = iota((8, mean.shape[1]), 0)
    return jnp.where(row == 0, mean, jnp.where(row == 1, rstd, 0.0))


def entry_kernel(scal, tokens, entry, stats):
    side = scal[1]
    for quad in range(4):
        lane = iota((1, 256), 1) + quad * 256
        row, col = token_place(lane)
        natural = row * SIDE + col
        pick = one_hot(iota((TOKENS, 256), 0) == natural)
        mask = jnp.where((row < side) & (col < side), 1.0, 0.0)
        entry[:, quad * 256 : quad * 256 + 256] = (dot(tokens[...], pick) * mask).astype(BF16)

    def body(tile):
        values = entry[:, lanes(tile)].astype(F32)
        mean = jnp.mean(values, axis=0, keepdims=True)
        centred = values - mean
        rstd = lax.rsqrt(jnp.mean(centred * centred, axis=0, keepdims=True) + EPS)
        stats[:, lanes(tile)] = stat_rows(mean, rstd)

    loop(8, body)


def small_table(me, low, high):
    gathered = jnp.concatenate(
        [half[:, SMALL_ROW : SMALL_ROW + 8, :].astype(F32).reshape(128, 128) for half in (low, high)], axis=0
    ).astype(BF16)
    vector = iota((128, 256), 0)
    place = iota((128, 256), 1)
    row = place & 7
    owner = xor_of(place >> 3) ^ me
    first = (7 * owner) >> 3
    straight = (
        ((row == 0) & (vector == 3 * owner))
        | ((row == 1) & (vector == 3 * owner + 2))
        | ((row == 2) & (vector == 96 + first))
    )
    turned = ((row == 0) & (vector == 3 * owner + 1)) | ((row == 2) & (vector == 97 + first))
    rows = dot(one_hot(straight), gathered) + pltpu.roll(dot(one_hot(turned), gathered), 64, 1)
    return jnp.transpose(rows)[0:64, :]


def project_kernel(scal, low, high, entry, stats, wq, wkv, wr, wo, first, qs, raw, stat_r, red, kv, kt, vt, bt, main, square, redin):
    me = scal[0]
    bt[...] = small_table(me, low, high)
    main[512:, :] = jnp.zeros((512, 1280), BF16)
    for half, source in enumerate((low, high)):

        def chunk(c, half=half, source=source):
            block = source[:, pl.ds(pl.multiple_of(16 * c, 16), 16), :].reshape(256, 128)
            main[256 * half : 256 * half + 256, lanes(c)] = block

        loop(10, chunk)
        block = source[:, 160:208, :].astype(F32)
        for c in range(5):
            part = block[:, 8 * c : 8 * c + 8].reshape(128, 128).astype(BF16)
            for odd in range(2):
                at = 512 + 256 * odd + 128 * half
                main[at : at + 128, 256 * c + 128 * odd : 256 * c + 128 * odd + 128] = part
    row = iota((2 * D, 1), 0)
    pick = jnp.concatenate(
        [one_hot(iota((2 * D, 512), 1) == place_a(row, me, None))]
        + [one_hot(iota((2 * D, 256), 1) == place_a(row, me, odd)) for odd in range(2)],
        axis=1,
    )

    def assemble(p):
        block = dot(pick, main[:, lanes(p, 256)]).astype(BF16)
        wr[:, lanes(p, 256)] = block[0:D]
        square[:, lanes(p, 256)] = block[D:]

    loop(5, assemble)
    wq[:, 0:256] = square[:, 0:256]
    wo[:, 0:256] = square[:, 1024:1280]
    tails = square[:, 768:1024].astype(F32)
    turned = pltpu.roll(tails, 64, 1)
    wq[:, 256:320] = tails[:, 0:64].astype(BF16)
    wo[:, 256:320] = turned[:, 0:64].astype(BF16)
    lower, upper = keyval_rows((2 * D, D), 1, False), keyval_rows((2 * D, D), 1, True)
    wkv[:, 0:256] = (dot(lower, square[:, 256:512]) + dot(upper, square[:, 512:768])).astype(BF16)
    tail = dot(lower, turned[:, 128:256].astype(BF16)) + dot(upper, tails[:, 128:256].astype(BF16))
    wkv[:, 256:320] = tail[:, 0:64].astype(BF16)

    gain, shift = column(bt, G_1, 5), column(bt, C_1, 5)

    def body(tile):
        centred = entry[:, lanes(tile)].astype(F32) - stats[0:1, lanes(tile)]
        first[:, lanes(tile)] = (centred * stats[1:2, lanes(tile)] * gain + shift).astype(BF16)

    loop(8, body)
    for quad in range(4):
        redin[D * quad : D * quad + D, :] = first[:, 256 * quad : 256 * quad + 256]
    bias = column(bt, B_R, 5)
    bias = jnp.concatenate([bias, bias], axis=1)
    raw[...] = dot(wr[...], redin[...]) + bias
    gain, shift = column(bt, G_R, 5), column(bt, C_R, 5)
    for tile in range(2):
        at = slice(128 * tile, 128 * tile + 128)
        values, mean, rstd = norm(raw[:, at], gain, shift)
        red[:, at] = values.astype(BF16)
        stat_r[:, at] = stat_rows(mean, rstd)
    keyval = dot(wkv[...], red[...])
    kv[...] = keyval.astype(BF16)
    turned = jnp.transpose(keyval)
    for h in range(HEADS):
        kt[h] = turned[:, 64 * h : 64 * h + 64].astype(BF16)
        vt[h] = turned[:, D + 64 * h : D + 64 * h + 64].astype(BF16)
    bias = column(bt, B_Q, 5)
    bias = jnp.concatenate([bias, bias], axis=1)

    def query(quad):
        at = lanes(quad, 256)
        qs[:, at] = (dot(wq[...], first[:, at]) + bias).astype(BF16) * BF16(0.125)

    loop(4, query)


def key_bias(side):
    i, j = key_place(iota((QUARTER, 1), 0))
    return jnp.where((i < (side >> 1)) & (j < (side >> 1)), 0.0, -10000.0)


def attend_kernel(scal, kt, qs, kv, att, lse):
    bias = key_bias(scal[1])

    def head(h):
        rows = pl.ds(pl.multiple_of(64 * h, 64), 64)
        values = kv[pl.ds(pl.multiple_of(D + 64 * h, 64), 64), :]
        for quad in range(4):
            at = slice(256 * quad, 256 * quad + 256)
            scores = dot(kt[h], qs[rows, at]) + bias
            top = jnp.max(scores, axis=0, keepdims=True)
            weights = jnp.exp(scores - top)
            total = jnp.sum(weights, axis=0, keepdims=True)
            lse[h, :, at] = top + jnp.log(total)
            probs = (weights * (1.0 / total)).astype(BF16)
            att[rows, at] = dot(values, probs).astype(BF16)

    loop(HEADS, head)


def middle_kernel(scal, bt, wo, att, entry, mid, sec, stats, work):
    side = scal[1]
    work[...] = dot(wo[...], att[...])
    bias, gain, shift = column(bt, B_O, 5), column(bt, G_2, 5), column(bt, C_2, 5)

    def body(tile):
        at = lanes(tile)
        mask = token_mask(tile, side)
        values = entry[:, at].astype(F32) + mask * (work[:, at] + bias)
        mid[:, at] = values
        normed, mean, rstd = norm(values, gain, shift)
        stats[:, at] = stat_rows(mean, rstd)
        sec[0:D, at] = (normed.astype(BF16).astype(F32) * mask).astype(BF16)
        sec[D : D + 64, at] = jnp.where(iota((64, 128), 0) == 9, mask, 0.0).astype(BF16)

    loop(8, body)


def ffn_weights_kernel(scal, bt, low, high, w1, w1t, w2, w2t, taps, main, rest, wide, picks):
    me = scal[0]
    for half, source in enumerate((low, high)):
        for p in range(5):
            block = source[:, 16 * p : 16 * p + 16, :].reshape(256, 128)
            main[256 * half : 256 * half + 256, 128 * p : 128 * p + 128] = block
        block = source[:, 80:112, :].astype(F32)
        for c in range(3):
            part = block[:, 8 * c : 8 * c + 8].reshape(128, 128).astype(BF16)
            rest[128 * half : 128 * half + 128, 128 * c : 128 * c + 128] = part

        def expansion(slot, half=half, source=source):
            owner = ((slot << 1) | half) ^ me
            block = source[slot, 80:224, :].astype(F32)
            rows = pl.ds(pl.multiple_of(40 * owner, 8), 40)
            for c in range(3):
                wide[rows, 128 * c : 128 * c + 128] = block[24 + 40 * c : 64 + 40 * c]

        loop(16, expansion)
    row = iota((2 * D, 1), 0)
    for group in range(2):
        picks[group, :, 0:512] = one_hot(iota((2 * D, 512), 1) == place_b(row, me, None))
        picks[group, :, 512:768] = one_hot(iota((2 * D, 256), 1) == place_b(row, me, group))

    def contraction(p):
        source = jnp.concatenate([main[:, lanes(p)], rest[:, lanes(p >> 1)]], axis=0)
        block = dot(picks[p & 1], source)
        block = jnp.concatenate([block[0:D], block[D:]], axis=1)
        w2[:, lanes(p, 256)] = block.astype(BF16)
        w2t[pl.ds(pl.multiple_of(256 * p, 256), 256), :] = jnp.transpose(block).astype(BF16)

    loop(5, contraction)
    bias = column(bt, B_1, 20)
    lane = iota((FF, 128), 1)
    tail = wide[:, 256:384]
    low_tail = tail.astype(BF16)

    def spread(tap):
        taps[tap] = dot(low_tail, one_hot(iota((128, 128), 0) == 64 + tap))

    loop(9, spread)
    taps[9] = column(bt, B_DW, 20)
    w1[:, 0:256] = wide[:, 0:256].astype(BF16)
    w1[:, 256:384] = jnp.where(lane < 64, tail, jnp.where(lane == 73, bias, 0.0)).astype(BF16)

    def turn(p):
        rows = pl.ds(pl.multiple_of(256 * p, 256), 256)
        w1t[:, lanes(p, 256)] = jnp.transpose(wide[rows, :])[0:D].astype(BF16)

    loop(5, turn)


def edge_masks():
    lane = iota((1, 128), 1)
    j = lane & 15
    return jnp.where(j != 0, 1.0, 0.0), jnp.where(j != 15, 1.0, 0.0), lane >= 16, lane < 112


def left_of(tiles):
    return [pltpu.roll(tile, 1, 1) for tile in tiles]


def right_of(tiles):
    return [pltpu.roll(tile, 127, 1) for tile in tiles]


def above(tiles, inside):
    turned = [pltpu.roll(tile, 16, 1) for tile in tiles]
    return [jnp.where(inside, turned[0], 0.0), jnp.where(inside, turned[1], turned[0])]


def below(tiles, inside):
    turned = [pltpu.roll(tile, 112, 1) for tile in tiles]
    return [jnp.where(inside, turned[0], turned[1]), jnp.where(inside, turned[1], 0.0)]


def times(tiles, factor):
    return [tile * factor for tile in tiles]


def plus(*many):
    return [functools.reduce(lambda a, b: a + b, tiles) for tiles in zip(*many)]


def tile_at(a, e, half):
    start = 256 * (2 * a + e) + 128 * half
    return slice(start, start + 128)


def quads(ref, rows):
    return [[[ref[rows, tile_at(a, e, half)] for half in range(2)] for e in range(2)] for a in range(2)]


LOG2E = float(np.log2(np.e))


def gelu_parts(x):
    y = x * np.float32(0.5**0.5)
    cdf = lax.erf(y) * 0.5 + 0.5
    bell = jnp.exp2(y * y * np.float32(-LOG2E) + np.float32(-0.5 * np.log2(2.0 * np.pi)))
    return x * cdf, cdf + x * bell


def ffn_kernel(scal, w1, taps, sec, act, slope, hid):
    j_first, j_last, i_first, i_last = edge_masks()

    def block(step):
        start = pl.multiple_of(step * 256, 256)
        hid[...] = dot(w1[pl.ds(start, 256), :], sec[...])

        def group(index):
            rows = pl.ds(pl.multiple_of(index * 16, 16), 16)
            out_rows = pl.ds(pl.multiple_of(start + index * 16, 16), 16)
            k = [taps[n, out_rows, :] for n in range(10)]
            first = [k[3 * r] * j_first for r in range(3)]
            last = [k[3 * r + 2] * j_last for r in range(3)]
            quad = quads(hid, rows)
            left = [left_of(quad[a][1]) for a in range(2)]
            right = [right_of(quad[a][0]) for a in range(2)]

            def across(a, e, r):
                if e == 0:
                    parts = zip(left[a], quad[a][0], quad[a][1])
                    return [first[r] * x + k[3 * r + 1] * y + k[3 * r + 2] * z for x, y, z in parts]
                parts = zip(quad[a][0], quad[a][1], right[a])
                return [k[3 * r] * x + k[3 * r + 1] * y + last[r] * z for x, y, z in parts]

            for e in range(2):
                up = above(across(1, e, 0), i_first)
                down = below(across(0, e, 2), i_last)
                outs = (plus(across(0, e, 1), across(1, e, 2), up), plus(across(0, e, 0), across(1, e, 1), down))
                for a in range(2):
                    for half in range(2):
                        value, grad = gelu_parts(outs[a][half] + k[9])
                        act[out_rows, tile_at(a, e, half)] = value.astype(BF16)
                        slope[out_rows, tile_at(a, e, half)] = grad.astype(BF16)

        loop(16, group)

    loop(5, block)


def ending_kernel(scal, bt, w2, act, mid, end, sect, stats, work):
    side = scal[1]
    work[...] = dot(w2[...], act[...])
    bias, gain, shift = column(bt, B_2, 5), column(bt, G_S, 5), column(bt, C_S, 5)

    def body(tile):
        at = lanes(tile)
        mask = token_mask(tile, side)
        values = mid[:, at] + mask * (work[:, at] + bias)
        end[:, at] = values
        normed, mean, rstd = norm(values, gain, shift)
        stats[:, at] = stat_rows(mean, rstd)
        sect[:, at] = (normed.astype(BF16).astype(F32) * mask).astype(BF16)

    loop(8, body)


def lane_sum(values):
    return jnp.sum(values, axis=1, keepdims=True)


def merge_kernel(scal, bt, c_low, c_high, sect, end, stats, cot, four, keep, send, end_grad, branch, grads, wm, patch, mg, back, work, natural):
    me, side = scal[0], scal[1]
    grads[...] = jnp.zeros_like(grads)
    for half, source in enumerate((c_low, c_high)):

        def place(c, half=half, source=source):
            block = source[:, pl.ds(pl.multiple_of(16 * c, 16), 16), :].reshape(256, 128)
            wm[256 * half : 256 * half + 256, lanes(c)] = block

        loop(23, place)

    def reorder(to_owner):
        def one(slot):
            at = pl.ds(pl.multiple_of(16 * slot, 16), 16)
            owner = pl.ds(pl.multiple_of((xor_of(slot) ^ me) * 16, 16), 16)
            to_owner(at, owner)

        loop(32, one)

    j_first, j_last, i_first, i_last = edge_masks()
    quad = [[[t.astype(F32) for t in pair] for pair in row] for row in quads(sect, slice(None))]
    left = [times(left_of(quad[a][1]), j_first) for a in range(2)]
    pieces = (
        above(left[1], i_first),
        above(quad[1][0], i_first),
        above(quad[1][1], i_first),
        left[0],
        quad[0][0],
        quad[0][1],
        left[1],
        quad[1][0],
        quad[1][1],
    )
    for n, piece in enumerate(pieces):
        for half in range(2):
            patch[D * n : D * n + D, 128 * half : 128 * half + 128] = piece[half].astype(BF16)
    patch[9 * D :, :] = jnp.zeros((MERGE_PAD - 9 * D, 256), BF16)
    bias, gain, shift = column(bt, B_M, 8), column(bt, G_M, 8), column(bt, C_M, 8)
    work[...] = dot(wm[...], patch[...])

    def from_slots(at, owner):
        natural[owner, :] = work[at, :]

    reorder(from_slots)
    half_side = side >> 1
    for tile in range(2):
        at = slice(128 * tile, 128 * tile + 128)
        i, j = key_place(iota((1, 128), 1) + 128 * tile)
        mask = jnp.where((i < half_side) & (j < half_side), 1.0, 0.0)
        values = natural[:, at] + bias
        mean = jnp.mean(values, axis=0, keepdims=True)
        centred = values - mean
        rstd = lax.rsqrt(jnp.mean(centred * centred, axis=0, keepdims=True) + EPS)
        hat = centred * rstd
        four[:, at] = ((hat * gain + shift) * mask).astype(BF16)
        grad = cot[:, at].astype(F32) * mask
        low = norm_back(grad, hat, rstd, gain).astype(BF16)
        natural[:, at] = low.astype(F32)
        parts = (grad * hat, grad, low.astype(F32))
        sums = parts if tile == 0 else [s + v for s, v in zip(sums, parts)]
    put_column(grads, G_M, lane_sum(sums[0]))
    put_column(grads, C_M, lane_sum(sums[1]))
    put_column(grads, B_M, lane_sum(sums[2]))

    def to_slots(at, owner):
        mg[at, :] = natural[owner, :].astype(BF16)

    reorder(to_slots)

    def widths(body):
        loop(11, lambda c: body(pl.multiple_of(c * 256, 256), 256))
        body(11 * 256, 128)

    def patch_grad(start, width):
        back[pl.ds(start, width), :] = dot_tn(wm[:, pl.ds(start, width)], mg[...])

    widths(patch_grad)

    def piece(n):
        return [back[D * n : D * n + D, 128 * half : 128 * half + 128] for half in range(2)]

    results = (
        piece(4),
        plus(piece(5), times(right_of(piece(3)), j_last)),
        plus(piece(7), below(piece(1), i_last)),
        plus(
            piece(8),
            times(right_of(piece(6)), j_last),
            below(plus(piece(2), times(right_of(piece(0)), j_last)), i_last),
        ),
    )
    for n, values in enumerate(results):
        for half in range(2):
            end_grad[:, 256 * n + 128 * half : 256 * n + 128 * half + 128] = values[half]
    gain = column(bt, G_S, 5)
    zeros = jnp.zeros((D, 128), F32)

    def body(tile, carry):
        at = lanes(tile)
        mask = token_mask(tile, side)
        grad = end_grad[:, at] * mask
        hat = (end[:, at] - stats[0:1, at]) * stats[1:2, at]
        result = norm_back(grad, hat, stats[1:2, at], gain)
        end_grad[:, at] = result
        low = (result * mask).astype(BF16)
        branch[:, at] = low
        return carry[0] + grad * hat, carry[1] + grad, carry[2] + low.astype(F32)

    sums = lax.fori_loop(0, 8, body, (zeros, zeros, zeros))
    put_column(grads, G_S, lane_sum(sums[0]))
    put_column(grads, C_S, lane_sum(sums[1]))
    put_column(grads, B_2, lane_sum(sums[2]))

    def give(start, width):
        block = dot_nt(mg[...], patch[pl.ds(start, width), :]).astype(BF16)
        for c in range(width // 128):
            to = pl.ds(pl.multiple_of((start >> 3) + 16 * c, 16), 16)
            part = block[:, 128 * c : 128 * c + 128].reshape(32, 16, 128)
            keep[:, to, :] = part[0:16]
            send[:, to, :] = part[16:32]

    widths(give)


def ffn_back_kernel(first_part, count, scal, w1, w2t, taps, sec, slope, branch, hg, dkx, hid, cg):
    side = scal[1]
    j_first, j_last, i_first, i_last = edge_masks()
    masks = [token_mask(tile, side) for tile in range(8)]
    lane = iota((16, 128), 1)

    def part(number):
        block = pl.ds(pl.multiple_of(256 * (first_part + number), 256), 256)
        cg[...] = dot(w2t[block, :], branch[...])
        hid[...] = dot(w1[block, :], sec[...])
        loop(16, functools.partial(group, number))

    def group(number, index):
        rows = pl.ds(pl.multiple_of(index * 16, 16), 16)
        from_rows = pl.ds(pl.multiple_of(256 * (first_part + number) + index * 16, 16), 16)
        to_rows = pl.ds(pl.multiple_of(256 * number + index * 16, 16), 16)
        k = [taps[n, from_rows, :] for n in range(9)]
        quad = quads(cg, rows)
        weight = quads(slope, from_rows)
        quad = [
            [[quad[a][e][h] * weight[a][e][h].astype(F32) for h in range(2)] for e in range(2)] for a in range(2)
        ]
        bias = functools.reduce(lambda x, y: x + y, [t for row in quad for pair in row for t in pair])
        across = [
            (
                (times(left_of(quad[a][1]), j_first), quad[a][0], quad[a][1]),
                (quad[a][0], quad[a][1], times(right_of(quad[a][0]), j_last)),
            )
            for a in range(2)
        ]
        sums = [None] * 10
        for e in range(2):
            upper = [above(tiles, i_first) for tiles in across[1][e]]
            lower = [below(tiles, i_last) for tiles in across[0][e]]
            for a, near in ((0, (upper, across[0][e], across[1][e])), (1, (across[0][e], across[1][e], lower))):
                for half in range(2):
                    value = hid[rows, tile_at(a, e, half)]
                    total = None
                    for r in range(3):
                        for c in range(3):
                            tap = 3 * (2 - r) + (2 - c)
                            term = k[tap] * near[r][c][half]
                            total = term if total is None else total + term
                            term = value * near[r][c][half]
                            sums[tap] = term if sums[tap] is None else sums[tap] + term
                    low = (total * masks[2 * (2 * a + e) + half]).astype(BF16)
                    hg[to_rows, tile_at(a, e, half)] = low
                    low = low.astype(F32)
                    sums[9] = low if sums[9] is None else sums[9] + low
        table = jnp.where(lane == 9, lane_sum(bias), 0.0)
        for n in range(10):
            table = jnp.where(lane == (n if n < 9 else 10), lane_sum(sums[n]), table)
        dkx[to_rows, :] = table

    loop(count, part)


def middle_back_kernel(scal, bt, w1t, hg0, hg1, hg2, end_grad, mid, stats, mid_grad, low_grad, grads, work):
    side = scal[1]
    work[...] = sum(
        dot(w1t[:, 256 * at : 256 * (at + count)], hg[...]) for hg, (at, count) in zip((hg0, hg1, hg2), PARTS)
    )
    grads[...] = jnp.zeros_like(grads)
    gain = column(bt, G_2, 5)
    zeros = jnp.zeros((D, 128), F32)

    def body(tile, carry):
        at = lanes(tile)
        mask = token_mask(tile, side)
        grad = work[:, at]
        hat = (mid[:, at] - stats[0:1, at]) * stats[1:2, at]
        result = end_grad[:, at] + norm_back(grad, hat, stats[1:2, at], gain)
        mid_grad[:, at] = result
        low = (result * mask).astype(BF16)
        low_grad[:, at] = low
        return carry[0] + grad * hat, carry[1] + grad, carry[2] + low.astype(F32)

    sums = lax.fori_loop(0, 8, body, (zeros, zeros, zeros))
    put_column(grads, G_2, lane_sum(sums[0]))
    put_column(grads, C_2, lane_sum(sums[1]))
    put_column(grads, B_O, lane_sum(sums[2]))


def pack_b_kernel(scal, hg0, hg1, hg2, dk0, dk1, dk2, sec, branch, act, keep, send, dw1, gather):
    me = scal[0]
    lane = iota((256, 128), 1)
    for hg, dkx, (at, count) in zip((hg0, hg1, hg2), (dk0, dk1, dk2), PARTS):

        def outer(n, hg=hg, dkx=dkx, at=at):
            rows = pl.ds(pl.multiple_of(256 * n, 256), 256)
            to = pl.ds(pl.multiple_of(256 * (n + at), 256), 256)
            part = dot_nt(hg[rows, :], sec[...])
            dw1[to, 0:256] = part[:, 0:256]
            turned = pltpu.roll(dkx[rows, :], 64, 1)
            dw1[to, 256:384] = jnp.where(lane < 64, part[:, 256:384], jnp.where(lane < 73, turned, 0.0))

        loop(count, outer)
    row = iota((1, 2 * D), 1)
    give = one_hot(iota((512, 2 * D), 0) == place_b(row, me, None))
    gather[:, 0:24, :] = jnp.zeros((32, 24, 128), F32)

    def contraction(p):
        block = dot_nt(branch[...], act[pl.ds(pl.multiple_of(256 * p, 256), 256), :]).astype(BF16)
        block = jnp.concatenate([block[:, 0:128], block[:, 128:256]], axis=0)
        full = dot(give, block).astype(BF16).reshape(32, 16, 128)
        to = pl.ds(pl.multiple_of(16 * p, 16), 16)
        keep[:, to, :] = full[0:16]
        send[:, to, :] = full[16:32]
        more = one_hot(iota((256, 2 * D), 0) == place_b(row, me, p & 1))
        to = pl.ds(pl.multiple_of(8 * (p >> 1), 8), 8)
        gather[:, to, :] += dot(more, block).reshape(32, 8, 128)

    loop(5, contraction)

    def expansion(owner):
        slot = slot_of(owner ^ me)
        rows = pl.ds(pl.multiple_of(40 * owner, 8), 40)
        for c in range(3):
            gather[slot, 24 + 40 * c : 64 + 40 * c, :] = dw1[rows, 128 * c : 128 * c + 128]

    loop(32, expansion)
    keep[:, 80:224, :] = gather[0:16].astype(BF16)
    send[:, 80:224, :] = gather[16:32].astype(BF16)


def attend_back_kernel(scal, kt, vt, qs, kv, wo, low_grad, att, lse, dwo, dq, dkv, og):
    bias = key_bias(scal[1])
    dwo[...] = dot_nt(low_grad[...], att[...]).astype(BF16)
    og[...] = dot_tn(wo[...], low_grad[...]).astype(BF16)

    def head(h):
        rows = pl.ds(pl.multiple_of(64 * h, 64), 64)
        more = pl.ds(pl.multiple_of(D + 64 * h, 64), 64)
        dk = jnp.zeros((64, 256), F32)
        dv = jnp.zeros((64, 256), F32)
        for quad in range(4):
            at = slice(256 * quad, 256 * quad + 256)
            probs = jnp.exp(dot(kt[h], qs[rows, at]) + bias - lse[h, :, at])
            grad = dot(vt[h], og[rows, at])
            mean = jnp.sum(probs * grad, axis=0, keepdims=True)
            score = (probs * (grad - mean)).astype(BF16)
            dq[rows, at] = (dot(kv[rows, :], score) * 0.125).astype(BF16)
            dk += dot_nt(qs[rows, at], score)
            dv += dot_nt(og[rows, at], probs.astype(BF16))
        dkv[rows, :] = dk.astype(BF16)
        dkv[more, :] = dv.astype(BF16)

    loop(HEADS, head)


def first_kernel(scal, bt, wq, wkv, wr, first, red, raw, stat_r, dq, dkv, dwo, dk0, dk1, dk2, entry, stats, g_one, g_two, keep, send, work, grads, wide, redin, stack, tails_of):
    me = scal[0]
    grads[...] = g_one[...] + g_two[...]
    for dkx, (at, count) in zip((dk0, dk1, dk2), PARTS):
        for m in range(4 * count):
            block = dkx[64 * m : 64 * m + 64, :]
            n = 4 * at + m
            grads[:, B_1 + n : B_1 + n + 1] = block[:, 10:11]
            grads[:, B_DW + n : B_DW + n + 1] = block[:, 9:10]
    for quad in range(4):
        redin[D * quad : D * quad + D, :] = first[:, 256 * quad : 256 * quad + 256]
    dred = dot_tn(wkv[...], dkv[...])
    gain = column(bt, G_R, 5)
    lows = []
    for tile in range(2):
        at = slice(128 * tile, 128 * tile + 128)
        grad = dred[:, at]
        hat = (raw[:, at] - stat_r[0:1, at]) * stat_r[1:2, at]
        low = norm_back(grad, hat, stat_r[1:2, at], gain).astype(BF16)
        lows.append(low)
        parts = (grad * hat, grad, low.astype(F32))
        sums = parts if tile == 0 else [s + v for s, v in zip(sums, parts)]
    put_column(grads, G_R, lane_sum(sums[0]))
    put_column(grads, C_R, lane_sum(sums[1]))
    put_column(grads, B_R, lane_sum(sums[2]))
    low = jnp.concatenate(lows, axis=1)
    wide[...] = dot_tn(wr[...], low)
    straight = dot_tn(wq[...], dq[...])
    for quad in range(4):
        at = slice(256 * quad, 256 * quad + 256)
        work[:, at] = straight[:, at] + wide[D * quad : D * quad + D, :]
    zeros = jnp.zeros((D, 128), F32)

    def body(tile, carry):
        at = lanes(tile)
        grad = work[:, at]
        hat = (entry[:, at].astype(F32) - stats[0:1, at]) * stats[1:2, at]
        return carry[0] + grad * hat, carry[1] + grad, carry[2] + dq[:, at].astype(F32)

    sums = lax.fori_loop(0, 8, body, (zeros, zeros, zeros))
    put_column(grads, G_1, lane_sum(sums[0]))
    put_column(grads, C_1, lane_sum(sums[1]))
    put_column(grads, B_Q, lane_sum(sums[2]))
    stack[0:D, :] = dot_nt(low, redin[...]).astype(BF16)
    dwq = dot_nt(dq[...], first[...])
    dwkv = dot_nt(dkv[...], red[...]).astype(BF16)
    lower = dot(keyval_rows((D, 2 * D), 0, False), dwkv)
    upper = dot(keyval_rows((D, 2 * D), 0, True), dwkv)
    stack[D:, 0:256] = dwq[:, 0:256].astype(BF16)
    stack[D:, 256:512] = lower[:, 0:256].astype(BF16)
    stack[D:, 512:768] = upper[:, 0:256].astype(BF16)
    tails = jnp.concatenate(
        [dwq[:, 256:320], lower[:, 256:320], upper[:, 256:320], dwo[:, 256:320].astype(F32)], axis=1
    )
    stack[D:, 768:1024] = tails.astype(BF16)
    stack[D:, 1024:1280] = dwo[:, 0:256]
    row = iota((1, 2 * D), 1)
    give = one_hot(iota((512, 2 * D), 0) == place_a(row, me, None))
    even = one_hot(iota((256, 2 * D), 0) == place_a(row, me, 0))
    odd = one_hot(iota((256, 2 * D), 0) == place_a(row, me, 1))

    def pack(p):
        block = stack[:, lanes(p, 256)]
        full = dot(give, block).astype(BF16)
        for e in range(2):
            part = full[:, 128 * e : 128 * e + 128].reshape(32, 16, 128)
            to = pl.ds(pl.multiple_of(32 * p + 16 * e, 16), 16)
            keep[:, to, :] = part[0:16]
            send[:, to, :] = part[16:32]
        tail = dot(even, block[:, 0:128]) + dot(odd, block[:, 128:256])
        to = pl.ds(pl.multiple_of(8 * p, 8), 8)
        tails_of[:, to, :] = tail.reshape(32, 8, 128)

    loop(5, pack)
    rows = jnp.transpose(jnp.concatenate([grads[...], jnp.zeros((64, 128), F32)], axis=0)).astype(BF16)
    place = iota((256, 128), 0)
    vector = iota((256, 128), 1)
    line = place & 7
    owner = xor_of(place >> 3) ^ me
    start = (7 * owner) >> 3
    straight = (
        ((line == 0) & (vector == 3 * owner))
        | ((line == 1) & (vector == 3 * owner + 2))
        | ((line == 2) & (vector == 96 + start))
    )
    turned = ((line == 0) & (vector == 3 * owner + 1)) | ((line == 2) & (vector == 97 + start))
    small = dot(one_hot(straight), rows) + pltpu.roll(dot(one_hot(turned), rows), 64, 1)
    tails_of[:, 40:48, :] = small.reshape(32, 8, 128)
    keep[:, 160:208, :] = tails_of[0:16].astype(BF16)
    send[:, 160:208, :] = tails_of[16:32].astype(BF16)


def token_kernel(scal, bt, grad_in, mid_grad, entry, stats, tok, high, rest):
    side = scal[1]
    gain = column(bt, G_1, 5)

    def body(tile):
        at = lanes(tile)
        hat = (entry[:, at].astype(F32) - stats[0:1, at]) * stats[1:2, at]
        result = mid_grad[:, at] + norm_back(grad_in[:, at], hat, stats[1:2, at], gain)
        result = result * token_mask(tile, side)
        upper = result.astype(BF16)
        high[:, at] = upper
        rest[:, at] = (result - upper.astype(F32)).astype(BF16)

    loop(8, body)
    row, col = token_place(iota((TOKENS, 1), 0))
    natural = row * SIDE + col

    def quad(index):
        at = lanes(index, 256)
        pick = one_hot(iota((TOKENS, 256), 1) + 256 * index == natural)
        tok[:, at] = dot(high[...], pick) + dot(rest[...], pick)

    loop(4, quad)


def cost(micros):
    return pl.CostEstimate(flops=int(micros * 1e9), bytes_accessed=1000, transcendentals=0)


def call(kernel, args, outs, scratch=(), micros=5):
    return pl.pallas_call(
        kernel,
        in_specs=[pl.BlockSpec(memory_space=pltpu.SMEM if arg.dtype == I32 else pltpu.VMEM) for arg in args],
        out_shape=[jax.ShapeDtypeStruct(shape, dtype) for shape, dtype in outs],
        scratch_shapes=[pltpu.VMEM(shape, dtype) for shape, dtype in scratch],
        compiler_params=pltpu.CompilerParams(vmem_limit_bytes=VMEM_LIMIT),
        cost_estimate=cost(micros),
    )(*args)


def local(group, axes, *arrays):
    return step_of(group, axes, *arrays)


def step_of(group, axes, tokens, image_side, cotangent, *shards):
    index = lax.axis_index(axes[0]) * lax.axis_size(axes[1]) + lax.axis_index(axes[1])
    me = index // group
    devices = SUPER * group

    def flip(values, mask):
        pairs = [(i, ((i // group) ^ mask) * group + i % group) for i in range(devices)]
        return lax.ppermute(values, axes, pairs)

    def gather(block, split=0):
        held = block[None]
        for mask in FLIPS[:2]:
            held = jnp.concatenate([held, flip(held, mask)], axis=0)
        if split:
            one, two = held[:, :split], held[:, split:]
            one, two = (jnp.concatenate([one, flip(one, 8)], axis=0), jnp.concatenate([two, flip(two, 16)], axis=0))
            far, near = flip(one, 16), flip(two, 8)
            two = jnp.concatenate([two[:4], near[:4], two[4:], near[4:]], axis=0)
            held = jnp.concatenate([jnp.concatenate([one, far], axis=0), two], axis=1)
        else:
            for mask in FLIPS[2:]:
                held = jnp.concatenate([held, flip(held, mask)], axis=0)
        return held, flip(held, 1)

    def scatter(keep, send, split=0):
        def step(held, mask):
            return flip(held, mask).astype(F32)

        def halve(held, mask):
            half = held.shape[0] // 2
            return held[:half].astype(F32) + step(held[half:], mask)

        held = (keep.astype(F32) + step(send, 1)).astype(BF16)
        if split:
            one, two = held[:, :split], held[:, split:].reshape(2, 2, 4, -1, 128)
            one, two = (
                halve(one, 16).astype(BF16),
                (two[:, 0].astype(F32) + step(two[:, 1], 8)).astype(BF16).reshape(8, -1, 128),
            )
            held = jnp.concatenate([halve(one, 8), halve(two, 16)], axis=1).astype(BF16)
        else:
            held = halve(held, 16).astype(BF16)
            held = halve(held, 8).astype(BF16)
        held = halve(held, 4).astype(BF16)
        return halve(held, 2)[0]

    if group > 1:
        per = lax.axis_size(axes[1])
        start = (index % per) // group * group

        def join(shard):
            full = lax.all_gather(shard, axes[1], axis=0)
            return lax.dynamic_slice_in_dim(full, start, group, axis=0).reshape(-1)

        shards = [join(shard) for shard in shards]
    query, keyval, reduce_w, output, expand, depth, contract, merge, gains, biases = shards

    def rows(flat):
        return flat.reshape(-1, 128)

    scal = jnp.stack([me.astype(I32), image_side[0].astype(I32)])
    taps = jnp.pad(depth.reshape(40, 9), ((0, 0), (64, 55)))
    (block_a,) = select(
        [rows(query), rows(output), rows(keyval), rows(reduce_w)],
        table_a, [A_ROWS], BF16, False, "in", (scal, biases[None], gains[None]),
    )
    (block_b,) = select([rows(contract), rows(expand), taps], table_b, [B_ROWS], BF16, False)
    (block_c,) = select([rows(merge)], table_c, [C_ROWS], BF16, False)
    a_low, a_high = gather(block_a, A_SPLIT)
    b_low, b_high = gather(block_b)
    c_low, c_high = gather(block_c)

    big, narrow = (D, TOKENS), (D, QUARTER)
    entry, stats_1 = call(entry_kernel, (scal, tokens[0]), [(big, BF16), ((8, TOKENS), F32)], micros=3.5)
    wq, wkv, wr, wo, first, qs, raw, stat_r, red, kv, kt, vt, bt = call(
        project_kernel,
        (scal, a_low, a_high, entry, stats_1),
        [
            ((D, D), BF16), ((2 * D, D), BF16), ((D, 4 * D), BF16), ((D, D), BF16), (big, BF16), (big, BF16),
            (narrow, F32), ((8, QUARTER), F32), (narrow, BF16), ((2 * D, QUARTER), BF16),
            ((HEADS, QUARTER, 64), BF16), ((HEADS, QUARTER, 64), BF16), ((64, 128), F32),
        ],
        [((1024, 1280), BF16), ((D, 1280), BF16), ((4 * D, QUARTER), BF16)],
        micros=8,
    )
    att, lse = call(attend_kernel, (scal, kt, qs, kv), [(big, BF16), ((HEADS, 1, TOKENS), F32)], micros=8.5)
    mid, sec, stats_2 = call(
        middle_kernel, (scal, bt, wo, att, entry), [(big, F32), ((384, TOKENS), BF16), ((8, TOKENS), F32)], [(big, F32)],
        micros=5,
    )
    w1, w1t, w2, w2t, taps = call(
        ffn_weights_kernel,
        (scal, bt, b_low, b_high),
        [((FF, 384), BF16), ((D, FF), BF16), ((D, FF), BF16), ((FF, D), BF16), ((10, FF, 128), F32)],
        [((512, 640), BF16), ((256, 384), BF16), ((FF, 384), F32), ((2, 2 * D, 768), BF16)],
        micros=8,
    )
    act, slope = call(
        ffn_kernel,
        (scal, w1, taps, sec),
        [((FF, TOKENS), BF16), ((FF, TOKENS), BF16)],
        [((256, TOKENS), F32)],
        micros=20,
    )
    end, sect, stats_s = call(
        ending_kernel, (scal, bt, w2, act, mid), [(big, F32), (big, BF16), ((8, TOKENS), F32)], [(big, F32)], micros=5
    )
    four, c_keep, c_send, end_grad, branch, g_one = call(
        merge_kernel,
        (scal, bt, c_low, c_high, sect, end, stats_s, cotangent[0]),
        [
            ((OUT_D, QUARTER), BF16), ((16, C_ROWS, 128), BF16), ((16, C_ROWS, 128), BF16), (big, F32), (big, BF16),
            ((64, 128), F32),
        ],
        [
            ((OUT_D, MERGE_PAD), BF16), ((MERGE_PAD, QUARTER), BF16), ((OUT_D, QUARTER), BF16),
            ((MERGE_PAD, QUARTER), F32), ((OUT_D, QUARTER), F32), ((OUT_D, QUARTER), F32),
        ],
        micros=20,
    )
    sum_c = scatter(c_keep, c_send)
    hgs, dks = [], []
    for at, count in PARTS:
        hg, dk = call(
            functools.partial(ffn_back_kernel, at, count),
            (scal, w1, w2t, taps, sec, slope, branch),
            [((256 * count, TOKENS), BF16), ((256 * count, 128), F32)],
            [((256, TOKENS), F32), ((256, TOKENS), F32)],
            micros=6 * count,
        )
        hgs.append(hg)
        dks.append(dk)
    b_keep, b_send = call(
        pack_b_kernel,
        (scal, *hgs, *dks, sec, branch, act),
        [((16, B_ROWS, 128), BF16), ((16, B_ROWS, 128), BF16)],
        [((FF, 384), F32), ((32, 144, 128), F32)],
        micros=9,
    )
    sum_b = scatter(b_keep, b_send)
    mid_grad, low_grad, g_two = call(
        middle_back_kernel,
        (scal, bt, w1t, *hgs, end_grad, mid, stats_2),
        [(big, F32), (big, BF16), ((64, 128), F32)],
        [(big, F32)],
        micros=6,
    )
    dwo, dq, dkv = call(
        attend_back_kernel,
        (scal, kt, vt, qs, kv, wo, low_grad, att, lse),
        [((D, D), BF16), (big, BF16), ((2 * D, QUARTER), BF16)],
        [(big, BF16)],
        micros=10,
    )
    a_keep, a_send, first_grad = call(
        first_kernel,
        (
            scal, bt, wq, wkv, wr, first, red, raw, stat_r, dq, dkv, dwo, *dks, entry, stats_1, g_one, g_two,
        ),
        [((16, A_ROWS, 128), BF16), ((16, A_ROWS, 128), BF16), (big, F32)],
        [
            ((64, 128), F32), ((4 * D, QUARTER), F32), ((4 * D, QUARTER), BF16), ((2 * D, 1280), BF16),
            ((32, 48, 128), F32),
        ],
        micros=11,
    )
    sum_a = scatter(a_keep, a_send, A_SPLIT)
    (token_grad,) = call(
        token_kernel,
        (scal, bt, first_grad, mid_grad, entry, stats_1),
        [(big, F32)],
        [(big, BF16), (big, BF16)],
        micros=5,
    )
    if group > 1:

        def total(part):
            full = lax.all_gather(part, axes[1], axis=0)
            return jnp.sum(lax.dynamic_slice_in_dim(full, start, group, axis=0), axis=0)

        sum_a, sum_b, sum_c = total(sum_a), total(sum_b), total(sum_c)
    query_g, output_g, keyval_g, reduce_g, biases_g, gains_g = select(
        [sum_a], table_out_a, [25, 25, 50, 100], F32, True, "out", (scal, biases[None], gains[None])
    )
    contract_g, expand_g = select([sum_b], table_out_b, [100, 100], F32, True)
    (merge_g,) = select([sum_c], table_out_c, [360], F32, True)
    depth_g = sum_b[184:224, 64:73]
    grads = [query_g, keyval_g, reduce_g, output_g, expand_g, depth_g, contract_g, merge_g, gains_g, biases_g]
    grads = [grad.reshape(-1) for grad in grads]
    if group > 1:
        mine = index % group
        grads = [lax.dynamic_index_in_dim(grad.reshape(group, -1), mine, keepdims=False) for grad in grads]
    return (four[None], token_grad[None], *grads)


def solution(mesh):
    axes = ("dp", "fs")
    devices = mesh.shape["dp"] * mesh.shape["fs"]
    group = devices // SUPER
    if devices != SUPER * group or mesh.shape["fs"] % group:
        raise ValueError("unsupported mesh")
    one, three = P(axes), P(axes, None, None)
    return jax.shard_map(
        functools.partial(local, group, axes),
        mesh=mesh,
        in_specs=(three, one, three) + (one,) * 10,
        out_specs=(three, three) + (one,) * 10,
        check_vma=False,
    )
```

```python
import functools

import jax
import jax.numpy as jnp
import numpy as np
from jax import lax
from jax.experimental import pallas as pl
from jax.experimental.pallas import tpu as pltpu
from jax.sharding import PartitionSpec as P


D = 320
HEADS = 5
FF = 1280
OUT_D = 512
SIDE = 32
QUARTER = 256
TOKENS = SIDE * SIDE
MERGE_PAD = 2944
SUPER = 32
FLIPS = (2, 4, 8, 16)
EPS = 1e-06
F32, BF16, I32 = jnp.float32, jnp.bfloat16, jnp.int32

B_Q, B_R, C_R, B_O, C_1, C_2, B_1, B_DW, B_2, C_S, B_M, C_M = 0, 5, 10, 15, 20, 25, 30, 50, 70, 75, 80, 88
G_R, G_1, G_2, G_S, G_M = 96, 101, 106, 111, 116

PARTS = ((0, 1), (1, 4))
A_ROWS, B_ROWS, C_ROWS = 208, 224, 368
SMALL_ROW = 200
A_SPLIT = 104
VMEM_LIMIT = 24 * 1024 * 1024
VMEM_ALL = 60 * 1024 * 1024


def slot_of(xor):
    return (xor >> 1) | ((xor & 1) << 4)


def xor_of(slot):
    return ((slot & 15) << 1) | (slot >> 4)


def dot(a, b):
    return jnp.dot(a, b, preferred_element_type=F32)


def dot_nt(a, b):
    return lax.dot_general(a, b, (((1,), (1,)), ((), ())), preferred_element_type=F32)


def dot_tn(a, b):
    return lax.dot_general(a, b, (((0,), (0,)), ((), ())), preferred_element_type=F32)


def iota(shape, axis):
    return lax.broadcasted_iota(I32, shape, axis)


def one_hot(test):
    return jnp.where(test, 1.0, 0.0).astype(BF16)


def lanes(index, width=128):
    return pl.ds(pl.multiple_of(index * width, width), width)


def loop(count, body):
    def step(index, carry):
        body(index)
        return carry

    lax.fori_loop(0, count, step, 0)


def column(table, start, count):
    return jnp.concatenate(
        [jnp.broadcast_to(table[:, h : h + 1], (64, 128)) for h in range(start, start + count)], axis=0
    )


def put_column(table, start, values):
    for h in range(values.shape[0] // 64):
        table[:, start + h : start + h + 1] = values[64 * h : 64 * h + 64, 0:1]


def token_place(lane):
    quad = lane >> 8
    row = 2 * ((lane >> 4) & 15) + (quad >> 1)
    col = 2 * (lane & 15) + (quad & 1)
    return row, col


def token_mask(tile, side, width=128):
    row, col = token_place(iota((1, width), 1) + tile * width)
    return jnp.where((row < side) & (col < side), 1.0, 0.0)


def key_place(index):
    return index >> 4, index & 15


def select_kernel(count, bases, exact, small, me_at, *refs):
    sources, refs = refs[:count], refs[count:]
    if small:
        scal, biases, gains = refs[:3]
        refs = refs[3:]
    low_ref, high_ref = refs[:2]
    rows_ref, sems, held = refs[-count - 2], refs[-count - 1], refs[-count:]
    outs = refs[2 : -count - 2]
    copies = [
        pltpu.make_async_copy(source, place, sems.at[n]) for n, (source, place) in enumerate(zip(sources, held))
    ]
    for copy in copies:
        copy.start()
    half = rows_ref.shape[0] // 2
    rows_ref[...] = jnp.zeros_like(rows_ref)
    total_rows = low_ref.shape[0]
    place = iota((total_rows, 2 * half), 1)
    pick_low = one_hot(place == low_ref[...])
    pick_high = one_hot(place == high_ref[...])
    for copy in copies:
        copy.wait()
    for source, base in zip(held, bases):
        rows_ref[base : base + source.shape[0], :] = source[...].astype(F32)
    if small == "in":
        rows_ref[me_at : me_at + 1, :] = biases[:, 0:128].astype(F32)
        rows_ref[me_at + 1 : me_at + 2, 0:64] = biases[:, 128:192].astype(F32)
        wide = jnp.concatenate([gains[...].astype(F32), jnp.zeros((1, 72), F32)], axis=1)
        wide = jnp.broadcast_to(wide, (8, 128))
        rows_ref[me_at + 2 : me_at + 3, :] = pltpu.roll(wide, (56 * scal[0]) & 63, 1)[0:1, :]
    rows_ref[half:, :] = pltpu.roll(rows_ref[0:half, :], 64, 1)
    total = rows_ref[...]
    high = total.astype(BF16)
    pieces = [high]
    if exact:
        pieces.append((total - high.astype(F32)).astype(BF16))
    low = sum(dot(pick_low, piece) for piece in pieces)
    upper = sum(dot(pick_high, piece) for piece in pieces)
    chosen = jnp.where(iota((total_rows, 128), 1) < 64, low, upper)
    at = 0
    for out in outs:
        rows = out.shape[0]
        if rows == 1:
            continue
        out[...] = chosen[at : at + rows, :].astype(out.dtype)
        at += -(-rows // 16) * 16
    if small == "out":
        bias_out, gain_out = outs[-2:]
        bias_out[:, 0:128] = held[0][me_at : me_at + 1, :]
        bias_out[:, 128:192] = held[0][me_at + 1 : me_at + 2, 0:64]
        wide = jnp.broadcast_to(held[0][me_at + 2 : me_at + 3, :], (8, 128))
        gain_out[...] = pltpu.roll(wide, (128 - ((56 * scal[0]) & 63)) & 127, 1)[0:1, 0:56]


def select(sources, table, out_rows, dtype, exact, small="", vectors=()):
    bases, at = [], 0
    for source in sources:
        bases.append(at)
        at += -(-source.shape[0] // 16) * 16
    half = at + (16 if small == "in" else 0)
    low, high = table(bases + [at], half)
    total = sum(-(-rows // 16) * 16 for rows in out_rows)
    low = np.concatenate([low, np.full(total - len(low), -1)]).astype(np.int32)[:, None]
    high = np.concatenate([high, np.full(total - len(high), -1)]).astype(np.int32)[:, None]
    outs = [jax.ShapeDtypeStruct((rows, 128), dtype) for rows in out_rows]
    specs = [pl.BlockSpec(memory_space=pltpu.VMEM if exact else pltpu.HBM)] * len(sources)
    if small:
        specs += [pl.BlockSpec(memory_space=pltpu.SMEM)] + [pl.BlockSpec(memory_space=pltpu.VMEM)] * 2
    specs += [pl.BlockSpec(memory_space=pltpu.VMEM)] * 2
    if small == "out":
        outs += [jax.ShapeDtypeStruct((1, 192), F32), jax.ShapeDtypeStruct((1, 56), F32)]
    return pl.pallas_call(
        functools.partial(select_kernel, len(sources), tuple(bases), exact, small, at if small == "in" else SMALL_ROW),
        in_specs=specs,
        out_shape=outs,
        scratch_shapes=[pltpu.VMEM((2 * half, 128), F32), pltpu.SemaphoreType.DMA((len(sources),))]
        + [pltpu.VMEM(source.shape, source.dtype) for source in sources],
        compiler_params=pltpu.CompilerParams(vmem_limit_bytes=VMEM_ALL if small == "in" else VMEM_LIMIT),
        cost_estimate=cost(2),
    )(*sources, *vectors, low, high)


def pair(half, low_src, high_src):
    low = -1 if low_src is None else low_src[0] + low_src[1] // 2 + half * (low_src[1] % 2)
    high = -1 if high_src is None else high_src[0] + high_src[1] // 2 + half * (1 - high_src[1] % 2)
    return low, high


def chunk_sources(bases, row, c):
    q, o, kv = bases
    if c < 6 or c >= 8:
        base, first = ((q, 0), (kv, 0), (kv, 10), None, (o, 0))[c // 2]
        at = 5 * (first + row) + 2 * (c % 2)
        return (base, at), (base, at + 1)
    if c == 6:
        return (q, 5 * row + 4), (kv, 5 * row + 4)
    return (kv, 5 * (10 + row) + 4), (o, 5 * row + 4)


def a_place(kind, row, c):
    if row < 8:
        return 16 * c + 8 * kind + row
    return 160 + 8 * (c // 2) + 4 * kind + 2 * (c % 2) + row - 8


def b_place(row, c):
    if row < 8:
        return 8 * c + row
    return 80 + 8 * (c // 4) + 2 * (c % 4) + row - 8


def table_a(bases, half):
    q, o, kv, r, small = bases
    rows = [(-1, -1)] * A_ROWS
    for c in range(10):
        for row in range(10):
            at = 20 * row + 2 * c
            rows[a_place(0, row, c)] = pair(half, (r, at), (r, at + 1))
            rows[a_place(1, row, c)] = pair(half, *chunk_sources((q, o, kv), row, c))
    for row in range(3):
        rows[SMALL_ROW + row] = pair(half, (small, 2 * row), (small, 2 * row + 1))
    return np.array(rows).T


def table_b(bases, half):
    w2, w1, dw, _ = bases
    rows = [(-1, -1)] * B_ROWS
    for c in range(10):
        for row in range(10):
            at = 20 * row + 2 * c
            rows[b_place(row, c)] = pair(half, (w2, at), (w2, at + 1))
    for c in range(3):
        for row in range(40):
            at = 5 * row + 2 * c
            rows[104 + 40 * c + row] = pair(half, (w1, at), (w1, at + 1) if c < 2 else (dw, 2 * row + 1))
    return np.array(rows).T


def table_c(bases, half):
    m, _ = bases
    rows = []
    for c in range(23):
        for row in range(16):
            at = 45 * row + 2 * c
            rows.append(pair(half, (m, at), (m, at + 1) if c < 22 else None))
    return np.array(rows).T


def padded(rows):
    return rows + [(-1, -1)] * (-len(rows) % 16)


def table_out_a(bases, half):
    a, _ = bases

    def square(first, tail, count):
        def source(at):
            row, piece = divmod(at, 5)
            pick = row // 10
            if piece < 4:
                return (a + a_place(1, row % 10, first[pick] + piece // 2), piece % 2)
            chunk, side = tail[pick]
            return (a + a_place(1, row % 10, chunk), side)

        return [source(at) for at in range(count)]

    wide = [(a + a_place(0, at // 20, at % 20 // 2), at % 2) for at in range(200)]

    def emit(sources):
        rows = [pair(half, s, t) for s, t in zip(sources[0::2], sources[1::2])]
        return padded(rows)

    rows = emit(square((0,), ((6, 0),), 50))
    rows += emit(square((8,), ((7, 1),), 50))
    rows += emit(square((2, 4), ((6, 1), (7, 0)), 100))
    rows += emit(wide)
    return np.array(rows).T


def table_out_b(bases, half):
    b, _ = bases

    def w1(at):
        row, piece = divmod(at, 5)
        return (b + 104 + piece // 2 * 40 + row, piece % 2)

    rows = []
    wide = [(b + b_place(at // 20, at % 20 // 2), at % 2) for at in range(200)]
    for sources in (wide, [w1(at) for at in range(200)]):
        rows += padded([pair(half, s, t) for s, t in zip(sources[0::2], sources[1::2])])
    return np.array(rows).T


def table_out_c(bases, half):
    c, _ = bases

    def source(at):
        row, piece = divmod(at, 45)
        return (c + piece // 2 * 16 + row, piece % 2)

    sources = [source(at) for at in range(720)]
    return np.array(padded([pair(half, s, t) for s, t in zip(sources[0::2], sources[1::2])])).T


def split_ten(row, per, magic):
    owner = (row * magic) >> 16
    return owner, row - per * owner


def place_a(row, me, rest_of):
    kind = jnp.where(row >= D, 1, 0)
    owner, rest = split_ten(row - D * kind, 10, 6554)
    slot = slot_of(owner ^ me)
    if rest_of is None:
        return jnp.where(rest < 8, slot * 16 + 8 * kind + rest, -1)
    return jnp.where(rest >= 8, slot * 8 + 4 * kind + 2 * rest_of + rest - 8, -1)


def place_b(row, me, group):
    odd = jnp.where(row >= D, 1, 0)
    owner, rest = split_ten(row - D * odd, 10, 6554)
    slot = slot_of(owner ^ me)
    if group is None:
        return jnp.where(rest < 8, slot * 16 + 8 * odd + rest, -1)
    return jnp.where(rest >= 8, slot * 8 + 4 * group + 2 * odd + rest - 8, -1)


def keyval_rows(shape, ten_axis, upper):
    ten = iota(shape, ten_axis)
    owner, rest = split_ten(ten, 10, 6554)
    return one_hot(iota(shape, 1 - ten_axis) == 20 * owner + rest + (10 if upper else 0))


def norm(values, gain, shift):
    mean = jnp.mean(values, axis=0, keepdims=True)
    centred = values - mean
    rstd = lax.rsqrt(jnp.mean(centred * centred, axis=0, keepdims=True) + EPS)
    return centred * rstd * gain + shift, mean, rstd


def norm_back(grad, hat, rstd, gain):
    scaled = grad * gain
    return rstd * (
        scaled
        - jnp.mean(scaled, axis=0, keepdims=True)
        - hat * jnp.mean(scaled * hat, axis=0, keepdims=True)
    )


def stat_rows(mean, rstd):
    row = iota((8, mean.shape[1]), 0)
    return jnp.where(row == 0, mean, jnp.where(row == 1, rstd, 0.0))


def entry_kernel(scal, tokens, entry, stats):
    side = scal[1]
    for quad in range(4):
        lane = iota((1, 256), 1) + quad * 256
        row, col = token_place(lane)
        natural = row * SIDE + col
        pick = one_hot(iota((TOKENS, 256), 0) == natural)
        mask = jnp.where((row < side) & (col < side), 1.0, 0.0)
        entry[:, quad * 256 : quad * 256 + 256] = (dot(tokens[...], pick) * mask).astype(BF16)

    def body(tile):
        values = entry[:, lanes(tile)].astype(F32)
        mean = jnp.mean(values, axis=0, keepdims=True)
        centred = values - mean
        rstd = lax.rsqrt(jnp.mean(centred * centred, axis=0, keepdims=True) + EPS)
        stats[:, lanes(tile)] = stat_rows(mean, rstd)

    loop(8, body)


def small_table(me, low, high):
    gathered = jnp.concatenate(
        [half[:, SMALL_ROW : SMALL_ROW + 8, :].astype(F32).reshape(128, 128) for half in (low, high)], axis=0
    ).astype(BF16)
    vector = iota((128, 256), 0)
    place = iota((128, 256), 1)
    row = place & 7
    owner = xor_of(place >> 3) ^ me
    first = (7 * owner) >> 3
    straight = (
        ((row == 0) & (vector == 3 * owner))
        | ((row == 1) & (vector == 3 * owner + 2))
        | ((row == 2) & (vector == 96 + first))
    )
    turned = ((row == 0) & (vector == 3 * owner + 1)) | ((row == 2) & (vector == 97 + first))
    rows = dot(one_hot(straight), gathered) + pltpu.roll(dot(one_hot(turned), gathered), 64, 1)
    return jnp.transpose(rows)[0:64, :]


def project_kernel(scal, low, high, entry, stats, wq, wkv, wr, wo, first, qs, raw, stat_r, red, kv, kt, vt, bt, main, square, redin):
    me = scal[0]
    bt[...] = small_table(me, low, high)
    main[512:, :] = jnp.zeros((512, 1280), BF16)
    for half, source in enumerate((low, high)):

        def chunk(c, half=half, source=source):
            block = source[:, pl.ds(pl.multiple_of(16 * c, 16), 16), :].reshape(256, 128)
            main[256 * half : 256 * half + 256, lanes(c)] = block

        loop(10, chunk)
        block = source[:, 160:208, :].astype(F32)
        for c in range(5):
            part = block[:, 8 * c : 8 * c + 8].reshape(128, 128).astype(BF16)
            for odd in range(2):
                at = 512 + 256 * odd + 128 * half
                main[at : at + 128, 256 * c + 128 * odd : 256 * c + 128 * odd + 128] = part
    row = iota((2 * D, 1), 0)
    pick = jnp.concatenate(
        [one_hot(iota((2 * D, 512), 1) == place_a(row, me, None))]
        + [one_hot(iota((2 * D, 256), 1) == place_a(row, me, odd)) for odd in range(2)],
        axis=1,
    )

    def assemble(p):
        block = dot(pick, main[:, lanes(p, 256)]).astype(BF16)
        wr[:, lanes(p, 256)] = block[0:D]
        square[:, lanes(p, 256)] = block[D:]

    loop(5, assemble)
    wq[:, 0:256] = square[:, 0:256]
    wo[:, 0:256] = square[:, 1024:1280]
    tails = square[:, 768:1024].astype(F32)
    turned = pltpu.roll(tails, 64, 1)
    wq[:, 256:320] = tails[:, 0:64].astype(BF16)
    wo[:, 256:320] = turned[:, 0:64].astype(BF16)
    lower, upper = keyval_rows((2 * D, D), 1, False), keyval_rows((2 * D, D), 1, True)
    wkv[:, 0:256] = (dot(lower, square[:, 256:512]) + dot(upper, square[:, 512:768])).astype(BF16)
    tail = dot(lower, turned[:, 128:256].astype(BF16)) + dot(upper, tails[:, 128:256].astype(BF16))
    wkv[:, 256:320] = tail[:, 0:64].astype(BF16)

    gain, shift = column(bt, G_1, 5), column(bt, C_1, 5)

    def body(tile):
        centred = entry[:, lanes(tile)].astype(F32) - stats[0:1, lanes(tile)]
        first[:, lanes(tile)] = (centred * stats[1:2, lanes(tile)] * gain + shift).astype(BF16)

    loop(8, body)
    for quad in range(4):
        redin[D * quad : D * quad + D, :] = first[:, 256 * quad : 256 * quad + 256]
    bias = column(bt, B_R, 5)
    bias = jnp.concatenate([bias, bias], axis=1)
    raw[...] = dot(wr[...], redin[...]) + bias
    gain, shift = column(bt, G_R, 5), column(bt, C_R, 5)
    for tile in range(2):
        at = slice(128 * tile, 128 * tile + 128)
        values, mean, rstd = norm(raw[:, at], gain, shift)
        red[:, at] = values.astype(BF16)
        stat_r[:, at] = stat_rows(mean, rstd)
    keyval = dot(wkv[...], red[...])
    kv[...] = keyval.astype(BF16)
    turned = jnp.transpose(keyval)
    for h in range(HEADS):
        kt[h] = turned[:, 64 * h : 64 * h + 64].astype(BF16)
        vt[h] = turned[:, D + 64 * h : D + 64 * h + 64].astype(BF16)
    bias = column(bt, B_Q, 5)
    bias = jnp.concatenate([bias, bias], axis=1)

    def query(quad):
        at = lanes(quad, 256)
        qs[:, at] = (dot(wq[...], first[:, at]) + bias).astype(BF16) * BF16(0.125)

    loop(4, query)


def key_bias(side):
    i, j = key_place(iota((QUARTER, 1), 0))
    return jnp.where((i < (side >> 1)) & (j < (side >> 1)), 0.0, -10000.0)


def attend_kernel(scal, kt, qs, kv, att, lse, scores, probs):
    bias = key_bias(scal[1])

    def score(h):
        scores[h & 1] = dot(kt[h], qs[pl.ds(pl.multiple_of(64 * h, 64), 64), :])

    score(0)

    def head(h):
        score(h + 1)
        finish(h)

    def finish(h):
        rows = pl.ds(pl.multiple_of(64 * h, 64), 64)
        values = kv[pl.ds(pl.multiple_of(D + 64 * h, 64), 64), :]
        for tile in range(8):
            at = slice(128 * tile, 128 * tile + 128)
            part = scores[h & 1, :, at] + bias
            top = jnp.max(part, axis=0, keepdims=True)
            weights = jnp.exp(part - top)
            total = jnp.sum(weights, axis=0, keepdims=True)
            lse[h, :, at] = top + jnp.log(total)
            probs[:, at] = (weights * (1.0 / total)).astype(BF16)
        att[rows, :] = dot(values, probs[...]).astype(BF16)

    loop(HEADS - 1, head)
    finish(HEADS - 1)


def middle_kernel(scal, bt, wo, att, entry, mid, sec, stats, work):
    side = scal[1]
    work[...] = dot(wo[...], att[...])
    bias, gain, shift = column(bt, B_O, 5), column(bt, G_2, 5), column(bt, C_2, 5)

    def body(tile):
        at = lanes(tile)
        mask = token_mask(tile, side)
        values = entry[:, at].astype(F32) + mask * (work[:, at] + bias)
        mid[:, at] = values
        normed, mean, rstd = norm(values, gain, shift)
        stats[:, at] = stat_rows(mean, rstd)
        sec[0:D, at] = (normed.astype(BF16).astype(F32) * mask).astype(BF16)
        sec[D : D + 64, at] = jnp.where(iota((64, 128), 0) == 9, mask, 0.0).astype(BF16)

    loop(8, body)


def ffn_weights_kernel(scal, bt, low, high, w1, w1t, w2, w2t, taps, main, rest, wide, picks):
    me = scal[0]
    for half, source in enumerate((low, high)):
        for p in range(5):
            block = source[:, 16 * p : 16 * p + 16, :].reshape(256, 128)
            main[256 * half : 256 * half + 256, 128 * p : 128 * p + 128] = block
        block = source[:, 80:112, :].astype(F32)
        for c in range(3):
            part = block[:, 8 * c : 8 * c + 8].reshape(128, 128).astype(BF16)
            rest[128 * half : 128 * half + 128, 128 * c : 128 * c + 128] = part

        def expansion(slot, half=half, source=source):
            owner = ((slot << 1) | half) ^ me
            block = source[slot, 80:224, :].astype(F32)
            rows = pl.ds(pl.multiple_of(40 * owner, 8), 40)
            for c in range(3):
                wide[rows, 128 * c : 128 * c + 128] = block[24 + 40 * c : 64 + 40 * c]

        loop(16, expansion)
    row = iota((2 * D, 1), 0)
    for group in range(2):
        picks[group, :, 0:512] = one_hot(iota((2 * D, 512), 1) == place_b(row, me, None))
        picks[group, :, 512:768] = one_hot(iota((2 * D, 256), 1) == place_b(row, me, group))

    def contraction(p):
        source = jnp.concatenate([main[:, lanes(p)], rest[:, lanes(p >> 1)]], axis=0)
        block = dot(picks[p & 1], source)
        block = jnp.concatenate([block[0:D], block[D:]], axis=1)
        w2[:, lanes(p, 256)] = block.astype(BF16)
        w2t[pl.ds(pl.multiple_of(256 * p, 256), 256), :] = jnp.transpose(block).astype(BF16)

    loop(5, contraction)
    bias = column(bt, B_1, 20)
    lane = iota((FF, 128), 1)
    tail = wide[:, 256:384]
    low_tail = tail.astype(BF16)

    def spread(tap):
        taps[tap] = dot(low_tail, one_hot(iota((128, 128), 0) == 64 + tap))

    loop(9, spread)
    taps[9] = column(bt, B_DW, 20)
    w1[:, 0:256] = wide[:, 0:256].astype(BF16)
    w1[:, 256:384] = jnp.where(lane < 64, tail, jnp.where(lane == 73, bias, 0.0)).astype(BF16)

    def turn(p):
        rows = pl.ds(pl.multiple_of(256 * p, 256), 256)
        w1t[:, lanes(p, 256)] = jnp.transpose(wide[rows, :])[0:D].astype(BF16)

    loop(5, turn)


def edge_masks():
    lane = iota((1, 128), 1)
    j = lane & 15
    return jnp.where(j != 0, 1.0, 0.0), jnp.where(j != 15, 1.0, 0.0), lane >= 16, lane < 112


def left_of(tiles):
    return [pltpu.roll(tile, 1, 1) for tile in tiles]


def right_of(tiles):
    return [pltpu.roll(tile, 127, 1) for tile in tiles]


def above(tiles, inside):
    turned = [pltpu.roll(tile, 16, 1) for tile in tiles]
    return [jnp.where(inside, turned[0], 0.0), jnp.where(inside, turned[1], turned[0])]


def below(tiles, inside):
    turned = [pltpu.roll(tile, 112, 1) for tile in tiles]
    return [jnp.where(inside, turned[0], turned[1]), jnp.where(inside, turned[1], 0.0)]


def times(tiles, factor):
    return [tile * factor for tile in tiles]


def plus(*many):
    return [functools.reduce(lambda a, b: a + b, tiles) for tiles in zip(*many)]


def tile_at(a, e, half):
    start = 256 * (2 * a + e) + 128 * half
    return slice(start, start + 128)


def quads(ref, rows):
    return [[[ref[rows, tile_at(a, e, half)] for half in range(2)] for e in range(2)] for a in range(2)]


LOG2E = float(np.log2(np.e))


def gelu_parts(x):
    y = x * np.float32(0.5**0.5)
    cdf = lax.erf(y) * 0.5 + 0.5
    bell = jnp.exp2(y * y * np.float32(-LOG2E) + np.float32(-0.5 * np.log2(2.0 * np.pi)))
    return x * cdf, cdf + x * bell


def ffn_kernel(scal, w1, taps, sec, act, slope, hid_a, hid_b):
    j_first, j_last, i_first, i_last = edge_masks()

    def fill(hid, step):
        rows = pl.ds(pl.multiple_of(jnp.minimum(step, FF // 64 - 1) * 64, 64), 64)
        hid[...] = dot(w1[rows, :], sec[...])

    def group(hid, step, index):
        rows = slice(16 * index, 16 * index + 16)
        out_rows = pl.ds(pl.multiple_of(64 * step + 16 * index, 16), 16)
        k = [taps[n, out_rows, :] for n in range(10)]
        first = [k[3 * r] * j_first for r in range(3)]
        last = [k[3 * r + 2] * j_last for r in range(3)]
        quad = quads(hid, rows)
        left = [left_of(quad[a][1]) for a in range(2)]
        right = [right_of(quad[a][0]) for a in range(2)]

        def across(a, e, r):
            if e == 0:
                parts = zip(left[a], quad[a][0], quad[a][1])
                return [first[r] * x + k[3 * r + 1] * y + k[3 * r + 2] * z for x, y, z in parts]
            parts = zip(quad[a][0], quad[a][1], right[a])
            return [k[3 * r] * x + k[3 * r + 1] * y + last[r] * z for x, y, z in parts]

        for e in range(2):
            up = above(across(1, e, 0), i_first)
            down = below(across(0, e, 2), i_last)
            outs = (plus(across(0, e, 1), across(1, e, 2), up), plus(across(0, e, 0), across(1, e, 1), down))
            for a in range(2):
                for half in range(2):
                    value, grad = gelu_parts(outs[a][half] + k[9])
                    act[out_rows, tile_at(a, e, half)] = value.astype(BF16)
                    slope[out_rows, tile_at(a, e, half)] = grad.astype(BF16)

    fill(hid_a, 0)

    def two(index):
        fill(hid_b, 2 * index + 1)
        for n in range(4):
            group(hid_a, 2 * index, n)
        fill(hid_a, 2 * index + 2)
        for n in range(4):
            group(hid_b, 2 * index + 1, n)

    loop(FF // 128, two)


def ending_kernel(scal, bt, w2, act, mid, end, sect, stats, work):
    side = scal[1]
    work[...] = dot(w2[...], act[...])
    bias, gain, shift = column(bt, B_2, 5), column(bt, G_S, 5), column(bt, C_S, 5)

    def body(tile):
        at = lanes(tile)
        mask = token_mask(tile, side)
        values = mid[:, at] + mask * (work[:, at] + bias)
        end[:, at] = values
        normed, mean, rstd = norm(values, gain, shift)
        stats[:, at] = stat_rows(mean, rstd)
        sect[:, at] = (normed.astype(BF16).astype(F32) * mask).astype(BF16)

    loop(8, body)


def lane_sum(values):
    return jnp.sum(values, axis=1, keepdims=True)


def merge_kernel(scal, bt, c_low, c_high, sect, end, stats, cot, four, keep, send, end_grad, branch, grads, wm, patch, mg, back, work, natural):
    me, side = scal[0], scal[1]
    grads[...] = jnp.zeros_like(grads)
    for half, source in enumerate((c_low, c_high)):

        def place(c, half=half, source=source):
            block = source[:, pl.ds(pl.multiple_of(16 * c, 16), 16), :].reshape(256, 128)
            wm[256 * half : 256 * half + 256, lanes(c)] = block

        loop(23, place)

    def reorder(to_owner):
        def one(slot):
            at = pl.ds(pl.multiple_of(16 * slot, 16), 16)
            owner = pl.ds(pl.multiple_of((xor_of(slot) ^ me) * 16, 16), 16)
            to_owner(at, owner)

        loop(32, one)

    j_first, j_last, i_first, i_last = edge_masks()
    quad = [[[t.astype(F32) for t in pair] for pair in row] for row in quads(sect, slice(None))]
    left = [times(left_of(quad[a][1]), j_first) for a in range(2)]
    pieces = (
        above(left[1], i_first),
        above(quad[1][0], i_first),
        above(quad[1][1], i_first),
        left[0],
        quad[0][0],
        quad[0][1],
        left[1],
        quad[1][0],
        quad[1][1],
    )
    for n, piece in enumerate(pieces):
        for half in range(2):
            patch[D * n : D * n + D, 128 * half : 128 * half + 128] = piece[half].astype(BF16)
    patch[9 * D :, :] = jnp.zeros((MERGE_PAD - 9 * D, 256), BF16)
    bias, gain, shift = column(bt, B_M, 8), column(bt, G_M, 8), column(bt, C_M, 8)
    work[...] = dot(wm[...], patch[...])

    def from_slots(at, owner):
        natural[owner, :] = work[at, :]

    reorder(from_slots)
    half_side = side >> 1
    for tile in range(2):
        at = slice(128 * tile, 128 * tile + 128)
        i, j = key_place(iota((1, 128), 1) + 128 * tile)
        mask = jnp.where((i < half_side) & (j < half_side), 1.0, 0.0)
        values = natural[:, at] + bias
        mean = jnp.mean(values, axis=0, keepdims=True)
        centred = values - mean
        rstd = lax.rsqrt(jnp.mean(centred * centred, axis=0, keepdims=True) + EPS)
        hat = centred * rstd
        four[:, at] = ((hat * gain + shift) * mask).astype(BF16)
        grad = cot[:, at].astype(F32) * mask
        low = norm_back(grad, hat, rstd, gain).astype(BF16)
        natural[:, at] = low.astype(F32)
        parts = (grad * hat, grad, low.astype(F32))
        sums = parts if tile == 0 else [s + v for s, v in zip(sums, parts)]
    put_column(grads, G_M, lane_sum(sums[0]))
    put_column(grads, C_M, lane_sum(sums[1]))
    put_column(grads, B_M, lane_sum(sums[2]))

    def to_slots(at, owner):
        mg[at, :] = natural[owner, :].astype(BF16)

    reorder(to_slots)

    def widths(body):
        loop(11, lambda c: body(pl.multiple_of(c * 256, 256), 256))
        body(11 * 256, 128)

    def patch_grad(start, width):
        back[pl.ds(start, width), :] = dot_tn(wm[:, pl.ds(start, width)], mg[...])

    widths(patch_grad)

    def piece(n):
        return [back[D * n : D * n + D, 128 * half : 128 * half + 128] for half in range(2)]

    results = (
        piece(4),
        plus(piece(5), times(right_of(piece(3)), j_last)),
        plus(piece(7), below(piece(1), i_last)),
        plus(
            piece(8),
            times(right_of(piece(6)), j_last),
            below(plus(piece(2), times(right_of(piece(0)), j_last)), i_last),
        ),
    )
    for n, values in enumerate(results):
        for half in range(2):
            end_grad[:, 256 * n + 128 * half : 256 * n + 128 * half + 128] = values[half]
    gain = column(bt, G_S, 5)
    zeros = jnp.zeros((D, 128), F32)

    def body(tile, carry):
        at = lanes(tile)
        mask = token_mask(tile, side)
        grad = end_grad[:, at] * mask
        hat = (end[:, at] - stats[0:1, at]) * stats[1:2, at]
        result = norm_back(grad, hat, stats[1:2, at], gain)
        end_grad[:, at] = result
        low = (result * mask).astype(BF16)
        branch[:, at] = low
        return carry[0] + grad * hat, carry[1] + grad, carry[2] + low.astype(F32)

    sums = lax.fori_loop(0, 8, body, (zeros, zeros, zeros))
    put_column(grads, G_S, lane_sum(sums[0]))
    put_column(grads, C_S, lane_sum(sums[1]))
    put_column(grads, B_2, lane_sum(sums[2]))

    def give(start, width):
        block = dot_nt(mg[...], patch[pl.ds(start, width), :]).astype(BF16)
        for c in range(width // 128):
            to = pl.ds(pl.multiple_of((start >> 3) + 16 * c, 16), 16)
            part = block[:, 128 * c : 128 * c + 128].reshape(32, 16, 128)
            keep[:, to, :] = part[0:16]
            send[:, to, :] = part[16:32]

    widths(give)


def ffn_back_kernel(first_part, count, scal, w1, w2t, taps, sec, slope, branch, hg, dkx, hid_a, hid_b, cg_a, cg_b):
    start, steps = 256 * first_part, 4 * count
    j_first, j_last, i_first, i_last = edge_masks()
    lane = iota((16, 128), 1)

    def fill(hid, cg, step):
        rows = pl.ds(pl.multiple_of(start + jnp.minimum(step, steps - 1) * 64, 64), 64)
        cg[...] = dot(w2t[rows, :], branch[...]) * slope[rows, :].astype(F32)
        hid[...] = dot(w1[rows, :], sec[...])

    def group(hid, cg, step, index):
        rows = slice(16 * index, 16 * index + 16)
        from_rows = pl.ds(pl.multiple_of(start + 64 * step + 16 * index, 16), 16)
        to_rows = pl.ds(pl.multiple_of(64 * step + 16 * index, 16), 16)
        k = [taps[n, from_rows, :] for n in range(9)]
        quad = quads(cg, rows)
        bias = functools.reduce(lambda x, y: x + y, [t for row in quad for pair in row for t in pair])
        across = [
            (
                (times(left_of(quad[a][1]), j_first), quad[a][0], quad[a][1]),
                (quad[a][0], quad[a][1], times(right_of(quad[a][0]), j_last)),
            )
            for a in range(2)
        ]
        sums = [None] * 9
        for e in range(2):
            upper = [above(tiles, i_first) for tiles in across[1][e]]
            lower = [below(tiles, i_last) for tiles in across[0][e]]
            for a, near in ((0, (upper, across[0][e], across[1][e])), (1, (across[0][e], across[1][e], lower))):
                for half in range(2):
                    value = hid[rows, tile_at(a, e, half)]
                    total = None
                    for r in range(3):
                        for c in range(3):
                            tap = 3 * (2 - r) + (2 - c)
                            term = k[tap] * near[r][c][half]
                            total = term if total is None else total + term
                            term = value * near[r][c][half]
                            sums[tap] = term if sums[tap] is None else sums[tap] + term
                    hg[to_rows, tile_at(a, e, half)] = total.astype(BF16)
        table = jnp.where(lane == 9, lane_sum(bias), 0.0)
        for n in range(9):
            table = jnp.where(lane == n, lane_sum(sums[n]), table)
        dkx[to_rows, :] = table

    fill(hid_a, cg_a, 0)

    def two(index):
        fill(hid_b, cg_b, 2 * index + 1)
        for n in range(4):
            group(hid_a, cg_a, 2 * index, n)
        fill(hid_a, cg_a, 2 * index + 2)
        for n in range(4):
            group(hid_b, cg_b, 2 * index + 1, n)

    loop(steps // 2, two)


def middle_back_kernel(scal, bt, w1t, hg0, hg1, end_grad, mid, stats, mid_grad, low_grad, grads, work):
    side = scal[1]
    work[...] = sum(
        dot(w1t[:, 256 * at : 256 * (at + count)], hg[...]) for hg, (at, count) in zip((hg0, hg1), PARTS)
    )
    grads[...] = jnp.zeros_like(grads)
    gain = column(bt, G_2, 5)
    zeros = jnp.zeros((D, 128), F32)

    def body(tile, carry):
        at = lanes(tile)
        mask = token_mask(tile, side)
        grad = work[:, at] * mask
        hat = (mid[:, at] - stats[0:1, at]) * stats[1:2, at]
        result = end_grad[:, at] + norm_back(grad, hat, stats[1:2, at], gain)
        mid_grad[:, at] = result
        low = (result * mask).astype(BF16)
        low_grad[:, at] = low
        return carry[0] + grad * hat, carry[1] + grad, carry[2] + low.astype(F32)

    sums = lax.fori_loop(0, 8, body, (zeros, zeros, zeros))
    put_column(grads, G_2, lane_sum(sums[0]))
    put_column(grads, C_2, lane_sum(sums[1]))
    put_column(grads, B_O, lane_sum(sums[2]))


def pack_b_kernel(scal, hg0, hg1, dk0, dk1, sec, branch, act, keep, send, grads, dw1, gather):
    me = scal[0]
    grads[...] = jnp.zeros_like(grads)
    lane = iota((256, 128), 1)
    for hg, dkx, (at, count) in zip((hg0, hg1), (dk0, dk1), PARTS):

        def outer(n, hg=hg, dkx=dkx, at=at):
            rows = pl.ds(pl.multiple_of(256 * n, 256), 256)
            to = pl.ds(pl.multiple_of(256 * (n + at), 256), 256)
            part = dot_nt(hg[rows, :], sec[...])
            dw1[to, 0:256] = part[:, 0:256]
            turned = pltpu.roll(dkx[rows, :], 64, 1)
            dw1[to, 256:384] = jnp.where(lane < 64, part[:, 256:384], jnp.where(lane < 73, turned, 0.0))
            table = grads[...]
            for m in range(4):
                here = slice(64 * m, 64 * m + 64)
                number = 4 * (n + at) + m
                table = jnp.where(lane[here] == B_1 + number, part[here, 329:330], table)
                table = jnp.where(lane[here] == B_DW + number, dkx[rows, :][here, 9:10], table)
            grads[...] = table

        loop(count, outer)
    row = iota((1, 2 * D), 1)
    give = one_hot(iota((512, 2 * D), 0) == place_b(row, me, None))
    gather[:, 0:24, :] = jnp.zeros((32, 24, 128), F32)

    def contraction(p):
        block = dot_nt(branch[...], act[pl.ds(pl.multiple_of(256 * p, 256), 256), :]).astype(BF16)
        block = jnp.concatenate([block[:, 0:128], block[:, 128:256]], axis=0)
        full = dot(give, block).astype(BF16).reshape(32, 16, 128)
        to = pl.ds(pl.multiple_of(16 * p, 16), 16)
        keep[:, to, :] = full[0:16]
        send[:, to, :] = full[16:32]
        more = one_hot(iota((256, 2 * D), 0) == place_b(row, me, p & 1))
        to = pl.ds(pl.multiple_of(8 * (p >> 1), 8), 8)
        gather[:, to, :] += dot(more, block).reshape(32, 8, 128)

    loop(5, contraction)

    def expansion(owner):
        slot = slot_of(owner ^ me)
        rows = pl.ds(pl.multiple_of(40 * owner, 8), 40)
        for c in range(3):
            gather[slot, 24 + 40 * c : 64 + 40 * c, :] = dw1[rows, 128 * c : 128 * c + 128]

    loop(32, expansion)
    keep[:, 80:224, :] = gather[0:16].astype(BF16)
    send[:, 80:224, :] = gather[16:32].astype(BF16)


def attend_back_kernel(scal, kt, vt, qs, kv, wo, low_grad, att, lse, dwo, dq, dkv, og, scores, grads, probs, back):
    bias = key_bias(scal[1])
    dwo[...] = dot_nt(low_grad[...], att[...]).astype(BF16)
    og[...] = dot_tn(wo[...], low_grad[...]).astype(BF16)

    def score(h):
        rows = pl.ds(pl.multiple_of(64 * h, 64), 64)
        scores[h & 1] = dot(kt[h], qs[rows, :])
        grads[h & 1] = dot(vt[h], og[rows, :])

    score(0)

    def head(h):
        score(h + 1)
        finish(h)

    def finish(h):
        rows = pl.ds(pl.multiple_of(64 * h, 64), 64)
        more = pl.ds(pl.multiple_of(D + 64 * h, 64), 64)
        for tile in range(8):
            at = slice(128 * tile, 128 * tile + 128)
            weights = jnp.exp(scores[h & 1, :, at] + bias - lse[h, :, at])
            grad = grads[h & 1, :, at]
            mean = jnp.sum(weights * grad, axis=0, keepdims=True)
            back[:, at] = (weights * (grad - mean)).astype(BF16)
            probs[:, at] = weights.astype(BF16)
        dq[rows, :] = (dot(kv[rows, :], back[...]) * 0.125).astype(BF16)
        dkv[rows, :] = dot_nt(qs[rows, :], back[...]).astype(BF16)
        dkv[more, :] = dot_nt(og[rows, :], probs[...]).astype(BF16)

    loop(HEADS - 1, head)
    finish(HEADS - 1)


def first_kernel(scal, bt, wq, wkv, wr, first, red, raw, stat_r, dq, dkv, dwo, entry, stats, g_one, g_two, g_three, keep, send, work, grads, wide, redin, stack, tails_of):
    me = scal[0]
    grads[...] = g_one[...] + g_two[...] + g_three[...]
    for quad in range(4):
        redin[D * quad : D * quad + D, :] = first[:, 256 * quad : 256 * quad + 256]
    dred = dot_tn(wkv[...], dkv[...])
    gain = column(bt, G_R, 5)
    lows = []
    for tile in range(2):
        at = slice(128 * tile, 128 * tile + 128)
        grad = dred[:, at]
        hat = (raw[:, at] - stat_r[0:1, at]) * stat_r[1:2, at]
        low = norm_back(grad, hat, stat_r[1:2, at], gain).astype(BF16)
        lows.append(low)
        parts = (grad * hat, grad, low.astype(F32))
        sums = parts if tile == 0 else [s + v for s, v in zip(sums, parts)]
    put_column(grads, G_R, lane_sum(sums[0]))
    put_column(grads, C_R, lane_sum(sums[1]))
    put_column(grads, B_R, lane_sum(sums[2]))
    low = jnp.concatenate(lows, axis=1)
    wide[...] = dot_tn(wr[...], low)
    straight = dot_tn(wq[...], dq[...])
    for quad in range(4):
        at = slice(256 * quad, 256 * quad + 256)
        work[:, at] = straight[:, at] + wide[D * quad : D * quad + D, :]
    zeros = jnp.zeros((D, 128), F32)

    def body(tile, carry):
        at = lanes(tile)
        grad = work[:, at]
        hat = (entry[:, at].astype(F32) - stats[0:1, at]) * stats[1:2, at]
        return carry[0] + grad * hat, carry[1] + grad, carry[2] + dq[:, at].astype(F32)

    sums = lax.fori_loop(0, 8, body, (zeros, zeros, zeros))
    put_column(grads, G_1, lane_sum(sums[0]))
    put_column(grads, C_1, lane_sum(sums[1]))
    put_column(grads, B_Q, lane_sum(sums[2]))
    stack[0:D, :] = dot_nt(low, redin[...]).astype(BF16)
    dwq = dot_nt(dq[...], first[...])
    dwkv = dot_nt(dkv[...], red[...]).astype(BF16)
    lower = dot(keyval_rows((D, 2 * D), 0, False), dwkv)
    upper = dot(keyval_rows((D, 2 * D), 0, True), dwkv)
    stack[D:, 0:256] = dwq[:, 0:256].astype(BF16)
    stack[D:, 256:512] = lower[:, 0:256].astype(BF16)
    stack[D:, 512:768] = upper[:, 0:256].astype(BF16)
    tails = jnp.concatenate(
        [dwq[:, 256:320], lower[:, 256:320], upper[:, 256:320], dwo[:, 256:320].astype(F32)], axis=1
    )
    stack[D:, 768:1024] = tails.astype(BF16)
    stack[D:, 1024:1280] = dwo[:, 0:256]
    row = iota((1, 2 * D), 1)
    give = one_hot(iota((512, 2 * D), 0) == place_a(row, me, None))
    even = one_hot(iota((256, 2 * D), 0) == place_a(row, me, 0))
    odd = one_hot(iota((256, 2 * D), 0) == place_a(row, me, 1))

    def pack(p):
        block = stack[:, lanes(p, 256)]
        full = dot(give, block).astype(BF16)
        for e in range(2):
            part = full[:, 128 * e : 128 * e + 128].reshape(32, 16, 128)
            to = pl.ds(pl.multiple_of(32 * p + 16 * e, 16), 16)
            keep[:, to, :] = part[0:16]
            send[:, to, :] = part[16:32]
        tail = dot(even, block[:, 0:128]) + dot(odd, block[:, 128:256])
        to = pl.ds(pl.multiple_of(8 * p, 8), 8)
        tails_of[:, to, :] = tail.reshape(32, 8, 128)

    loop(5, pack)
    rows = jnp.transpose(jnp.concatenate([grads[...], jnp.zeros((64, 128), F32)], axis=0)).astype(BF16)
    place = iota((256, 128), 0)
    vector = iota((256, 128), 1)
    line = place & 7
    owner = xor_of(place >> 3) ^ me
    start = (7 * owner) >> 3
    straight = (
        ((line == 0) & (vector == 3 * owner))
        | ((line == 1) & (vector == 3 * owner + 2))
        | ((line == 2) & (vector == 96 + start))
    )
    turned = ((line == 0) & (vector == 3 * owner + 1)) | ((line == 2) & (vector == 97 + start))
    small = dot(one_hot(straight), rows) + pltpu.roll(dot(one_hot(turned), rows), 64, 1)
    tails_of[:, 40:48, :] = small.reshape(32, 8, 128)
    keep[:, 160:208, :] = tails_of[0:16].astype(BF16)
    send[:, 160:208, :] = tails_of[16:32].astype(BF16)


def token_kernel(scal, bt, grad_in, mid_grad, entry, stats, tok, high, rest):
    side = scal[1]
    gain = column(bt, G_1, 5)

    def body(tile):
        at = lanes(tile)
        hat = (entry[:, at].astype(F32) - stats[0:1, at]) * stats[1:2, at]
        result = mid_grad[:, at] + norm_back(grad_in[:, at], hat, stats[1:2, at], gain)
        result = result * token_mask(tile, side)
        upper = result.astype(BF16)
        high[:, at] = upper
        rest[:, at] = (result - upper.astype(F32)).astype(BF16)

    loop(8, body)
    row, col = token_place(iota((TOKENS, 1), 0))
    natural = row * SIDE + col

    def quad(index):
        at = lanes(index, 256)
        pick = one_hot(iota((TOKENS, 256), 1) + 256 * index == natural)
        tok[:, at] = dot(high[...], pick) + dot(rest[...], pick)

    loop(4, quad)


def cost(micros):
    return pl.CostEstimate(flops=int(micros * 1e9), bytes_accessed=1000, transcendentals=0)


def call(kernel, args, outs, scratch=(), micros=5):
    return pl.pallas_call(
        kernel,
        in_specs=[pl.BlockSpec(memory_space=pltpu.SMEM if arg.dtype == I32 else pltpu.VMEM) for arg in args],
        out_shape=[jax.ShapeDtypeStruct(shape, dtype) for shape, dtype in outs],
        scratch_shapes=[pltpu.VMEM(shape, dtype) for shape, dtype in scratch],
        compiler_params=pltpu.CompilerParams(vmem_limit_bytes=VMEM_LIMIT),
        cost_estimate=cost(micros),
    )(*args)


def local(group, axes, *arrays):
    return step_of(group, axes, *arrays)


def step_of(group, axes, tokens, image_side, cotangent, *shards):
    index = lax.axis_index(axes[0]) * lax.axis_size(axes[1]) + lax.axis_index(axes[1])
    me = index // group
    devices = SUPER * group

    def flip(values, mask):
        pairs = [(i, ((i // group) ^ mask) * group + i % group) for i in range(devices)]
        return lax.ppermute(values, axes, pairs)

    def gather(block, split=0):
        held = block[None]
        for mask in FLIPS[:2]:
            held = jnp.concatenate([held, flip(held, mask)], axis=0)
        if split:
            one, two = held[:, :split], held[:, split:]
            one, two = (jnp.concatenate([one, flip(one, 8)], axis=0), jnp.concatenate([two, flip(two, 16)], axis=0))
            far, near = flip(one, 16), flip(two, 8)
            two = jnp.concatenate([two[:4], near[:4], two[4:], near[4:]], axis=0)
            held = jnp.concatenate([jnp.concatenate([one, far], axis=0), two], axis=1)
        else:
            for mask in FLIPS[2:]:
                held = jnp.concatenate([held, flip(held, mask)], axis=0)
        return held, flip(held, 1)

    def scatter(keep, send, split=0):
        def step(held, mask):
            return flip(held, mask).astype(F32)

        def halve(held, mask):
            half = held.shape[0] // 2
            return held[:half].astype(F32) + step(held[half:], mask)

        held = (keep.astype(F32) + step(send, 1)).astype(BF16)
        if split:
            one, two = held[:, :split], held[:, split:].reshape(2, 2, 4, -1, 128)
            one, two = (
                halve(one, 16).astype(BF16),
                (two[:, 0].astype(F32) + step(two[:, 1], 8)).astype(BF16).reshape(8, -1, 128),
            )
            held = jnp.concatenate([halve(one, 8), halve(two, 16)], axis=1).astype(BF16)
        else:
            held = halve(held, 16).astype(BF16)
            held = halve(held, 8).astype(BF16)
        held = halve(held, 4).astype(BF16)
        return halve(held, 2)[0]

    if group > 1:
        per = lax.axis_size(axes[1])
        start = (index % per) // group * group

        def join(shard):
            full = lax.all_gather(shard, axes[1], axis=0)
            return lax.dynamic_slice_in_dim(full, start, group, axis=0).reshape(-1)

        shards = [join(shard) for shard in shards]
    query, keyval, reduce_w, output, expand, depth, contract, merge, gains, biases = shards

    def rows(flat):
        return flat.reshape(-1, 128)

    scal = jnp.stack([me.astype(I32), image_side[0].astype(I32)])
    taps = jnp.pad(depth.reshape(40, 9), ((0, 0), (64, 55)))
    (block_a,) = select(
        [rows(query), rows(output), rows(keyval), rows(reduce_w)],
        table_a, [A_ROWS], BF16, False, "in", (scal, biases[None], gains[None]),
    )
    (block_b,) = select([rows(contract), rows(expand), taps], table_b, [B_ROWS], BF16, False)
    (block_c,) = select([rows(merge)], table_c, [C_ROWS], BF16, False)
    a_low, a_high = gather(block_a, A_SPLIT)
    b_low, b_high = gather(block_b)
    c_low, c_high = gather(block_c, C_ROWS // 2)

    big, narrow = (D, TOKENS), (D, QUARTER)
    entry, stats_1 = call(entry_kernel, (scal, tokens[0]), [(big, BF16), ((8, TOKENS), F32)], micros=3.5)
    wq, wkv, wr, wo, first, qs, raw, stat_r, red, kv, kt, vt, bt = call(
        project_kernel,
        (scal, a_low, a_high, entry, stats_1),
        [
            ((D, D), BF16), ((2 * D, D), BF16), ((D, 4 * D), BF16), ((D, D), BF16), (big, BF16), (big, BF16),
            (narrow, F32), ((8, QUARTER), F32), (narrow, BF16), ((2 * D, QUARTER), BF16),
            ((HEADS, QUARTER, 64), BF16), ((HEADS, QUARTER, 64), BF16), ((64, 128), F32),
        ],
        [((1024, 1280), BF16), ((D, 1280), BF16), ((4 * D, QUARTER), BF16)],
        micros=8,
    )
    att, lse = call(attend_kernel, (scal, kt, qs, kv), [(big, BF16), ((HEADS, 1, TOKENS), F32)],
        [((2, QUARTER, TOKENS), F32), ((QUARTER, TOKENS), BF16)], micros=8.5)
    mid, sec, stats_2 = call(
        middle_kernel, (scal, bt, wo, att, entry), [(big, F32), ((384, TOKENS), BF16), ((8, TOKENS), F32)], [(big, F32)],
        micros=5,
    )
    w1, w1t, w2, w2t, taps = call(
        ffn_weights_kernel,
        (scal, bt, b_low, b_high),
        [((FF, 384), BF16), ((D, FF), BF16), ((D, FF), BF16), ((FF, D), BF16), ((10, FF, 128), F32)],
        [((512, 640), BF16), ((256, 384), BF16), ((FF, 384), F32), ((2, 2 * D, 768), BF16)],
        micros=8,
    )
    act, slope = call(
        ffn_kernel,
        (scal, w1, taps, sec),
        [((FF, TOKENS), BF16), ((FF, TOKENS), BF16)],
        [((64, TOKENS), F32), ((64, TOKENS), F32)],
        micros=17,
    )
    end, sect, stats_s = call(
        ending_kernel, (scal, bt, w2, act, mid), [(big, F32), (big, BF16), ((8, TOKENS), F32)], [(big, F32)], micros=5
    )
    four, c_keep, c_send, end_grad, branch, g_one = call(
        merge_kernel,
        (scal, bt, c_low, c_high, sect, end, stats_s, cotangent[0]),
        [
            ((OUT_D, QUARTER), BF16), ((16, C_ROWS, 128), BF16), ((16, C_ROWS, 128), BF16), (big, F32), (big, BF16),
            ((64, 128), F32),
        ],
        [
            ((OUT_D, MERGE_PAD), BF16), ((MERGE_PAD, QUARTER), BF16), ((OUT_D, QUARTER), BF16),
            ((MERGE_PAD, QUARTER), F32), ((OUT_D, QUARTER), F32), ((OUT_D, QUARTER), F32),
        ],
        micros=20,
    )
    sum_c = scatter(c_keep, c_send, C_ROWS // 2)
    hgs, dks = [], []
    for at, count in PARTS:
        hg, dk = call(
            functools.partial(ffn_back_kernel, at, count),
            (scal, w1, w2t, taps, sec, slope, branch),
            [((256 * count, TOKENS), BF16), ((256 * count, 128), F32)],
            [((64, TOKENS), F32)] * 4,
            micros=6 * count,
        )
        hgs.append(hg)
        dks.append(dk)
    b_keep, b_send, g_three = call(
        pack_b_kernel,
        (scal, *hgs, *dks, sec, branch, act),
        [((16, B_ROWS, 128), BF16), ((16, B_ROWS, 128), BF16), ((64, 128), F32)],
        [((FF, 384), F32), ((32, 144, 128), F32)],
        micros=9,
    )
    sum_b = scatter(b_keep, b_send)
    mid_grad, low_grad, g_two = call(
        middle_back_kernel,
        (scal, bt, w1t, *hgs, end_grad, mid, stats_2),
        [(big, F32), (big, BF16), ((64, 128), F32)],
        [(big, F32)],
        micros=6,
    )
    dwo, dq, dkv = call(
        attend_back_kernel,
        (scal, kt, vt, qs, kv, wo, low_grad, att, lse),
        [((D, D), BF16), (big, BF16), ((2 * D, QUARTER), BF16)],
        [
            (big, BF16), ((2, QUARTER, TOKENS), F32), ((2, QUARTER, TOKENS), F32), ((QUARTER, TOKENS), BF16),
            ((QUARTER, TOKENS), BF16),
        ],
        micros=10,
    )
    a_keep, a_send, first_grad = call(
        first_kernel,
        (
            scal, bt, wq, wkv, wr, first, red, raw, stat_r, dq, dkv, dwo, entry, stats_1, g_one, g_two, g_three,
        ),
        [((16, A_ROWS, 128), BF16), ((16, A_ROWS, 128), BF16), (big, F32)],
        [
            ((64, 128), F32), ((4 * D, QUARTER), F32), ((4 * D, QUARTER), BF16), ((2 * D, 1280), BF16),
            ((32, 48, 128), F32),
        ],
        micros=11,
    )
    sum_a = scatter(a_keep, a_send, A_SPLIT)
    (token_grad,) = call(
        token_kernel,
        (scal, bt, first_grad, mid_grad, entry, stats_1),
        [(big, F32)],
        [(big, BF16), (big, BF16)],
        micros=5,
    )
    if group > 1:

        def total(part):
            full = lax.all_gather(part, axes[1], axis=0)
            return jnp.sum(lax.dynamic_slice_in_dim(full, start, group, axis=0), axis=0)

        sum_a, sum_b, sum_c = total(sum_a), total(sum_b), total(sum_c)
    query_g, output_g, keyval_g, reduce_g, biases_g, gains_g = select(
        [sum_a], table_out_a, [25, 25, 50, 100], F32, True, "out", (scal, biases[None], gains[None])
    )
    contract_g, expand_g = select([sum_b], table_out_b, [100, 100], F32, True)
    (merge_g,) = select([sum_c], table_out_c, [360], F32, True)
    depth_g = sum_b[184:224, 64:73]
    grads = [query_g, keyval_g, reduce_g, output_g, expand_g, depth_g, contract_g, merge_g, gains_g, biases_g]
    grads = [grad.reshape(-1) for grad in grads]
    if group > 1:
        mine = index % group
        grads = [lax.dynamic_index_in_dim(grad.reshape(group, -1), mine, keepdims=False) for grad in grads]
    return (four[None], token_grad[None], *grads)


def solution(mesh):
    axes = ("dp", "fs")
    devices = mesh.shape["dp"] * mesh.shape["fs"]
    group = devices // SUPER
    if devices != SUPER * group or mesh.shape["fs"] % group:
        raise ValueError("unsupported mesh")
    one, three = P(axes), P(axes, None, None)
    return jax.shard_map(
        functools.partial(local, group, axes),
        mesh=mesh,
        in_specs=(three, one, three) + (one,) * 10,
        out_specs=(three, three) + (one,) * 10,
        check_vma=False,
    )
```

```python
import functools

import jax
import jax.numpy as jnp
import numpy as np
from jax import lax
from jax.experimental import pallas as pl
from jax.experimental.pallas import tpu as pltpu
from jax.sharding import PartitionSpec as P


D = 320
HEADS = 5
FF = 1280
OUT_D = 512
SIDE = 32
QUARTER = 256
TOKENS = SIDE * SIDE
MERGE_PAD = 2944
SUPER = 32
FLIPS = (2, 4, 8, 16)
EPS = 1e-06
F32, BF16, I32 = jnp.float32, jnp.bfloat16, jnp.int32

B_Q, B_R, C_R, B_O, C_1, C_2, B_1, B_DW, B_2, C_S, B_M, C_M = 0, 5, 10, 15, 20, 25, 30, 50, 70, 75, 80, 88
G_R, G_1, G_2, G_S, G_M = 96, 101, 106, 111, 116

PARTS = ((0, 1), (1, 4))
A_ROWS, B_ROWS, C_ROWS = 208, 224, 368
SMALL_ROW = 200
A_SPLIT = 104
VMEM_LIMIT = 24 * 1024 * 1024
VMEM_ALL = 60 * 1024 * 1024


def slot_of(xor):
    return (xor >> 1) | ((xor & 1) << 4)


def xor_of(slot):
    return ((slot & 15) << 1) | (slot >> 4)


def dot(a, b):
    return jnp.dot(a, b, preferred_element_type=F32)


def dot_nt(a, b):
    return lax.dot_general(a, b, (((1,), (1,)), ((), ())), preferred_element_type=F32)


def dot_tn(a, b):
    return lax.dot_general(a, b, (((0,), (0,)), ((), ())), preferred_element_type=F32)


def iota(shape, axis):
    return lax.broadcasted_iota(I32, shape, axis)


def one_hot(test):
    return jnp.where(test, 1.0, 0.0).astype(BF16)


def lanes(index, width=128):
    return pl.ds(pl.multiple_of(index * width, width), width)


def loop(count, body):
    def step(index, carry):
        body(index)
        return carry

    lax.fori_loop(0, count, step, 0)


def column(table, start, count):
    return jnp.concatenate(
        [jnp.broadcast_to(table[:, h : h + 1], (64, 128)) for h in range(start, start + count)], axis=0
    )


def put_column(table, start, values):
    for h in range(values.shape[0] // 64):
        table[:, start + h : start + h + 1] = values[64 * h : 64 * h + 64, 0:1]


def token_place(lane):
    quad = lane >> 8
    row = 2 * ((lane >> 4) & 15) + (quad >> 1)
    col = 2 * (lane & 15) + (quad & 1)
    return row, col


def token_mask(tile, side, width=128):
    row, col = token_place(iota((1, width), 1) + tile * width)
    return jnp.where((row < side) & (col < side), 1.0, 0.0)


def key_place(index):
    return index >> 4, index & 15


def select_kernel(count, bases, small, small_at, *refs):
    sources, refs = refs[:count], refs[count:]
    if small:
        scal, biases, gains = refs[:3]
        refs = refs[3:]
    low_ref, high_ref, out, rows_ref, sems = refs[:5]
    held = refs[5:]
    copies = [
        pltpu.make_async_copy(source, place, sems.at[n]) for n, (source, place) in enumerate(zip(sources, held))
    ]
    for copy in copies:
        copy.start()
    half = rows_ref.shape[0] // 2
    rows_ref[...] = jnp.zeros_like(rows_ref)
    place = iota((out.shape[0], 2 * half), 1)
    pick_low = one_hot(place == low_ref[...])
    pick_high = one_hot(place == high_ref[...])
    for copy in copies:
        copy.wait()
    for source, base in zip(held, bases):
        rows_ref[base : base + source.shape[0], :] = source[...].astype(F32)
    if small:
        rows_ref[small_at : small_at + 1, :] = biases[:, 0:128].astype(F32)
        rows_ref[small_at + 1 : small_at + 2, 0:64] = biases[:, 128:192].astype(F32)
        wide = jnp.concatenate([gains[...].astype(F32), jnp.zeros((1, 72), F32)], axis=1)
        wide = jnp.broadcast_to(wide, (8, 128))
        rows_ref[small_at + 2 : small_at + 3, :] = pltpu.roll(wide, (56 * scal[0]) & 63, 1)[0:1, :]
    rows_ref[half:, :] = pltpu.roll(rows_ref[0:half, :], 64, 1)
    total = rows_ref[...].astype(BF16)
    low, upper = dot(pick_low, total), dot(pick_high, total)
    out[...] = jnp.where(iota((out.shape[0], 128), 1) < 64, low, upper).astype(BF16)


def select(sources, table, rows, vectors=()):
    bases, at = [], 0
    for source in sources:
        bases.append(at)
        at += -(-source.shape[0] // 16) * 16
    small = len(vectors) > 0
    half = at + (16 if small else 0)
    low, high = table(bases + [at], half).astype(np.int32)[:, :, None]
    specs = [pl.BlockSpec(memory_space=pltpu.HBM)] * len(sources)
    if small:
        specs += [pl.BlockSpec(memory_space=pltpu.SMEM)] + [pl.BlockSpec(memory_space=pltpu.VMEM)] * 2
    specs += [pl.BlockSpec(memory_space=pltpu.VMEM)] * 2
    return pl.pallas_call(
        functools.partial(select_kernel, len(sources), tuple(bases), small, at),
        in_specs=specs,
        out_shape=jax.ShapeDtypeStruct((rows, 128), BF16),
        scratch_shapes=[pltpu.VMEM((2 * half, 128), F32), pltpu.SemaphoreType.DMA((len(sources),))]
        + [pltpu.VMEM(source.shape, source.dtype) for source in sources],
        compiler_params=pltpu.CompilerParams(vmem_limit_bytes=VMEM_ALL if small else VMEM_LIMIT),
        cost_estimate=cost(2),
    )(*sources, *vectors, low, high)


def pair(half, low_src, high_src):
    low = -1 if low_src is None else low_src[0] + low_src[1] // 2 + half * (low_src[1] % 2)
    high = -1 if high_src is None else high_src[0] + high_src[1] // 2 + half * (1 - high_src[1] % 2)
    return low, high


def chunk_sources(bases, row, c):
    q, o, kv = bases
    if c < 6 or c >= 8:
        base, first = ((q, 0), (kv, 0), (kv, 10), None, (o, 0))[c // 2]
        at = 5 * (first + row) + 2 * (c % 2)
        return (base, at), (base, at + 1)
    if c == 6:
        return (q, 5 * row + 4), (kv, 5 * row + 4)
    return (kv, 5 * (10 + row) + 4), (o, 5 * row + 4)


def a_place(kind, row, c):
    if row < 8:
        return 16 * c + 8 * kind + row
    return 160 + 8 * (c // 2) + 4 * kind + 2 * (c % 2) + row - 8


def b_place(row, c):
    if row < 8:
        return 8 * c + row
    return 80 + 8 * (c // 4) + 2 * (c % 4) + row - 8


def table_a(bases, half):
    q, o, kv, r, small = bases
    rows = [(-1, -1)] * A_ROWS
    for c in range(10):
        for row in range(10):
            at = 20 * row + 2 * c
            rows[a_place(0, row, c)] = pair(half, (r, at), (r, at + 1))
            rows[a_place(1, row, c)] = pair(half, *chunk_sources((q, o, kv), row, c))
    for row in range(3):
        rows[SMALL_ROW + row] = pair(half, (small, 2 * row), (small, 2 * row + 1))
    return np.array(rows).T


def table_b(bases, half):
    w2, w1, dw, _ = bases
    rows = [(-1, -1)] * B_ROWS
    for c in range(10):
        for row in range(10):
            at = 20 * row + 2 * c
            rows[b_place(row, c)] = pair(half, (w2, at), (w2, at + 1))
    for c in range(3):
        for row in range(40):
            at = 5 * row + 2 * c
            rows[104 + 40 * c + row] = pair(half, (w1, at), (w1, at + 1) if c < 2 else (dw, 2 * row + 1))
    return np.array(rows).T


def table_c(bases, half):
    m, _ = bases
    rows = []
    for c in range(23):
        for row in range(16):
            at = 45 * row + 2 * c
            rows.append(pair(half, (m, at), (m, at + 1) if c < 22 else None))
    return np.array(rows).T


def turn(rows):
    return pltpu.roll(rows, 64, 1)


def halves(low, high):
    return jnp.where(iota((1, 128), 1) < 64, low, high)


def put_rows(out, first, count, stride, rows):
    out[pl.ds(first, count, stride=stride), :] = rows


def put_320(out, first, count, load):
    even, odd = ([load(chunk, parity) for chunk in range(3)] for parity in range(2))
    turned = [turn(rows) for rows in odd]
    for at, rows in enumerate(
        (even[0], even[1], halves(even[2], turned[0]), halves(turned[0], turned[1]), halves(turned[1], turned[2]))
    ):
        put_rows(out, first + at, count // 2, 5, rows)


def every_other(ref, start, count):
    return ref[pl.ds(start, count, stride=2), :]


def out_a_kernel(scal, sums, q, o, kv, r, biases, gains):
    squares = (
        (q, 0, (0, 1, 6), False),
        (o, 0, (8, 9, 7), True),
        (kv, 0, (2, 3, 6), True),
        (kv, 25, (4, 5, 7), False),
    )
    for out, first, chunks, high in squares:
        for start, count, lane_row in ((0, 8, 0), (8, 2, 20)):

            def load(chunk, parity, chunks=chunks, high=high, start=start, count=count):
                rows = every_other(sums, a_place(1, start, chunks[chunk]) + parity, count // 2)
                return turn(rows) if chunk == 2 and high else rows

            put_320(out, first + lane_row, count, load)
    for c in range(10):
        for start, count in ((0, 8), (8, 2)):
            put_rows(r, 10 * start + c, count, 10, sums[pl.ds(a_place(0, start, c), count), :])
    small = sums[SMALL_ROW : SMALL_ROW + 8, :]
    biases[:, 0:128] = small[0:1]
    biases[:, 128:192] = small[1:2, 0:64]
    gains[...] = pltpu.roll(small, (128 - ((56 * scal[0]) & 63)) & 127, 1)[2:3, 0:56]


def out_b_kernel(scal, sums, w2, w1):
    for c in range(10):
        for start, count in ((0, 8), (8, 2)):
            put_rows(w2, 10 * start + c, count, 10, sums[pl.ds(b_place(start, c), count), :])
    put_320(w1, 0, 40, lambda chunk, parity: every_other(sums, 104 + 40 * chunk + parity, 20))


def out_c_kernel(scal, sums, m):
    even = [every_other(sums, 16 * c, 8) for c in range(23)]
    turned = [turn(every_other(sums, 16 * c + 1, 8)) for c in range(23)]
    for c in range(22):
        put_rows(m, c, 8, 45, even[c])
        put_rows(m, 23 + c, 8, 45, halves(turned[c], turned[c + 1]))
    put_rows(m, 22, 8, 45, halves(even[22], turned[0]))


def split_ten(row, per, magic):
    owner = (row * magic) >> 16
    return owner, row - per * owner


def tens(row, me):
    owner, rest = split_ten(row, 10, 6554)
    slot = slot_of(owner ^ me)
    return jnp.where(rest < 8, slot * 8 + rest, 248 + slot * 2 + rest)


def from_tens(me):
    return one_hot(iota((D, D), 1) == tens(iota((D, 1), 0), me))


def to_tens(me):
    return one_hot(iota((D, D), 0) == tens(iota((1, D), 1), me))


def keyval_tens(row, me, upper):
    owner, rest = split_ten(row, 20, 3277)
    inside = (rest >= 10) if upper else (rest < 10)
    return jnp.where(inside, tens(10 * owner + rest - (10 if upper else 0), me), -1)


def rest_row(row):
    return 64 * ((row & 7) >> 1) + 2 * (row >> 3) + (row & 1)


def norm(values, gain, shift):
    mean = jnp.mean(values, axis=0, keepdims=True)
    centred = values - mean
    rstd = lax.rsqrt(jnp.mean(centred * centred, axis=0, keepdims=True) + EPS)
    return centred * rstd * gain + shift, mean, rstd


def norm_back(grad, hat, rstd, gain):
    scaled = grad * gain
    return rstd * (
        scaled
        - jnp.mean(scaled, axis=0, keepdims=True)
        - hat * jnp.mean(scaled * hat, axis=0, keepdims=True)
    )


def stat_rows(mean, rstd):
    row = iota((8, mean.shape[1]), 0)
    return jnp.where(row == 0, mean, jnp.where(row == 1, rstd, 0.0))


def entry_kernel(scal, tokens, entry, stats):
    side = scal[1]
    for quad in range(4):
        lane = iota((1, 256), 1) + quad * 256
        row, col = token_place(lane)
        natural = row * SIDE + col
        pick = one_hot(iota((TOKENS, 256), 0) == natural)
        mask = jnp.where((row < side) & (col < side), 1.0, 0.0)
        entry[:, quad * 256 : quad * 256 + 256] = (dot(tokens[...], pick) * mask).astype(BF16)

    def body(tile):
        values = entry[:, lanes(tile)].astype(F32)
        mean = jnp.mean(values, axis=0, keepdims=True)
        centred = values - mean
        rstd = lax.rsqrt(jnp.mean(centred * centred, axis=0, keepdims=True) + EPS)
        stats[:, lanes(tile)] = stat_rows(mean, rstd)

    loop(8, body)


def small_table(me, low, high):
    gathered = jnp.concatenate(
        [half[:, SMALL_ROW : SMALL_ROW + 8, :].astype(F32).reshape(128, 128) for half in (low, high)], axis=0
    ).astype(BF16)
    vector = iota((128, 256), 0)
    place = iota((128, 256), 1)
    row = place & 7
    owner = xor_of(place >> 3) ^ me
    first = (7 * owner) >> 3
    straight = (
        ((row == 0) & (vector == 3 * owner))
        | ((row == 1) & (vector == 3 * owner + 2))
        | ((row == 2) & (vector == 96 + first))
    )
    turned = ((row == 0) & (vector == 3 * owner + 1)) | ((row == 2) & (vector == 97 + first))
    rows = dot(one_hot(straight), gathered) + pltpu.roll(dot(one_hot(turned), gathered), 64, 1)
    return jnp.transpose(rows)[0:64, :]


def project_kernel(scal, low, high, entry, stats, wq, wkv, wrs, wo, first, qs, raw, stat_r, red, kv, kt, vt, bt, square, rest, redin):
    me = scal[0]
    bt[...] = small_table(me, low, high)
    for half, source in enumerate((low, high)):

        def chunk(c, half=half, source=source):
            block = source[:, pl.ds(pl.multiple_of(16 * c, 16), 16), :].astype(F32)
            rows = slice(128 * half, 128 * half + 128)
            wrs[rows, lanes(c)] = block[:, 0:8].reshape(128, 128).astype(BF16)
            square[rows, lanes(c)] = block[:, 8:16].reshape(128, 128).astype(BF16)

        loop(10, chunk)
        block = source[:, 160:208, :].astype(F32)
        for c in range(5):
            part = block[:, 8 * c : 8 * c + 8].reshape(128, 128).astype(BF16)
            rest[128 * half : 128 * half + 128, 128 * c : 128 * c + 128] = part
    spread = one_hot(iota((256, 256), 0) == rest_row(iota((1, 256), 1)))

    def last_two(p):
        part = dot(spread, rest[:, lanes(p)]).astype(BF16)
        wrs[256:320, lanes(p, 256)] = jnp.concatenate([part[0:64], part[64:128]], axis=1)
        square[256:320, lanes(p, 256)] = jnp.concatenate([part[128:192], part[192:256]], axis=1)

    loop(5, last_two)
    order = from_tens(me)
    wq[:, 0:256] = dot(order, square[:, 0:256]).astype(BF16)
    wo[:, 0:256] = dot(order, square[:, 1024:1280]).astype(BF16)
    tails = dot(order, square[:, 768:1024])
    wq[:, 256:320] = tails[:, 0:64].astype(BF16)
    wo[:, 256:320] = pltpu.roll(tails, 64, 1)[:, 0:64].astype(BF16)
    row = iota((2 * D, 1), 0)
    place = iota((2 * D, D), 1)
    lower = one_hot(place == keyval_tens(row, me, False))
    upper = one_hot(place == keyval_tens(row, me, True))
    wkv[:, 0:256] = (dot(lower, square[:, 256:512]) + dot(upper, square[:, 512:768])).astype(BF16)
    tail = pltpu.roll(dot(lower, square[:, 768:896]), 64, 1) + dot(upper, square[:, 896:1024])
    wkv[:, 256:320] = tail[:, 0:64].astype(BF16)

    gain, shift = column(bt, G_1, 5), column(bt, C_1, 5)

    def body(tile):
        centred = entry[:, lanes(tile)].astype(F32) - stats[0:1, lanes(tile)]
        first[:, lanes(tile)] = (centred * stats[1:2, lanes(tile)] * gain + shift).astype(BF16)

    loop(8, body)
    for quad in range(4):
        redin[D * quad : D * quad + D, :] = first[:, 256 * quad : 256 * quad + 256]
    bias = column(bt, B_R, 5)
    bias = jnp.concatenate([bias, bias], axis=1)
    mixed = dot(wrs[...], redin[...])
    total = bias
    for part in range(3):
        piece = mixed.astype(BF16)
        total = total + dot(order, piece)
        mixed = mixed - piece.astype(F32)
    raw[...] = total
    gain, shift = column(bt, G_R, 5), column(bt, C_R, 5)
    for tile in range(2):
        at = slice(128 * tile, 128 * tile + 128)
        values, mean, rstd = norm(raw[:, at], gain, shift)
        red[:, at] = values.astype(BF16)
        stat_r[:, at] = stat_rows(mean, rstd)
    keyval = dot(wkv[...], red[...])
    kv[...] = keyval.astype(BF16)
    turned = jnp.transpose(keyval)
    for h in range(HEADS):
        kt[h] = turned[:, 64 * h : 64 * h + 64].astype(BF16)
        vt[h] = turned[:, D + 64 * h : D + 64 * h + 64].astype(BF16)
    bias = column(bt, B_Q, 5)
    bias = jnp.concatenate([bias, bias], axis=1)

    def query(quad):
        at = lanes(quad, 256)
        qs[:, at] = (dot(wq[...], first[:, at]) + bias).astype(BF16) * BF16(0.125)

    loop(4, query)


def key_bias(side):
    i, j = key_place(iota((QUARTER, 1), 0))
    return jnp.where((i < (side >> 1)) & (j < (side >> 1)), 0.0, -10000.0)


def attend_kernel(scal, kt, qs, kv, att, lse, scores, probs):
    bias = key_bias(scal[1])

    def score(h, slot):
        scores[slot] = dot(kt[h], qs[pl.ds(pl.multiple_of(64 * h, 64), 64), :])

    score(0, 0)

    def head(h):
        score(jnp.minimum(h + 1, HEADS - 1), 1 - (h & 1))
        rows = pl.ds(pl.multiple_of(64 * h, 64), 64)
        values = kv[pl.ds(pl.multiple_of(D + 64 * h, 64), 64), :]
        for tile in range(8):
            at = slice(128 * tile, 128 * tile + 128)
            part = scores[h & 1, :, at] + bias
            top = jnp.max(part, axis=0, keepdims=True)
            weights = jnp.exp(part - top)
            total = jnp.sum(weights, axis=0, keepdims=True)
            lse[h, :, at] = top + jnp.log(total)
            probs[:, at] = (weights * (1.0 / total)).astype(BF16)
        att[rows, :] = dot(values, probs[...]).astype(BF16)

    loop(HEADS, head)


def middle_kernel(scal, bt, wo, att, entry, mid, sec, stats, work):
    side = scal[1]
    work[...] = dot(wo[...], att[...])
    bias, gain, shift = column(bt, B_O, 5), column(bt, G_2, 5), column(bt, C_2, 5)

    def body(tile):
        at = lanes(tile)
        mask = token_mask(tile, side)
        values = entry[:, at].astype(F32) + mask * (work[:, at] + bias)
        mid[:, at] = values
        normed, mean, rstd = norm(values, gain, shift)
        stats[:, at] = stat_rows(mean, rstd)
        sec[0:D, at] = (normed.astype(BF16).astype(F32) * mask).astype(BF16)
        sec[D : D + 64, at] = jnp.where(iota((64, 128), 0) == 9, mask, 0.0).astype(BF16)

    loop(8, body)


def ffn_weights_kernel(scal, bt, low, high, w1, w1t, w2, w2t, taps, main, rest, wide):
    me = scal[0]
    for half, source in enumerate((low, high)):
        def chunks(p, half=half, source=source):
            block = source[:, pl.ds(pl.multiple_of(16 * p, 16), 16), :].astype(F32)
            both = jnp.concatenate([block[:, 0:8].reshape(128, 128), block[:, 8:16].reshape(128, 128)], axis=1)
            main[128 * half : 128 * half + 128, lanes(p, 256)] = both.astype(BF16)

        loop(5, chunks)
        block = source[:, 80:112, :].astype(F32)
        for c in range(3):
            part = block[:, 8 * c : 8 * c + 8].reshape(128, 128).astype(BF16)
            rest[128 * half : 128 * half + 128, 128 * c : 128 * c + 128] = part

        def expansion(slot, half=half, source=source):
            owner = ((slot << 1) | half) ^ me
            block = source[slot, 80:224, :].astype(F32)
            rows = pl.ds(pl.multiple_of(40 * owner, 8), 40)
            for c in range(3):
                wide[rows, 128 * c : 128 * c + 128] = block[24 + 40 * c : 64 + 40 * c]

        loop(16, expansion)
    spread = one_hot(iota((256, 256), 0) == rest_row(iota((1, 256), 1)))
    for j in range(3):
        part = dot(spread, rest[:, 128 * j : 128 * j + 128]).astype(BF16)
        for k in range(4 if j < 2 else 2):
            c = 4 * j + k
            main[256:320, 128 * c : 128 * c + 128] = part[64 * k : 64 * k + 64]
    order = from_tens(me)

    def contraction(p):
        block = dot(order, main[:, lanes(p, 256)])
        w2[:, lanes(p, 256)] = block.astype(BF16)
        w2t[pl.ds(pl.multiple_of(256 * p, 256), 256), :] = jnp.transpose(block).astype(BF16)

    loop(5, contraction)
    bias = column(bt, B_1, 20)
    lane = iota((FF, 128), 1)
    tail = wide[:, 256:384]
    low_tail = tail.astype(BF16)

    def spread(tap):
        taps[tap] = dot(low_tail, one_hot(iota((128, 128), 0) == 64 + tap))

    loop(9, spread)
    taps[9] = column(bt, B_DW, 20)
    w1[:, 0:256] = wide[:, 0:256].astype(BF16)
    w1[:, 256:384] = jnp.where(lane < 64, tail, jnp.where(lane == 73, bias, 0.0)).astype(BF16)

    def turn(p):
        rows = pl.ds(pl.multiple_of(256 * p, 256), 256)
        w1t[:, lanes(p, 256)] = jnp.transpose(wide[rows, :])[0:D].astype(BF16)

    loop(5, turn)


def edge_masks():
    lane = iota((1, 128), 1)
    j = lane & 15
    return jnp.where(j != 0, 1.0, 0.0), jnp.where(j != 15, 1.0, 0.0), lane >= 16, lane < 112


def left_of(tiles):
    return [pltpu.roll(tile, 1, 1) for tile in tiles]


def right_of(tiles):
    return [pltpu.roll(tile, 127, 1) for tile in tiles]


def above(tiles, inside):
    turned = [pltpu.roll(tile, 16, 1) for tile in tiles]
    return [jnp.where(inside, turned[0], 0.0), jnp.where(inside, turned[1], turned[0])]


def below(tiles, inside):
    turned = [pltpu.roll(tile, 112, 1) for tile in tiles]
    return [jnp.where(inside, turned[0], turned[1]), jnp.where(inside, turned[1], 0.0)]


def times(tiles, factor):
    return [tile * factor for tile in tiles]


def plus(*many):
    return [functools.reduce(lambda a, b: a + b, tiles) for tiles in zip(*many)]


def tile_at(a, e, half):
    start = 256 * (2 * a + e) + 128 * half
    return slice(start, start + 128)


def quads(ref, rows):
    return [[[ref[rows, tile_at(a, e, half)] for half in range(2)] for e in range(2)] for a in range(2)]


LOG2E = float(np.log2(np.e))


def gelu_parts(x):
    y = x * np.float32(0.5**0.5)
    cdf = lax.erf(y) * 0.5 + 0.5
    bell = jnp.exp2(y * y * np.float32(-LOG2E) + np.float32(-0.5 * np.log2(2.0 * np.pi)))
    return x * cdf, cdf + x * bell


def ffn_kernel(scal, w1, taps, sec, act, slope, hid_a, hid_b):
    j_first, j_last, i_first, i_last = edge_masks()

    def fill(hid, step):
        rows = pl.ds(pl.multiple_of(jnp.minimum(step, FF // 64 - 1) * 64, 64), 64)
        hid[...] = dot(w1[rows, :], sec[...])

    def group(hid, step, index):
        rows = slice(16 * index, 16 * index + 16)
        out_rows = pl.ds(pl.multiple_of(64 * step + 16 * index, 16), 16)
        k = [taps[n, out_rows, :] for n in range(10)]
        first = [k[3 * r] * j_first for r in range(3)]
        last = [k[3 * r + 2] * j_last for r in range(3)]
        quad = quads(hid, rows)
        left = [left_of(quad[a][1]) for a in range(2)]
        right = [right_of(quad[a][0]) for a in range(2)]

        def across(a, e, r):
            if e == 0:
                parts = zip(left[a], quad[a][0], quad[a][1])
                return [first[r] * x + k[3 * r + 1] * y + k[3 * r + 2] * z for x, y, z in parts]
            parts = zip(quad[a][0], quad[a][1], right[a])
            return [k[3 * r] * x + k[3 * r + 1] * y + last[r] * z for x, y, z in parts]

        for e in range(2):
            up = above(across(1, e, 0), i_first)
            down = below(across(0, e, 2), i_last)
            outs = (plus(across(0, e, 1), across(1, e, 2), up), plus(across(0, e, 0), across(1, e, 1), down))
            for a in range(2):
                for half in range(2):
                    value, grad = gelu_parts(outs[a][half] + k[9])
                    act[out_rows, tile_at(a, e, half)] = value.astype(BF16)
                    slope[out_rows, tile_at(a, e, half)] = grad.astype(BF16)

    fill(hid_a, 0)

    def two(index):
        fill(hid_b, 2 * index + 1)
        for n in range(4):
            group(hid_a, 2 * index, n)
        fill(hid_a, 2 * index + 2)
        for n in range(4):
            group(hid_b, 2 * index + 1, n)

    loop(FF // 128, two)


def ending_kernel(scal, bt, w2, act, mid, end, sect, stats, work):
    side = scal[1]
    work[...] = dot(w2[...], act[...])
    bias, gain, shift = column(bt, B_2, 5), column(bt, G_S, 5), column(bt, C_S, 5)

    def body(tile):
        at = lanes(tile)
        mask = token_mask(tile, side)
        values = mid[:, at] + mask * (work[:, at] + bias)
        end[:, at] = values
        normed, mean, rstd = norm(values, gain, shift)
        stats[:, at] = stat_rows(mean, rstd)
        sect[:, at] = (normed.astype(BF16).astype(F32) * mask).astype(BF16)

    loop(8, body)


def lane_sum(values):
    return jnp.sum(values, axis=1, keepdims=True)


def merge_kernel(scal, bt, c_low, c_high, sect, end, stats, cot, four, keep, send, end_grad, branch, grads, wm, patch, mg, back, work, natural):
    me, side = scal[0], scal[1]
    grads[...] = jnp.zeros_like(grads)
    for half, source in enumerate((c_low, c_high)):

        def place(c, half=half, source=source):
            block = source[:, pl.ds(pl.multiple_of(16 * c, 16), 16), :].reshape(256, 128)
            wm[256 * half : 256 * half + 256, lanes(c)] = block

        loop(23, place)

    def reorder(to_owner):
        def one(slot):
            at = pl.ds(pl.multiple_of(16 * slot, 16), 16)
            owner = pl.ds(pl.multiple_of((xor_of(slot) ^ me) * 16, 16), 16)
            to_owner(at, owner)

        loop(32, one)

    j_first, j_last, i_first, i_last = edge_masks()
    quad = [[[t.astype(F32) for t in pair] for pair in row] for row in quads(sect, slice(None))]
    left = [times(left_of(quad[a][1]), j_first) for a in range(2)]
    pieces = (
        above(left[1], i_first),
        above(quad[1][0], i_first),
        above(quad[1][1], i_first),
        left[0],
        quad[0][0],
        quad[0][1],
        left[1],
        quad[1][0],
        quad[1][1],
    )
    for n, piece in enumerate(pieces):
        for half in range(2):
            patch[D * n : D * n + D, 128 * half : 128 * half + 128] = piece[half].astype(BF16)
    patch[9 * D :, :] = jnp.zeros((MERGE_PAD - 9 * D, 256), BF16)
    bias, gain, shift = column(bt, B_M, 8), column(bt, G_M, 8), column(bt, C_M, 8)
    work[...] = dot(wm[...], patch[...])

    def from_slots(at, owner):
        natural[owner, :] = work[at, :]

    reorder(from_slots)
    half_side = side >> 1
    for tile in range(2):
        at = slice(128 * tile, 128 * tile + 128)
        i, j = key_place(iota((1, 128), 1) + 128 * tile)
        mask = jnp.where((i < half_side) & (j < half_side), 1.0, 0.0)
        values = natural[:, at] + bias
        mean = jnp.mean(values, axis=0, keepdims=True)
        centred = values - mean
        rstd = lax.rsqrt(jnp.mean(centred * centred, axis=0, keepdims=True) + EPS)
        hat = centred * rstd
        four[:, at] = ((hat * gain + shift) * mask).astype(BF16)
        grad = cot[:, at].astype(F32) * mask
        low = norm_back(grad, hat, rstd, gain).astype(BF16)
        natural[:, at] = low.astype(F32)
        parts = (grad * hat, grad, low.astype(F32))
        sums = parts if tile == 0 else [s + v for s, v in zip(sums, parts)]
    put_column(grads, G_M, lane_sum(sums[0]))
    put_column(grads, C_M, lane_sum(sums[1]))
    put_column(grads, B_M, lane_sum(sums[2]))

    def to_slots(at, owner):
        mg[at, :] = natural[owner, :].astype(BF16)

    reorder(to_slots)

    def widths(body):
        loop(11, lambda c: body(pl.multiple_of(c * 256, 256), 256))
        body(11 * 256, 128)

    def patch_grad(start, width):
        back[pl.ds(start, width), :] = dot_tn(wm[:, pl.ds(start, width)], mg[...])

    widths(patch_grad)

    def piece(n):
        return [back[D * n : D * n + D, 128 * half : 128 * half + 128] for half in range(2)]

    results = (
        piece(4),
        plus(piece(5), times(right_of(piece(3)), j_last)),
        plus(piece(7), below(piece(1), i_last)),
        plus(
            piece(8),
            times(right_of(piece(6)), j_last),
            below(plus(piece(2), times(right_of(piece(0)), j_last)), i_last),
        ),
    )
    for n, values in enumerate(results):
        for half in range(2):
            end_grad[:, 256 * n + 128 * half : 256 * n + 128 * half + 128] = values[half]
    gain = column(bt, G_S, 5)
    zeros = jnp.zeros((D, 128), F32)

    def body(tile, carry):
        at = lanes(tile)
        mask = token_mask(tile, side)
        grad = end_grad[:, at] * mask
        hat = (end[:, at] - stats[0:1, at]) * stats[1:2, at]
        result = norm_back(grad, hat, stats[1:2, at], gain)
        end_grad[:, at] = result
        low = (result * mask).astype(BF16)
        branch[:, at] = low
        return carry[0] + grad * hat, carry[1] + grad, carry[2] + low.astype(F32)

    sums = lax.fori_loop(0, 8, body, (zeros, zeros, zeros))
    put_column(grads, G_S, lane_sum(sums[0]))
    put_column(grads, C_S, lane_sum(sums[1]))
    put_column(grads, B_2, lane_sum(sums[2]))

    def give(start, width):
        block = dot_nt(mg[...], patch[pl.ds(start, width), :]).astype(BF16)
        for c in range(width // 128):
            to = pl.ds(pl.multiple_of((start >> 3) + 16 * c, 16), 16)
            part = block[:, 128 * c : 128 * c + 128].reshape(32, 16, 128)
            keep[:, to, :] = part[0:16]
            send[:, to, :] = part[16:32]

    widths(give)


def ffn_back_kernel(first_part, count, scal, w1, w2t, taps, sec, slope, branch, hg, dkx, hid_a, hid_b, cg_a, cg_b):
    start, steps = 256 * first_part, 4 * count
    j_first, j_last, i_first, i_last = edge_masks()
    lane = iota((16, 128), 1)

    def fill(hid, cg, step):
        rows = pl.ds(pl.multiple_of(start + jnp.minimum(step, steps - 1) * 64, 64), 64)
        cg[...] = dot(w2t[rows, :], branch[...]) * slope[rows, :].astype(F32)
        hid[...] = dot(w1[rows, :], sec[...])

    def group(hid, cg, step, index):
        rows = slice(16 * index, 16 * index + 16)
        from_rows = pl.ds(pl.multiple_of(start + 64 * step + 16 * index, 16), 16)
        to_rows = pl.ds(pl.multiple_of(64 * step + 16 * index, 16), 16)
        k = [taps[n, from_rows, :] for n in range(9)]
        quad = quads(cg, rows)
        bias = functools.reduce(lambda x, y: x + y, [t for row in quad for pair in row for t in pair])
        across = [
            (
                (times(left_of(quad[a][1]), j_first), quad[a][0], quad[a][1]),
                (quad[a][0], quad[a][1], times(right_of(quad[a][0]), j_last)),
            )
            for a in range(2)
        ]
        sums = [None] * 9
        for e in range(2):
            upper = [above(tiles, i_first) for tiles in across[1][e]]
            lower = [below(tiles, i_last) for tiles in across[0][e]]
            for a, near in ((0, (upper, across[0][e], across[1][e])), (1, (across[0][e], across[1][e], lower))):
                for half in range(2):
                    value = hid[rows, tile_at(a, e, half)]
                    total = None
                    for r in range(3):
                        for c in range(3):
                            tap = 3 * (2 - r) + (2 - c)
                            term = k[tap] * near[r][c][half]
                            total = term if total is None else total + term
                            term = value * near[r][c][half]
                            sums[tap] = term if sums[tap] is None else sums[tap] + term
                    hg[to_rows, tile_at(a, e, half)] = total.astype(BF16)
        table = jnp.where(lane == 9, lane_sum(bias), 0.0)
        for n in range(9):
            table = jnp.where(lane == n, lane_sum(sums[n]), table)
        dkx[to_rows, :] = table

    fill(hid_a, cg_a, 0)

    def two(index):
        fill(hid_b, cg_b, 2 * index + 1)
        for n in range(4):
            group(hid_a, cg_a, 2 * index, n)
        fill(hid_a, cg_a, 2 * index + 2)
        for n in range(4):
            group(hid_b, cg_b, 2 * index + 1, n)

    loop(steps // 2, two)


def middle_back_kernel(scal, bt, w1t, hg0, hg1, end_grad, mid, stats, mid_grad, low_grad, grads, work):
    side = scal[1]
    work[...] = sum(
        dot(w1t[:, 256 * at : 256 * (at + count)], hg[...]) for hg, (at, count) in zip((hg0, hg1), PARTS)
    )
    grads[...] = jnp.zeros_like(grads)
    gain = column(bt, G_2, 5)
    zeros = jnp.zeros((D, 128), F32)

    def body(tile, carry):
        at = lanes(tile)
        mask = token_mask(tile, side)
        grad = work[:, at] * mask
        hat = (mid[:, at] - stats[0:1, at]) * stats[1:2, at]
        result = end_grad[:, at] + norm_back(grad, hat, stats[1:2, at], gain)
        mid_grad[:, at] = result
        low = (result * mask).astype(BF16)
        low_grad[:, at] = low
        return carry[0] + grad * hat, carry[1] + grad, carry[2] + low.astype(F32)

    sums = lax.fori_loop(0, 8, body, (zeros, zeros, zeros))
    put_column(grads, G_2, lane_sum(sums[0]))
    put_column(grads, C_2, lane_sum(sums[1]))
    put_column(grads, B_O, lane_sum(sums[2]))


def pack_b_kernel(scal, hg0, hg1, dk0, dk1, sec, branch, act, keep, send, grads, dw1, gather, mixed):
    me = scal[0]
    grads[...] = jnp.zeros_like(grads)
    lane = iota((256, 128), 1)
    for hg, dkx, (at, count) in zip((hg0, hg1), (dk0, dk1), PARTS):

        def outer(n, hg=hg, dkx=dkx, at=at):
            rows = pl.ds(pl.multiple_of(256 * n, 256), 256)
            to = pl.ds(pl.multiple_of(256 * (n + at), 256), 256)
            part = dot_nt(hg[rows, :], sec[...])
            dw1[to, 0:256] = part[:, 0:256]
            turned = pltpu.roll(dkx[rows, :], 64, 1)
            dw1[to, 256:384] = jnp.where(lane < 64, part[:, 256:384], jnp.where(lane < 73, turned, 0.0))
            table = grads[...]
            for m in range(4):
                here = slice(64 * m, 64 * m + 64)
                number = 4 * (n + at) + m
                table = jnp.where(lane[here] == B_1 + number, part[here, 329:330], table)
                table = jnp.where(lane[here] == B_DW + number, dkx[rows, :][here, 9:10], table)
            grads[...] = table

        loop(count, outer)
    mixed[...] = dot(to_tens(me), branch[...]).astype(BF16)
    gather[:, 0:24, :] = jnp.zeros((32, 24, 128), F32)

    def contraction(p):
        block = dot_nt(mixed[...], act[pl.ds(pl.multiple_of(256 * p, 256), 256), :])
        parts = [block[0:256, 128 * e : 128 * e + 128].reshape(32, 1, 8, 128) for e in range(2)]
        full = jnp.concatenate(parts, axis=1).reshape(32, 16, 128).astype(BF16)
        to = pl.ds(pl.multiple_of(16 * p, 16), 16)
        keep[:, to, :] = full[0:16]
        send[:, to, :] = full[16:32]
        tail = jnp.concatenate([block[256:320, 0:128], block[256:320, 128:256]], axis=0).astype(BF16)
        place = rest_row(iota((256, 1), 0)) - 128 * (p & 1)
        to = pl.ds(pl.multiple_of(8 * (p >> 1), 8), 8)
        gather[:, to, :] += dot(one_hot(iota((256, 128), 1) == place), tail).reshape(32, 8, 128)

    loop(5, contraction)

    def expansion(owner):
        slot = slot_of(owner ^ me)
        rows = pl.ds(pl.multiple_of(40 * owner, 8), 40)
        for c in range(3):
            gather[slot, 24 + 40 * c : 64 + 40 * c, :] = dw1[rows, 128 * c : 128 * c + 128]

    loop(32, expansion)
    keep[:, 80:224, :] = gather[0:16].astype(BF16)
    send[:, 80:224, :] = gather[16:32].astype(BF16)


def attend_back_kernel(scal, kt, vt, qs, kv, wo, low_grad, lse, dq, dkv, og):
    bias = key_bias(scal[1])
    og[...] = dot_tn(wo[...], low_grad[...]).astype(BF16)

    def head(h):
        rows = pl.ds(pl.multiple_of(64 * h, 64), 64)
        more = pl.ds(pl.multiple_of(D + 64 * h, 64), 64)
        dk = jnp.zeros((64, 256), F32)
        dv = jnp.zeros((64, 256), F32)
        for quad in range(4):
            at = slice(256 * quad, 256 * quad + 256)
            probs = jnp.exp(dot(kt[h], qs[rows, at]) + bias - lse[h, :, at])
            grad = dot(vt[h], og[rows, at])
            mean = jnp.sum(probs * grad, axis=0, keepdims=True)
            score = (probs * (grad - mean)).astype(BF16)
            dq[rows, at] = (dot(kv[rows, :], score) * 0.125).astype(BF16)
            dk += dot_nt(qs[rows, at], score)
            dv += dot_nt(og[rows, at], probs.astype(BF16))
        dkv[rows, :] = dk.astype(BF16)
        dkv[more, :] = dv.astype(BF16)

    loop(HEADS, head)


def first_kernel(scal, bt, wq, wkv, wrs, first, red, raw, stat_r, dq, dkv, low_grad, att, entry, stats, g_one, g_two, g_three, keep, send, work, grads, wide, redin, stack_r, stack_z, tails_of):
    me = scal[0]
    grads[...] = g_one[...] + g_two[...] + g_three[...]
    for quad in range(4):
        redin[D * quad : D * quad + D, :] = first[:, 256 * quad : 256 * quad + 256]
    dred = dot_tn(wkv[...], dkv[...])
    gain = column(bt, G_R, 5)
    lows = []
    for tile in range(2):
        at = slice(128 * tile, 128 * tile + 128)
        grad = dred[:, at]
        hat = (raw[:, at] - stat_r[0:1, at]) * stat_r[1:2, at]
        low = norm_back(grad, hat, stat_r[1:2, at], gain).astype(BF16)
        lows.append(low)
        parts = (grad * hat, grad, low.astype(F32))
        sums = parts if tile == 0 else [s + v for s, v in zip(sums, parts)]
    put_column(grads, G_R, lane_sum(sums[0]))
    put_column(grads, C_R, lane_sum(sums[1]))
    put_column(grads, B_R, lane_sum(sums[2]))
    low = jnp.concatenate(lows, axis=1)
    order = to_tens(me)
    low = dot(order, low).astype(BF16)
    wide[...] = dot_tn(wrs[...], low)
    straight = dot_tn(wq[...], dq[...])
    for quad in range(4):
        at = slice(256 * quad, 256 * quad + 256)
        work[:, at] = straight[:, at] + wide[D * quad : D * quad + D, :]
    zeros = jnp.zeros((D, 128), F32)

    def body(tile, carry):
        at = lanes(tile)
        grad = work[:, at]
        hat = (entry[:, at].astype(F32) - stats[0:1, at]) * stats[1:2, at]
        return carry[0] + grad * hat, carry[1] + grad, carry[2] + dq[:, at].astype(F32)

    sums = lax.fori_loop(0, 8, body, (zeros, zeros, zeros))
    put_column(grads, G_1, lane_sum(sums[0]))
    put_column(grads, C_1, lane_sum(sums[1]))
    put_column(grads, B_Q, lane_sum(sums[2]))
    stack_r[...] = dot_nt(low, redin[...])

    def outer(pick, grad, value):
        return dot_nt(dot(pick, grad[...]).astype(BF16), value[...])

    row = iota((1, 2 * D), 1)
    place = iota((D, 2 * D), 0)
    parts = (
        outer(order, dq, first),
        outer(one_hot(place == keyval_tens(row, me, False)), dkv, red),
        outer(one_hot(place == keyval_tens(row, me, True)), dkv, red),
        outer(order, low_grad, att),
    )
    for part, at in zip(parts, (0, 256, 512, 1024)):
        stack_z[:, at : at + 256] = part[:, 0:256]
    stack_z[:, 768:1024] = jnp.concatenate([part[:, 256:320] for part in parts], axis=1)
    spread = one_hot(iota((256, 256), 1) == rest_row(iota((256, 1), 0)))

    def pack(p):
        at = lanes(p, 256)
        both = stack_r[:, at], stack_z[:, at]
        for e in range(2):
            pieces = [block[0:256, 128 * e : 128 * e + 128].reshape(32, 1, 8, 128) for block in both]
            full = jnp.concatenate(pieces, axis=1).reshape(32, 16, 128).astype(BF16)
            to = pl.ds(pl.multiple_of(32 * p + 16 * e, 16), 16)
            keep[:, to, :] = full[0:16]
            send[:, to, :] = full[16:32]
        tail = jnp.concatenate(
            [block[256:320, 128 * e : 128 * e + 128] for block in both for e in range(2)], axis=0
        ).astype(BF16)
        to = pl.ds(pl.multiple_of(8 * p, 8), 8)
        tails_of[:, to, :] = dot(spread, tail).reshape(32, 8, 128)

    loop(5, pack)
    rows = jnp.transpose(jnp.concatenate([grads[...], jnp.zeros((64, 128), F32)], axis=0)).astype(BF16)
    place = iota((256, 128), 0)
    vector = iota((256, 128), 1)
    line = place & 7
    owner = xor_of(place >> 3) ^ me
    start = (7 * owner) >> 3
    straight = (
        ((line == 0) & (vector == 3 * owner))
        | ((line == 1) & (vector == 3 * owner + 2))
        | ((line == 2) & (vector == 96 + start))
    )
    turned = ((line == 0) & (vector == 3 * owner + 1)) | ((line == 2) & (vector == 97 + start))
    small = dot(one_hot(straight), rows) + pltpu.roll(dot(one_hot(turned), rows), 64, 1)
    tails_of[:, 40:48, :] = small.reshape(32, 8, 128)
    keep[:, 160:208, :] = tails_of[0:16].astype(BF16)
    send[:, 160:208, :] = tails_of[16:32].astype(BF16)


def token_kernel(scal, bt, grad_in, mid_grad, entry, stats, tok, high, rest):
    side = scal[1]
    gain = column(bt, G_1, 5)

    def body(tile):
        at = lanes(tile)
        hat = (entry[:, at].astype(F32) - stats[0:1, at]) * stats[1:2, at]
        result = mid_grad[:, at] + norm_back(grad_in[:, at], hat, stats[1:2, at], gain)
        result = result * token_mask(tile, side)
        upper = result.astype(BF16)
        high[:, at] = upper
        rest[:, at] = (result - upper.astype(F32)).astype(BF16)

    loop(8, body)
    row, col = token_place(iota((TOKENS, 1), 0))
    natural = row * SIDE + col

    def quad(index):
        at = lanes(index, 256)
        pick = one_hot(iota((TOKENS, 256), 1) + 256 * index == natural)
        tok[:, at] = dot(high[...], pick) + dot(rest[...], pick)

    loop(4, quad)


def cost(micros):
    return pl.CostEstimate(flops=int(micros * 1e9), bytes_accessed=1000, transcendentals=0)


def call(kernel, args, outs, scratch=(), micros=5):
    return pl.pallas_call(
        kernel,
        in_specs=[pl.BlockSpec(memory_space=pltpu.SMEM if arg.dtype == I32 else pltpu.VMEM) for arg in args],
        out_shape=[jax.ShapeDtypeStruct(shape, dtype) for shape, dtype in outs],
        scratch_shapes=[pltpu.VMEM(shape, dtype) for shape, dtype in scratch],
        compiler_params=pltpu.CompilerParams(vmem_limit_bytes=VMEM_LIMIT),
        cost_estimate=cost(micros),
    )(*args)


def local(group, axes, *arrays):
    return step_of(group, axes, *arrays)


def step_of(group, axes, tokens, image_side, cotangent, *shards):
    index = lax.axis_index(axes[0]) * lax.axis_size(axes[1]) + lax.axis_index(axes[1])
    me = index // group
    devices = SUPER * group

    def flip(values, mask):
        pairs = [(i, ((i // group) ^ mask) * group + i % group) for i in range(devices)]
        return lax.ppermute(values, axes, pairs)

    def gather(block, split=0):
        held = block[None]
        for mask in FLIPS[:2]:
            held = jnp.concatenate([held, flip(held, mask)], axis=0)
        if split:
            one, two = held[:, :split], held[:, split:]
            one, two = (jnp.concatenate([one, flip(one, 8)], axis=0), jnp.concatenate([two, flip(two, 16)], axis=0))
            far, near = flip(one, 16), flip(two, 8)
            two = jnp.concatenate([two[:4], near[:4], two[4:], near[4:]], axis=0)
            held = jnp.concatenate([jnp.concatenate([one, far], axis=0), two], axis=1)
        else:
            for mask in FLIPS[2:]:
                held = jnp.concatenate([held, flip(held, mask)], axis=0)
        return held, flip(held, 1)

    def scatter(keep, send, split=0):
        def step(held, mask):
            return flip(held, mask).astype(F32)

        def halve(held, mask):
            half = held.shape[0] // 2
            return held[:half].astype(F32) + step(held[half:], mask)

        held = (keep.astype(F32) + step(send, 1)).astype(BF16)
        if split:
            one, two = held[:, :split], held[:, split:].reshape(2, 2, 4, -1, 128)
            one, two = (
                halve(one, 16).astype(BF16),
                (two[:, 0].astype(F32) + step(two[:, 1], 8)).astype(BF16).reshape(8, -1, 128),
            )
            held = jnp.concatenate([halve(one, 8), halve(two, 16)], axis=1).astype(BF16)
        else:
            held = halve(held, 16).astype(BF16)
            held = halve(held, 8).astype(BF16)
        held = halve(held, 4).astype(BF16)
        return halve(held, 2)[0]

    if group > 1:
        per = lax.axis_size(axes[1])
        start = (index % per) // group * group

        def join(shard):
            full = lax.all_gather(shard, axes[1], axis=0)
            return lax.dynamic_slice_in_dim(full, start, group, axis=0).reshape(-1)

        shards = [join(shard) for shard in shards]
    query, keyval, reduce_w, output, expand, depth, contract, merge, gains, biases = shards

    def rows(flat):
        return flat.reshape(-1, 128)

    scal = jnp.stack([me.astype(I32), image_side[0].astype(I32)])
    taps = jnp.pad(depth.reshape(40, 9), ((0, 0), (64, 55)))
    block_a = select(
        [rows(query), rows(output), rows(keyval), rows(reduce_w)],
        table_a, A_ROWS, (scal, biases[None], gains[None]),
    )
    block_b = select([rows(contract), rows(expand), taps], table_b, B_ROWS)
    block_c = select([rows(merge)], table_c, C_ROWS)
    a_low, a_high = gather(block_a, A_SPLIT)
    b_low, b_high = gather(block_b)
    c_low, c_high = gather(block_c, C_ROWS // 2)

    big, narrow = (D, TOKENS), (D, QUARTER)
    entry, stats_1 = call(entry_kernel, (scal, tokens[0]), [(big, BF16), ((8, TOKENS), F32)], micros=3.5)
    wq, wkv, wr, wo, first, qs, raw, stat_r, red, kv, kt, vt, bt = call(
        project_kernel,
        (scal, a_low, a_high, entry, stats_1),
        [
            ((D, D), BF16), ((2 * D, D), BF16), ((D, 4 * D), BF16), ((D, D), BF16), (big, BF16), (big, BF16),
            (narrow, F32), ((8, QUARTER), F32), (narrow, BF16), ((2 * D, QUARTER), BF16),
            ((HEADS, QUARTER, 64), BF16), ((HEADS, QUARTER, 64), BF16), ((64, 128), F32),
        ],
        [((D, 1280), BF16), ((256, 640), BF16), ((4 * D, QUARTER), BF16)],
        micros=8,
    )
    att, lse = call(attend_kernel, (scal, kt, qs, kv), [(big, BF16), ((HEADS, 1, TOKENS), F32)],
        [((2, QUARTER, TOKENS), F32), ((QUARTER, TOKENS), BF16)], micros=8.5)
    mid, sec, stats_2 = call(
        middle_kernel, (scal, bt, wo, att, entry), [(big, F32), ((384, TOKENS), BF16), ((8, TOKENS), F32)], [(big, F32)],
        micros=5,
    )
    w1, w1t, w2, w2t, taps = call(
        ffn_weights_kernel,
        (scal, bt, b_low, b_high),
        [((FF, 384), BF16), ((D, FF), BF16), ((D, FF), BF16), ((FF, D), BF16), ((10, FF, 128), F32)],
        [((D, FF), BF16), ((256, 384), BF16), ((FF, 384), F32)],
        micros=8,
    )
    act, slope = call(
        ffn_kernel,
        (scal, w1, taps, sec),
        [((FF, TOKENS), BF16), ((FF, TOKENS), BF16)],
        [((64, TOKENS), F32), ((64, TOKENS), F32)],
        micros=17,
    )
    end, sect, stats_s = call(
        ending_kernel, (scal, bt, w2, act, mid), [(big, F32), (big, BF16), ((8, TOKENS), F32)], [(big, F32)], micros=5
    )
    four, c_keep, c_send, end_grad, branch, g_one = call(
        merge_kernel,
        (scal, bt, c_low, c_high, sect, end, stats_s, cotangent[0]),
        [
            ((OUT_D, QUARTER), BF16), ((16, C_ROWS, 128), BF16), ((16, C_ROWS, 128), BF16), (big, F32), (big, BF16),
            ((64, 128), F32),
        ],
        [
            ((OUT_D, MERGE_PAD), BF16), ((MERGE_PAD, QUARTER), BF16), ((OUT_D, QUARTER), BF16),
            ((MERGE_PAD, QUARTER), F32), ((OUT_D, QUARTER), F32), ((OUT_D, QUARTER), F32),
        ],
        micros=20,
    )
    sum_c = scatter(c_keep, c_send, C_ROWS // 2)
    hgs, dks = [], []
    for at, count in PARTS:
        hg, dk = call(
            functools.partial(ffn_back_kernel, at, count),
            (scal, w1, w2t, taps, sec, slope, branch),
            [((256 * count, TOKENS), BF16), ((256 * count, 128), F32)],
            [((64, TOKENS), F32)] * 4,
            micros=6 * count,
        )
        hgs.append(hg)
        dks.append(dk)
    b_keep, b_send, g_three = call(
        pack_b_kernel,
        (scal, *hgs, *dks, sec, branch, act),
        [((16, B_ROWS, 128), BF16), ((16, B_ROWS, 128), BF16), ((64, 128), F32)],
        [((FF, 384), F32), ((32, 144, 128), F32), (big, BF16)],
        micros=9,
    )
    sum_b = scatter(b_keep, b_send)
    mid_grad, low_grad, g_two = call(
        middle_back_kernel,
        (scal, bt, w1t, *hgs, end_grad, mid, stats_2),
        [(big, F32), (big, BF16), ((64, 128), F32)],
        [(big, F32)],
        micros=6,
    )
    dq, dkv = call(
        attend_back_kernel,
        (scal, kt, vt, qs, kv, wo, low_grad, lse),
        [(big, BF16), ((2 * D, QUARTER), BF16)],
        [(big, BF16)],
        micros=9,
    )
    a_keep, a_send, first_grad = call(
        first_kernel,
        (
            scal, bt, wq, wkv, wr, first, red, raw, stat_r, dq, dkv, low_grad, att, entry, stats_1, g_one, g_two, g_three,
        ),
        [((16, A_ROWS, 128), BF16), ((16, A_ROWS, 128), BF16), (big, F32)],
        [
            ((64, 128), F32), ((4 * D, QUARTER), F32), ((4 * D, QUARTER), BF16), ((D, 1280), F32), ((D, 1280), F32),
            ((32, 48, 128), F32),
        ],
        micros=11,
    )
    sum_a = scatter(a_keep, a_send, A_SPLIT)
    (token_grad,) = call(
        token_kernel,
        (scal, bt, first_grad, mid_grad, entry, stats_1),
        [(big, F32)],
        [(big, BF16), (big, BF16)],
        micros=5,
    )
    if group > 1:

        def total(part):
            full = lax.all_gather(part, axes[1], axis=0)
            return jnp.sum(lax.dynamic_slice_in_dim(full, start, group, axis=0), axis=0)

        sum_a, sum_b, sum_c = total(sum_a), total(sum_b), total(sum_c)

    def flat(count):
        return (count, 128), F32

    query_g, output_g, keyval_g, reduce_g, biases_g, gains_g = call(
        out_a_kernel,
        (scal, sum_a),
        [flat(25), flat(25), flat(50), flat(100), ((1, 192), F32), ((1, 56), F32)],
        micros=1,
    )
    contract_g, expand_g = call(out_b_kernel, (scal, sum_b), [flat(100), flat(100)], micros=1)
    (merge_g,) = call(out_c_kernel, (scal, sum_c), [flat(360)], micros=1)
    depth_g = sum_b[184:224, 64:73]
    grads = [query_g, keyval_g, reduce_g, output_g, expand_g, depth_g, contract_g, merge_g, gains_g, biases_g]
    grads = [grad.reshape(-1) for grad in grads]
    if group > 1:
        mine = index % group
        grads = [lax.dynamic_index_in_dim(grad.reshape(group, -1), mine, keepdims=False) for grad in grads]
    return (four[None], token_grad[None], *grads)


def solution(mesh):
    axes = ("dp", "fs")
    devices = mesh.shape["dp"] * mesh.shape["fs"]
    group = devices // SUPER
    if devices != SUPER * group or mesh.shape["fs"] % group:
        raise ValueError("unsupported mesh")
    one, three = P(axes), P(axes, None, None)
    return jax.shard_map(
        functools.partial(local, group, axes),
        mesh=mesh,
        in_specs=(three, one, three) + (one,) * 10,
        out_specs=(three, three) + (one,) * 10,
        check_vma=False,
    )
```

```python
import functools

import jax
import jax.numpy as jnp
import numpy as np
from jax import lax
from jax.experimental import pallas as pl
from jax.experimental.pallas import tpu as pltpu
from jax.sharding import PartitionSpec as P


D = 320
HEADS = 5
FF = 1280
OUT_D = 512
SIDE = 32
QUARTER = 256
TOKENS = SIDE * SIDE
MERGE_PAD = 2944
SUPER = 32
FLIPS = (2, 4, 8, 16)
EPS = 1e-06
F32, BF16, I32 = jnp.float32, jnp.bfloat16, jnp.int32

B_Q, B_R, C_R, B_O, C_1, C_2, B_1, B_DW, B_2, C_S, B_M, C_M = 0, 5, 10, 15, 20, 25, 30, 50, 70, 75, 80, 88
G_R, G_1, G_2, G_S, G_M = 96, 101, 106, 111, 116

PARTS = ((0, 1), (1, 4))
A_ROWS, B_ROWS, C_ROWS = 208, 224, 368
SMALL_ROW = 200
A_SPLIT = 104
VMEM_LIMIT = 24 * 1024 * 1024
VMEM_ALL = 60 * 1024 * 1024


def slot_of(xor):
    return (xor >> 1) | ((xor & 1) << 4)


def xor_of(slot):
    return ((slot & 15) << 1) | (slot >> 4)


def dot(a, b):
    return jnp.dot(a, b, preferred_element_type=F32)


def dot_nt(a, b):
    return lax.dot_general(a, b, (((1,), (1,)), ((), ())), preferred_element_type=F32)


def dot_tn(a, b):
    return lax.dot_general(a, b, (((0,), (0,)), ((), ())), preferred_element_type=F32)


def iota(shape, axis):
    return lax.broadcasted_iota(I32, shape, axis)


def one_hot(test):
    return jnp.where(test, 1.0, 0.0).astype(BF16)


def lanes(index, width=128):
    return pl.ds(pl.multiple_of(index * width, width), width)


def loop(count, body):
    def step(index, carry):
        body(index)
        return carry

    lax.fori_loop(0, count, step, 0)


def column(table, start, count):
    return jnp.concatenate(
        [jnp.broadcast_to(table[:, h : h + 1], (64, 128)) for h in range(start, start + count)], axis=0
    )


def put_column(table, start, values):
    for h in range(values.shape[0] // 64):
        table[:, start + h : start + h + 1] = values[64 * h : 64 * h + 64, 0:1]


def token_place(lane):
    quad = lane >> 8
    row = 2 * ((lane >> 4) & 15) + (quad >> 1)
    col = 2 * (lane & 15) + (quad & 1)
    return row, col


def token_mask(tile, side, width=128):
    row, col = token_place(iota((1, width), 1) + tile * width)
    return jnp.where((row < side) & (col < side), 1.0, 0.0)


def key_place(index):
    return index >> 4, index & 15


def select_kernel(count, bases, small, small_at, *refs):
    sources, refs = refs[:count], refs[count:]
    if small:
        scal, biases, gains = refs[:3]
        refs = refs[3:]
    low_ref, high_ref, out, rows_ref, sems = refs[:5]
    held = refs[5:]
    copies = [
        pltpu.make_async_copy(source, place, sems.at[n]) for n, (source, place) in enumerate(zip(sources, held))
    ]
    for copy in copies:
        copy.start()
    half = rows_ref.shape[0] // 2
    rows_ref[...] = jnp.zeros_like(rows_ref)
    place = iota((out.shape[0], 2 * half), 1)
    pick_low = one_hot(place == low_ref[...])
    pick_high = one_hot(place == high_ref[...])
    for copy in copies:
        copy.wait()
    for source, base in zip(held, bases):
        rows_ref[base : base + source.shape[0], :] = source[...].astype(F32)
    if small:
        rows_ref[small_at : small_at + 1, :] = biases[:, 0:128].astype(F32)
        rows_ref[small_at + 1 : small_at + 2, 0:64] = biases[:, 128:192].astype(F32)
        wide = jnp.concatenate([gains[...].astype(F32), jnp.zeros((1, 72), F32)], axis=1)
        wide = jnp.broadcast_to(wide, (8, 128))
        rows_ref[small_at + 2 : small_at + 3, :] = pltpu.roll(wide, (56 * scal[0]) & 63, 1)[0:1, :]
    rows_ref[half:, :] = pltpu.roll(rows_ref[0:half, :], 64, 1)
    total = rows_ref[...].astype(BF16)
    low, upper = dot(pick_low, total), dot(pick_high, total)
    out[...] = jnp.where(iota((out.shape[0], 128), 1) < 64, low, upper).astype(BF16)


def select(sources, table, rows, vectors=()):
    bases, at = [], 0
    for source in sources:
        bases.append(at)
        at += -(-source.shape[0] // 16) * 16
    small = len(vectors) > 0
    half = at + (16 if small else 0)
    low, high = table(bases + [at], half).astype(np.int32)[:, :, None]
    specs = [pl.BlockSpec(memory_space=pltpu.HBM)] * len(sources)
    if small:
        specs += [pl.BlockSpec(memory_space=pltpu.SMEM)] + [pl.BlockSpec(memory_space=pltpu.VMEM)] * 2
    specs += [pl.BlockSpec(memory_space=pltpu.VMEM)] * 2
    return pl.pallas_call(
        functools.partial(select_kernel, len(sources), tuple(bases), small, at),
        in_specs=specs,
        out_shape=jax.ShapeDtypeStruct((rows, 128), BF16),
        scratch_shapes=[pltpu.VMEM((2 * half, 128), F32), pltpu.SemaphoreType.DMA((len(sources),))]
        + [pltpu.VMEM(source.shape, source.dtype) for source in sources],
        compiler_params=pltpu.CompilerParams(vmem_limit_bytes=VMEM_ALL if small else VMEM_LIMIT),
        cost_estimate=cost(2),
    )(*sources, *vectors, low, high)


def pair(half, low_src, high_src):
    low = -1 if low_src is None else low_src[0] + low_src[1] // 2 + half * (low_src[1] % 2)
    high = -1 if high_src is None else high_src[0] + high_src[1] // 2 + half * (1 - high_src[1] % 2)
    return low, high


def chunk_sources(bases, row, c):
    q, o, kv = bases
    if c < 6 or c >= 8:
        base, first = ((q, 0), (kv, 0), (kv, 10), None, (o, 0))[c // 2]
        at = 5 * (first + row) + 2 * (c % 2)
        return (base, at), (base, at + 1)
    if c == 6:
        return (q, 5 * row + 4), (kv, 5 * row + 4)
    return (kv, 5 * (10 + row) + 4), (o, 5 * row + 4)


def a_place(kind, row, c):
    if row < 8:
        return 16 * c + 8 * kind + row
    return 160 + 8 * (c // 2) + 4 * kind + 2 * (c % 2) + row - 8


def b_place(row, c):
    if row < 8:
        return 8 * c + row
    return 80 + 8 * (c // 4) + 2 * (c % 4) + row - 8


def table_a(bases, half):
    q, o, kv, r, small = bases
    rows = [(-1, -1)] * A_ROWS
    for c in range(10):
        for row in range(10):
            at = 20 * row + 2 * c
            rows[a_place(0, row, c)] = pair(half, (r, at), (r, at + 1))
            rows[a_place(1, row, c)] = pair(half, *chunk_sources((q, o, kv), row, c))
    for row in range(3):
        rows[SMALL_ROW + row] = pair(half, (small, 2 * row), (small, 2 * row + 1))
    return np.array(rows).T


def table_b(bases, half):
    w2, w1, dw, _ = bases
    rows = [(-1, -1)] * B_ROWS
    for c in range(10):
        for row in range(10):
            at = 20 * row + 2 * c
            rows[b_place(row, c)] = pair(half, (w2, at), (w2, at + 1))
    for c in range(3):
        for row in range(40):
            at = 5 * row + 2 * c
            rows[104 + 40 * c + row] = pair(half, (w1, at), (w1, at + 1) if c < 2 else (dw, 2 * row + 1))
    return np.array(rows).T


def table_c(bases, half):
    m, _ = bases
    rows = []
    for c in range(23):
        for row in range(16):
            at = 45 * row + 2 * c
            rows.append(pair(half, (m, at), (m, at + 1) if c < 22 else None))
    return np.array(rows).T


def turn(rows):
    return pltpu.roll(rows, 64, 1)


def halves(low, high):
    return jnp.where(iota((1, 128), 1) < 64, low, high)


def put_rows(out, first, count, stride, rows):
    out[pl.ds(first, count, stride=stride), :] = rows


def put_320(out, first, count, load):
    even, odd = ([load(chunk, parity) for chunk in range(3)] for parity in range(2))
    turned = [turn(rows) for rows in odd]
    for at, rows in enumerate(
        (even[0], even[1], halves(even[2], turned[0]), halves(turned[0], turned[1]), halves(turned[1], turned[2]))
    ):
        put_rows(out, first + at, count // 2, 5, rows)


def every_other(ref, start, count):
    return ref[pl.ds(start, count, stride=2), :]


def out_a_kernel(scal, sums, q, o, kv, r, biases, gains):
    squares = (
        (q, 0, (0, 1, 6), False),
        (o, 0, (8, 9, 7), True),
        (kv, 0, (2, 3, 6), True),
        (kv, 25, (4, 5, 7), False),
    )
    for out, first, chunks, high in squares:
        for start, count, lane_row in ((0, 8, 0), (8, 2, 20)):

            def load(chunk, parity, chunks=chunks, high=high, start=start, count=count):
                rows = every_other(sums, a_place(1, start, chunks[chunk]) + parity, count // 2)
                return turn(rows) if chunk == 2 and high else rows

            put_320(out, first + lane_row, count, load)
    for c in range(10):
        for start, count in ((0, 8), (8, 2)):
            put_rows(r, 10 * start + c, count, 10, sums[pl.ds(a_place(0, start, c), count), :])
    small = sums[SMALL_ROW : SMALL_ROW + 8, :]
    biases[:, 0:128] = small[0:1]
    biases[:, 128:192] = small[1:2, 0:64]
    gains[...] = pltpu.roll(small, (128 - ((56 * scal[0]) & 63)) & 127, 1)[2:3, 0:56]


def out_b_kernel(scal, sums, w2, w1):
    for c in range(10):
        for start, count in ((0, 8), (8, 2)):
            put_rows(w2, 10 * start + c, count, 10, sums[pl.ds(b_place(start, c), count), :])
    put_320(w1, 0, 40, lambda chunk, parity: every_other(sums, 104 + 40 * chunk + parity, 20))


def out_c_kernel(scal, sums, m):
    even = [every_other(sums, 16 * c, 8) for c in range(23)]
    turned = [turn(every_other(sums, 16 * c + 1, 8)) for c in range(23)]
    for c in range(22):
        put_rows(m, c, 8, 45, even[c])
        put_rows(m, 23 + c, 8, 45, halves(turned[c], turned[c + 1]))
    put_rows(m, 22, 8, 45, halves(even[22], turned[0]))


def split_ten(row, per, magic):
    owner = (row * magic) >> 16
    return owner, row - per * owner


def tens(row, me):
    owner, rest = split_ten(row, 10, 6554)
    slot = slot_of(owner ^ me)
    return jnp.where(rest < 8, slot * 8 + rest, 248 + slot * 2 + rest)


def from_tens(me):
    return one_hot(iota((D, D), 1) == tens(iota((D, 1), 0), me))


def to_tens(me):
    return one_hot(iota((D, D), 0) == tens(iota((1, D), 1), me))


def keyval_tens(row, me, upper):
    owner, rest = split_ten(row, 20, 3277)
    inside = (rest >= 10) if upper else (rest < 10)
    return jnp.where(inside, tens(10 * owner + rest - (10 if upper else 0), me), -1)


def rest_row(row):
    return 64 * ((row & 7) >> 1) + 2 * (row >> 3) + (row & 1)


def norm(values, gain, shift):
    mean = jnp.mean(values, axis=0, keepdims=True)
    centred = values - mean
    rstd = lax.rsqrt(jnp.mean(centred * centred, axis=0, keepdims=True) + EPS)
    return centred * rstd * gain + shift, mean, rstd


def norm_back(grad, hat, rstd, gain):
    scaled = grad * gain
    return rstd * (
        scaled
        - jnp.mean(scaled, axis=0, keepdims=True)
        - hat * jnp.mean(scaled * hat, axis=0, keepdims=True)
    )


def stat_rows(mean, rstd):
    row = iota((8, mean.shape[1]), 0)
    return jnp.where(row == 0, mean, jnp.where(row == 1, rstd, 0.0))


def entry_kernel(scal, tokens, entry, stats):
    side = scal[1]
    for quad in range(4):
        lane = iota((1, 256), 1) + quad * 256
        row, col = token_place(lane)
        natural = row * SIDE + col
        pick = one_hot(iota((TOKENS, 256), 0) == natural)
        mask = jnp.where((row < side) & (col < side), 1.0, 0.0)
        entry[:, quad * 256 : quad * 256 + 256] = (dot(tokens[...], pick) * mask).astype(BF16)

    def body(tile):
        values = entry[:, lanes(tile)].astype(F32)
        mean = jnp.mean(values, axis=0, keepdims=True)
        centred = values - mean
        rstd = lax.rsqrt(jnp.mean(centred * centred, axis=0, keepdims=True) + EPS)
        stats[:, lanes(tile)] = stat_rows(mean, rstd)

    loop(8, body)


def small_table(me, low, high):
    gathered = jnp.concatenate(
        [half[:, SMALL_ROW : SMALL_ROW + 8, :].astype(F32).reshape(128, 128) for half in (low, high)], axis=0
    ).astype(BF16)
    vector = iota((128, 256), 0)
    place = iota((128, 256), 1)
    row = place & 7
    owner = xor_of(place >> 3) ^ me
    first = (7 * owner) >> 3
    straight = (
        ((row == 0) & (vector == 3 * owner))
        | ((row == 1) & (vector == 3 * owner + 2))
        | ((row == 2) & (vector == 96 + first))
    )
    turned = ((row == 0) & (vector == 3 * owner + 1)) | ((row == 2) & (vector == 97 + first))
    rows = dot(one_hot(straight), gathered) + pltpu.roll(dot(one_hot(turned), gathered), 64, 1)
    return jnp.transpose(rows)[0:64, :]


def project_kernel(scal, low, high, entry, stats, wq, wkv, wrs, wo, first, qs, raw, stat_r, red, kv, kt, vt, bt, square, rest, redin):
    me = scal[0]
    bt[...] = small_table(me, low, high)
    for half, source in enumerate((low, high)):

        def chunk(c, half=half, source=source):
            block = source[:, pl.ds(pl.multiple_of(16 * c, 16), 16), :].astype(F32)
            rows = slice(128 * half, 128 * half + 128)
            wrs[rows, lanes(c)] = block[:, 0:8].reshape(128, 128).astype(BF16)
            square[rows, lanes(c)] = block[:, 8:16].reshape(128, 128).astype(BF16)

        loop(10, chunk)
        block = source[:, 160:208, :].astype(F32)
        for c in range(5):
            part = block[:, 8 * c : 8 * c + 8].reshape(128, 128).astype(BF16)
            rest[128 * half : 128 * half + 128, 128 * c : 128 * c + 128] = part
    spread = one_hot(iota((256, 256), 0) == rest_row(iota((1, 256), 1)))

    def last_two(p):
        part = dot(spread, rest[:, lanes(p)]).astype(BF16)
        wrs[256:320, lanes(p, 256)] = jnp.concatenate([part[0:64], part[64:128]], axis=1)
        square[256:320, lanes(p, 256)] = jnp.concatenate([part[128:192], part[192:256]], axis=1)

    loop(5, last_two)
    order = from_tens(me)
    wq[:, 0:256] = dot(order, square[:, 0:256]).astype(BF16)
    wo[:, 0:256] = dot(order, square[:, 1024:1280]).astype(BF16)
    tails = dot(order, square[:, 768:1024])
    wq[:, 256:320] = tails[:, 0:64].astype(BF16)
    wo[:, 256:320] = pltpu.roll(tails, 64, 1)[:, 0:64].astype(BF16)
    row = iota((2 * D, 1), 0)
    place = iota((2 * D, D), 1)
    lower = one_hot(place == keyval_tens(row, me, False))
    upper = one_hot(place == keyval_tens(row, me, True))
    wkv[:, 0:256] = (dot(lower, square[:, 256:512]) + dot(upper, square[:, 512:768])).astype(BF16)
    tail = pltpu.roll(dot(lower, square[:, 768:896]), 64, 1) + dot(upper, square[:, 896:1024])
    wkv[:, 256:320] = tail[:, 0:64].astype(BF16)

    gain, shift = column(bt, G_1, 5), column(bt, C_1, 5)

    def body(tile):
        centred = entry[:, lanes(tile)].astype(F32) - stats[0:1, lanes(tile)]
        first[:, lanes(tile)] = (centred * stats[1:2, lanes(tile)] * gain + shift).astype(BF16)

    loop(8, body)
    for quad in range(4):
        redin[D * quad : D * quad + D, :] = first[:, 256 * quad : 256 * quad + 256]
    bias = column(bt, B_R, 5)
    bias = jnp.concatenate([bias, bias], axis=1)
    mixed = dot(wrs[...], redin[...])
    total = bias
    for part in range(3):
        piece = mixed.astype(BF16)
        total = total + dot(order, piece)
        mixed = mixed - piece.astype(F32)
    raw[...] = total
    gain, shift = column(bt, G_R, 5), column(bt, C_R, 5)
    for tile in range(2):
        at = slice(128 * tile, 128 * tile + 128)
        values, mean, rstd = norm(raw[:, at], gain, shift)
        red[:, at] = values.astype(BF16)
        stat_r[:, at] = stat_rows(mean, rstd)
    keyval = dot(wkv[...], red[...])
    kv[...] = keyval.astype(BF16)
    turned = jnp.transpose(keyval)
    for h in range(HEADS):
        kt[h] = turned[:, 64 * h : 64 * h + 64].astype(BF16)
        vt[h] = turned[:, D + 64 * h : D + 64 * h + 64].astype(BF16)
    bias = column(bt, B_Q, 5)
    bias = jnp.concatenate([bias, bias], axis=1)

    def query(quad):
        at = lanes(quad, 256)
        qs[:, at] = (dot(wq[...], first[:, at]) + bias).astype(BF16) * BF16(0.125)

    loop(4, query)


def key_bias(side):
    i, j = key_place(iota((QUARTER, 1), 0))
    return jnp.where((i < (side >> 1)) & (j < (side >> 1)), 0.0, -10000.0)


def attend_kernel(scal, kt, qs, kv, att, lse, scores, probs):
    bias = key_bias(scal[1])

    def score(h, slot):
        scores[slot] = dot(kt[h], qs[pl.ds(pl.multiple_of(64 * h, 64), 64), :])

    score(0, 0)

    def head(h):
        score(jnp.minimum(h + 1, HEADS - 1), 1 - (h & 1))
        rows = pl.ds(pl.multiple_of(64 * h, 64), 64)
        values = kv[pl.ds(pl.multiple_of(D + 64 * h, 64), 64), :]
        for tile in range(8):
            at = slice(128 * tile, 128 * tile + 128)
            part = scores[h & 1, :, at] + bias
            top = jnp.max(part, axis=0, keepdims=True)
            weights = jnp.exp(part - top)
            total = jnp.sum(weights, axis=0, keepdims=True)
            lse[h, :, at] = top + jnp.log(total)
            probs[:, at] = (weights * (1.0 / total)).astype(BF16)
        att[rows, :] = dot(values, probs[...]).astype(BF16)

    loop(HEADS, head)


def middle_kernel(scal, bt, wo, att, entry, mid, sec, stats, work):
    side = scal[1]
    work[...] = dot(wo[...], att[...])
    bias, gain, shift = column(bt, B_O, 5), column(bt, G_2, 5), column(bt, C_2, 5)

    def body(tile):
        at = lanes(tile)
        mask = token_mask(tile, side)
        values = entry[:, at].astype(F32) + mask * (work[:, at] + bias)
        mid[:, at] = values
        normed, mean, rstd = norm(values, gain, shift)
        stats[:, at] = stat_rows(mean, rstd)
        sec[0:D, at] = (normed.astype(BF16).astype(F32) * mask).astype(BF16)
        sec[D : D + 64, at] = jnp.where(iota((64, 128), 0) == 9, mask, 0.0).astype(BF16)

    loop(8, body)


def ffn_weights_kernel(scal, bt, low, high, w1, w1t, w2, w2t, taps, main, rest, wide):
    me = scal[0]
    for half, source in enumerate((low, high)):
        def chunks(p, half=half, source=source):
            block = source[:, pl.ds(pl.multiple_of(16 * p, 16), 16), :].astype(F32)
            both = jnp.concatenate([block[:, 0:8].reshape(128, 128), block[:, 8:16].reshape(128, 128)], axis=1)
            main[128 * half : 128 * half + 128, lanes(p, 256)] = both.astype(BF16)

        loop(5, chunks)
        block = source[:, 80:112, :].astype(F32)
        for c in range(3):
            part = block[:, 8 * c : 8 * c + 8].reshape(128, 128).astype(BF16)
            rest[128 * half : 128 * half + 128, 128 * c : 128 * c + 128] = part

        def expansion(slot, half=half, source=source):
            owner = ((slot << 1) | half) ^ me
            block = source[slot, 80:224, :].astype(F32)
            rows = pl.ds(pl.multiple_of(40 * owner, 8), 40)
            for c in range(3):
                wide[rows, 128 * c : 128 * c + 128] = block[24 + 40 * c : 64 + 40 * c]

        loop(16, expansion)
    spread = one_hot(iota((256, 256), 0) == rest_row(iota((1, 256), 1)))
    for j in range(3):
        part = dot(spread, rest[:, 128 * j : 128 * j + 128]).astype(BF16)
        for k in range(4 if j < 2 else 2):
            c = 4 * j + k
            main[256:320, 128 * c : 128 * c + 128] = part[64 * k : 64 * k + 64]
    order = from_tens(me)

    def contraction(p):
        block = dot(order, main[:, lanes(p, 256)])
        w2[:, lanes(p, 256)] = block.astype(BF16)
        w2t[pl.ds(pl.multiple_of(256 * p, 256), 256), :] = jnp.transpose(block).astype(BF16)

    loop(5, contraction)
    bias = column(bt, B_1, 20)
    lane = iota((FF, 128), 1)
    tail = wide[:, 256:384]
    low_tail = tail.astype(BF16)

    def spread(tap):
        taps[tap] = dot(low_tail, one_hot(iota((128, 128), 0) == 64 + tap))

    loop(9, spread)
    taps[9] = column(bt, B_DW, 20)
    w1[:, 0:256] = wide[:, 0:256].astype(BF16)
    w1[:, 256:384] = jnp.where(lane < 64, tail, jnp.where(lane == 73, bias, 0.0)).astype(BF16)

    def turn(p):
        rows = pl.ds(pl.multiple_of(256 * p, 256), 256)
        w1t[:, lanes(p, 256)] = jnp.transpose(wide[rows, :])[0:D].astype(BF16)

    loop(5, turn)


def edge_masks():
    lane = iota((1, 128), 1)
    j = lane & 15
    return jnp.where(j != 0, 1.0, 0.0), jnp.where(j != 15, 1.0, 0.0), lane >= 16, lane < 112


def left_of(tiles):
    return [pltpu.roll(tile, 1, 1) for tile in tiles]


def right_of(tiles):
    return [pltpu.roll(tile, 127, 1) for tile in tiles]


def above(tiles, inside):
    turned = [pltpu.roll(tile, 16, 1) for tile in tiles]
    return [jnp.where(inside, turned[0], 0.0), jnp.where(inside, turned[1], turned[0])]


def below(tiles, inside):
    turned = [pltpu.roll(tile, 112, 1) for tile in tiles]
    return [jnp.where(inside, turned[0], turned[1]), jnp.where(inside, turned[1], 0.0)]


def times(tiles, factor):
    return [tile * factor for tile in tiles]


def plus(*many):
    return [functools.reduce(lambda a, b: a + b, tiles) for tiles in zip(*many)]


def tile_at(a, e, half):
    start = 256 * (2 * a + e) + 128 * half
    return slice(start, start + 128)


def quads(ref, rows):
    return [[[ref[rows, tile_at(a, e, half)] for half in range(2)] for e in range(2)] for a in range(2)]


LOG2E = float(np.log2(np.e))


def gelu_parts(x):
    y = x * np.float32(0.5**0.5)
    cdf = lax.erf(y) * 0.5 + 0.5
    bell = jnp.exp2(y * y * np.float32(-LOG2E) + np.float32(-0.5 * np.log2(2.0 * np.pi)))
    return x * cdf, cdf + x * bell


def ffn_kernel(scal, w1, taps, sec, act, slope, hid_a, hid_b):
    j_first, j_last, i_first, i_last = edge_masks()

    def fill(hid, step):
        rows = pl.ds(pl.multiple_of(jnp.minimum(step, FF // 64 - 1) * 64, 64), 64)
        hid[...] = dot(w1[rows, :], sec[...])

    def group(hid, step, index):
        rows = slice(16 * index, 16 * index + 16)
        out_rows = pl.ds(pl.multiple_of(64 * step + 16 * index, 16), 16)
        k = [taps[n, out_rows, :] for n in range(10)]
        first = [k[3 * r] * j_first for r in range(3)]
        last = [k[3 * r + 2] * j_last for r in range(3)]
        quad = quads(hid, rows)
        left = [left_of(quad[a][1]) for a in range(2)]
        right = [right_of(quad[a][0]) for a in range(2)]

        def across(a, e, r):
            if e == 0:
                parts = zip(left[a], quad[a][0], quad[a][1])
                return [first[r] * x + k[3 * r + 1] * y + k[3 * r + 2] * z for x, y, z in parts]
            parts = zip(quad[a][0], quad[a][1], right[a])
            return [k[3 * r] * x + k[3 * r + 1] * y + last[r] * z for x, y, z in parts]

        for e in range(2):
            up = above(across(1, e, 0), i_first)
            down = below(across(0, e, 2), i_last)
            outs = (plus(across(0, e, 1), across(1, e, 2), up), plus(across(0, e, 0), across(1, e, 1), down))
            for a in range(2):
                for half in range(2):
                    value, grad = gelu_parts(outs[a][half] + k[9])
                    act[out_rows, tile_at(a, e, half)] = value.astype(BF16)
                    slope[out_rows, tile_at(a, e, half)] = grad.astype(BF16)

    fill(hid_a, 0)

    def two(index):
        fill(hid_b, 2 * index + 1)
        for n in range(4):
            group(hid_a, 2 * index, n)
        fill(hid_a, 2 * index + 2)
        for n in range(4):
            group(hid_b, 2 * index + 1, n)

    loop(FF // 128, two)


def ending_kernel(scal, bt, w2, act, mid, end, sect, stats, work):
    side = scal[1]
    work[...] = dot(w2[...], act[...])
    bias, gain, shift = column(bt, B_2, 5), column(bt, G_S, 5), column(bt, C_S, 5)

    def body(tile):
        at = lanes(tile)
        mask = token_mask(tile, side)
        values = mid[:, at] + mask * (work[:, at] + bias)
        end[:, at] = values
        normed, mean, rstd = norm(values, gain, shift)
        stats[:, at] = stat_rows(mean, rstd)
        sect[:, at] = (normed.astype(BF16).astype(F32) * mask).astype(BF16)

    loop(8, body)


def lane_sum(values):
    return jnp.sum(values, axis=1, keepdims=True)


def merge_kernel(scal, bt, c_low, c_high, sect, end, stats, cot, four, keep, send, end_grad, branch, grads, wm, patch, mg, back, work, natural):
    me, side = scal[0], scal[1]
    grads[...] = jnp.zeros_like(grads)
    for half, source in enumerate((c_low, c_high)):

        def place(c, half=half, source=source):
            block = source[:, pl.ds(pl.multiple_of(16 * c, 16), 16), :].reshape(256, 128)
            wm[256 * half : 256 * half + 256, lanes(c)] = block

        loop(23, place)

    def reorder(to_owner):
        def one(slot):
            at = pl.ds(pl.multiple_of(16 * slot, 16), 16)
            owner = pl.ds(pl.multiple_of((xor_of(slot) ^ me) * 16, 16), 16)
            to_owner(at, owner)

        loop(32, one)

    j_first, j_last, i_first, i_last = edge_masks()
    quad = [[[t.astype(F32) for t in pair] for pair in row] for row in quads(sect, slice(None))]
    left = [times(left_of(quad[a][1]), j_first) for a in range(2)]
    pieces = (
        above(left[1], i_first),
        above(quad[1][0], i_first),
        above(quad[1][1], i_first),
        left[0],
        quad[0][0],
        quad[0][1],
        left[1],
        quad[1][0],
        quad[1][1],
    )
    for n, piece in enumerate(pieces):
        for half in range(2):
            patch[D * n : D * n + D, 128 * half : 128 * half + 128] = piece[half].astype(BF16)
    patch[9 * D :, :] = jnp.zeros((MERGE_PAD - 9 * D, 256), BF16)
    bias, gain, shift = column(bt, B_M, 8), column(bt, G_M, 8), column(bt, C_M, 8)
    work[...] = dot(wm[...], patch[...])

    def from_slots(at, owner):
        natural[owner, :] = work[at, :]

    reorder(from_slots)
    half_side = side >> 1
    for tile in range(2):
        at = slice(128 * tile, 128 * tile + 128)
        i, j = key_place(iota((1, 128), 1) + 128 * tile)
        mask = jnp.where((i < half_side) & (j < half_side), 1.0, 0.0)
        values = natural[:, at] + bias
        mean = jnp.mean(values, axis=0, keepdims=True)
        centred = values - mean
        rstd = lax.rsqrt(jnp.mean(centred * centred, axis=0, keepdims=True) + EPS)
        hat = centred * rstd
        four[:, at] = ((hat * gain + shift) * mask).astype(BF16)
        grad = cot[:, at].astype(F32) * mask
        low = norm_back(grad, hat, rstd, gain).astype(BF16)
        natural[:, at] = low.astype(F32)
        parts = (grad * hat, grad, low.astype(F32))
        sums = parts if tile == 0 else [s + v for s, v in zip(sums, parts)]
    put_column(grads, G_M, lane_sum(sums[0]))
    put_column(grads, C_M, lane_sum(sums[1]))
    put_column(grads, B_M, lane_sum(sums[2]))

    def to_slots(at, owner):
        mg[at, :] = natural[owner, :].astype(BF16)

    reorder(to_slots)

    def widths(body):
        loop(11, lambda c: body(pl.multiple_of(c * 256, 256), 256))
        body(11 * 256, 128)

    def patch_grad(start, width):
        back[pl.ds(start, width), :] = dot_tn(wm[:, pl.ds(start, width)], mg[...])

    widths(patch_grad)

    def piece(n):
        return [back[D * n : D * n + D, 128 * half : 128 * half + 128] for half in range(2)]

    results = (
        piece(4),
        plus(piece(5), times(right_of(piece(3)), j_last)),
        plus(piece(7), below(piece(1), i_last)),
        plus(
            piece(8),
            times(right_of(piece(6)), j_last),
            below(plus(piece(2), times(right_of(piece(0)), j_last)), i_last),
        ),
    )
    for n, values in enumerate(results):
        for half in range(2):
            end_grad[:, 256 * n + 128 * half : 256 * n + 128 * half + 128] = values[half]
    gain = column(bt, G_S, 5)
    zeros = jnp.zeros((D, 128), F32)

    def body(tile, carry):
        at = lanes(tile)
        mask = token_mask(tile, side)
        grad = end_grad[:, at] * mask
        hat = (end[:, at] - stats[0:1, at]) * stats[1:2, at]
        result = norm_back(grad, hat, stats[1:2, at], gain)
        end_grad[:, at] = result
        low = (result * mask).astype(BF16)
        branch[:, at] = low
        return carry[0] + grad * hat, carry[1] + grad, carry[2] + low.astype(F32)

    sums = lax.fori_loop(0, 8, body, (zeros, zeros, zeros))
    put_column(grads, G_S, lane_sum(sums[0]))
    put_column(grads, C_S, lane_sum(sums[1]))
    put_column(grads, B_2, lane_sum(sums[2]))

    def give(start, width):
        block = dot_nt(mg[...], patch[pl.ds(start, width), :]).astype(BF16)
        for c in range(width // 128):
            to = pl.ds(pl.multiple_of((start >> 3) + 16 * c, 16), 16)
            part = block[:, 128 * c : 128 * c + 128].reshape(32, 16, 128)
            keep[:, to, :] = part[0:16]
            send[:, to, :] = part[16:32]

    widths(give)


def ffn_back_kernel(first_part, count, scal, w1, w2t, taps, sec, slope, branch, hg, dkx, hid_a, hid_b, cg_a, cg_b):
    start, steps = 256 * first_part, 4 * count
    j_first, j_last, i_first, i_last = edge_masks()
    lane = iota((16, 128), 1)

    def fill(hid, cg, step):
        rows = pl.ds(pl.multiple_of(start + jnp.minimum(step, steps - 1) * 64, 64), 64)
        cg[...] = dot(w2t[rows, :], branch[...]) * slope[rows, :].astype(F32)
        hid[...] = dot(w1[rows, :], sec[...])

    def group(hid, cg, step, index):
        rows = slice(16 * index, 16 * index + 16)
        from_rows = pl.ds(pl.multiple_of(start + 64 * step + 16 * index, 16), 16)
        to_rows = pl.ds(pl.multiple_of(64 * step + 16 * index, 16), 16)
        k = [taps[n, from_rows, :] for n in range(9)]
        quad = quads(cg, rows)
        bias = functools.reduce(lambda x, y: x + y, [t for row in quad for pair in row for t in pair])
        across = [
            (
                (times(left_of(quad[a][1]), j_first), quad[a][0], quad[a][1]),
                (quad[a][0], quad[a][1], times(right_of(quad[a][0]), j_last)),
            )
            for a in range(2)
        ]
        sums = [None] * 9
        for e in range(2):
            upper = [above(tiles, i_first) for tiles in across[1][e]]
            lower = [below(tiles, i_last) for tiles in across[0][e]]
            for a, near in ((0, (upper, across[0][e], across[1][e])), (1, (across[0][e], across[1][e], lower))):
                for half in range(2):
                    value = hid[rows, tile_at(a, e, half)]
                    total = None
                    for r in range(3):
                        for c in range(3):
                            tap = 3 * (2 - r) + (2 - c)
                            term = k[tap] * near[r][c][half]
                            total = term if total is None else total + term
                            term = value * near[r][c][half]
                            sums[tap] = term if sums[tap] is None else sums[tap] + term
                    hg[to_rows, tile_at(a, e, half)] = total.astype(BF16)
        table = jnp.where(lane == 9, lane_sum(bias), 0.0)
        for n in range(9):
            table = jnp.where(lane == n, lane_sum(sums[n]), table)
        dkx[to_rows, :] = table

    fill(hid_a, cg_a, 0)

    def two(index):
        fill(hid_b, cg_b, 2 * index + 1)
        for n in range(4):
            group(hid_a, cg_a, 2 * index, n)
        fill(hid_a, cg_a, 2 * index + 2)
        for n in range(4):
            group(hid_b, cg_b, 2 * index + 1, n)

    loop(steps // 2, two)


def middle_back_kernel(scal, bt, w1t, hg0, hg1, end_grad, mid, stats, mid_grad, low_grad, grads, work):
    side = scal[1]
    work[...] = sum(
        dot(w1t[:, 256 * at : 256 * (at + count)], hg[...]) for hg, (at, count) in zip((hg0, hg1), PARTS)
    )
    grads[...] = jnp.zeros_like(grads)
    gain = column(bt, G_2, 5)
    zeros = jnp.zeros((D, 128), F32)

    def body(tile, carry):
        at = lanes(tile)
        mask = token_mask(tile, side)
        grad = work[:, at] * mask
        hat = (mid[:, at] - stats[0:1, at]) * stats[1:2, at]
        result = end_grad[:, at] + norm_back(grad, hat, stats[1:2, at], gain)
        mid_grad[:, at] = result
        low = (result * mask).astype(BF16)
        low_grad[:, at] = low
        return carry[0] + grad * hat, carry[1] + grad, carry[2] + low.astype(F32)

    sums = lax.fori_loop(0, 8, body, (zeros, zeros, zeros))
    put_column(grads, G_2, lane_sum(sums[0]))
    put_column(grads, C_2, lane_sum(sums[1]))
    put_column(grads, B_O, lane_sum(sums[2]))


def pack_b_kernel(scal, hg0, hg1, dk0, dk1, sec, branch, act, keep, send, grads, dw1, gather, mixed):
    me = scal[0]
    grads[...] = jnp.zeros_like(grads)
    lane = iota((256, 128), 1)
    for hg, dkx, (at, count) in zip((hg0, hg1), (dk0, dk1), PARTS):

        def outer(n, hg=hg, dkx=dkx, at=at):
            rows = pl.ds(pl.multiple_of(256 * n, 256), 256)
            to = pl.ds(pl.multiple_of(256 * (n + at), 256), 256)
            part = dot_nt(hg[rows, :], sec[...])
            dw1[to, 0:256] = part[:, 0:256]
            turned = pltpu.roll(dkx[rows, :], 64, 1)
            dw1[to, 256:384] = jnp.where(lane < 64, part[:, 256:384], jnp.where(lane < 73, turned, 0.0))
            table = grads[...]
            for m in range(4):
                here = slice(64 * m, 64 * m + 64)
                number = 4 * (n + at) + m
                table = jnp.where(lane[here] == B_1 + number, part[here, 329:330], table)
                table = jnp.where(lane[here] == B_DW + number, dkx[rows, :][here, 9:10], table)
            grads[...] = table

        loop(count, outer)
    mixed[...] = dot(to_tens(me), branch[...]).astype(BF16)
    gather[:, 0:24, :] = jnp.zeros((32, 24, 128), F32)

    def contraction(p):
        block = dot_nt(mixed[...], act[pl.ds(pl.multiple_of(256 * p, 256), 256), :])
        parts = [block[0:256, 128 * e : 128 * e + 128].reshape(32, 1, 8, 128) for e in range(2)]
        full = jnp.concatenate(parts, axis=1).reshape(32, 16, 128).astype(BF16)
        to = pl.ds(pl.multiple_of(16 * p, 16), 16)
        keep[:, to, :] = full[0:16]
        send[:, to, :] = full[16:32]
        tail = jnp.concatenate([block[256:320, 0:128], block[256:320, 128:256]], axis=0).astype(BF16)
        place = rest_row(iota((256, 1), 0)) - 128 * (p & 1)
        to = pl.ds(pl.multiple_of(8 * (p >> 1), 8), 8)
        gather[:, to, :] += dot(one_hot(iota((256, 128), 1) == place), tail).reshape(32, 8, 128)

    loop(5, contraction)

    def expansion(owner):
        slot = slot_of(owner ^ me)
        rows = pl.ds(pl.multiple_of(40 * owner, 8), 40)
        for c in range(3):
            gather[slot, 24 + 40 * c : 64 + 40 * c, :] = dw1[rows, 128 * c : 128 * c + 128]

    loop(32, expansion)
    keep[:, 80:224, :] = gather[0:16].astype(BF16)
    send[:, 80:224, :] = gather[16:32].astype(BF16)


def attend_back_kernel(scal, kt, vt, qs, kv, wo, low_grad, lse, dq, dkv, og):
    bias = key_bias(scal[1])
    og[...] = dot_tn(wo[...], low_grad[...]).astype(BF16)

    def head(h):
        rows = pl.ds(pl.multiple_of(64 * h, 64), 64)
        more = pl.ds(pl.multiple_of(D + 64 * h, 64), 64)
        dk = jnp.zeros((64, 256), F32)
        dv = jnp.zeros((64, 256), F32)
        for quad in range(4):
            at = slice(256 * quad, 256 * quad + 256)
            probs = jnp.exp(dot(kt[h], qs[rows, at]) + bias - lse[h, :, at])
            grad = dot(vt[h], og[rows, at])
            mean = jnp.sum(probs * grad, axis=0, keepdims=True)
            score = (probs * (grad - mean)).astype(BF16)
            dq[rows, at] = (dot(kv[rows, :], score) * 0.125).astype(BF16)
            dk += dot_nt(qs[rows, at], score)
            dv += dot_nt(og[rows, at], probs.astype(BF16))
        dkv[rows, :] = dk.astype(BF16)
        dkv[more, :] = dv.astype(BF16)

    loop(HEADS, head)


def first_kernel(scal, bt, wq, wkv, wrs, first, red, raw, stat_r, dq, dkv, low_grad, att, entry, stats, g_one, g_two, g_three, keep, send, work, grads, wide, redin, stack_r, stack_z, tails_of):
    me = scal[0]
    grads[...] = g_one[...] + g_two[...] + g_three[...]
    for quad in range(4):
        redin[D * quad : D * quad + D, :] = first[:, 256 * quad : 256 * quad + 256]
    dred = dot_tn(wkv[...], dkv[...])
    gain = column(bt, G_R, 5)
    lows = []
    for tile in range(2):
        at = slice(128 * tile, 128 * tile + 128)
        grad = dred[:, at]
        hat = (raw[:, at] - stat_r[0:1, at]) * stat_r[1:2, at]
        low = norm_back(grad, hat, stat_r[1:2, at], gain).astype(BF16)
        lows.append(low)
        parts = (grad * hat, grad, low.astype(F32))
        sums = parts if tile == 0 else [s + v for s, v in zip(sums, parts)]
    put_column(grads, G_R, lane_sum(sums[0]))
    put_column(grads, C_R, lane_sum(sums[1]))
    put_column(grads, B_R, lane_sum(sums[2]))
    low = jnp.concatenate(lows, axis=1)
    order = to_tens(me)
    low = dot(order, low).astype(BF16)
    wide[...] = dot_tn(wrs[...], low)
    straight = dot_tn(wq[...], dq[...])
    for quad in range(4):
        at = slice(256 * quad, 256 * quad + 256)
        work[:, at] = straight[:, at] + wide[D * quad : D * quad + D, :]
    zeros = jnp.zeros((D, 128), F32)

    def body(tile, carry):
        at = lanes(tile)
        grad = work[:, at]
        hat = (entry[:, at].astype(F32) - stats[0:1, at]) * stats[1:2, at]
        return carry[0] + grad * hat, carry[1] + grad, carry[2] + dq[:, at].astype(F32)

    sums = lax.fori_loop(0, 8, body, (zeros, zeros, zeros))
    put_column(grads, G_1, lane_sum(sums[0]))
    put_column(grads, C_1, lane_sum(sums[1]))
    put_column(grads, B_Q, lane_sum(sums[2]))
    stack_r[...] = dot_nt(low, redin[...])

    def outer(pick, grad, value):
        return dot_nt(dot(pick, grad[...]).astype(BF16), value[...])

    row = iota((1, 2 * D), 1)
    place = iota((D, 2 * D), 0)
    parts = (
        outer(order, dq, first),
        outer(one_hot(place == keyval_tens(row, me, False)), dkv, red),
        outer(one_hot(place == keyval_tens(row, me, True)), dkv, red),
        outer(order, low_grad, att),
    )
    for part, at in zip(parts, (0, 256, 512, 1024)):
        stack_z[:, at : at + 256] = part[:, 0:256]
    stack_z[:, 768:1024] = jnp.concatenate([part[:, 256:320] for part in parts], axis=1)
    spread = one_hot(iota((256, 256), 1) == rest_row(iota((256, 1), 0)))

    def pack(p):
        at = lanes(p, 256)
        both = stack_r[:, at], stack_z[:, at]
        for e in range(2):
            pieces = [block[0:256, 128 * e : 128 * e + 128].reshape(32, 1, 8, 128) for block in both]
            full = jnp.concatenate(pieces, axis=1).reshape(32, 16, 128).astype(BF16)
            to = pl.ds(pl.multiple_of(32 * p + 16 * e, 16), 16)
            keep[:, to, :] = full[0:16]
            send[:, to, :] = full[16:32]
        tail = jnp.concatenate(
            [block[256:320, 128 * e : 128 * e + 128] for block in both for e in range(2)], axis=0
        ).astype(BF16)
        to = pl.ds(pl.multiple_of(8 * p, 8), 8)
        tails_of[:, to, :] = dot(spread, tail).reshape(32, 8, 128)

    loop(5, pack)
    rows = jnp.transpose(jnp.concatenate([grads[...], jnp.zeros((64, 128), F32)], axis=0)).astype(BF16)
    place = iota((256, 128), 0)
    vector = iota((256, 128), 1)
    line = place & 7
    owner = xor_of(place >> 3) ^ me
    start = (7 * owner) >> 3
    straight = (
        ((line == 0) & (vector == 3 * owner))
        | ((line == 1) & (vector == 3 * owner + 2))
        | ((line == 2) & (vector == 96 + start))
    )
    turned = ((line == 0) & (vector == 3 * owner + 1)) | ((line == 2) & (vector == 97 + start))
    small = dot(one_hot(straight), rows) + pltpu.roll(dot(one_hot(turned), rows), 64, 1)
    tails_of[:, 40:48, :] = small.reshape(32, 8, 128)
    keep[:, 160:208, :] = tails_of[0:16].astype(BF16)
    send[:, 160:208, :] = tails_of[16:32].astype(BF16)


def token_kernel(scal, bt, grad_in, mid_grad, entry, stats, tok, high, rest):
    side = scal[1]
    gain = column(bt, G_1, 5)

    def body(tile):
        at = lanes(tile)
        hat = (entry[:, at].astype(F32) - stats[0:1, at]) * stats[1:2, at]
        result = mid_grad[:, at] + norm_back(grad_in[:, at], hat, stats[1:2, at], gain)
        result = result * token_mask(tile, side)
        upper = result.astype(BF16)
        high[:, at] = upper
        rest[:, at] = (result - upper.astype(F32)).astype(BF16)

    loop(8, body)
    row, col = token_place(iota((TOKENS, 1), 0))
    natural = row * SIDE + col

    def quad(index):
        at = lanes(index, 256)
        pick = one_hot(iota((TOKENS, 256), 1) + 256 * index == natural)
        tok[:, at] = dot(high[...], pick) + dot(rest[...], pick)

    loop(4, quad)


def cost(micros):
    return pl.CostEstimate(flops=int(micros * 1e9), bytes_accessed=1000, transcendentals=0)


def call(kernel, args, outs, scratch=(), micros=5):
    return pl.pallas_call(
        kernel,
        in_specs=[pl.BlockSpec(memory_space=pltpu.SMEM if arg.dtype == I32 else pltpu.VMEM) for arg in args],
        out_shape=[jax.ShapeDtypeStruct(shape, dtype) for shape, dtype in outs],
        scratch_shapes=[pltpu.VMEM(shape, dtype) for shape, dtype in scratch],
        compiler_params=pltpu.CompilerParams(vmem_limit_bytes=VMEM_LIMIT),
        cost_estimate=cost(micros),
    )(*args)


def local(group, axes, *arrays):
    return step_of(group, axes, *arrays)


def step_of(group, axes, tokens, image_side, cotangent, *shards):
    index = lax.axis_index(axes[0]) * lax.axis_size(axes[1]) + lax.axis_index(axes[1])
    me = index // group
    devices = SUPER * group

    def flip(values, mask):
        pairs = [(i, ((i // group) ^ mask) * group + i % group) for i in range(devices)]
        return lax.ppermute(values, axes, pairs)

    def gather(block, split=0, direct=False):
        held = block[None]
        if direct:
            held = jnp.concatenate([held, flip(held, 2), flip(held, 4), flip(held, 6)], axis=0)
        else:
            for mask in FLIPS[:2]:
                held = jnp.concatenate([held, flip(held, mask)], axis=0)
        if split:
            one, two = held[:, :split], held[:, split:]
            one, two = (jnp.concatenate([one, flip(one, 8)], axis=0), jnp.concatenate([two, flip(two, 16)], axis=0))
            far, near = flip(one, 16), flip(two, 8)
            two = jnp.concatenate([two[:4], near[:4], two[4:], near[4:]], axis=0)
            held = jnp.concatenate([jnp.concatenate([one, far], axis=0), two], axis=1)
        else:
            for mask in FLIPS[2:]:
                held = jnp.concatenate([held, flip(held, mask)], axis=0)
        return held, flip(held, 1)

    def scatter(keep, send, split=0, direct=False):
        def step(held, mask):
            return flip(held, mask).astype(F32)

        def halve(held, mask):
            half = held.shape[0] // 2
            return held[:half].astype(F32) + step(held[half:], mask)

        held = (keep.astype(F32) + step(send, 1)).astype(BF16)
        if split:
            one, two = held[:, :split], held[:, split:].reshape(2, 2, 4, -1, 128)
            one, two = (
                halve(one, 16).astype(BF16),
                (two[:, 0].astype(F32) + step(two[:, 1], 8)).astype(BF16).reshape(8, -1, 128),
            )
            held = jnp.concatenate([halve(one, 8), halve(two, 16)], axis=1).astype(BF16)
        else:
            held = halve(held, 16).astype(BF16)
            held = halve(held, 8).astype(BF16)
        if direct:
            far = step(held[2:3], 4), step(held[3:4], 6), step(held[1:2], 2)
            return (held[0:1].astype(F32) + far[2] + far[0] + far[1])[0]
        held = halve(held, 4).astype(BF16)
        return halve(held, 2)[0]

    if group > 1:
        per = lax.axis_size(axes[1])
        start = (index % per) // group * group

        def join(shard):
            full = lax.all_gather(shard, axes[1], axis=0)
            return lax.dynamic_slice_in_dim(full, start, group, axis=0).reshape(-1)

        shards = [join(shard) for shard in shards]
    query, keyval, reduce_w, output, expand, depth, contract, merge, gains, biases = shards

    def rows(flat):
        return flat.reshape(-1, 128)

    scal = jnp.stack([me.astype(I32), image_side[0].astype(I32)])
    taps = jnp.pad(depth.reshape(40, 9), ((0, 0), (64, 55)))
    block_a = select(
        [rows(query), rows(output), rows(keyval), rows(reduce_w)],
        table_a, A_ROWS, (scal, biases[None], gains[None]),
    )
    block_b = select([rows(contract), rows(expand), taps], table_b, B_ROWS)
    block_c = select([rows(merge)], table_c, C_ROWS)
    a_low, a_high = gather(block_a, A_SPLIT, True)
    b_low, b_high = gather(block_b, B_ROWS // 2, True)
    c_low, c_high = gather(block_c, C_ROWS // 2)

    big, narrow = (D, TOKENS), (D, QUARTER)
    entry, stats_1 = call(entry_kernel, (scal, tokens[0]), [(big, BF16), ((8, TOKENS), F32)], micros=3.5)
    wq, wkv, wr, wo, first, qs, raw, stat_r, red, kv, kt, vt, bt = call(
        project_kernel,
        (scal, a_low, a_high, entry, stats_1),
        [
            ((D, D), BF16), ((2 * D, D), BF16), ((D, 4 * D), BF16), ((D, D), BF16), (big, BF16), (big, BF16),
            (narrow, F32), ((8, QUARTER), F32), (narrow, BF16), ((2 * D, QUARTER), BF16),
            ((HEADS, QUARTER, 64), BF16), ((HEADS, QUARTER, 64), BF16), ((64, 128), F32),
        ],
        [((D, 1280), BF16), ((256, 640), BF16), ((4 * D, QUARTER), BF16)],
        micros=8,
    )
    att, lse = call(attend_kernel, (scal, kt, qs, kv), [(big, BF16), ((HEADS, 1, TOKENS), F32)],
        [((2, QUARTER, TOKENS), F32), ((QUARTER, TOKENS), BF16)], micros=8.5)
    mid, sec, stats_2 = call(
        middle_kernel, (scal, bt, wo, att, entry), [(big, F32), ((384, TOKENS), BF16), ((8, TOKENS), F32)], [(big, F32)],
        micros=5,
    )
    w1, w1t, w2, w2t, taps = call(
        ffn_weights_kernel,
        (scal, bt, b_low, b_high),
        [((FF, 384), BF16), ((D, FF), BF16), ((D, FF), BF16), ((FF, D), BF16), ((10, FF, 128), F32)],
        [((D, FF), BF16), ((256, 384), BF16), ((FF, 384), F32)],
        micros=8,
    )
    act, slope = call(
        ffn_kernel,
        (scal, w1, taps, sec),
        [((FF, TOKENS), BF16), ((FF, TOKENS), BF16)],
        [((64, TOKENS), F32), ((64, TOKENS), F32)],
        micros=17,
    )
    end, sect, stats_s = call(
        ending_kernel, (scal, bt, w2, act, mid), [(big, F32), (big, BF16), ((8, TOKENS), F32)], [(big, F32)], micros=5
    )
    four, c_keep, c_send, end_grad, branch, g_one = call(
        merge_kernel,
        (scal, bt, c_low, c_high, sect, end, stats_s, cotangent[0]),
        [
            ((OUT_D, QUARTER), BF16), ((16, C_ROWS, 128), BF16), ((16, C_ROWS, 128), BF16), (big, F32), (big, BF16),
            ((64, 128), F32),
        ],
        [
            ((OUT_D, MERGE_PAD), BF16), ((MERGE_PAD, QUARTER), BF16), ((OUT_D, QUARTER), BF16),
            ((MERGE_PAD, QUARTER), F32), ((OUT_D, QUARTER), F32), ((OUT_D, QUARTER), F32),
        ],
        micros=20,
    )
    sum_c = scatter(c_keep, c_send, C_ROWS // 2)
    hgs, dks = [], []
    for at, count in PARTS:
        hg, dk = call(
            functools.partial(ffn_back_kernel, at, count),
            (scal, w1, w2t, taps, sec, slope, branch),
            [((256 * count, TOKENS), BF16), ((256 * count, 128), F32)],
            [((64, TOKENS), F32)] * 4,
            micros=6 * count,
        )
        hgs.append(hg)
        dks.append(dk)
    b_keep, b_send, g_three = call(
        pack_b_kernel,
        (scal, *hgs, *dks, sec, branch, act),
        [((16, B_ROWS, 128), BF16), ((16, B_ROWS, 128), BF16), ((64, 128), F32)],
        [((FF, 384), F32), ((32, 144, 128), F32), (big, BF16)],
        micros=9,
    )
    sum_b = scatter(b_keep, b_send, 0, True)
    mid_grad, low_grad, g_two = call(
        middle_back_kernel,
        (scal, bt, w1t, *hgs, end_grad, mid, stats_2),
        [(big, F32), (big, BF16), ((64, 128), F32)],
        [(big, F32)],
        micros=6,
    )
    dq, dkv = call(
        attend_back_kernel,
        (scal, kt, vt, qs, kv, wo, low_grad, lse),
        [(big, BF16), ((2 * D, QUARTER), BF16)],
        [(big, BF16)],
        micros=9,
    )
    a_keep, a_send, first_grad = call(
        first_kernel,
        (
            scal, bt, wq, wkv, wr, first, red, raw, stat_r, dq, dkv, low_grad, att, entry, stats_1, g_one, g_two, g_three,
        ),
        [((16, A_ROWS, 128), BF16), ((16, A_ROWS, 128), BF16), (big, F32)],
        [
            ((64, 128), F32), ((4 * D, QUARTER), F32), ((4 * D, QUARTER), BF16), ((D, 1280), F32), ((D, 1280), F32),
            ((32, 48, 128), F32),
        ],
        micros=11,
    )
    sum_a = scatter(a_keep, a_send, A_SPLIT, True)
    (token_grad,) = call(
        token_kernel,
        (scal, bt, first_grad, mid_grad, entry, stats_1),
        [(big, F32)],
        [(big, BF16), (big, BF16)],
        micros=5,
    )
    if group > 1:

        def total(part):
            full = lax.all_gather(part, axes[1], axis=0)
            return jnp.sum(lax.dynamic_slice_in_dim(full, start, group, axis=0), axis=0)

        sum_a, sum_b, sum_c = total(sum_a), total(sum_b), total(sum_c)

    def flat(count):
        return (count, 128), F32

    query_g, output_g, keyval_g, reduce_g, biases_g, gains_g = call(
        out_a_kernel,
        (scal, sum_a),
        [flat(25), flat(25), flat(50), flat(100), ((1, 192), F32), ((1, 56), F32)],
        micros=1,
    )
    contract_g, expand_g = call(out_b_kernel, (scal, sum_b), [flat(100), flat(100)], micros=1)
    (merge_g,) = call(out_c_kernel, (scal, sum_c), [flat(360)], micros=1)
    depth_g = sum_b[184:224, 64:73]
    grads = [query_g, keyval_g, reduce_g, output_g, expand_g, depth_g, contract_g, merge_g, gains_g, biases_g]
    grads = [grad.reshape(-1) for grad in grads]
    if group > 1:
        mine = index % group
        grads = [lax.dynamic_index_in_dim(grad.reshape(group, -1), mine, keepdims=False) for grad in grads]
    return (four[None], token_grad[None], *grads)


def solution(mesh):
    axes = ("dp", "fs")
    devices = mesh.shape["dp"] * mesh.shape["fs"]
    group = devices // SUPER
    if devices != SUPER * group or mesh.shape["fs"] % group:
        raise ValueError("unsupported mesh")
    one, three = P(axes), P(axes, None, None)
    return jax.shard_map(
        functools.partial(local, group, axes),
        mesh=mesh,
        in_specs=(three, one, three) + (one,) * 10,
        out_specs=(three, three) + (one,) * 10,
        check_vma=False,
    )
```

```python
import functools

import jax
import jax.numpy as jnp
import numpy as np
from jax import lax
from jax.experimental import pallas as pl
from jax.experimental.pallas import tpu as pltpu
from jax.sharding import PartitionSpec as P


D = 320
HEADS = 5
FF = 1280
OUT_D = 512
SIDE = 32
QUARTER = 256
TOKENS = SIDE * SIDE
MERGE_PAD = 2944
SUPER = 32
FLIPS = (2, 4, 8, 16)
EPS = 1e-06
F32, BF16, I32 = jnp.float32, jnp.bfloat16, jnp.int32

B_Q, B_R, C_R, B_O, C_1, C_2, B_1, B_DW, B_2, C_S, B_M, C_M = 0, 5, 10, 15, 20, 25, 30, 50, 70, 75, 80, 88
G_R, G_1, G_2, G_S, G_M = 96, 101, 106, 111, 116

PARTS = ((0, 1), (1, 4))
A_ROWS, B_ROWS, C_ROWS = 208, 224, 368
SMALL_ROW = 200
A_SPLIT = 104
VMEM_LIMIT = 24 * 1024 * 1024
VMEM_ALL = 60 * 1024 * 1024


def slot_of(xor):
    return (xor >> 1) | ((xor & 1) << 4)


def xor_of(slot):
    return ((slot & 15) << 1) | (slot >> 4)


def dot(a, b):
    return jnp.dot(a, b, preferred_element_type=F32)


def dot_nt(a, b):
    return lax.dot_general(a, b, (((1,), (1,)), ((), ())), preferred_element_type=F32)


def dot_tn(a, b):
    return lax.dot_general(a, b, (((0,), (0,)), ((), ())), preferred_element_type=F32)


def iota(shape, axis):
    return lax.broadcasted_iota(I32, shape, axis)


def one_hot(test):
    return jnp.where(test, 1.0, 0.0).astype(BF16)


def lanes(index, width=128):
    return pl.ds(pl.multiple_of(index * width, width), width)


def loop(count, body):
    def step(index, carry):
        body(index)
        return carry

    lax.fori_loop(0, count, step, 0)


def column(table, start, count):
    return jnp.concatenate(
        [jnp.broadcast_to(table[:, h : h + 1], (64, 128)) for h in range(start, start + count)], axis=0
    )


def put_column(table, start, values):
    for h in range(values.shape[0] // 64):
        table[:, start + h : start + h + 1] = values[64 * h : 64 * h + 64, 0:1]


def token_place(lane):
    quad = lane >> 8
    row = 2 * ((lane >> 4) & 15) + (quad >> 1)
    col = 2 * (lane & 15) + (quad & 1)
    return row, col


def token_mask(tile, side, width=128):
    row, col = token_place(iota((1, width), 1) + tile * width)
    return jnp.where((row < side) & (col < side), 1.0, 0.0)


def key_place(index):
    return index >> 4, index & 15


def select_kernel(count, bases, small, small_at, *refs):
    sources, refs = refs[:count], refs[count:]
    if small:
        scal, biases, gains = refs[:3]
        refs = refs[3:]
    low_ref, high_ref, out, rows_ref, sems = refs[:5]
    held = refs[5:]
    copies = [
        pltpu.make_async_copy(source, place, sems.at[n]) for n, (source, place) in enumerate(zip(sources, held))
    ]
    for copy in copies:
        copy.start()
    half = rows_ref.shape[0] // 2
    rows_ref[...] = jnp.zeros_like(rows_ref)
    place = iota((out.shape[0], 2 * half), 1)
    pick_low = one_hot(place == low_ref[...])
    pick_high = one_hot(place == high_ref[...])
    for copy in copies:
        copy.wait()
    for source, base in zip(held, bases):
        rows_ref[base : base + source.shape[0], :] = source[...].astype(F32)
    if small:
        rows_ref[small_at : small_at + 1, :] = biases[:, 0:128].astype(F32)
        rows_ref[small_at + 1 : small_at + 2, 0:64] = biases[:, 128:192].astype(F32)
        wide = jnp.concatenate([gains[...].astype(F32), jnp.zeros((1, 72), F32)], axis=1)
        wide = jnp.broadcast_to(wide, (8, 128))
        rows_ref[small_at + 2 : small_at + 3, :] = pltpu.roll(wide, (56 * scal[0]) & 63, 1)[0:1, :]
    rows_ref[half:, :] = pltpu.roll(rows_ref[0:half, :], 64, 1)
    total = rows_ref[...].astype(BF16)
    low, upper = dot(pick_low, total), dot(pick_high, total)
    out[...] = jnp.where(iota((out.shape[0], 128), 1) < 64, low, upper).astype(BF16)


def select(sources, table, rows, vectors=()):
    bases, at = [], 0
    for source in sources:
        bases.append(at)
        at += -(-source.shape[0] // 16) * 16
    small = len(vectors) > 0
    half = at + (16 if small else 0)
    low, high = table(bases + [at], half).astype(np.int32)[:, :, None]
    specs = [pl.BlockSpec(memory_space=pltpu.HBM)] * len(sources)
    if small:
        specs += [pl.BlockSpec(memory_space=pltpu.SMEM)] + [pl.BlockSpec(memory_space=pltpu.VMEM)] * 2
    specs += [pl.BlockSpec(memory_space=pltpu.VMEM)] * 2
    return pl.pallas_call(
        functools.partial(select_kernel, len(sources), tuple(bases), small, at),
        in_specs=specs,
        out_shape=jax.ShapeDtypeStruct((rows, 128), BF16),
        scratch_shapes=[pltpu.VMEM((2 * half, 128), F32), pltpu.SemaphoreType.DMA((len(sources),))]
        + [pltpu.VMEM(source.shape, source.dtype) for source in sources],
        compiler_params=pltpu.CompilerParams(vmem_limit_bytes=VMEM_ALL if small else VMEM_LIMIT),
        cost_estimate=cost(2),
    )(*sources, *vectors, low, high)


def pair(half, low_src, high_src):
    low = -1 if low_src is None else low_src[0] + low_src[1] // 2 + half * (low_src[1] % 2)
    high = -1 if high_src is None else high_src[0] + high_src[1] // 2 + half * (1 - high_src[1] % 2)
    return low, high


def chunk_sources(bases, row, c):
    q, o, kv = bases
    if c < 6 or c >= 8:
        base, first = ((q, 0), (kv, 0), (kv, 10), None, (o, 0))[c // 2]
        at = 5 * (first + row) + 2 * (c % 2)
        return (base, at), (base, at + 1)
    if c == 6:
        return (q, 5 * row + 4), (kv, 5 * row + 4)
    return (kv, 5 * (10 + row) + 4), (o, 5 * row + 4)


def a_place(kind, row, c):
    if row < 8:
        return 16 * c + 8 * kind + row
    return 160 + 8 * (c // 2) + 4 * kind + 2 * (c % 2) + row - 8


def b_place(row, c):
    if row < 8:
        return 8 * c + row
    return 80 + 8 * (c // 4) + 2 * (c % 4) + row - 8


def table_a(bases, half):
    q, o, kv, r, small = bases
    rows = [(-1, -1)] * A_ROWS
    for c in range(10):
        for row in range(10):
            at = 20 * row + 2 * c
            rows[a_place(0, row, c)] = pair(half, (r, at), (r, at + 1))
            rows[a_place(1, row, c)] = pair(half, *chunk_sources((q, o, kv), row, c))
    for row in range(3):
        rows[SMALL_ROW + row] = pair(half, (small, 2 * row), (small, 2 * row + 1))
    return np.array(rows).T


def table_b(bases, half):
    w2, w1, dw, _ = bases
    rows = [(-1, -1)] * B_ROWS
    for c in range(10):
        for row in range(10):
            at = 20 * row + 2 * c
            rows[b_place(row, c)] = pair(half, (w2, at), (w2, at + 1))
    for c in range(3):
        for row in range(40):
            at = 5 * row + 2 * c
            rows[104 + 40 * c + row] = pair(half, (w1, at), (w1, at + 1) if c < 2 else (dw, 2 * row + 1))
    return np.array(rows).T


def table_c(bases, half):
    m, _ = bases
    rows = []
    for c in range(23):
        for row in range(16):
            at = 45 * row + 2 * c
            rows.append(pair(half, (m, at), (m, at + 1) if c < 22 else None))
    return np.array(rows).T


def turn(rows):
    return pltpu.roll(rows, 64, 1)


def halves(low, high):
    return jnp.where(iota((1, 128), 1) < 64, low, high)


def put_rows(out, first, count, stride, rows):
    out[pl.ds(first, count, stride=stride), :] = rows


def put_320(out, first, count, load):
    even, odd = ([load(chunk, parity) for chunk in range(3)] for parity in range(2))
    turned = [turn(rows) for rows in odd]
    for at, rows in enumerate(
        (even[0], even[1], halves(even[2], turned[0]), halves(turned[0], turned[1]), halves(turned[1], turned[2]))
    ):
        put_rows(out, first + at, count // 2, 5, rows)


def every_other(ref, start, count):
    return ref[pl.ds(start, count, stride=2), :]


def out_a_kernel(scal, sums, q, o, kv, r, biases, gains):
    squares = (
        (q, 0, (0, 1, 6), False),
        (o, 0, (8, 9, 7), True),
        (kv, 0, (2, 3, 6), True),
        (kv, 25, (4, 5, 7), False),
    )
    for out, first, chunks, high in squares:
        for start, count, lane_row in ((0, 8, 0), (8, 2, 20)):

            def load(chunk, parity, chunks=chunks, high=high, start=start, count=count):
                rows = every_other(sums, a_place(1, start, chunks[chunk]) + parity, count // 2)
                return turn(rows) if chunk == 2 and high else rows

            put_320(out, first + lane_row, count, load)
    for c in range(10):
        for start, count in ((0, 8), (8, 2)):
            put_rows(r, 10 * start + c, count, 10, sums[pl.ds(a_place(0, start, c), count), :])
    small = sums[SMALL_ROW : SMALL_ROW + 8, :]
    biases[:, 0:128] = small[0:1]
    biases[:, 128:192] = small[1:2, 0:64]
    gains[...] = pltpu.roll(small, (128 - ((56 * scal[0]) & 63)) & 127, 1)[2:3, 0:56]


def out_b_kernel(scal, sums, w2, w1):
    for c in range(10):
        for start, count in ((0, 8), (8, 2)):
            put_rows(w2, 10 * start + c, count, 10, sums[pl.ds(b_place(start, c), count), :])
    put_320(w1, 0, 40, lambda chunk, parity: every_other(sums, 104 + 40 * chunk + parity, 20))


def out_c_kernel(scal, sums, m):
    even = [every_other(sums, 16 * c, 8) for c in range(23)]
    turned = [turn(every_other(sums, 16 * c + 1, 8)) for c in range(23)]
    for c in range(22):
        put_rows(m, c, 8, 45, even[c])
        put_rows(m, 23 + c, 8, 45, halves(turned[c], turned[c + 1]))
    put_rows(m, 22, 8, 45, halves(even[22], turned[0]))


def split_ten(row, per, magic):
    owner = (row * magic) >> 16
    return owner, row - per * owner


def tens(row, me):
    owner, rest = split_ten(row, 10, 6554)
    slot = slot_of(owner ^ me)
    return jnp.where(rest < 8, slot * 8 + rest, 248 + slot * 2 + rest)


def keyval_tens(row, me, upper):
    owner, rest = split_ten(row, 20, 3277)
    inside = (rest >= 10) if upper else (rest < 10)
    return jnp.where(inside, tens(10 * owner + rest - (10 if upper else 0), me), -1)


def rest_row(row):
    return 64 * ((row & 7) >> 1) + 2 * (row >> 3) + (row & 1)


def orders_kernel(scal, from_tens, to_tens, from_lower, from_upper, to_lower, to_upper, from_rest, to_rest):
    me = scal[0]
    from_tens[...] = one_hot(iota((D, D), 1) == tens(iota((D, 1), 0), me))
    to_tens[...] = one_hot(iota((D, D), 0) == tens(iota((1, D), 1), me))
    for upper, down, up in ((False, from_lower, to_lower), (True, from_upper, to_upper)):
        down[...] = one_hot(iota((2 * D, D), 1) == keyval_tens(iota((2 * D, 1), 0), me, upper))
        up[...] = one_hot(iota((D, 2 * D), 0) == keyval_tens(iota((1, 2 * D), 1), me, upper))
    from_rest[...] = one_hot(iota((256, 256), 0) == rest_row(iota((1, 256), 1)))
    to_rest[...] = one_hot(iota((256, 256), 1) == rest_row(iota((256, 1), 0)))


def norm(values, gain, shift):
    mean = jnp.mean(values, axis=0, keepdims=True)
    centred = values - mean
    rstd = lax.rsqrt(jnp.mean(centred * centred, axis=0, keepdims=True) + EPS)
    return centred * rstd * gain + shift, mean, rstd


def norm_back(grad, hat, rstd, gain):
    scaled = grad * gain
    return rstd * (
        scaled
        - jnp.mean(scaled, axis=0, keepdims=True)
        - hat * jnp.mean(scaled * hat, axis=0, keepdims=True)
    )


def stat_rows(mean, rstd):
    row = iota((8, mean.shape[1]), 0)
    return jnp.where(row == 0, mean, jnp.where(row == 1, rstd, 0.0))


def entry_kernel(scal, tokens, entry, stats, turned):
    side = scal[1]
    for quad in range(4):
        lane = iota((1, 256), 1) + quad * 256
        row, col = token_place(lane)
        natural = row * SIDE + col
        pick = one_hot(iota((TOKENS, 256), 0) == natural)
        turned[:, quad * 256 : quad * 256 + 256] = pick
        mask = jnp.where((row < side) & (col < side), 1.0, 0.0)
        entry[:, quad * 256 : quad * 256 + 256] = (dot(tokens[...], pick) * mask).astype(BF16)

    def body(tile):
        values = entry[:, lanes(tile)].astype(F32)
        mean = jnp.mean(values, axis=0, keepdims=True)
        centred = values - mean
        rstd = lax.rsqrt(jnp.mean(centred * centred, axis=0, keepdims=True) + EPS)
        stats[:, lanes(tile)] = stat_rows(mean, rstd)

    loop(8, body)


def small_table(me, low, high):
    gathered = jnp.concatenate(
        [half[:, SMALL_ROW : SMALL_ROW + 8, :].astype(F32).reshape(128, 128) for half in (low, high)], axis=0
    ).astype(BF16)
    vector = iota((128, 256), 0)
    place = iota((128, 256), 1)
    row = place & 7
    owner = xor_of(place >> 3) ^ me
    first = (7 * owner) >> 3
    straight = (
        ((row == 0) & (vector == 3 * owner))
        | ((row == 1) & (vector == 3 * owner + 2))
        | ((row == 2) & (vector == 96 + first))
    )
    turned = ((row == 0) & (vector == 3 * owner + 1)) | ((row == 2) & (vector == 97 + first))
    rows = dot(one_hot(straight), gathered) + pltpu.roll(dot(one_hot(turned), gathered), 64, 1)
    return jnp.transpose(rows)[0:64, :]


def project_kernel(scal, from_tens, from_lower, from_upper, from_rest, low, high, entry, stats, wq, wkv, wrs, wo, first, qs, raw, stat_r, red, kv, kt, vt, bt, square, rest, redin):
    me = scal[0]
    bt[...] = small_table(me, low, high)
    for half, source in enumerate((low, high)):

        def chunk(c, half=half, source=source):
            block = source[:, pl.ds(pl.multiple_of(16 * c, 16), 16), :].astype(F32)
            rows = slice(128 * half, 128 * half + 128)
            wrs[rows, lanes(c)] = block[:, 0:8].reshape(128, 128).astype(BF16)
            square[rows, lanes(c)] = block[:, 8:16].reshape(128, 128).astype(BF16)

        loop(10, chunk)
        block = source[:, 160:208, :].astype(F32)
        for c in range(5):
            part = block[:, 8 * c : 8 * c + 8].reshape(128, 128).astype(BF16)
            rest[128 * half : 128 * half + 128, 128 * c : 128 * c + 128] = part

    def last_two(p):
        part = dot(from_rest[...], rest[:, lanes(p)]).astype(BF16)
        wrs[256:320, lanes(p, 256)] = jnp.concatenate([part[0:64], part[64:128]], axis=1)
        square[256:320, lanes(p, 256)] = jnp.concatenate([part[128:192], part[192:256]], axis=1)

    loop(5, last_two)
    wq[:, 0:256] = dot(from_tens[...], square[:, 0:256]).astype(BF16)
    wo[:, 0:256] = dot(from_tens[...], square[:, 1024:1280]).astype(BF16)
    tails = dot(from_tens[...], square[:, 768:1024])
    wq[:, 256:320] = tails[:, 0:64].astype(BF16)
    wo[:, 256:320] = pltpu.roll(tails, 64, 1)[:, 0:64].astype(BF16)
    wkv[:, 0:256] = (dot(from_lower[...], square[:, 256:512]) + dot(from_upper[...], square[:, 512:768])).astype(BF16)
    tail = pltpu.roll(dot(from_lower[...], square[:, 768:896]), 64, 1) + dot(from_upper[...], square[:, 896:1024])
    wkv[:, 256:320] = tail[:, 0:64].astype(BF16)

    gain, shift = column(bt, G_1, 5), column(bt, C_1, 5)

    def body(tile):
        centred = entry[:, lanes(tile)].astype(F32) - stats[0:1, lanes(tile)]
        first[:, lanes(tile)] = (centred * stats[1:2, lanes(tile)] * gain + shift).astype(BF16)

    loop(8, body)
    for quad in range(4):
        redin[D * quad : D * quad + D, :] = first[:, 256 * quad : 256 * quad + 256]
    bias = column(bt, B_R, 5)
    bias = jnp.concatenate([bias, bias], axis=1)
    mixed = dot(wrs[...], redin[...])
    total = bias
    for part in range(3):
        piece = mixed.astype(BF16)
        total = total + dot(from_tens[...], piece)
        mixed = mixed - piece.astype(F32)
    raw[...] = total
    gain, shift = column(bt, G_R, 5), column(bt, C_R, 5)
    for tile in range(2):
        at = slice(128 * tile, 128 * tile + 128)
        values, mean, rstd = norm(raw[:, at], gain, shift)
        red[:, at] = values.astype(BF16)
        stat_r[:, at] = stat_rows(mean, rstd)
    keyval = dot(wkv[...], red[...])
    kv[...] = keyval.astype(BF16)
    turned = jnp.transpose(keyval)
    for h in range(HEADS):
        kt[h] = turned[:, 64 * h : 64 * h + 64].astype(BF16)
        vt[h] = turned[:, D + 64 * h : D + 64 * h + 64].astype(BF16)
    bias = column(bt, B_Q, 5)
    bias = jnp.concatenate([bias, bias], axis=1)

    def query(quad):
        at = lanes(quad, 256)
        qs[:, at] = (dot(wq[...], first[:, at]) + bias).astype(BF16) * BF16(0.125)

    loop(4, query)


def key_bias(side):
    i, j = key_place(iota((QUARTER, 1), 0))
    return jnp.where((i < (side >> 1)) & (j < (side >> 1)), 0.0, -10000.0)


def head_rows(h):
    return pl.ds(pl.multiple_of(64 * h, 64), 64)


def attend_kernel(scal, kt, qs, kv, att, lse, scores_a, scores_b, probs_a, probs_b):
    bias = key_bias(scal[1])

    def score(scores, h, start):
        scores[...] = dot(kt[h], qs[head_rows(h), start : start + 512])

    def finish(scores, probs, h, start):
        for tile in range(4):
            at = slice(128 * tile, 128 * tile + 128)
            to = slice(start + 128 * tile, start + 128 * tile + 128)
            part = scores[:, at] + bias
            top = jnp.max(part, axis=0, keepdims=True)
            weights = jnp.exp(part - top)
            total = jnp.sum(weights, axis=0, keepdims=True)
            lse[h, :, to] = top + jnp.log(total)
            probs[:, at] = (weights * (1.0 / total)).astype(BF16)
        values = kv[pl.ds(pl.multiple_of(D + 64 * h, 64), 64), :]
        att[head_rows(h), start : start + 512] = dot(values, probs[...]).astype(BF16)

    score(scores_a, 0, 0)

    def head(h):
        score(scores_b, h, 512)
        finish(scores_a, probs_a, h, 0)
        score(scores_a, jnp.minimum(h + 1, HEADS - 1), 0)
        finish(scores_b, probs_b, h, 512)

    loop(HEADS, head)


def middle_kernel(scal, bt, wo, att, entry, mid, sec, stats, work):
    side = scal[1]
    work[...] = dot(wo[...], att[...])
    bias, gain, shift = column(bt, B_O, 5), column(bt, G_2, 5), column(bt, C_2, 5)

    def body(tile):
        at = lanes(tile)
        mask = token_mask(tile, side)
        values = entry[:, at].astype(F32) + mask * (work[:, at] + bias)
        mid[:, at] = values
        normed, mean, rstd = norm(values, gain, shift)
        stats[:, at] = stat_rows(mean, rstd)
        sec[0:D, at] = (normed.astype(BF16).astype(F32) * mask).astype(BF16)
        sec[D : D + 64, at] = jnp.where(iota((64, 128), 0) == 9, mask, 0.0).astype(BF16)

    loop(8, body)


def ffn_weights_kernel(scal, bt, from_tens, from_rest, low, high, w1, w1t, w2, w2t, taps, main, rest, wide):
    me = scal[0]
    for half, source in enumerate((low, high)):
        def chunks(p, half=half, source=source):
            block = source[:, pl.ds(pl.multiple_of(16 * p, 16), 16), :].astype(F32)
            both = jnp.concatenate([block[:, 0:8].reshape(128, 128), block[:, 8:16].reshape(128, 128)], axis=1)
            main[128 * half : 128 * half + 128, lanes(p, 256)] = both.astype(BF16)

        loop(5, chunks)
        block = source[:, 80:112, :].astype(F32)
        for c in range(3):
            part = block[:, 8 * c : 8 * c + 8].reshape(128, 128).astype(BF16)
            rest[128 * half : 128 * half + 128, 128 * c : 128 * c + 128] = part

        def expansion(slot, half=half, source=source):
            owner = ((slot << 1) | half) ^ me
            block = source[slot, 80:224, :].astype(F32)
            rows = pl.ds(pl.multiple_of(40 * owner, 8), 40)
            for c in range(3):
                wide[rows, 128 * c : 128 * c + 128] = block[24 + 40 * c : 64 + 40 * c]

        loop(16, expansion)
    for j in range(3):
        part = dot(from_rest[...], rest[:, 128 * j : 128 * j + 128]).astype(BF16)
        for k in range(4 if j < 2 else 2):
            c = 4 * j + k
            main[256:320, 128 * c : 128 * c + 128] = part[64 * k : 64 * k + 64]

    def block(p):
        rows = pl.ds(pl.multiple_of(256 * p, 256), 256)
        full = dot(from_tens[...], main[:, lanes(p, 256)])
        w2[:, lanes(p, 256)] = full.astype(BF16)
        w2t[rows, :] = jnp.transpose(full).astype(BF16)
        w1t[:, lanes(p, 256)] = jnp.transpose(wide[rows, :])[0:D].astype(BF16)

    loop(5, block)
    low_tail = wide[:, 256:384].astype(BF16)

    def spread(tap):
        taps[tap] = dot(low_tail, one_hot(iota((128, 128), 0) == 64 + tap))

    loop(9, spread)
    w1[:, 0:256] = wide[:, 0:256].astype(BF16)
    lane = iota((64, 128), 1)
    for h in range(20):
        rows = slice(64 * h, 64 * h + 64)
        taps[9, rows, :] = jnp.broadcast_to(bt[:, B_DW + h : B_DW + h + 1], (64, 128))
        beside = jnp.where(lane == 73, bt[:, B_1 + h : B_1 + h + 1], 0.0)
        w1[rows, 256:384] = jnp.where(lane < 64, wide[rows, 256:384], beside).astype(BF16)


def edge_masks():
    lane = iota((1, 128), 1)
    j = lane & 15
    return jnp.where(j != 0, 1.0, 0.0), jnp.where(j != 15, 1.0, 0.0), lane >= 16, lane < 112


def left_of(tiles):
    return [pltpu.roll(tile, 1, 1) for tile in tiles]


def right_of(tiles):
    return [pltpu.roll(tile, 127, 1) for tile in tiles]


def above(tiles, inside):
    turned = [pltpu.roll(tile, 16, 1) for tile in tiles]
    return [jnp.where(inside, turned[0], 0.0), jnp.where(inside, turned[1], turned[0])]


def below(tiles, inside):
    turned = [pltpu.roll(tile, 112, 1) for tile in tiles]
    return [jnp.where(inside, turned[0], turned[1]), jnp.where(inside, turned[1], 0.0)]


def times(tiles, factor):
    return [tile * factor for tile in tiles]


def plus(*many):
    return [functools.reduce(lambda a, b: a + b, tiles) for tiles in zip(*many)]


def tile_at(a, e, half):
    start = 256 * (2 * a + e) + 128 * half
    return slice(start, start + 128)


def quads(ref, rows):
    return [[[ref[rows, tile_at(a, e, half)] for half in range(2)] for e in range(2)] for a in range(2)]


LOG2E = float(np.log2(np.e))


def gelu_parts(x):
    y = x * np.float32(0.5**0.5)
    cdf = lax.erf(y) * 0.5 + 0.5
    bell = jnp.exp2(y * y * np.float32(-LOG2E) + np.float32(-0.5 * np.log2(2.0 * np.pi)))
    return x * cdf, cdf + x * bell


def ffn_kernel(scal, w1, taps, sec, act, slope, hid_a, hid_b):
    j_first, j_last, i_first, i_last = edge_masks()

    def fill(hid, step):
        rows = pl.ds(pl.multiple_of(jnp.minimum(step, FF // 64 - 1) * 64, 64), 64)
        hid[...] = dot(w1[rows, :], sec[...])

    def group(hid, step, index):
        rows = slice(16 * index, 16 * index + 16)
        out_rows = pl.ds(pl.multiple_of(64 * step + 16 * index, 16), 16)
        k = [taps[n, out_rows, :] for n in range(10)]
        first = [k[3 * r] * j_first for r in range(3)]
        last = [k[3 * r + 2] * j_last for r in range(3)]
        quad = quads(hid, rows)
        left = [left_of(quad[a][1]) for a in range(2)]
        right = [right_of(quad[a][0]) for a in range(2)]

        def across(a, e, r):
            if e == 0:
                parts = zip(left[a], quad[a][0], quad[a][1])
                return [first[r] * x + k[3 * r + 1] * y + k[3 * r + 2] * z for x, y, z in parts]
            parts = zip(quad[a][0], quad[a][1], right[a])
            return [k[3 * r] * x + k[3 * r + 1] * y + last[r] * z for x, y, z in parts]

        for e in range(2):
            up = above(across(1, e, 0), i_first)
            down = below(across(0, e, 2), i_last)
            outs = (plus(across(0, e, 1), across(1, e, 2), up), plus(across(0, e, 0), across(1, e, 1), down))
            for a in range(2):
                for half in range(2):
                    value, grad = gelu_parts(outs[a][half] + k[9])
                    act[out_rows, tile_at(a, e, half)] = value.astype(BF16)
                    slope[out_rows, tile_at(a, e, half)] = grad.astype(BF16)

    fill(hid_a, 0)

    def two(index):
        fill(hid_b, 2 * index + 1)
        for n in range(4):
            group(hid_a, 2 * index, n)
        fill(hid_a, 2 * index + 2)
        for n in range(4):
            group(hid_b, 2 * index + 1, n)

    loop(FF // 128, two)


def ending_kernel(scal, bt, w2, act, mid, end, sect, stats, work):
    side = scal[1]
    work[...] = dot(w2[...], act[...])
    bias, gain, shift = column(bt, B_2, 5), column(bt, G_S, 5), column(bt, C_S, 5)

    def body(tile):
        at = lanes(tile)
        mask = token_mask(tile, side)
        values = mid[:, at] + mask * (work[:, at] + bias)
        end[:, at] = values
        normed, mean, rstd = norm(values, gain, shift)
        stats[:, at] = stat_rows(mean, rstd)
        sect[:, at] = (normed.astype(BF16).astype(F32) * mask).astype(BF16)

    loop(8, body)


def lane_sum(values):
    return jnp.sum(values, axis=1, keepdims=True)


def merge_kernel(scal, bt, c_low, c_high, sect, end, stats, cot, four, keep, send, end_grad, branch, grads, wm, patch, mg, back, work, natural):
    me, side = scal[0], scal[1]
    grads[...] = jnp.zeros_like(grads)
    for half, source in enumerate((c_low, c_high)):

        def place(c, half=half, source=source):
            block = source[:, pl.ds(pl.multiple_of(16 * c, 16), 16), :].reshape(256, 128)
            wm[256 * half : 256 * half + 256, lanes(c)] = block

        loop(23, place)

    def reorder(to_owner):
        def one(slot):
            at = pl.ds(pl.multiple_of(16 * slot, 16), 16)
            owner = pl.ds(pl.multiple_of((xor_of(slot) ^ me) * 16, 16), 16)
            to_owner(at, owner)

        loop(32, one)

    j_first, j_last, i_first, i_last = edge_masks()
    quad = [[[t.astype(F32) for t in pair] for pair in row] for row in quads(sect, slice(None))]
    left = [times(left_of(quad[a][1]), j_first) for a in range(2)]
    pieces = (
        above(left[1], i_first),
        above(quad[1][0], i_first),
        above(quad[1][1], i_first),
        left[0],
        quad[0][0],
        quad[0][1],
        left[1],
        quad[1][0],
        quad[1][1],
    )
    for n, piece in enumerate(pieces):
        for half in range(2):
            patch[D * n : D * n + D, 128 * half : 128 * half + 128] = piece[half].astype(BF16)
    patch[9 * D :, :] = jnp.zeros((MERGE_PAD - 9 * D, 256), BF16)
    bias, gain, shift = column(bt, B_M, 8), column(bt, G_M, 8), column(bt, C_M, 8)
    work[...] = dot(wm[...], patch[...])

    def from_slots(at, owner):
        natural[owner, :] = work[at, :]

    reorder(from_slots)
    half_side = side >> 1
    for tile in range(2):
        at = slice(128 * tile, 128 * tile + 128)
        i, j = key_place(iota((1, 128), 1) + 128 * tile)
        mask = jnp.where((i < half_side) & (j < half_side), 1.0, 0.0)
        values = natural[:, at] + bias
        mean = jnp.mean(values, axis=0, keepdims=True)
        centred = values - mean
        rstd = lax.rsqrt(jnp.mean(centred * centred, axis=0, keepdims=True) + EPS)
        hat = centred * rstd
        four[:, at] = ((hat * gain + shift) * mask).astype(BF16)
        grad = cot[:, at].astype(F32) * mask
        low = norm_back(grad, hat, rstd, gain).astype(BF16)
        natural[:, at] = low.astype(F32)
        parts = (grad * hat, grad, low.astype(F32))
        sums = parts if tile == 0 else [s + v for s, v in zip(sums, parts)]
    put_column(grads, G_M, lane_sum(sums[0]))
    put_column(grads, C_M, lane_sum(sums[1]))
    put_column(grads, B_M, lane_sum(sums[2]))

    def to_slots(at, owner):
        mg[at, :] = natural[owner, :].astype(BF16)

    reorder(to_slots)

    def widths(body):
        loop(11, lambda c: body(pl.multiple_of(c * 256, 256), 256))
        body(11 * 256, 128)

    def patch_grad(start, width):
        back[pl.ds(start, width), :] = dot_tn(wm[:, pl.ds(start, width)], mg[...])


    def give(start, width):
        block = dot_nt(mg[...], patch[pl.ds(start, width), :]).astype(BF16)
        for c in range(width // 128):
            to = pl.ds(pl.multiple_of((start >> 3) + 16 * c, 16), 16)
            part = block[:, 128 * c : 128 * c + 128].reshape(32, 16, 128)
            keep[:, to, :] = part[0:16]
            send[:, to, :] = part[16:32]

    def both(start, width):
        patch_grad(start, width)
        give(start, width)

    widths(both)

    def piece(n):
        return [back[D * n : D * n + D, 128 * half : 128 * half + 128] for half in range(2)]

    results = (
        piece(4),
        plus(piece(5), times(right_of(piece(3)), j_last)),
        plus(piece(7), below(piece(1), i_last)),
        plus(
            piece(8),
            times(right_of(piece(6)), j_last),
            below(plus(piece(2), times(right_of(piece(0)), j_last)), i_last),
        ),
    )
    for n, values in enumerate(results):
        for half in range(2):
            end_grad[:, 256 * n + 128 * half : 256 * n + 128 * half + 128] = values[half]
    gain = column(bt, G_S, 5)
    zeros = jnp.zeros((D, 128), F32)

    def one(tile):
        at = lanes(tile)
        mask = token_mask(tile, side)
        grad = end_grad[:, at] * mask
        hat = (end[:, at] - stats[0:1, at]) * stats[1:2, at]
        result = norm_back(grad, hat, stats[1:2, at], gain)
        end_grad[:, at] = result
        low = (result * mask).astype(BF16)
        branch[:, at] = low
        return grad * hat, grad, low.astype(F32)

    def body(step, carry):
        pairs = zip(carry, one(2 * step), one(2 * step + 1))
        return tuple(total + (x + y) for total, x, y in pairs)

    sums = lax.fori_loop(0, 4, body, (zeros, zeros, zeros))
    put_column(grads, G_S, lane_sum(sums[0]))
    put_column(grads, C_S, lane_sum(sums[1]))
    put_column(grads, B_2, lane_sum(sums[2]))


def ffn_back_kernel(first_part, count, scal, w1, w2t, taps, sec, slope, branch, hg, dkx, hid_a, hid_b, cg_a, cg_b):
    start, steps = 256 * first_part, 4 * count
    j_first, j_last, i_first, i_last = edge_masks()
    lane = iota((16, 128), 1)

    def fill(hid, cg, step):
        rows = pl.ds(pl.multiple_of(start + jnp.minimum(step, steps - 1) * 64, 64), 64)
        cg[...] = dot(w2t[rows, :], branch[...]) * slope[rows, :].astype(F32)
        hid[...] = dot(w1[rows, :], sec[...])

    def group(hid, cg, step, index):
        rows = slice(16 * index, 16 * index + 16)
        from_rows = pl.ds(pl.multiple_of(start + 64 * step + 16 * index, 16), 16)
        to_rows = pl.ds(pl.multiple_of(64 * step + 16 * index, 16), 16)
        k = [taps[n, from_rows, :] for n in range(9)]
        quad = quads(cg, rows)
        bias = functools.reduce(lambda x, y: x + y, [t for row in quad for pair in row for t in pair])
        across = [
            (
                (times(left_of(quad[a][1]), j_first), quad[a][0], quad[a][1]),
                (quad[a][0], quad[a][1], times(right_of(quad[a][0]), j_last)),
            )
            for a in range(2)
        ]
        sums = [None] * 9
        for e in range(2):
            upper = [above(tiles, i_first) for tiles in across[1][e]]
            lower = [below(tiles, i_last) for tiles in across[0][e]]
            for a, near in ((0, (upper, across[0][e], across[1][e])), (1, (across[0][e], across[1][e], lower))):
                for half in range(2):
                    value = hid[rows, tile_at(a, e, half)]
                    total = None
                    for r in range(3):
                        for c in range(3):
                            tap = 3 * (2 - r) + (2 - c)
                            term = k[tap] * near[r][c][half]
                            total = term if total is None else total + term
                            term = value * near[r][c][half]
                            sums[tap] = term if sums[tap] is None else sums[tap] + term
                    hg[to_rows, tile_at(a, e, half)] = total.astype(BF16)
        table = jnp.where(lane == 9, lane_sum(bias), 0.0)
        for n in range(9):
            table = jnp.where(lane == n, lane_sum(sums[n]), table)
        dkx[to_rows, :] = table

    fill(hid_a, cg_a, 0)

    def two(index):
        fill(hid_b, cg_b, 2 * index + 1)
        for n in range(4):
            group(hid_a, cg_a, 2 * index, n)
        fill(hid_a, cg_a, 2 * index + 2)
        for n in range(4):
            group(hid_b, cg_b, 2 * index + 1, n)

    loop(steps // 2, two)


def middle_back_kernel(scal, bt, w1t, hg0, hg1, end_grad, mid, stats, mid_grad, low_grad, grads, work):
    side = scal[1]
    work[...] = sum(
        dot(w1t[:, 256 * at : 256 * (at + count)], hg[...]) for hg, (at, count) in zip((hg0, hg1), PARTS)
    )
    grads[...] = jnp.zeros_like(grads)
    gain = column(bt, G_2, 5)
    zeros = jnp.zeros((D, 128), F32)

    def one(tile):
        at = lanes(tile)
        mask = token_mask(tile, side)
        grad = work[:, at] * mask
        hat = (mid[:, at] - stats[0:1, at]) * stats[1:2, at]
        result = end_grad[:, at] + norm_back(grad, hat, stats[1:2, at], gain)
        mid_grad[:, at] = result
        low = (result * mask).astype(BF16)
        low_grad[:, at] = low
        return grad * hat, grad, low.astype(F32)

    def body(step, carry):
        pairs = zip(carry, one(2 * step), one(2 * step + 1))
        return tuple(total + (x + y) for total, x, y in pairs)

    sums = lax.fori_loop(0, 4, body, (zeros, zeros, zeros))
    put_column(grads, G_2, lane_sum(sums[0]))
    put_column(grads, C_2, lane_sum(sums[1]))
    put_column(grads, B_O, lane_sum(sums[2]))


def pack_b_kernel(scal, to_tens, hg0, hg1, dk0, dk1, sec, branch, act, keep, send, grads, dw1, gather, mixed):
    me = scal[0]
    grads[...] = jnp.zeros_like(grads)
    lane = iota((256, 128), 1)
    for hg, dkx, (at, count) in zip((hg0, hg1), (dk0, dk1), PARTS):

        def outer(n, hg=hg, dkx=dkx, at=at):
            rows = pl.ds(pl.multiple_of(256 * n, 256), 256)
            to = pl.ds(pl.multiple_of(256 * (n + at), 256), 256)
            part = dot_nt(hg[rows, :], sec[...])
            dw1[to, 0:256] = part[:, 0:256]
            turned = pltpu.roll(dkx[rows, :], 64, 1)
            dw1[to, 256:384] = jnp.where(lane < 64, part[:, 256:384], jnp.where(lane < 73, turned, 0.0))
            table = grads[...]
            for m in range(4):
                here = slice(64 * m, 64 * m + 64)
                number = 4 * (n + at) + m
                table = jnp.where(lane[here] == B_1 + number, part[here, 329:330], table)
                table = jnp.where(lane[here] == B_DW + number, dkx[rows, :][here, 9:10], table)
            grads[...] = table

        loop(count, outer)
    mixed[...] = dot(to_tens[...], branch[...]).astype(BF16)
    gather[:, 0:24, :] = jnp.zeros((32, 24, 128), F32)

    def contraction(p):
        block = dot_nt(mixed[...], act[pl.ds(pl.multiple_of(256 * p, 256), 256), :])
        parts = [block[0:256, 128 * e : 128 * e + 128].reshape(32, 1, 8, 128) for e in range(2)]
        full = jnp.concatenate(parts, axis=1).reshape(32, 16, 128).astype(BF16)
        to = pl.ds(pl.multiple_of(16 * p, 16), 16)
        keep[:, to, :] = full[0:16]
        send[:, to, :] = full[16:32]
        tail = jnp.concatenate([block[256:320, 0:128], block[256:320, 128:256]], axis=0).astype(BF16)
        place = rest_row(iota((256, 1), 0)) - 128 * (p & 1)
        to = pl.ds(pl.multiple_of(8 * (p >> 1), 8), 8)
        gather[:, to, :] += dot(one_hot(iota((256, 128), 1) == place), tail).reshape(32, 8, 128)

    loop(5, contraction)

    def expansion(owner):
        slot = slot_of(owner ^ me)
        rows = pl.ds(pl.multiple_of(40 * owner, 8), 40)
        for c in range(3):
            gather[slot, 24 + 40 * c : 64 + 40 * c, :] = dw1[rows, 128 * c : 128 * c + 128]

    loop(32, expansion)
    keep[:, 80:224, :] = gather[0:16].astype(BF16)
    send[:, 80:224, :] = gather[16:32].astype(BF16)


def attend_back_kernel(scal, kt, vt, qs, kv, wo, low_grad, lse, dq, dkv, og, scores_a, scores_b, grads_a, grads_b, probs_a, probs_b, back_a, back_b):
    bias = key_bias(scal[1])
    og[...] = dot_tn(wo[...], low_grad[...]).astype(BF16)

    def score(scores, grads, h, start):
        at = slice(start, start + 512)
        scores[...] = dot(kt[h], qs[head_rows(h), at])
        grads[...] = dot(vt[h], og[head_rows(h), at])

    def finish(scores, grads, probs, back, h, start):
        for tile in range(4):
            at = slice(128 * tile, 128 * tile + 128)
            to = slice(start + 128 * tile, start + 128 * tile + 128)
            weights = jnp.exp(scores[:, at] + bias - lse[h, :, to])
            grad = grads[:, at]
            mean = jnp.sum(weights * grad, axis=0, keepdims=True)
            back[:, at] = (weights * (grad - mean)).astype(BF16)
            probs[:, at] = weights.astype(BF16)
        rows, at = head_rows(h), slice(start, start + 512)
        dq[rows, at] = (dot(kv[rows, :], back[...]) * 0.125).astype(BF16)
        return dot_nt(qs[rows, at], back[...]), dot_nt(og[rows, at], probs[...])

    score(scores_a, grads_a, 0, 0)

    def head(h):
        score(scores_b, grads_b, h, 512)
        one = finish(scores_a, grads_a, probs_a, back_a, h, 0)
        score(scores_a, grads_a, jnp.minimum(h + 1, HEADS - 1), 0)
        two = finish(scores_b, grads_b, probs_b, back_b, h, 512)
        dkv[head_rows(h), :] = (one[0] + two[0]).astype(BF16)
        dkv[pl.ds(pl.multiple_of(D + 64 * h, 64), 64), :] = (one[1] + two[1]).astype(BF16)

    loop(HEADS, head)


def first_kernel(scal, bt, to_tens, to_lower, to_upper, to_rest, wq, wkv, wrs, first, red, raw, stat_r, dq, dkv, low_grad, att, entry, stats, g_one, g_two, g_three, keep, send, work, grads, wide, redin, stack_r, stack_z, tails_of):
    me = scal[0]
    grads[...] = g_one[...] + g_two[...] + g_three[...]
    for quad in range(4):
        redin[D * quad : D * quad + D, :] = first[:, 256 * quad : 256 * quad + 256]
    dred = dot_tn(wkv[...], dkv[...])
    gain = column(bt, G_R, 5)
    lows = []
    for tile in range(2):
        at = slice(128 * tile, 128 * tile + 128)
        grad = dred[:, at]
        hat = (raw[:, at] - stat_r[0:1, at]) * stat_r[1:2, at]
        low = norm_back(grad, hat, stat_r[1:2, at], gain).astype(BF16)
        lows.append(low)
        parts = (grad * hat, grad, low.astype(F32))
        sums = parts if tile == 0 else [s + v for s, v in zip(sums, parts)]
    put_column(grads, G_R, lane_sum(sums[0]))
    put_column(grads, C_R, lane_sum(sums[1]))
    put_column(grads, B_R, lane_sum(sums[2]))
    low = jnp.concatenate(lows, axis=1)
    low = dot(to_tens[...], low).astype(BF16)
    wide[...] = dot_tn(wrs[...], low)
    straight = dot_tn(wq[...], dq[...])
    for quad in range(4):
        at = slice(256 * quad, 256 * quad + 256)
        work[:, at] = straight[:, at] + wide[D * quad : D * quad + D, :]
    zeros = jnp.zeros((D, 128), F32)

    def one(tile):
        at = lanes(tile)
        grad = work[:, at]
        hat = (entry[:, at].astype(F32) - stats[0:1, at]) * stats[1:2, at]
        return grad * hat, grad, dq[:, at].astype(F32)

    def body(step, carry):
        pairs = zip(carry, one(2 * step), one(2 * step + 1))
        return tuple(total + (x + y) for total, x, y in pairs)

    sums = lax.fori_loop(0, 4, body, (zeros, zeros, zeros))
    put_column(grads, G_1, lane_sum(sums[0]))
    put_column(grads, C_1, lane_sum(sums[1]))
    put_column(grads, B_Q, lane_sum(sums[2]))
    stack_r[...] = dot_nt(low, redin[...])

    def outer(pick, grad, value):
        return dot_nt(dot(pick[...], grad[...]).astype(BF16), value[...])

    parts = (
        outer(to_tens, dq, first),
        outer(to_lower, dkv, red),
        outer(to_upper, dkv, red),
        outer(to_tens, low_grad, att),
    )
    for part, at in zip(parts, (0, 256, 512, 1024)):
        stack_z[:, at : at + 256] = part[:, 0:256]
    stack_z[:, 768:1024] = jnp.concatenate([part[:, 256:320] for part in parts], axis=1)

    def pack(p):
        at = lanes(p, 256)
        both = stack_r[:, at], stack_z[:, at]
        for e in range(2):
            pieces = [block[0:256, 128 * e : 128 * e + 128].reshape(32, 1, 8, 128) for block in both]
            full = jnp.concatenate(pieces, axis=1).reshape(32, 16, 128).astype(BF16)
            to = pl.ds(pl.multiple_of(32 * p + 16 * e, 16), 16)
            keep[:, to, :] = full[0:16]
            send[:, to, :] = full[16:32]
        tail = jnp.concatenate(
            [block[256:320, 128 * e : 128 * e + 128] for block in both for e in range(2)], axis=0
        ).astype(BF16)
        to = pl.ds(pl.multiple_of(8 * p, 8), 8)
        tails_of[:, to, :] = dot(to_rest[...], tail).reshape(32, 8, 128)

    loop(5, pack)
    rows = jnp.transpose(jnp.concatenate([grads[...], jnp.zeros((64, 128), F32)], axis=0)).astype(BF16)
    place = iota((256, 128), 0)
    vector = iota((256, 128), 1)
    line = place & 7
    owner = xor_of(place >> 3) ^ me
    start = (7 * owner) >> 3
    straight = (
        ((line == 0) & (vector == 3 * owner))
        | ((line == 1) & (vector == 3 * owner + 2))
        | ((line == 2) & (vector == 96 + start))
    )
    turned = ((line == 0) & (vector == 3 * owner + 1)) | ((line == 2) & (vector == 97 + start))
    small = dot(one_hot(straight), rows) + pltpu.roll(dot(one_hot(turned), rows), 64, 1)
    tails_of[:, 40:48, :] = small.reshape(32, 8, 128)
    keep[:, 160:208, :] = tails_of[0:16].astype(BF16)
    send[:, 160:208, :] = tails_of[16:32].astype(BF16)


def token_kernel(scal, bt, turned, grad_in, mid_grad, entry, stats, tok, high, rest):
    side = scal[1]
    gain = column(bt, G_1, 5)

    def body(tile):
        at = lanes(tile)
        hat = (entry[:, at].astype(F32) - stats[0:1, at]) * stats[1:2, at]
        result = mid_grad[:, at] + norm_back(grad_in[:, at], hat, stats[1:2, at], gain)
        result = result * token_mask(tile, side)
        upper = result.astype(BF16)
        high[:, at] = upper
        rest[:, at] = (result - upper.astype(F32)).astype(BF16)

    loop(8, body)

    def quad(index):
        pick = turned[pl.ds(pl.multiple_of(256 * index, 256), 256), :]
        tok[:, lanes(index, 256)] = dot_nt(high[...], pick) + dot_nt(rest[...], pick)

    loop(4, quad)


def cost(micros):
    return pl.CostEstimate(flops=int(micros * 1e9), bytes_accessed=1000, transcendentals=0)


def call(kernel, args, outs, scratch=(), micros=5):
    return pl.pallas_call(
        kernel,
        in_specs=[pl.BlockSpec(memory_space=pltpu.SMEM if arg.dtype == I32 else pltpu.VMEM) for arg in args],
        out_shape=[jax.ShapeDtypeStruct(shape, dtype) for shape, dtype in outs],
        scratch_shapes=[pltpu.VMEM(shape, dtype) for shape, dtype in scratch],
        compiler_params=pltpu.CompilerParams(vmem_limit_bytes=VMEM_LIMIT),
        cost_estimate=cost(micros),
    )(*args)


def local(group, axes, *arrays):
    return step_of(group, axes, *arrays)


def step_of(group, axes, tokens, image_side, cotangent, *shards):
    index = lax.axis_index(axes[0]) * lax.axis_size(axes[1]) + lax.axis_index(axes[1])
    me = index // group
    devices = SUPER * group

    def flip(values, mask):
        pairs = [(i, ((i // group) ^ mask) * group + i % group) for i in range(devices)]
        return lax.ppermute(values, axes, pairs)

    def gather(block, split=0, direct=False):
        held = block[None]
        if direct:
            held = jnp.concatenate([held, flip(held, 2), flip(held, 4), flip(held, 6)], axis=0)
        else:
            for mask in FLIPS[:2]:
                held = jnp.concatenate([held, flip(held, mask)], axis=0)
        if split:
            one, two = held[:, :split], held[:, split:]
            one, two = (jnp.concatenate([one, flip(one, 8)], axis=0), jnp.concatenate([two, flip(two, 16)], axis=0))
            far, near = flip(one, 16), flip(two, 8)
            two = jnp.concatenate([two[:4], near[:4], two[4:], near[4:]], axis=0)
            held = jnp.concatenate([jnp.concatenate([one, far], axis=0), two], axis=1)
        else:
            for mask in FLIPS[2:]:
                held = jnp.concatenate([held, flip(held, mask)], axis=0)
        return held, flip(held, 1)

    def scatter(keep, send, split=0, direct=False):
        def step(held, mask):
            return flip(held, mask).astype(F32)

        def halve(held, mask):
            half = held.shape[0] // 2
            return held[:half].astype(F32) + step(held[half:], mask)

        held = (keep.astype(F32) + step(send, 1)).astype(BF16)
        if split:
            one, two = held[:, :split], held[:, split:].reshape(2, 2, 4, -1, 128)
            one, two = (
                halve(one, 16).astype(BF16),
                (two[:, 0].astype(F32) + step(two[:, 1], 8)).astype(BF16).reshape(8, -1, 128),
            )
            held = jnp.concatenate([halve(one, 8), halve(two, 16)], axis=1).astype(BF16)
        else:
            held = halve(held, 16).astype(BF16)
            held = halve(held, 8).astype(BF16)
        if direct:
            far = step(held[2:3], 4), step(held[3:4], 6), step(held[1:2], 2)
            return (held[0:1].astype(F32) + far[2] + far[0] + far[1])[0]
        held = halve(held, 4).astype(BF16)
        return halve(held, 2)[0]

    if group > 1:
        per = lax.axis_size(axes[1])
        start = (index % per) // group * group

        def join(shard):
            full = lax.all_gather(shard, axes[1], axis=0)
            return lax.dynamic_slice_in_dim(full, start, group, axis=0).reshape(-1)

        shards = [join(shard) for shard in shards]
    query, keyval, reduce_w, output, expand, depth, contract, merge, gains, biases = shards

    def rows(flat):
        return flat.reshape(-1, 128)

    scal = jnp.stack([me.astype(I32), image_side[0].astype(I32)])
    taps = jnp.pad(depth.reshape(40, 9), ((0, 0), (64, 55)))
    block_a = select(
        [rows(query), rows(output), rows(keyval), rows(reduce_w)],
        table_a, A_ROWS, (scal, biases[None], gains[None]),
    )
    block_b = select([rows(contract), rows(expand), taps], table_b, B_ROWS)
    block_c = select([rows(merge)], table_c, C_ROWS)
    a_low, a_high = gather(block_a, A_SPLIT, True)
    b_low, b_high = gather(block_b, B_ROWS // 2, True)
    c_low, c_high = gather(block_c, C_ROWS // 2)

    big, narrow = (D, TOKENS), (D, QUARTER)
    from_tens, to_tens, from_lower, from_upper, to_lower, to_upper, from_rest, to_rest = call(
        orders_kernel,
        (scal,),
        [((D, D), BF16)] * 2 + [((2 * D, D), BF16)] * 2 + [((D, 2 * D), BF16)] * 2 + [((256, 256), BF16)] * 2,
        micros=2,
    )
    entry, stats_1, turned = call(
        entry_kernel, (scal, tokens[0]), [(big, BF16), ((8, TOKENS), F32), ((TOKENS, TOKENS), BF16)], micros=3.5)
    wq, wkv, wr, wo, first, qs, raw, stat_r, red, kv, kt, vt, bt = call(
        project_kernel,
        (scal, from_tens, from_lower, from_upper, from_rest, a_low, a_high, entry, stats_1),
        [
            ((D, D), BF16), ((2 * D, D), BF16), ((D, 4 * D), BF16), ((D, D), BF16), (big, BF16), (big, BF16),
            (narrow, F32), ((8, QUARTER), F32), (narrow, BF16), ((2 * D, QUARTER), BF16),
            ((HEADS, QUARTER, 64), BF16), ((HEADS, QUARTER, 64), BF16), ((64, 128), F32),
        ],
        [((D, 1280), BF16), ((256, 640), BF16), ((4 * D, QUARTER), BF16)],
        micros=8,
    )
    att, lse = call(attend_kernel, (scal, kt, qs, kv), [(big, BF16), ((HEADS, 1, TOKENS), F32)],
        [((QUARTER, 512), F32)] * 2 + [((QUARTER, 512), BF16)] * 2, micros=8.5)
    mid, sec, stats_2 = call(
        middle_kernel, (scal, bt, wo, att, entry), [(big, F32), ((384, TOKENS), BF16), ((8, TOKENS), F32)], [(big, F32)],
        micros=5,
    )
    w1, w1t, w2, w2t, taps = call(
        ffn_weights_kernel,
        (scal, bt, from_tens, from_rest, b_low, b_high),
        [((FF, 384), BF16), ((D, FF), BF16), ((D, FF), BF16), ((FF, D), BF16), ((10, FF, 128), F32)],
        [((D, FF), BF16), ((256, 384), BF16), ((FF, 384), F32)],
        micros=8,
    )
    act, slope = call(
        ffn_kernel,
        (scal, w1, taps, sec),
        [((FF, TOKENS), BF16), ((FF, TOKENS), BF16)],
        [((64, TOKENS), F32), ((64, TOKENS), F32)],
        micros=17,
    )
    end, sect, stats_s = call(
        ending_kernel, (scal, bt, w2, act, mid), [(big, F32), (big, BF16), ((8, TOKENS), F32)], [(big, F32)], micros=5
    )
    four, c_keep, c_send, end_grad, branch, g_one = call(
        merge_kernel,
        (scal, bt, c_low, c_high, sect, end, stats_s, cotangent[0]),
        [
            ((OUT_D, QUARTER), BF16), ((16, C_ROWS, 128), BF16), ((16, C_ROWS, 128), BF16), (big, F32), (big, BF16),
            ((64, 128), F32),
        ],
        [
            ((OUT_D, MERGE_PAD), BF16), ((MERGE_PAD, QUARTER), BF16), ((OUT_D, QUARTER), BF16),
            ((MERGE_PAD, QUARTER), F32), ((OUT_D, QUARTER), F32), ((OUT_D, QUARTER), F32),
        ],
        micros=20,
    )
    sum_c = scatter(c_keep, c_send, C_ROWS // 2)
    hgs, dks = [], []
    for at, count in PARTS:
        hg, dk = call(
            functools.partial(ffn_back_kernel, at, count),
            (scal, w1, w2t, taps, sec, slope, branch),
            [((256 * count, TOKENS), BF16), ((256 * count, 128), F32)],
            [((64, TOKENS), F32)] * 4,
            micros=6 * count,
        )
        hgs.append(hg)
        dks.append(dk)
    b_keep, b_send, g_three = call(
        pack_b_kernel,
        (scal, to_tens, *hgs, *dks, sec, branch, act),
        [((16, B_ROWS, 128), BF16), ((16, B_ROWS, 128), BF16), ((64, 128), F32)],
        [((FF, 384), F32), ((32, 144, 128), F32), (big, BF16)],
        micros=9,
    )
    sum_b = scatter(b_keep, b_send, B_ROWS // 2, True)
    mid_grad, low_grad, g_two = call(
        middle_back_kernel,
        (scal, bt, w1t, *hgs, end_grad, mid, stats_2),
        [(big, F32), (big, BF16), ((64, 128), F32)],
        [(big, F32)],
        micros=6,
    )
    dq, dkv = call(
        attend_back_kernel,
        (scal, kt, vt, qs, kv, wo, low_grad, lse),
        [(big, BF16), ((2 * D, QUARTER), BF16)],
        [(big, BF16)] + [((QUARTER, 512), F32)] * 4 + [((QUARTER, 512), BF16)] * 4,
        micros=9,
    )
    a_keep, a_send, first_grad = call(
        first_kernel,
        (
            scal, bt, to_tens, to_lower, to_upper, to_rest, wq, wkv, wr, first, red, raw, stat_r, dq, dkv, low_grad, att, entry, stats_1, g_one, g_two, g_three,
        ),
        [((16, A_ROWS, 128), BF16), ((16, A_ROWS, 128), BF16), (big, F32)],
        [
            ((64, 128), F32), ((4 * D, QUARTER), F32), ((4 * D, QUARTER), BF16), ((D, 1280), F32), ((D, 1280), F32),
            ((32, 48, 128), F32),
        ],
        micros=11,
    )
    sum_a = scatter(a_keep, a_send, A_SPLIT, True)
    (token_grad,) = call(
        token_kernel,
        (scal, bt, turned, first_grad, mid_grad, entry, stats_1),
        [(big, F32)],
        [(big, BF16), (big, BF16)],
        micros=5,
    )
    if group > 1:

        def total(part):
            full = lax.all_gather(part, axes[1], axis=0)
            return jnp.sum(lax.dynamic_slice_in_dim(full, start, group, axis=0), axis=0)

        sum_a, sum_b, sum_c = total(sum_a), total(sum_b), total(sum_c)

    def flat(count):
        return (count, 128), F32

    query_g, output_g, keyval_g, reduce_g, biases_g, gains_g = call(
        out_a_kernel,
        (scal, sum_a),
        [flat(25), flat(25), flat(50), flat(100), ((1, 192), F32), ((1, 56), F32)],
        micros=1,
    )
    contract_g, expand_g = call(out_b_kernel, (scal, sum_b), [flat(100), flat(100)], micros=1)
    (merge_g,) = call(out_c_kernel, (scal, sum_c), [flat(360)], micros=1)
    depth_g = sum_b[184:224, 64:73]
    grads = [query_g, keyval_g, reduce_g, output_g, expand_g, depth_g, contract_g, merge_g, gains_g, biases_g]
    grads = [grad.reshape(-1) for grad in grads]
    if group > 1:
        mine = index % group
        grads = [lax.dynamic_index_in_dim(grad.reshape(group, -1), mine, keepdims=False) for grad in grads]
    return (four[None], token_grad[None], *grads)


def solution(mesh):
    axes = ("dp", "fs")
    devices = mesh.shape["dp"] * mesh.shape["fs"]
    group = devices // SUPER
    if devices != SUPER * group or mesh.shape["fs"] % group:
        raise ValueError("unsupported mesh")
    one, three = P(axes), P(axes, None, None)
    return jax.shard_map(
        functools.partial(local, group, axes),
        mesh=mesh,
        in_specs=(three, one, three) + (one,) * 10,
        out_specs=(three, three) + (one,) * 10,
        check_vma=False,
    )
```

```python
import functools

import jax
import jax.numpy as jnp
import numpy as np
from jax import lax
from jax.experimental import pallas as pl
from jax.experimental.pallas import tpu as pltpu
from jax.sharding import PartitionSpec as P


D = 320
HEADS = 5
FF = 1280
OUT_D = 512
SIDE = 32
QUARTER = 256
TOKENS = SIDE * SIDE
MERGE_PAD = 2944
SUPER = 32
FLIPS = (2, 4, 8, 16)
EPS = 1e-06
F32, BF16, I32 = jnp.float32, jnp.bfloat16, jnp.int32

B_Q, B_R, C_R, B_O, C_1, C_2, B_1, B_DW, B_2, C_S, B_M, C_M = 0, 5, 10, 15, 20, 25, 30, 50, 70, 75, 80, 88
G_R, G_1, G_2, G_S, G_M = 96, 101, 106, 111, 116

PARTS = ((0, 1), (1, 4))
A_ROWS, B_ROWS, C_ROWS = 208, 224, 368
SMALL_ROW = 200
A_SPLIT = 104
VMEM_LIMIT = 24 * 1024 * 1024
VMEM_ALL = 60 * 1024 * 1024


def slot_of(xor):
    return (xor >> 1) | ((xor & 1) << 4)


def xor_of(slot):
    return ((slot & 15) << 1) | (slot >> 4)


def dot(a, b):
    return jnp.dot(a, b, preferred_element_type=F32)


def dot_nt(a, b):
    return lax.dot_general(a, b, (((1,), (1,)), ((), ())), preferred_element_type=F32)


def dot_tn(a, b):
    return lax.dot_general(a, b, (((0,), (0,)), ((), ())), preferred_element_type=F32)


def iota(shape, axis):
    return lax.broadcasted_iota(I32, shape, axis)


def one_hot(test):
    return jnp.where(test, 1.0, 0.0).astype(BF16)


def lanes(index, width=128):
    if isinstance(index, int):
        return slice(index * width, (index + 1) * width)
    return pl.ds(pl.multiple_of(index * width, width), width)


def loop(count, body):
    def step(index, carry):
        body(index)
        return carry

    lax.fori_loop(0, count, step, 0)


def column(table, start, count):
    return jnp.concatenate(
        [jnp.broadcast_to(table[:, h : h + 1], (64, 128)) for h in range(start, start + count)], axis=0
    )


def put_column(table, start, values):
    for h in range(values.shape[0] // 64):
        table[:, start + h : start + h + 1] = values[64 * h : 64 * h + 64, 0:1]


def token_place(lane):
    quad = lane >> 8
    row = 2 * ((lane >> 4) & 15) + (quad >> 1)
    col = 2 * (lane & 15) + (quad & 1)
    return row, col


def token_mask(tile, side, width=128):
    row, col = token_place(iota((1, width), 1) + tile * width)
    return jnp.where((row < side) & (col < side), 1.0, 0.0)


def key_place(index):
    return index >> 4, index & 15


def select_kernel(count, bases, small, small_at, *refs):
    sources, refs = refs[:count], refs[count:]
    if small:
        scal, biases, gains = refs[:3]
        refs = refs[3:]
    low_ref, high_ref, out, rows_ref, sems = refs[:5]
    held = refs[5:]
    copies = [
        pltpu.make_async_copy(source, place, sems.at[n]) for n, (source, place) in enumerate(zip(sources, held))
    ]
    for copy in copies:
        copy.start()
    half = rows_ref.shape[0] // 2
    rows_ref[...] = jnp.zeros_like(rows_ref)
    place = iota((out.shape[0], 2 * half), 1)
    pick_low = one_hot(place == low_ref[...])
    pick_high = one_hot(place == high_ref[...])
    for copy in copies:
        copy.wait()
    for source, base in zip(held, bases):
        rows_ref[base : base + source.shape[0], :] = source[...].astype(F32)
    if small:
        rows_ref[small_at : small_at + 1, :] = biases[:, 0:128].astype(F32)
        rows_ref[small_at + 1 : small_at + 2, 0:64] = biases[:, 128:192].astype(F32)
        wide = jnp.concatenate([gains[...].astype(F32), jnp.zeros((1, 72), F32)], axis=1)
        wide = jnp.broadcast_to(wide, (8, 128))
        rows_ref[small_at + 2 : small_at + 3, :] = pltpu.roll(wide, (56 * scal[0]) & 63, 1)[0:1, :]
    rows_ref[half:, :] = pltpu.roll(rows_ref[0:half, :], 64, 1)
    total = rows_ref[...].astype(BF16)
    low, upper = dot(pick_low, total), dot(pick_high, total)
    out[...] = jnp.where(iota((out.shape[0], 128), 1) < 64, low, upper).astype(BF16)


def select(sources, table, rows, vectors=()):
    bases, at = [], 0
    for source in sources:
        bases.append(at)
        at += -(-source.shape[0] // 16) * 16
    small = len(vectors) > 0
    half = at + (16 if small else 0)
    low, high = table(bases + [at], half).astype(np.int32)[:, :, None]
    specs = [pl.BlockSpec(memory_space=pltpu.HBM)] * len(sources)
    if small:
        specs += [pl.BlockSpec(memory_space=pltpu.SMEM)] + [pl.BlockSpec(memory_space=pltpu.VMEM)] * 2
    specs += [pl.BlockSpec(memory_space=pltpu.VMEM)] * 2
    return pl.pallas_call(
        functools.partial(select_kernel, len(sources), tuple(bases), small, at),
        in_specs=specs,
        out_shape=jax.ShapeDtypeStruct((rows, 128), BF16),
        scratch_shapes=[pltpu.VMEM((2 * half, 128), F32), pltpu.SemaphoreType.DMA((len(sources),))]
        + [pltpu.VMEM(source.shape, source.dtype) for source in sources],
        compiler_params=pltpu.CompilerParams(vmem_limit_bytes=VMEM_ALL if small else VMEM_LIMIT),
        cost_estimate=cost(2),
    )(*sources, *vectors, low, high)


def pair(half, low_src, high_src):
    low = -1 if low_src is None else low_src[0] + low_src[1] // 2 + half * (low_src[1] % 2)
    high = -1 if high_src is None else high_src[0] + high_src[1] // 2 + half * (1 - high_src[1] % 2)
    return low, high


def chunk_sources(bases, row, c):
    q, o, kv = bases
    if c < 6 or c >= 8:
        base, first = ((q, 0), (kv, 0), (kv, 10), None, (o, 0))[c // 2]
        at = 5 * (first + row) + 2 * (c % 2)
        return (base, at), (base, at + 1)
    if c == 6:
        return (q, 5 * row + 4), (kv, 5 * row + 4)
    return (kv, 5 * (10 + row) + 4), (o, 5 * row + 4)


def a_place(kind, row, c):
    if row < 8:
        return 16 * c + 8 * kind + row
    return 160 + 8 * (c // 2) + 4 * kind + 2 * (c % 2) + row - 8


def b_place(row, c):
    if row < 8:
        return 8 * c + row
    return 80 + 8 * (c // 4) + 2 * (c % 4) + row - 8


def table_a(bases, half):
    q, o, kv, r, small = bases
    rows = [(-1, -1)] * A_ROWS
    for c in range(10):
        for row in range(10):
            at = 20 * row + 2 * c
            rows[a_place(0, row, c)] = pair(half, (r, at), (r, at + 1))
            rows[a_place(1, row, c)] = pair(half, *chunk_sources((q, o, kv), row, c))
    for row in range(3):
        rows[SMALL_ROW + row] = pair(half, (small, 2 * row), (small, 2 * row + 1))
    return np.array(rows).T


def table_b(bases, half):
    w2, w1, dw, _ = bases
    rows = [(-1, -1)] * B_ROWS
    for c in range(10):
        for row in range(10):
            at = 20 * row + 2 * c
            rows[b_place(row, c)] = pair(half, (w2, at), (w2, at + 1))
    for c in range(3):
        for row in range(40):
            at = 5 * row + 2 * c
            rows[104 + 40 * c + row] = pair(half, (w1, at), (w1, at + 1) if c < 2 else (dw, 2 * row + 1))
    return np.array(rows).T


def table_c(bases, half):
    m, _ = bases
    rows = []
    for c in range(23):
        for row in range(16):
            at = 45 * row + 2 * c
            rows.append(pair(half, (m, at), (m, at + 1) if c < 22 else None))
    return np.array(rows).T


def turn(rows):
    return pltpu.roll(rows, 64, 1)


def halves(low, high):
    return jnp.where(iota((1, 128), 1) < 64, low, high)


def put_rows(out, first, count, stride, rows):
    out[pl.ds(first, count, stride=stride), :] = rows


def put_320(out, first, count, load):
    even, odd = ([load(chunk, parity) for chunk in range(3)] for parity in range(2))
    turned = [turn(rows) for rows in odd]
    for at, rows in enumerate(
        (even[0], even[1], halves(even[2], turned[0]), halves(turned[0], turned[1]), halves(turned[1], turned[2]))
    ):
        put_rows(out, first + at, count // 2, 5, rows)


def every_other(ref, start, count):
    return ref[pl.ds(start, count, stride=2), :]


def out_a_kernel(scal, sums, q, o, kv, r, biases, gains):
    squares = (
        (q, 0, (0, 1, 6), False),
        (o, 0, (8, 9, 7), True),
        (kv, 0, (2, 3, 6), True),
        (kv, 25, (4, 5, 7), False),
    )
    for out, first, chunks, high in squares:
        for start, count, lane_row in ((0, 8, 0), (8, 2, 20)):

            def load(chunk, parity, chunks=chunks, high=high, start=start, count=count):
                rows = every_other(sums, a_place(1, start, chunks[chunk]) + parity, count // 2)
                return turn(rows) if chunk == 2 and high else rows

            put_320(out, first + lane_row, count, load)
    for c in range(10):
        for start, count in ((0, 8), (8, 2)):
            put_rows(r, 10 * start + c, count, 10, sums[pl.ds(a_place(0, start, c), count), :])
    small = sums[SMALL_ROW : SMALL_ROW + 8, :]
    biases[:, 0:128] = small[0:1]
    biases[:, 128:192] = small[1:2, 0:64]
    gains[...] = pltpu.roll(small, (128 - ((56 * scal[0]) & 63)) & 127, 1)[2:3, 0:56]


def out_b_kernel(scal, sums, w2, w1):
    for c in range(10):
        for start, count in ((0, 8), (8, 2)):
            put_rows(w2, 10 * start + c, count, 10, sums[pl.ds(b_place(start, c), count), :])
    put_320(w1, 0, 40, lambda chunk, parity: every_other(sums, 104 + 40 * chunk + parity, 20))


def out_c_kernel(scal, sums, m):
    even = [every_other(sums, 16 * c, 8) for c in range(23)]
    turned = [turn(every_other(sums, 16 * c + 1, 8)) for c in range(23)]
    for c in range(22):
        put_rows(m, c, 8, 45, even[c])
        put_rows(m, 23 + c, 8, 45, halves(turned[c], turned[c + 1]))
    put_rows(m, 22, 8, 45, halves(even[22], turned[0]))


def split_ten(row, per, magic):
    owner = (row * magic) >> 16
    return owner, row - per * owner


def tens(row, me):
    owner, rest = split_ten(row, 10, 6554)
    slot = slot_of(owner ^ me)
    return jnp.where(rest < 8, slot * 8 + rest, 248 + slot * 2 + rest)


def keyval_tens(row, me, upper):
    owner, rest = split_ten(row, 20, 3277)
    inside = (rest >= 10) if upper else (rest < 10)
    return jnp.where(inside, tens(10 * owner + rest - (10 if upper else 0), me), -1)


def rest_row(row):
    return 64 * ((row & 7) >> 1) + 2 * (row >> 3) + (row & 1)


def orders_kernel(scal, from_tens, to_tens, from_lower, from_upper, to_lower, to_upper, from_rest, to_rest):
    me = scal[0]
    from_tens[...] = one_hot(iota((D, D), 1) == tens(iota((D, 1), 0), me))
    to_tens[...] = one_hot(iota((D, D), 0) == tens(iota((1, D), 1), me))
    for upper, down, up in ((False, from_lower, to_lower), (True, from_upper, to_upper)):
        down[...] = one_hot(iota((2 * D, D), 1) == keyval_tens(iota((2 * D, 1), 0), me, upper))
        up[...] = one_hot(iota((D, 2 * D), 0) == keyval_tens(iota((1, 2 * D), 1), me, upper))
    from_rest[...] = one_hot(iota((256, 256), 0) == rest_row(iota((1, 256), 1)))
    to_rest[...] = one_hot(iota((256, 256), 1) == rest_row(iota((256, 1), 0)))


def norm(values, gain, shift):
    mean = jnp.mean(values, axis=0, keepdims=True)
    centred = values - mean
    rstd = lax.rsqrt(jnp.mean(centred * centred, axis=0, keepdims=True) + EPS)
    return centred * rstd * gain + shift, mean, rstd


def norm_back(grad, hat, rstd, gain):
    scaled = grad * gain
    return rstd * (
        scaled
        - jnp.mean(scaled, axis=0, keepdims=True)
        - hat * jnp.mean(scaled * hat, axis=0, keepdims=True)
    )


def stat_rows(mean, rstd):
    row = iota((8, mean.shape[1]), 0)
    return jnp.where(row == 0, mean, jnp.where(row == 1, rstd, 0.0))


def entry_kernel(scal, tokens, entry, stats, turned):
    side = scal[1]
    for quad in range(4):
        lane = iota((1, 256), 1) + quad * 256
        row, col = token_place(lane)
        natural = row * SIDE + col
        pick = one_hot(iota((TOKENS, 256), 0) == natural)
        turned[:, quad * 256 : quad * 256 + 256] = pick
        mask = jnp.where((row < side) & (col < side), 1.0, 0.0)
        entry[:, quad * 256 : quad * 256 + 256] = (dot(tokens[...], pick) * mask).astype(BF16)

    def body(tile):
        values = entry[:, lanes(tile)].astype(F32)
        mean = jnp.mean(values, axis=0, keepdims=True)
        centred = values - mean
        rstd = lax.rsqrt(jnp.mean(centred * centred, axis=0, keepdims=True) + EPS)
        stats[:, lanes(tile)] = stat_rows(mean, rstd)

    loop(8, body)


def small_table(me, low, high):
    gathered = jnp.concatenate(
        [half[:, SMALL_ROW : SMALL_ROW + 8, :].astype(F32).reshape(128, 128) for half in (low, high)], axis=0
    ).astype(BF16)
    vector = iota((128, 256), 0)
    place = iota((128, 256), 1)
    row = place & 7
    owner = xor_of(place >> 3) ^ me
    first = (7 * owner) >> 3
    straight = (
        ((row == 0) & (vector == 3 * owner))
        | ((row == 1) & (vector == 3 * owner + 2))
        | ((row == 2) & (vector == 96 + first))
    )
    turned = ((row == 0) & (vector == 3 * owner + 1)) | ((row == 2) & (vector == 97 + first))
    rows = dot(one_hot(straight), gathered) + pltpu.roll(dot(one_hot(turned), gathered), 64, 1)
    return jnp.transpose(rows)[0:64, :]


def project_kernel(scal, from_tens, from_lower, from_upper, from_rest, low, high, entry, stats, wq, wkv, wrs, wo, first, qs, raw, stat_r, red, kv, kt, vt, bt, square, rest, redin):
    me = scal[0]
    bt[...] = small_table(me, low, high)
    for half, source in enumerate((low, high)):

        def chunk(c, half=half, source=source):
            block = source[:, pl.ds(pl.multiple_of(16 * c, 16), 16), :].astype(F32)
            rows = slice(128 * half, 128 * half + 128)
            wrs[rows, lanes(c)] = block[:, 0:8].reshape(128, 128).astype(BF16)
            square[rows, lanes(c)] = block[:, 8:16].reshape(128, 128).astype(BF16)

        loop(10, chunk)
        block = source[:, 160:208, :].astype(F32)
        for c in range(5):
            part = block[:, 8 * c : 8 * c + 8].reshape(128, 128).astype(BF16)
            rest[128 * half : 128 * half + 128, 128 * c : 128 * c + 128] = part

    def last_two(p):
        part = dot(from_rest[...], rest[:, lanes(p)]).astype(BF16)
        wrs[256:320, lanes(p, 256)] = jnp.concatenate([part[0:64], part[64:128]], axis=1)
        square[256:320, lanes(p, 256)] = jnp.concatenate([part[128:192], part[192:256]], axis=1)

    loop(5, last_two)
    wq[:, 0:256] = dot(from_tens[...], square[:, 0:256]).astype(BF16)
    wo[:, 0:256] = dot(from_tens[...], square[:, 1024:1280]).astype(BF16)
    tails = dot(from_tens[...], square[:, 768:1024])
    wq[:, 256:320] = tails[:, 0:64].astype(BF16)
    wo[:, 256:320] = pltpu.roll(tails, 64, 1)[:, 0:64].astype(BF16)
    wkv[:, 0:256] = (dot(from_lower[...], square[:, 256:512]) + dot(from_upper[...], square[:, 512:768])).astype(BF16)
    tail = pltpu.roll(dot(from_lower[...], square[:, 768:896]), 64, 1) + dot(from_upper[...], square[:, 896:1024])
    wkv[:, 256:320] = tail[:, 0:64].astype(BF16)

    gain, shift = column(bt, G_1, 5), column(bt, C_1, 5)

    def body(tile):
        centred = entry[:, lanes(tile)].astype(F32) - stats[0:1, lanes(tile)]
        first[:, lanes(tile)] = (centred * stats[1:2, lanes(tile)] * gain + shift).astype(BF16)

    loop(8, body)
    for quad in range(4):
        redin[D * quad : D * quad + D, :] = first[:, 256 * quad : 256 * quad + 256]
    bias = column(bt, B_Q, 5)
    bias = jnp.concatenate([bias, bias], axis=1)
    for quad in range(4):
        at = lanes(quad, 256)
        qs[:, at] = (dot(wq[...], first[:, at]) + bias).astype(BF16) * BF16(0.125)
    bias = column(bt, B_R, 5)
    bias = jnp.concatenate([bias, bias], axis=1)
    mixed = dot(wrs[...], redin[...])
    total = bias
    for part in range(3):
        piece = mixed.astype(BF16)
        total = total + dot(from_tens[...], piece)
        mixed = mixed - piece.astype(F32)
    raw[...] = total
    gain, shift = column(bt, G_R, 5), column(bt, C_R, 5)
    for tile in range(2):
        at = slice(128 * tile, 128 * tile + 128)
        values, mean, rstd = norm(raw[:, at], gain, shift)
        red[:, at] = values.astype(BF16)
        stat_r[:, at] = stat_rows(mean, rstd)
    keyval = dot(wkv[...], red[...])
    kv[...] = keyval.astype(BF16)
    turned = jnp.transpose(keyval)
    for h in range(HEADS):
        kt[h] = turned[:, 64 * h : 64 * h + 64].astype(BF16)
        vt[h] = turned[:, D + 64 * h : D + 64 * h + 64].astype(BF16)


def key_bias(side):
    i, j = key_place(iota((QUARTER, 1), 0))
    return jnp.where((i < (side >> 1)) & (j < (side >> 1)), 0.0, -10000.0)


def head_rows(h):
    return pl.ds(pl.multiple_of(64 * h, 64), 64)


def attend_kernel(scal, kt, qs, kv, att, lse, scores_a, scores_b, probs_a, probs_b):
    bias = key_bias(scal[1])

    def score(scores, h, start):
        scores[...] = dot(kt[h], qs[head_rows(h), start : start + 512])

    def finish(scores, probs, h, start):
        for tile in range(4):
            at = slice(128 * tile, 128 * tile + 128)
            to = slice(start + 128 * tile, start + 128 * tile + 128)
            part = scores[:, at] + bias
            top = jnp.max(part, axis=0, keepdims=True)
            weights = jnp.exp(part - top)
            total = jnp.sum(weights, axis=0, keepdims=True)
            lse[h, :, to] = top + jnp.log(total)
            probs[:, at] = (weights * (1.0 / total)).astype(BF16)
        values = kv[pl.ds(pl.multiple_of(D + 64 * h, 64), 64), :]
        att[head_rows(h), start : start + 512] = dot(values, probs[...]).astype(BF16)

    score(scores_a, 0, 0)

    def head(h):
        score(scores_b, h, 512)
        finish(scores_a, probs_a, h, 0)
        score(scores_a, jnp.minimum(h + 1, HEADS - 1), 0)
        finish(scores_b, probs_b, h, 512)

    loop(HEADS, head)


def middle_kernel(scal, bt, wo, att, entry, mid, sec, stats, work):
    side = scal[1]
    bias, gain, shift = column(bt, B_O, 5), column(bt, G_2, 5), column(bt, C_2, 5)

    def body(tile):
        at = lanes(tile)
        mask = token_mask(tile, side)
        values = entry[:, at].astype(F32) + mask * (work[:, at] + bias)
        mid[:, at] = values
        normed, mean, rstd = norm(values, gain, shift)
        stats[:, at] = stat_rows(mean, rstd)
        sec[0:D, at] = (normed.astype(BF16).astype(F32) * mask).astype(BF16)
        sec[D : D + 64, at] = jnp.where(iota((64, 128), 0) == 9, mask, 0.0).astype(BF16)

    for quad in range(4):
        at = lanes(quad, 256)
        work[:, at] = dot(wo[...], att[:, at])
        body(2 * quad)
        body(2 * quad + 1)


def ffn_weights_kernel(scal, bt, from_tens, from_rest, low, high, w1, w1t, w2, w2t, taps, main, rest, wide):
    me = scal[0]
    for half, source in enumerate((low, high)):
        def chunks(p, half=half, source=source):
            block = source[:, pl.ds(pl.multiple_of(16 * p, 16), 16), :].astype(F32)
            both = jnp.concatenate([block[:, 0:8].reshape(128, 128), block[:, 8:16].reshape(128, 128)], axis=1)
            main[128 * half : 128 * half + 128, lanes(p, 256)] = both.astype(BF16)

        loop(5, chunks)
        block = source[:, 80:112, :].astype(F32)
        for c in range(3):
            part = block[:, 8 * c : 8 * c + 8].reshape(128, 128).astype(BF16)
            rest[128 * half : 128 * half + 128, 128 * c : 128 * c + 128] = part

        def expansion(slot, half=half, source=source):
            owner = ((slot << 1) | half) ^ me
            block = source[slot, 80:224, :].astype(F32)
            rows = pl.ds(pl.multiple_of(40 * owner, 8), 40)
            for c in range(3):
                wide[rows, 128 * c : 128 * c + 128] = block[24 + 40 * c : 64 + 40 * c]

        loop(16, expansion)
    for j in range(3):
        part = dot(from_rest[...], rest[:, 128 * j : 128 * j + 128]).astype(BF16)
        for k in range(4 if j < 2 else 2):
            c = 4 * j + k
            main[256:320, 128 * c : 128 * c + 128] = part[64 * k : 64 * k + 64]

    def block(p):
        rows = lanes(p, 256)
        full = dot(from_tens[...], main[:, lanes(p, 256)])
        w2[:, lanes(p, 256)] = full.astype(BF16)
        w2t[rows, :] = jnp.transpose(full).astype(BF16)
        w1t[:, lanes(p, 256)] = jnp.transpose(wide[rows, :])[0:D].astype(BF16)

    for p in range(5):
        block(p)
    low_tail = wide[:, 256:384].astype(BF16)

    def spread(tap):
        taps[tap] = dot(low_tail, one_hot(iota((128, 128), 0) == 64 + tap))

    for tap in range(9):
        spread(tap)
    w1[:, 0:256] = wide[:, 0:256].astype(BF16)
    lane = iota((64, 128), 1)
    for h in range(20):
        rows = slice(64 * h, 64 * h + 64)
        taps[9, rows, :] = jnp.broadcast_to(bt[:, B_DW + h : B_DW + h + 1], (64, 128))
        beside = jnp.where(lane == 73, bt[:, B_1 + h : B_1 + h + 1], 0.0)
        w1[rows, 256:384] = jnp.where(lane < 64, wide[rows, 256:384], beside).astype(BF16)


def edge_masks():
    lane = iota((1, 128), 1)
    j = lane & 15
    return jnp.where(j != 0, 1.0, 0.0), jnp.where(j != 15, 1.0, 0.0), lane >= 16, lane < 112


def left_of(tiles):
    return [pltpu.roll(tile, 1, 1) for tile in tiles]


def right_of(tiles):
    return [pltpu.roll(tile, 127, 1) for tile in tiles]


def above(tiles, inside):
    turned = [pltpu.roll(tile, 16, 1) for tile in tiles]
    return [jnp.where(inside, turned[0], 0.0), jnp.where(inside, turned[1], turned[0])]


def below(tiles, inside):
    turned = [pltpu.roll(tile, 112, 1) for tile in tiles]
    return [jnp.where(inside, turned[0], turned[1]), jnp.where(inside, turned[1], 0.0)]


def times(tiles, factor):
    return [tile * factor for tile in tiles]


def plus(*many):
    return [functools.reduce(lambda a, b: a + b, tiles) for tiles in zip(*many)]


def tile_at(a, e, half):
    start = 256 * (2 * a + e) + 128 * half
    return slice(start, start + 128)


def quads(ref, rows):
    return [[[ref[rows, tile_at(a, e, half)] for half in range(2)] for e in range(2)] for a in range(2)]


LOG2E = float(np.log2(np.e))


def gelu_parts(x):
    y = x * np.float32(0.5**0.5)
    cdf = lax.erf(y) * 0.5 + 0.5
    bell = jnp.exp2(y * y * np.float32(-LOG2E) + np.float32(-0.5 * np.log2(2.0 * np.pi)))
    return x * cdf, cdf + x * bell


def ffn_kernel(scal, w1, taps, sec, act, slope, hid_a, hid_b):
    j_first, j_last, i_first, i_last = edge_masks()

    def fill(hid, step):
        rows = pl.ds(pl.multiple_of(jnp.minimum(step, FF // 64 - 1) * 64, 64), 64)
        hid[...] = dot(w1[rows, :], sec[...])

    def group(hid, step, index):
        rows = slice(16 * index, 16 * index + 16)
        out_rows = pl.ds(pl.multiple_of(64 * step + 16 * index, 16), 16)
        k = [taps[n, out_rows, :] for n in range(10)]
        first = [k[3 * r] * j_first for r in range(3)]
        last = [k[3 * r + 2] * j_last for r in range(3)]
        quad = quads(hid, rows)
        left = [left_of(quad[a][1]) for a in range(2)]
        right = [right_of(quad[a][0]) for a in range(2)]

        def across(a, e, r):
            if e == 0:
                parts = zip(left[a], quad[a][0], quad[a][1])
                return [first[r] * x + k[3 * r + 1] * y + k[3 * r + 2] * z for x, y, z in parts]
            parts = zip(quad[a][0], quad[a][1], right[a])
            return [k[3 * r] * x + k[3 * r + 1] * y + last[r] * z for x, y, z in parts]

        for e in range(2):
            up = above(across(1, e, 0), i_first)
            down = below(across(0, e, 2), i_last)
            outs = (plus(across(0, e, 1), across(1, e, 2), up), plus(across(0, e, 0), across(1, e, 1), down))
            for a in range(2):
                for half in range(2):
                    value, grad = gelu_parts(outs[a][half] + k[9])
                    act[out_rows, tile_at(a, e, half)] = value.astype(BF16)
                    slope[out_rows, tile_at(a, e, half)] = grad.astype(BF16)

    fill(hid_a, 0)

    def two(index):
        fill(hid_b, 2 * index + 1)
        for n in range(4):
            group(hid_a, 2 * index, n)
        fill(hid_a, 2 * index + 2)
        for n in range(4):
            group(hid_b, 2 * index + 1, n)

    loop(FF // 128, two)


def ending_kernel(scal, bt, w2, act, mid, end, sect, stats, work):
    side = scal[1]
    bias, gain, shift = column(bt, B_2, 5), column(bt, G_S, 5), column(bt, C_S, 5)

    def body(tile):
        at = lanes(tile)
        mask = token_mask(tile, side)
        values = mid[:, at] + mask * (work[:, at] + bias)
        end[:, at] = values
        normed, mean, rstd = norm(values, gain, shift)
        stats[:, at] = stat_rows(mean, rstd)
        sect[:, at] = (normed.astype(BF16).astype(F32) * mask).astype(BF16)

    for quad in range(4):
        at = lanes(quad, 256)
        work[:, at] = dot(w2[...], act[:, at])
        body(2 * quad)
        body(2 * quad + 1)


def lane_sum(values):
    return jnp.sum(values, axis=1, keepdims=True)


def merge_kernel(scal, bt, c_low, c_high, sect, end, stats, cot, four, keep, send, end_grad, branch, grads, wm, patch, mg, back, work, natural):
    me, side = scal[0], scal[1]
    grads[...] = jnp.zeros_like(grads)
    for half, source in enumerate((c_low, c_high)):

        def place(c, half=half, source=source):
            block = source[:, pl.ds(pl.multiple_of(16 * c, 16), 16), :].reshape(256, 128)
            wm[256 * half : 256 * half + 256, lanes(c)] = block

        loop(23, place)

    def reorder(to_owner):
        def one(slot):
            at = pl.ds(pl.multiple_of(16 * slot, 16), 16)
            owner = pl.ds(pl.multiple_of((xor_of(slot) ^ me) * 16, 16), 16)
            to_owner(at, owner)

        loop(32, one)

    j_first, j_last, i_first, i_last = edge_masks()
    quad = [[[t.astype(F32) for t in pair] for pair in row] for row in quads(sect, slice(None))]
    left = [times(left_of(quad[a][1]), j_first) for a in range(2)]
    pieces = (
        above(left[1], i_first),
        above(quad[1][0], i_first),
        above(quad[1][1], i_first),
        left[0],
        quad[0][0],
        quad[0][1],
        left[1],
        quad[1][0],
        quad[1][1],
    )
    for n, piece in enumerate(pieces):
        for half in range(2):
            patch[D * n : D * n + D, 128 * half : 128 * half + 128] = piece[half].astype(BF16)
    patch[9 * D :, :] = jnp.zeros((MERGE_PAD - 9 * D, 256), BF16)
    bias, gain, shift = column(bt, B_M, 8), column(bt, G_M, 8), column(bt, C_M, 8)
    work[...] = dot(wm[...], patch[...])

    def from_slots(at, owner):
        natural[owner, :] = work[at, :]

    reorder(from_slots)
    half_side = side >> 1
    for tile in range(2):
        at = slice(128 * tile, 128 * tile + 128)
        i, j = key_place(iota((1, 128), 1) + 128 * tile)
        mask = jnp.where((i < half_side) & (j < half_side), 1.0, 0.0)
        values = natural[:, at] + bias
        mean = jnp.mean(values, axis=0, keepdims=True)
        centred = values - mean
        rstd = lax.rsqrt(jnp.mean(centred * centred, axis=0, keepdims=True) + EPS)
        hat = centred * rstd
        four[:, at] = ((hat * gain + shift) * mask).astype(BF16)
        grad = cot[:, at].astype(F32) * mask
        low = norm_back(grad, hat, rstd, gain).astype(BF16)
        natural[:, at] = low.astype(F32)
        parts = (grad * hat, grad, low.astype(F32))
        sums = parts if tile == 0 else [s + v for s, v in zip(sums, parts)]
    put_column(grads, G_M, lane_sum(sums[0]))
    put_column(grads, C_M, lane_sum(sums[1]))
    put_column(grads, B_M, lane_sum(sums[2]))

    def to_slots(at, owner):
        mg[at, :] = natural[owner, :].astype(BF16)

    reorder(to_slots)

    def widths(body):
        loop(11, lambda c: body(pl.multiple_of(c * 256, 256), 256))
        body(11 * 256, 128)

    def patch_grad(start, width):
        back[pl.ds(start, width), :] = dot_tn(wm[:, pl.ds(start, width)], mg[...])


    def give(start, width):
        block = dot_nt(mg[...], patch[pl.ds(start, width), :]).astype(BF16)
        for c in range(width // 128):
            to = pl.ds(pl.multiple_of((start >> 3) + 16 * c, 16), 16)
            part = block[:, 128 * c : 128 * c + 128].reshape(32, 16, 128)
            keep[:, to, :] = part[0:16]
            send[:, to, :] = part[16:32]

    def both(start, width):
        patch_grad(start, width)
        give(start, width)

    widths(both)

    def piece(n):
        return [back[D * n : D * n + D, 128 * half : 128 * half + 128] for half in range(2)]

    results = (
        piece(4),
        plus(piece(5), times(right_of(piece(3)), j_last)),
        plus(piece(7), below(piece(1), i_last)),
        plus(
            piece(8),
            times(right_of(piece(6)), j_last),
            below(plus(piece(2), times(right_of(piece(0)), j_last)), i_last),
        ),
    )
    for n, values in enumerate(results):
        for half in range(2):
            end_grad[:, 256 * n + 128 * half : 256 * n + 128 * half + 128] = values[half]
    gain = column(bt, G_S, 5)
    zeros = jnp.zeros((D, 128), F32)

    def one(tile):
        at = lanes(tile)
        mask = token_mask(tile, side)
        grad = end_grad[:, at] * mask
        hat = (end[:, at] - stats[0:1, at]) * stats[1:2, at]
        result = norm_back(grad, hat, stats[1:2, at], gain)
        end_grad[:, at] = result
        low = (result * mask).astype(BF16)
        branch[:, at] = low
        return grad * hat, grad, low.astype(F32)

    sums = (zeros, zeros, zeros)
    for step in range(4):
        pairs = zip(sums, one(2 * step), one(2 * step + 1))
        sums = tuple(total + (x + y) for total, x, y in pairs)
    put_column(grads, G_S, lane_sum(sums[0]))
    put_column(grads, C_S, lane_sum(sums[1]))
    put_column(grads, B_2, lane_sum(sums[2]))


def ffn_back_kernel(first_part, count, scal, w1, w2t, taps, sec, slope, branch, hg, dkx, hid_a, hid_b, cg_a, cg_b):
    start, steps = 256 * first_part, 4 * count
    j_first, j_last, i_first, i_last = edge_masks()
    lane = iota((16, 128), 1)

    def fill(hid, cg, step):
        rows = pl.ds(pl.multiple_of(start + jnp.minimum(step, steps - 1) * 64, 64), 64)
        cg[...] = dot(w2t[rows, :], branch[...]) * slope[rows, :].astype(F32)
        hid[...] = dot(w1[rows, :], sec[...])

    def group(hid, cg, step, index):
        rows = slice(16 * index, 16 * index + 16)
        from_rows = pl.ds(pl.multiple_of(start + 64 * step + 16 * index, 16), 16)
        to_rows = pl.ds(pl.multiple_of(64 * step + 16 * index, 16), 16)
        k = [taps[n, from_rows, :] for n in range(9)]
        quad = quads(cg, rows)
        bias = functools.reduce(lambda x, y: x + y, [t for row in quad for pair in row for t in pair])
        across = [
            (
                (times(left_of(quad[a][1]), j_first), quad[a][0], quad[a][1]),
                (quad[a][0], quad[a][1], times(right_of(quad[a][0]), j_last)),
            )
            for a in range(2)
        ]
        sums = [None] * 9
        for e in range(2):
            upper = [above(tiles, i_first) for tiles in across[1][e]]
            lower = [below(tiles, i_last) for tiles in across[0][e]]
            for a, near in ((0, (upper, across[0][e], across[1][e])), (1, (across[0][e], across[1][e], lower))):
                for half in range(2):
                    value = hid[rows, tile_at(a, e, half)]
                    total = None
                    for r in range(3):
                        for c in range(3):
                            tap = 3 * (2 - r) + (2 - c)
                            term = k[tap] * near[r][c][half]
                            total = term if total is None else total + term
                            term = value * near[r][c][half]
                            sums[tap] = term if sums[tap] is None else sums[tap] + term
                    hg[to_rows, tile_at(a, e, half)] = total.astype(BF16)
        table = jnp.where(lane == 9, lane_sum(bias), 0.0)
        for n in range(9):
            table = jnp.where(lane == n, lane_sum(sums[n]), table)
        dkx[to_rows, :] = table

    fill(hid_a, cg_a, 0)

    def two(index):
        fill(hid_b, cg_b, 2 * index + 1)
        for n in range(4):
            group(hid_a, cg_a, 2 * index, n)
        fill(hid_a, cg_a, 2 * index + 2)
        for n in range(4):
            group(hid_b, cg_b, 2 * index + 1, n)

    loop(steps // 2, two)


def middle_back_kernel(scal, bt, w1t, hg0, hg1, end_grad, mid, stats, mid_grad, low_grad, grads, work):
    side = scal[1]
    grads[...] = jnp.zeros_like(grads)
    gain = column(bt, G_2, 5)
    zeros = jnp.zeros((D, 128), F32)

    def one(tile):
        at = lanes(tile)
        mask = token_mask(tile, side)
        grad = work[:, at] * mask
        hat = (mid[:, at] - stats[0:1, at]) * stats[1:2, at]
        result = end_grad[:, at] + norm_back(grad, hat, stats[1:2, at], gain)
        mid_grad[:, at] = result
        low = (result * mask).astype(BF16)
        low_grad[:, at] = low
        return grad * hat, grad, low.astype(F32)

    sums = (zeros, zeros, zeros)
    for quad in range(4):
        at = lanes(quad, 256)
        work[:, at] = sum(
            dot(w1t[:, 256 * start : 256 * (start + count)], hg[:, at]) for hg, (start, count) in zip((hg0, hg1), PARTS)
        )
        pairs = zip(sums, one(2 * quad), one(2 * quad + 1))
        sums = tuple(total + (x + y) for total, x, y in pairs)
    put_column(grads, G_2, lane_sum(sums[0]))
    put_column(grads, C_2, lane_sum(sums[1]))
    put_column(grads, B_O, lane_sum(sums[2]))


def pack_b_kernel(scal, to_tens, hg0, hg1, dk0, dk1, sec, branch, act, keep, send, grads, dw1, gather, mixed):
    me = scal[0]
    grads[...] = jnp.zeros_like(grads)
    lane = iota((256, 128), 1)
    mixed[...] = dot(to_tens[...], branch[...]).astype(BF16)
    gather[:, 0:24, :] = jnp.zeros((32, 24, 128), F32)

    def contraction(p):
        block = dot_nt(mixed[...], act[pl.ds(pl.multiple_of(256 * p, 256), 256), :])
        parts = [block[0:256, 128 * e : 128 * e + 128].reshape(32, 1, 8, 128) for e in range(2)]
        full = jnp.concatenate(parts, axis=1).reshape(32, 16, 128).astype(BF16)
        to = pl.ds(pl.multiple_of(16 * p, 16), 16)
        keep[:, to, :] = full[0:16]
        send[:, to, :] = full[16:32]
        tail = jnp.concatenate([block[256:320, 0:128], block[256:320, 128:256]], axis=0).astype(BF16)
        place = rest_row(iota((256, 1), 0)) - 128 * (p & 1)
        to = pl.ds(pl.multiple_of(8 * (p >> 1), 8), 8)
        gather[:, to, :] += dot(one_hot(iota((256, 128), 1) == place), tail).reshape(32, 8, 128)

    for hg, dkx, (at, count) in zip((hg0, hg1), (dk0, dk1), PARTS):

        def outer(n, hg=hg, dkx=dkx, at=at):
            rows = pl.ds(pl.multiple_of(256 * n, 256), 256)
            to = pl.ds(pl.multiple_of(256 * (n + at), 256), 256)
            part = dot_nt(hg[rows, :], sec[...])
            dw1[to, 0:256] = part[:, 0:256]
            turned = pltpu.roll(dkx[rows, :], 64, 1)
            dw1[to, 256:384] = jnp.where(lane < 64, part[:, 256:384], jnp.where(lane < 73, turned, 0.0))
            table = grads[...]
            for m in range(4):
                here = slice(64 * m, 64 * m + 64)
                number = 4 * (n + at) + m
                table = jnp.where(lane[here] == B_1 + number, part[here, 329:330], table)
                table = jnp.where(lane[here] == B_DW + number, dkx[rows, :][here, 9:10], table)
            grads[...] = table
            contraction(n + at)

        loop(count, outer)

    def expansion(owner):
        slot = slot_of(owner ^ me)
        rows = pl.ds(pl.multiple_of(40 * owner, 8), 40)
        for c in range(3):
            gather[slot, 24 + 40 * c : 64 + 40 * c, :] = dw1[rows, 128 * c : 128 * c + 128]

    loop(32, expansion)
    keep[:, 80:224, :] = gather[0:16].astype(BF16)
    send[:, 80:224, :] = gather[16:32].astype(BF16)


def attend_back_kernel(scal, kt, vt, qs, kv, wo, low_grad, lse, dq, dkv, og, scores_a, scores_b, grads_a, grads_b, probs_a, probs_b, back_a, back_b):
    bias = key_bias(scal[1])
    og[...] = dot_tn(wo[...], low_grad[...]).astype(BF16)

    def score(scores, grads, h, start):
        at = slice(start, start + 512)
        scores[...] = dot(kt[h], qs[head_rows(h), at])
        grads[...] = dot(vt[h], og[head_rows(h), at])

    def finish(scores, grads, probs, back, h, start):
        for tile in range(4):
            at = slice(128 * tile, 128 * tile + 128)
            to = slice(start + 128 * tile, start + 128 * tile + 128)
            weights = jnp.exp(scores[:, at] + bias - lse[h, :, to])
            grad = grads[:, at]
            mean = jnp.sum(weights * grad, axis=0, keepdims=True)
            back[:, at] = (weights * (grad - mean)).astype(BF16)
            probs[:, at] = weights.astype(BF16)
        rows, at = head_rows(h), slice(start, start + 512)
        dq[rows, at] = (dot(kv[rows, :], back[...]) * 0.125).astype(BF16)
        return dot_nt(qs[rows, at], back[...]), dot_nt(og[rows, at], probs[...])

    score(scores_a, grads_a, 0, 0)

    def head(h):
        score(scores_b, grads_b, h, 512)
        one = finish(scores_a, grads_a, probs_a, back_a, h, 0)
        score(scores_a, grads_a, jnp.minimum(h + 1, HEADS - 1), 0)
        two = finish(scores_b, grads_b, probs_b, back_b, h, 512)
        dkv[head_rows(h), :] = (one[0] + two[0]).astype(BF16)
        dkv[pl.ds(pl.multiple_of(D + 64 * h, 64), 64), :] = (one[1] + two[1]).astype(BF16)

    loop(HEADS, head)


def first_kernel(scal, bt, to_tens, to_lower, to_upper, to_rest, wq, wkv, wrs, first, red, raw, stat_r, dq, dkv, low_grad, att, entry, stats, g_one, g_two, g_three, keep, send, work, grads, wide, redin, stack_r, stack_z, tails_of):
    me = scal[0]
    grads[...] = g_one[...] + g_two[...] + g_three[...]
    for quad in range(4):
        redin[D * quad : D * quad + D, :] = first[:, 256 * quad : 256 * quad + 256]
    dred = dot_tn(wkv[...], dkv[...])
    gain = column(bt, G_R, 5)
    lows = []
    for tile in range(2):
        at = slice(128 * tile, 128 * tile + 128)
        grad = dred[:, at]
        hat = (raw[:, at] - stat_r[0:1, at]) * stat_r[1:2, at]
        low = norm_back(grad, hat, stat_r[1:2, at], gain).astype(BF16)
        lows.append(low)
        parts = (grad * hat, grad, low.astype(F32))
        sums = parts if tile == 0 else [s + v for s, v in zip(sums, parts)]
    put_column(grads, G_R, lane_sum(sums[0]))
    put_column(grads, C_R, lane_sum(sums[1]))
    put_column(grads, B_R, lane_sum(sums[2]))
    low = jnp.concatenate(lows, axis=1)
    low = dot(to_tens[...], low).astype(BF16)
    wide[...] = dot_tn(wrs[...], low)
    straight = dot_tn(wq[...], dq[...])
    for quad in range(4):
        at = slice(256 * quad, 256 * quad + 256)
        work[:, at] = straight[:, at] + wide[D * quad : D * quad + D, :]
    zeros = jnp.zeros((D, 128), F32)

    def one(tile):
        at = lanes(tile)
        grad = work[:, at]
        hat = (entry[:, at].astype(F32) - stats[0:1, at]) * stats[1:2, at]
        return grad * hat, grad, dq[:, at].astype(F32)

    sums = (zeros, zeros, zeros)
    for step in range(4):
        pairs = zip(sums, one(2 * step), one(2 * step + 1))
        sums = tuple(total + (x + y) for total, x, y in pairs)
    put_column(grads, G_1, lane_sum(sums[0]))
    put_column(grads, C_1, lane_sum(sums[1]))
    put_column(grads, B_Q, lane_sum(sums[2]))
    stack_r[...] = dot_nt(low, redin[...])

    def outer(pick, grad, value):
        return dot_nt(dot(pick[...], grad[...]).astype(BF16), value[...])

    parts = (
        outer(to_tens, dq, first),
        outer(to_lower, dkv, red),
        outer(to_upper, dkv, red),
        outer(to_tens, low_grad, att),
    )
    for part, at in zip(parts, (0, 256, 512, 1024)):
        stack_z[:, at : at + 256] = part[:, 0:256]
    stack_z[:, 768:1024] = jnp.concatenate([part[:, 256:320] for part in parts], axis=1)

    def pack(p):
        at = lanes(p, 256)
        both = stack_r[:, at], stack_z[:, at]
        for e in range(2):
            pieces = [block[0:256, 128 * e : 128 * e + 128].reshape(32, 1, 8, 128) for block in both]
            full = jnp.concatenate(pieces, axis=1).reshape(32, 16, 128).astype(BF16)
            to = pl.ds(pl.multiple_of(32 * p + 16 * e, 16), 16)
            keep[:, to, :] = full[0:16]
            send[:, to, :] = full[16:32]
        tail = jnp.concatenate(
            [block[256:320, 128 * e : 128 * e + 128] for block in both for e in range(2)], axis=0
        ).astype(BF16)
        to = pl.ds(pl.multiple_of(8 * p, 8), 8)
        tails_of[:, to, :] = dot(to_rest[...], tail).reshape(32, 8, 128)

    loop(5, pack)
    rows = jnp.transpose(jnp.concatenate([grads[...], jnp.zeros((64, 128), F32)], axis=0)).astype(BF16)
    place = iota((256, 128), 0)
    vector = iota((256, 128), 1)
    line = place & 7
    owner = xor_of(place >> 3) ^ me
    start = (7 * owner) >> 3
    straight = (
        ((line == 0) & (vector == 3 * owner))
        | ((line == 1) & (vector == 3 * owner + 2))
        | ((line == 2) & (vector == 96 + start))
    )
    turned = ((line == 0) & (vector == 3 * owner + 1)) | ((line == 2) & (vector == 97 + start))
    small = dot(one_hot(straight), rows) + pltpu.roll(dot(one_hot(turned), rows), 64, 1)
    tails_of[:, 40:48, :] = small.reshape(32, 8, 128)
    keep[:, 160:208, :] = tails_of[0:16].astype(BF16)
    send[:, 160:208, :] = tails_of[16:32].astype(BF16)


def token_kernel(scal, bt, turned, grad_in, mid_grad, entry, stats, tok, high, rest):
    side = scal[1]
    gain = column(bt, G_1, 5)

    def body(tile):
        at = lanes(tile)
        hat = (entry[:, at].astype(F32) - stats[0:1, at]) * stats[1:2, at]
        result = mid_grad[:, at] + norm_back(grad_in[:, at], hat, stats[1:2, at], gain)
        result = result * token_mask(tile, side)
        upper = result.astype(BF16)
        high[:, at] = upper
        rest[:, at] = (result - upper.astype(F32)).astype(BF16)

    for tile in range(8):
        body(tile)

    def quad(index):
        pick = turned[pl.ds(pl.multiple_of(256 * index, 256), 256), :]
        tok[:, lanes(index, 256)] = dot_nt(high[...], pick) + dot_nt(rest[...], pick)

    loop(4, quad)


def cost(micros):
    return pl.CostEstimate(flops=int(micros * 1e9), bytes_accessed=1000, transcendentals=0)


def call(kernel, args, outs, scratch=(), micros=5):
    return pl.pallas_call(
        kernel,
        in_specs=[pl.BlockSpec(memory_space=pltpu.SMEM if arg.dtype == I32 else pltpu.VMEM) for arg in args],
        out_shape=[jax.ShapeDtypeStruct(shape, dtype) for shape, dtype in outs],
        scratch_shapes=[pltpu.VMEM(shape, dtype) for shape, dtype in scratch],
        compiler_params=pltpu.CompilerParams(vmem_limit_bytes=VMEM_LIMIT),
        cost_estimate=cost(micros),
    )(*args)


def local(group, axes, *arrays):
    return step_of(group, axes, *arrays)


def step_of(group, axes, tokens, image_side, cotangent, *shards):
    index = lax.axis_index(axes[0]) * lax.axis_size(axes[1]) + lax.axis_index(axes[1])
    me = index // group
    devices = SUPER * group

    def flip(values, mask):
        pairs = [(i, ((i // group) ^ mask) * group + i % group) for i in range(devices)]
        return lax.ppermute(values, axes, pairs)

    def gather(block, split=0, direct=False):
        held = block[None]
        if direct:
            held = jnp.concatenate([held, flip(held, 2), flip(held, 4), flip(held, 6)], axis=0)
        else:
            for mask in FLIPS[:2]:
                held = jnp.concatenate([held, flip(held, mask)], axis=0)
        if split:
            one, two = held[:, :split], held[:, split:]
            one, two = (jnp.concatenate([one, flip(one, 8)], axis=0), jnp.concatenate([two, flip(two, 16)], axis=0))
            far, near = flip(one, 16), flip(two, 8)
            two = jnp.concatenate([two[:4], near[:4], two[4:], near[4:]], axis=0)
            held = jnp.concatenate([jnp.concatenate([one, far], axis=0), two], axis=1)
        else:
            for mask in FLIPS[2:]:
                held = jnp.concatenate([held, flip(held, mask)], axis=0)
        return held, flip(held, 1)

    def scatter(keep, send, split=0, direct=False):
        def step(held, mask):
            return flip(held, mask).astype(F32)

        def halve(held, mask):
            half = held.shape[0] // 2
            return held[:half].astype(F32) + step(held[half:], mask)

        held = (keep.astype(F32) + step(send, 1)).astype(BF16)
        if split:
            one, two = held[:, :split], held[:, split:].reshape(2, 2, 4, -1, 128)
            one, two = (
                halve(one, 16).astype(BF16),
                (two[:, 0].astype(F32) + step(two[:, 1], 8)).astype(BF16).reshape(8, -1, 128),
            )
            held = jnp.concatenate([halve(one, 8), halve(two, 16)], axis=1).astype(BF16)
        else:
            held = halve(held, 16).astype(BF16)
            held = halve(held, 8).astype(BF16)
        if direct:
            far = step(held[2:3], 4), step(held[3:4], 6), step(held[1:2], 2)
            return (held[0:1].astype(F32) + far[2] + far[0] + far[1])[0]
        held = halve(held, 4).astype(BF16)
        return halve(held, 2)[0]

    if group > 1:
        per = lax.axis_size(axes[1])
        start = (index % per) // group * group

        def join(shard):
            full = lax.all_gather(shard, axes[1], axis=0)
            return lax.dynamic_slice_in_dim(full, start, group, axis=0).reshape(-1)

        shards = [join(shard) for shard in shards]
    query, keyval, reduce_w, output, expand, depth, contract, merge, gains, biases = shards

    def rows(flat):
        return flat.reshape(-1, 128)

    scal = jnp.stack([me.astype(I32), image_side[0].astype(I32)])
    taps = jnp.pad(depth.reshape(40, 9), ((0, 0), (64, 55)))
    block_a = select(
        [rows(query), rows(output), rows(keyval), rows(reduce_w)],
        table_a, A_ROWS, (scal, biases[None], gains[None]),
    )
    block_b = select([rows(contract), rows(expand), taps], table_b, B_ROWS)
    block_c = select([rows(merge)], table_c, C_ROWS)
    a_low, a_high = gather(block_a, A_SPLIT, True)
    b_low, b_high = gather(block_b, B_ROWS // 2, True)
    c_low, c_high = gather(block_c, C_ROWS // 2)

    big, narrow = (D, TOKENS), (D, QUARTER)
    from_tens, to_tens, from_lower, from_upper, to_lower, to_upper, from_rest, to_rest = call(
        orders_kernel,
        (scal,),
        [((D, D), BF16)] * 2 + [((2 * D, D), BF16)] * 2 + [((D, 2 * D), BF16)] * 2 + [((256, 256), BF16)] * 2,
        micros=2,
    )
    entry, stats_1, turned = call(
        entry_kernel, (scal, tokens[0]), [(big, BF16), ((8, TOKENS), F32), ((TOKENS, TOKENS), BF16)], micros=3.5)
    wq, wkv, wr, wo, first, qs, raw, stat_r, red, kv, kt, vt, bt = call(
        project_kernel,
        (scal, from_tens, from_lower, from_upper, from_rest, a_low, a_high, entry, stats_1),
        [
            ((D, D), BF16), ((2 * D, D), BF16), ((D, 4 * D), BF16), ((D, D), BF16), (big, BF16), (big, BF16),
            (narrow, F32), ((8, QUARTER), F32), (narrow, BF16), ((2 * D, QUARTER), BF16),
            ((HEADS, QUARTER, 64), BF16), ((HEADS, QUARTER, 64), BF16), ((64, 128), F32),
        ],
        [((D, 1280), BF16), ((256, 640), BF16), ((4 * D, QUARTER), BF16)],
        micros=8,
    )
    att, lse = call(attend_kernel, (scal, kt, qs, kv), [(big, BF16), ((HEADS, 1, TOKENS), F32)],
        [((QUARTER, 512), F32)] * 2 + [((QUARTER, 512), BF16)] * 2, micros=8.5)
    mid, sec, stats_2 = call(
        middle_kernel, (scal, bt, wo, att, entry), [(big, F32), ((384, TOKENS), BF16), ((8, TOKENS), F32)], [(big, F32)],
        micros=5,
    )
    w1, w1t, w2, w2t, taps = call(
        ffn_weights_kernel,
        (scal, bt, from_tens, from_rest, b_low, b_high),
        [((FF, 384), BF16), ((D, FF), BF16), ((D, FF), BF16), ((FF, D), BF16), ((10, FF, 128), F32)],
        [((D, FF), BF16), ((256, 384), BF16), ((FF, 384), F32)],
        micros=8,
    )
    act, slope = call(
        ffn_kernel,
        (scal, w1, taps, sec),
        [((FF, TOKENS), BF16), ((FF, TOKENS), BF16)],
        [((64, TOKENS), F32), ((64, TOKENS), F32)],
        micros=17,
    )
    end, sect, stats_s = call(
        ending_kernel, (scal, bt, w2, act, mid), [(big, F32), (big, BF16), ((8, TOKENS), F32)], [(big, F32)], micros=5
    )
    four, c_keep, c_send, end_grad, branch, g_one = call(
        merge_kernel,
        (scal, bt, c_low, c_high, sect, end, stats_s, cotangent[0]),
        [
            ((OUT_D, QUARTER), BF16), ((16, C_ROWS, 128), BF16), ((16, C_ROWS, 128), BF16), (big, F32), (big, BF16),
            ((64, 128), F32),
        ],
        [
            ((OUT_D, MERGE_PAD), BF16), ((MERGE_PAD, QUARTER), BF16), ((OUT_D, QUARTER), BF16),
            ((MERGE_PAD, QUARTER), F32), ((OUT_D, QUARTER), F32), ((OUT_D, QUARTER), F32),
        ],
        micros=20,
    )
    sum_c = scatter(c_keep, c_send, C_ROWS // 2)
    hgs, dks = [], []
    for at, count in PARTS:
        hg, dk = call(
            functools.partial(ffn_back_kernel, at, count),
            (scal, w1, w2t, taps, sec, slope, branch),
            [((256 * count, TOKENS), BF16), ((256 * count, 128), F32)],
            [((64, TOKENS), F32)] * 4,
            micros=6 * count,
        )
        hgs.append(hg)
        dks.append(dk)
    b_keep, b_send, g_three = call(
        pack_b_kernel,
        (scal, to_tens, *hgs, *dks, sec, branch, act),
        [((16, B_ROWS, 128), BF16), ((16, B_ROWS, 128), BF16), ((64, 128), F32)],
        [((FF, 384), F32), ((32, 144, 128), F32), (big, BF16)],
        micros=9,
    )
    sum_b = scatter(b_keep, b_send, B_ROWS // 2, True)
    mid_grad, low_grad, g_two = call(
        middle_back_kernel,
        (scal, bt, w1t, *hgs, end_grad, mid, stats_2),
        [(big, F32), (big, BF16), ((64, 128), F32)],
        [(big, F32)],
        micros=6,
    )
    dq, dkv = call(
        attend_back_kernel,
        (scal, kt, vt, qs, kv, wo, low_grad, lse),
        [(big, BF16), ((2 * D, QUARTER), BF16)],
        [(big, BF16)] + [((QUARTER, 512), F32)] * 4 + [((QUARTER, 512), BF16)] * 4,
        micros=9,
    )
    a_keep, a_send, first_grad = call(
        first_kernel,
        (
            scal, bt, to_tens, to_lower, to_upper, to_rest, wq, wkv, wr, first, red, raw, stat_r, dq, dkv, low_grad, att, entry, stats_1, g_one, g_two, g_three,
        ),
        [((16, A_ROWS, 128), BF16), ((16, A_ROWS, 128), BF16), (big, F32)],
        [
            ((64, 128), F32), ((4 * D, QUARTER), F32), ((4 * D, QUARTER), BF16), ((D, 1280), F32), ((D, 1280), F32),
            ((32, 48, 128), F32),
        ],
        micros=11,
    )
    sum_a = scatter(a_keep, a_send, A_SPLIT, True)
    (token_grad,) = call(
        token_kernel,
        (scal, bt, turned, first_grad, mid_grad, entry, stats_1),
        [(big, F32)],
        [(big, BF16), (big, BF16)],
        micros=5,
    )
    if group > 1:

        def total(part):
            full = lax.all_gather(part, axes[1], axis=0)
            return jnp.sum(lax.dynamic_slice_in_dim(full, start, group, axis=0), axis=0)

        sum_a, sum_b, sum_c = total(sum_a), total(sum_b), total(sum_c)

    def flat(count):
        return (count, 128), F32

    query_g, output_g, keyval_g, reduce_g, biases_g, gains_g = call(
        out_a_kernel,
        (scal, sum_a),
        [flat(25), flat(25), flat(50), flat(100), ((1, 192), F32), ((1, 56), F32)],
        micros=1,
    )
    contract_g, expand_g = call(out_b_kernel, (scal, sum_b), [flat(100), flat(100)], micros=1)
    (merge_g,) = call(out_c_kernel, (scal, sum_c), [flat(360)], micros=1)
    depth_g = sum_b[184:224, 64:73]
    grads = [query_g, keyval_g, reduce_g, output_g, expand_g, depth_g, contract_g, merge_g, gains_g, biases_g]
    grads = [grad.reshape(-1) for grad in grads]
    if group > 1:
        mine = index % group
        grads = [lax.dynamic_index_in_dim(grad.reshape(group, -1), mine, keepdims=False) for grad in grads]
    return (four[None], token_grad[None], *grads)


def solution(mesh):
    axes = ("dp", "fs")
    devices = mesh.shape["dp"] * mesh.shape["fs"]
    group = devices // SUPER
    if devices != SUPER * group or mesh.shape["fs"] % group:
        raise ValueError("unsupported mesh")
    one, three = P(axes), P(axes, None, None)
    return jax.shard_map(
        functools.partial(local, group, axes),
        mesh=mesh,
        in_specs=(three, one, three) + (one,) * 10,
        out_specs=(three, three) + (one,) * 10,
        check_vma=False,
    )
```

```python
import functools

import jax
import jax.numpy as jnp
import numpy as np
from jax import lax
from jax.experimental import pallas as pl
from jax.experimental.pallas import tpu as pltpu
from jax.sharding import PartitionSpec as P


D = 320
HEADS = 5
FF = 1280
OUT_D = 512
SIDE = 32
QUARTER = 256
TOKENS = SIDE * SIDE
MERGE_PAD = 2944
SUPER = 32
FLIPS = (2, 4, 8, 16)
EPS = 1e-06
F32, BF16, I32 = jnp.float32, jnp.bfloat16, jnp.int32

B_Q, B_R, C_R, B_O, C_1, C_2, B_1, B_DW, B_2, C_S, B_M, C_M = 0, 5, 10, 15, 20, 25, 30, 50, 70, 75, 80, 88
G_R, G_1, G_2, G_S, G_M = 96, 101, 106, 111, 116

PARTS = ((0, 1), (1, 4))
A_ROWS, B_ROWS, C_ROWS = 208, 224, 368
SMALL_ROW = 200
A_SPLIT = 104
VMEM_LIMIT = 24 * 1024 * 1024
VMEM_ALL = 60 * 1024 * 1024


def slot_of(xor):
    return (xor >> 1) | ((xor & 1) << 4)


def xor_of(slot):
    return ((slot & 15) << 1) | (slot >> 4)


def dot(a, b):
    return jnp.dot(a, b, preferred_element_type=F32)


def dot_nt(a, b):
    return lax.dot_general(a, b, (((1,), (1,)), ((), ())), preferred_element_type=F32)


def dot_tn(a, b):
    return lax.dot_general(a, b, (((0,), (0,)), ((), ())), preferred_element_type=F32)


def iota(shape, axis):
    return lax.broadcasted_iota(I32, shape, axis)


def one_hot(test):
    return jnp.where(test, 1.0, 0.0).astype(BF16)


def lanes(index, width=128):
    if isinstance(index, int):
        return slice(index * width, (index + 1) * width)
    return pl.ds(pl.multiple_of(index * width, width), width)


def loop(count, body):
    def step(index, carry):
        body(index)
        return carry

    lax.fori_loop(0, count, step, 0)


def column(table, start, count):
    return jnp.concatenate(
        [jnp.broadcast_to(table[:, h : h + 1], (64, 128)) for h in range(start, start + count)], axis=0
    )


def put_column(table, start, values):
    for h in range(values.shape[0] // 64):
        table[:, start + h : start + h + 1] = values[64 * h : 64 * h + 64, 0:1]


def token_place(lane):
    quad = lane >> 8
    row = 2 * ((lane >> 4) & 15) + (quad >> 1)
    col = 2 * (lane & 15) + (quad & 1)
    return row, col


def token_mask(tile, side, width=128):
    row, col = token_place(iota((1, width), 1) + tile * width)
    return jnp.where((row < side) & (col < side), 1.0, 0.0)


def key_place(index):
    return index >> 4, index & 15


def select_kernel(count, bases, small, small_at, *refs):
    sources, refs = refs[:count], refs[count:]
    if small:
        scal, biases, gains = refs[:3]
        refs = refs[3:]
    low_ref, high_ref, out, rows_ref, sems = refs[:5]
    held = refs[5:]
    copies = [
        pltpu.make_async_copy(source, place, sems.at[n]) for n, (source, place) in enumerate(zip(sources, held))
    ]
    for copy in copies:
        copy.start()
    half = rows_ref.shape[0] // 2
    rows_ref[...] = jnp.zeros_like(rows_ref)
    place = iota((out.shape[0], 2 * half), 1)
    pick_low = one_hot(place == low_ref[...])
    pick_high = one_hot(place == high_ref[...])
    for copy in copies:
        copy.wait()
    for source, base in zip(held, bases):
        rows_ref[base : base + source.shape[0], :] = source[...].astype(F32)
    if small:
        rows_ref[small_at : small_at + 1, :] = biases[:, 0:128].astype(F32)
        rows_ref[small_at + 1 : small_at + 2, 0:64] = biases[:, 128:192].astype(F32)
        wide = jnp.concatenate([gains[...].astype(F32), jnp.zeros((1, 72), F32)], axis=1)
        wide = jnp.broadcast_to(wide, (8, 128))
        rows_ref[small_at + 2 : small_at + 3, :] = pltpu.roll(wide, (56 * scal[0]) & 63, 1)[0:1, :]
    rows_ref[half:, :] = pltpu.roll(rows_ref[0:half, :], 64, 1)
    total = rows_ref[...].astype(BF16)
    low, upper = dot(pick_low, total), dot(pick_high, total)
    out[...] = jnp.where(iota((out.shape[0], 128), 1) < 64, low, upper).astype(BF16)


def select(sources, table, rows, vectors=()):
    bases, at = [], 0
    for source in sources:
        bases.append(at)
        at += -(-source.shape[0] // 16) * 16
    small = len(vectors) > 0
    half = at + (16 if small else 0)
    low, high = table(bases + [at], half).astype(np.int32)[:, :, None]
    specs = [pl.BlockSpec(memory_space=pltpu.HBM)] * len(sources)
    if small:
        specs += [pl.BlockSpec(memory_space=pltpu.SMEM)] + [pl.BlockSpec(memory_space=pltpu.VMEM)] * 2
    specs += [pl.BlockSpec(memory_space=pltpu.VMEM)] * 2
    return pl.pallas_call(
        functools.partial(select_kernel, len(sources), tuple(bases), small, at),
        in_specs=specs,
        out_shape=jax.ShapeDtypeStruct((rows, 128), BF16),
        scratch_shapes=[pltpu.VMEM((2 * half, 128), F32), pltpu.SemaphoreType.DMA((len(sources),))]
        + [pltpu.VMEM(source.shape, source.dtype) for source in sources],
        compiler_params=pltpu.CompilerParams(vmem_limit_bytes=VMEM_ALL if small else VMEM_LIMIT),
        cost_estimate=cost(2),
    )(*sources, *vectors, low, high)


def pair(half, low_src, high_src):
    low = -1 if low_src is None else low_src[0] + low_src[1] // 2 + half * (low_src[1] % 2)
    high = -1 if high_src is None else high_src[0] + high_src[1] // 2 + half * (1 - high_src[1] % 2)
    return low, high


def chunk_sources(bases, row, c):
    q, o, kv = bases
    if c < 6 or c >= 8:
        base, first = ((q, 0), (kv, 0), (kv, 10), None, (o, 0))[c // 2]
        at = 5 * (first + row) + 2 * (c % 2)
        return (base, at), (base, at + 1)
    if c == 6:
        return (q, 5 * row + 4), (kv, 5 * row + 4)
    return (kv, 5 * (10 + row) + 4), (o, 5 * row + 4)


def a_place(kind, row, c):
    if row < 8:
        return 16 * c + 8 * kind + row
    return 160 + 8 * (c // 2) + 4 * kind + 2 * (c % 2) + row - 8


def b_place(row, c):
    if row < 8:
        return 8 * c + row
    return 80 + 8 * (c // 4) + 2 * (c % 4) + row - 8


def table_a(bases, half):
    q, o, kv, r, small = bases
    rows = [(-1, -1)] * A_ROWS
    for c in range(10):
        for row in range(10):
            at = 20 * row + 2 * c
            rows[a_place(0, row, c)] = pair(half, (r, at), (r, at + 1))
            rows[a_place(1, row, c)] = pair(half, *chunk_sources((q, o, kv), row, c))
    for row in range(3):
        rows[SMALL_ROW + row] = pair(half, (small, 2 * row), (small, 2 * row + 1))
    return np.array(rows).T


def table_b(bases, half):
    w2, w1, dw, _ = bases
    rows = [(-1, -1)] * B_ROWS
    for c in range(10):
        for row in range(10):
            at = 20 * row + 2 * c
            rows[b_place(row, c)] = pair(half, (w2, at), (w2, at + 1))
    for c in range(3):
        for row in range(40):
            at = 5 * row + 2 * c
            rows[104 + 40 * c + row] = pair(half, (w1, at), (w1, at + 1) if c < 2 else (dw, 2 * row + 1))
    return np.array(rows).T


def table_c(bases, half):
    m, _ = bases
    rows = []
    for c in range(23):
        for row in range(16):
            at = 45 * row + 2 * c
            rows.append(pair(half, (m, at), (m, at + 1) if c < 22 else None))
    return np.array(rows).T


def turn(rows):
    return pltpu.roll(rows, 64, 1)


def halves(low, high):
    return jnp.where(iota((1, 128), 1) < 64, low, high)


def put_rows(out, first, count, stride, rows):
    out[pl.ds(first, count, stride=stride), :] = rows


def put_320(out, first, count, load):
    even, odd = ([load(chunk, parity) for chunk in range(3)] for parity in range(2))
    turned = [turn(rows) for rows in odd]
    for at, rows in enumerate(
        (even[0], even[1], halves(even[2], turned[0]), halves(turned[0], turned[1]), halves(turned[1], turned[2]))
    ):
        put_rows(out, first + at, count // 2, 5, rows)


def every_other(ref, start, count):
    return ref[pl.ds(start, count, stride=2), :]


def out_a_kernel(scal, sums, q, o, kv, r, biases, gains):
    squares = (
        (q, 0, (0, 1, 6), False),
        (o, 0, (8, 9, 7), True),
        (kv, 0, (2, 3, 6), True),
        (kv, 25, (4, 5, 7), False),
    )
    for out, first, chunks, high in squares:
        for start, count, lane_row in ((0, 8, 0), (8, 2, 20)):

            def load(chunk, parity, chunks=chunks, high=high, start=start, count=count):
                rows = every_other(sums, a_place(1, start, chunks[chunk]) + parity, count // 2)
                return turn(rows) if chunk == 2 and high else rows

            put_320(out, first + lane_row, count, load)
    for c in range(10):
        for start, count in ((0, 8), (8, 2)):
            put_rows(r, 10 * start + c, count, 10, sums[pl.ds(a_place(0, start, c), count), :])
    small = sums[SMALL_ROW : SMALL_ROW + 8, :]
    biases[:, 0:128] = small[0:1]
    biases[:, 128:192] = small[1:2, 0:64]
    gains[...] = pltpu.roll(small, (128 - ((56 * scal[0]) & 63)) & 127, 1)[2:3, 0:56]


def out_b_kernel(scal, sums, w2, w1):
    for c in range(10):
        for start, count in ((0, 8), (8, 2)):
            put_rows(w2, 10 * start + c, count, 10, sums[pl.ds(b_place(start, c), count), :])
    put_320(w1, 0, 40, lambda chunk, parity: every_other(sums, 104 + 40 * chunk + parity, 20))


def out_c_kernel(scal, sums, m):
    even = [every_other(sums, 16 * c, 8) for c in range(23)]
    turned = [turn(every_other(sums, 16 * c + 1, 8)) for c in range(23)]
    for c in range(22):
        put_rows(m, c, 8, 45, even[c])
        put_rows(m, 23 + c, 8, 45, halves(turned[c], turned[c + 1]))
    put_rows(m, 22, 8, 45, halves(even[22], turned[0]))


def split_ten(row, per, magic):
    owner = (row * magic) >> 16
    return owner, row - per * owner


def tens(row, me):
    owner, rest = split_ten(row, 10, 6554)
    slot = slot_of(owner ^ me)
    return jnp.where(rest < 8, slot * 8 + rest, 248 + slot * 2 + rest)


def keyval_tens(row, me, upper):
    owner, rest = split_ten(row, 20, 3277)
    inside = (rest >= 10) if upper else (rest < 10)
    return jnp.where(inside, tens(10 * owner + rest - (10 if upper else 0), me), -1)


def rest_row(row):
    return 64 * ((row & 7) >> 1) + 2 * (row >> 3) + (row & 1)


def orders_kernel(scal, from_tens, to_tens, from_lower, from_upper, to_lower, to_upper, from_rest, to_rest):
    me = scal[0]
    from_tens[...] = one_hot(iota((D, D), 1) == tens(iota((D, 1), 0), me))
    to_tens[...] = one_hot(iota((D, D), 0) == tens(iota((1, D), 1), me))
    for upper, down, up in ((False, from_lower, to_lower), (True, from_upper, to_upper)):
        down[...] = one_hot(iota((2 * D, D), 1) == keyval_tens(iota((2 * D, 1), 0), me, upper))
        up[...] = one_hot(iota((D, 2 * D), 0) == keyval_tens(iota((1, 2 * D), 1), me, upper))
    from_rest[...] = one_hot(iota((256, 256), 0) == rest_row(iota((1, 256), 1)))
    to_rest[...] = one_hot(iota((256, 256), 1) == rest_row(iota((256, 1), 0)))


def norm(values, gain, shift):
    mean = jnp.mean(values, axis=0, keepdims=True)
    centred = values - mean
    rstd = lax.rsqrt(jnp.mean(centred * centred, axis=0, keepdims=True) + EPS)
    return centred * rstd * gain + shift, mean, rstd


def norm_back(grad, hat, rstd, gain):
    scaled = grad * gain
    return rstd * (
        scaled
        - jnp.mean(scaled, axis=0, keepdims=True)
        - hat * jnp.mean(scaled * hat, axis=0, keepdims=True)
    )


def stat_rows(mean, rstd):
    row = iota((8, mean.shape[1]), 0)
    return jnp.where(row == 0, mean, jnp.where(row == 1, rstd, 0.0))


def entry_kernel(scal, tokens, entry, stats, turned):
    side = scal[1]
    for quad in range(4):
        lane = iota((1, 256), 1) + quad * 256
        row, col = token_place(lane)
        natural = row * SIDE + col
        pick = one_hot(iota((TOKENS, 256), 0) == natural)
        turned[:, quad * 256 : quad * 256 + 256] = pick
        mask = jnp.where((row < side) & (col < side), 1.0, 0.0)
        entry[:, quad * 256 : quad * 256 + 256] = (dot(tokens[...], pick) * mask).astype(BF16)

    def body(tile):
        values = entry[:, lanes(tile)].astype(F32)
        mean = jnp.mean(values, axis=0, keepdims=True)
        centred = values - mean
        rstd = lax.rsqrt(jnp.mean(centred * centred, axis=0, keepdims=True) + EPS)
        stats[:, lanes(tile)] = stat_rows(mean, rstd)

    loop(8, body)


def small_table(me, low, high):
    gathered = jnp.concatenate(
        [half[:, SMALL_ROW : SMALL_ROW + 8, :].astype(F32).reshape(128, 128) for half in (low, high)], axis=0
    ).astype(BF16)
    vector = iota((128, 256), 0)
    place = iota((128, 256), 1)
    row = place & 7
    owner = xor_of(place >> 3) ^ me
    first = (7 * owner) >> 3
    straight = (
        ((row == 0) & (vector == 3 * owner))
        | ((row == 1) & (vector == 3 * owner + 2))
        | ((row == 2) & (vector == 96 + first))
    )
    turned = ((row == 0) & (vector == 3 * owner + 1)) | ((row == 2) & (vector == 97 + first))
    rows = dot(one_hot(straight), gathered) + pltpu.roll(dot(one_hot(turned), gathered), 64, 1)
    return jnp.transpose(rows)[0:64, :]


def project_kernel(scal, from_tens, from_lower, from_upper, from_rest, low, high, entry, stats, wq, wkv, wrs, wo, first, qs, raw, stat_r, red, kv, kt, vt, bt, square, rest, redin):
    me = scal[0]
    bt[...] = small_table(me, low, high)
    for half, source in enumerate((low, high)):

        def chunk(c, half=half, source=source):
            block = source[:, 16 * c : 16 * c + 16, :].astype(F32)
            rows = slice(128 * half, 128 * half + 128)
            wrs[rows, lanes(c)] = block[:, 0:8].reshape(128, 128).astype(BF16)
            square[rows, lanes(c)] = block[:, 8:16].reshape(128, 128).astype(BF16)

        for c in range(10):
            chunk(c)
        block = source[:, 160:208, :].astype(F32)
        for c in range(5):
            part = block[:, 8 * c : 8 * c + 8].reshape(128, 128).astype(BF16)
            rest[128 * half : 128 * half + 128, 128 * c : 128 * c + 128] = part

    def last_two(p):
        part = dot(from_rest[...], rest[:, lanes(p)]).astype(BF16)
        wrs[256:320, lanes(p, 256)] = jnp.concatenate([part[0:64], part[64:128]], axis=1)
        square[256:320, lanes(p, 256)] = jnp.concatenate([part[128:192], part[192:256]], axis=1)

    for p in range(5):
        last_two(p)
    wq[:, 0:256] = dot(from_tens[...], square[:, 0:256]).astype(BF16)
    wo[:, 0:256] = dot(from_tens[...], square[:, 1024:1280]).astype(BF16)
    tails = dot(from_tens[...], square[:, 768:1024])
    wq[:, 256:320] = tails[:, 0:64].astype(BF16)
    wo[:, 256:320] = pltpu.roll(tails, 64, 1)[:, 0:64].astype(BF16)
    wkv[:, 0:256] = (dot(from_lower[...], square[:, 256:512]) + dot(from_upper[...], square[:, 512:768])).astype(BF16)
    tail = pltpu.roll(dot(from_lower[...], square[:, 768:896]), 64, 1) + dot(from_upper[...], square[:, 896:1024])
    wkv[:, 256:320] = tail[:, 0:64].astype(BF16)

    gain, shift = column(bt, G_1, 5), column(bt, C_1, 5)

    def body(tile):
        centred = entry[:, lanes(tile)].astype(F32) - stats[0:1, lanes(tile)]
        first[:, lanes(tile)] = (centred * stats[1:2, lanes(tile)] * gain + shift).astype(BF16)

    for tile in range(8):
        body(tile)
    for quad in range(4):
        redin[D * quad : D * quad + D, :] = first[:, 256 * quad : 256 * quad + 256]
    bias = column(bt, B_Q, 5)
    bias = jnp.concatenate([bias, bias], axis=1)
    for quad in range(4):
        at = lanes(quad, 256)
        qs[:, at] = (dot(wq[...], first[:, at]) + bias).astype(BF16) * BF16(0.125)
    bias = column(bt, B_R, 5)
    bias = jnp.concatenate([bias, bias], axis=1)
    mixed = dot(wrs[...], redin[...])
    total = bias
    for part in range(3):
        piece = mixed.astype(BF16)
        total = total + dot(from_tens[...], piece)
        mixed = mixed - piece.astype(F32)
    raw[...] = total
    gain, shift = column(bt, G_R, 5), column(bt, C_R, 5)
    for tile in range(2):
        at = slice(128 * tile, 128 * tile + 128)
        values, mean, rstd = norm(raw[:, at], gain, shift)
        red[:, at] = values.astype(BF16)
        stat_r[:, at] = stat_rows(mean, rstd)
    keyval = dot(wkv[...], red[...])
    kv[...] = keyval.astype(BF16)
    turned = jnp.transpose(keyval)
    for h in range(HEADS):
        kt[h] = turned[:, 64 * h : 64 * h + 64].astype(BF16)
        vt[h] = turned[:, D + 64 * h : D + 64 * h + 64].astype(BF16)


def key_bias(side):
    i, j = key_place(iota((QUARTER, 1), 0))
    return jnp.where((i < (side >> 1)) & (j < (side >> 1)), 0.0, -10000.0)


def head_rows(h):
    return pl.ds(pl.multiple_of(64 * h, 64), 64)


def attend_kernel(scal, kt, qs, kv, att, lse, scores_a, scores_b, probs_a, probs_b):
    bias = key_bias(scal[1])

    def score(scores, h, start):
        scores[...] = dot(kt[h], qs[head_rows(h), start : start + 512])

    def finish(scores, probs, h, start):
        for tile in range(4):
            at = slice(128 * tile, 128 * tile + 128)
            to = slice(start + 128 * tile, start + 128 * tile + 128)
            part = scores[:, at] + bias
            top = jnp.max(part, axis=0, keepdims=True)
            weights = jnp.exp(part - top)
            total = jnp.sum(weights, axis=0, keepdims=True)
            lse[h, :, to] = top + jnp.log(total)
            probs[:, at] = (weights * (1.0 / total)).astype(BF16)
        values = kv[pl.ds(pl.multiple_of(D + 64 * h, 64), 64), :]
        att[head_rows(h), start : start + 512] = dot(values, probs[...]).astype(BF16)

    score(scores_a, 0, 0)

    def head(h):
        score(scores_b, h, 512)
        finish(scores_a, probs_a, h, 0)
        score(scores_a, jnp.minimum(h + 1, HEADS - 1), 0)
        finish(scores_b, probs_b, h, 512)

    loop(HEADS, head)


def middle_kernel(scal, bt, wo, att, entry, mid, sec, stats, work):
    side = scal[1]
    bias, gain, shift = column(bt, B_O, 5), column(bt, G_2, 5), column(bt, C_2, 5)

    def body(tile):
        at = lanes(tile)
        mask = token_mask(tile, side)
        values = entry[:, at].astype(F32) + mask * (work[:, at] + bias)
        mid[:, at] = values
        normed, mean, rstd = norm(values, gain, shift)
        stats[:, at] = stat_rows(mean, rstd)
        sec[0:D, at] = (normed.astype(BF16).astype(F32) * mask).astype(BF16)
        sec[D : D + 64, at] = jnp.where(iota((64, 128), 0) == 9, mask, 0.0).astype(BF16)

    for quad in range(4):
        at = lanes(quad, 256)
        work[:, at] = dot(wo[...], att[:, at])
        body(2 * quad)
        body(2 * quad + 1)


def ffn_weights_kernel(scal, bt, from_tens, from_rest, low, high, w1, w1t, w2, w2t, taps, main, rest, wide):
    me = scal[0]
    for half, source in enumerate((low, high)):
        def chunks(p, half=half, source=source):
            block = source[:, pl.ds(pl.multiple_of(16 * p, 16), 16), :].astype(F32)
            both = jnp.concatenate([block[:, 0:8].reshape(128, 128), block[:, 8:16].reshape(128, 128)], axis=1)
            main[128 * half : 128 * half + 128, lanes(p, 256)] = both.astype(BF16)

        loop(5, chunks)
        block = source[:, 80:112, :].astype(F32)
        for c in range(3):
            part = block[:, 8 * c : 8 * c + 8].reshape(128, 128).astype(BF16)
            rest[128 * half : 128 * half + 128, 128 * c : 128 * c + 128] = part

        def expansion(slot, half=half, source=source):
            owner = ((slot << 1) | half) ^ me
            block = source[slot, 80:224, :].astype(F32)
            rows = pl.ds(pl.multiple_of(40 * owner, 8), 40)
            for c in range(3):
                wide[rows, 128 * c : 128 * c + 128] = block[24 + 40 * c : 64 + 40 * c]

        loop(16, expansion)
    for j in range(3):
        part = dot(from_rest[...], rest[:, 128 * j : 128 * j + 128]).astype(BF16)
        for k in range(4 if j < 2 else 2):
            c = 4 * j + k
            main[256:320, 128 * c : 128 * c + 128] = part[64 * k : 64 * k + 64]

    def block(p):
        rows = lanes(p, 256)
        full = dot(from_tens[...], main[:, lanes(p, 256)])
        w2[:, lanes(p, 256)] = full.astype(BF16)
        w2t[rows, :] = jnp.transpose(full).astype(BF16)
        w1t[:, lanes(p, 256)] = jnp.transpose(wide[rows, :])[0:D].astype(BF16)

    for p in range(5):
        block(p)
    low_tail = wide[:, 256:384].astype(BF16)

    def spread(tap):
        taps[tap] = dot(low_tail, one_hot(iota((128, 128), 0) == 64 + tap))

    for tap in range(9):
        spread(tap)
    w1[:, 0:256] = wide[:, 0:256].astype(BF16)
    lane = iota((64, 128), 1)
    for h in range(20):
        rows = slice(64 * h, 64 * h + 64)
        taps[9, rows, :] = jnp.broadcast_to(bt[:, B_DW + h : B_DW + h + 1], (64, 128))
        beside = jnp.where(lane == 73, bt[:, B_1 + h : B_1 + h + 1], 0.0)
        w1[rows, 256:384] = jnp.where(lane < 64, wide[rows, 256:384], beside).astype(BF16)


def edge_masks():
    lane = iota((1, 128), 1)
    j = lane & 15
    return jnp.where(j != 0, 1.0, 0.0), jnp.where(j != 15, 1.0, 0.0), lane >= 16, lane < 112


def left_of(tiles):
    return [pltpu.roll(tile, 1, 1) for tile in tiles]


def right_of(tiles):
    return [pltpu.roll(tile, 127, 1) for tile in tiles]


def above(tiles, inside):
    turned = [pltpu.roll(tile, 16, 1) for tile in tiles]
    return [jnp.where(inside, turned[0], 0.0), jnp.where(inside, turned[1], turned[0])]


def below(tiles, inside):
    turned = [pltpu.roll(tile, 112, 1) for tile in tiles]
    return [jnp.where(inside, turned[0], turned[1]), jnp.where(inside, turned[1], 0.0)]


def times(tiles, factor):
    return [tile * factor for tile in tiles]


def plus(*many):
    return [functools.reduce(lambda a, b: a + b, tiles) for tiles in zip(*many)]


def tile_at(a, e, half):
    start = 256 * (2 * a + e) + 128 * half
    return slice(start, start + 128)


def quads(ref, rows):
    return [[[ref[rows, tile_at(a, e, half)] for half in range(2)] for e in range(2)] for a in range(2)]


LOG2E = float(np.log2(np.e))


def gelu_parts(x):
    y = x * np.float32(0.5**0.5)
    cdf = lax.erf(y) * 0.5 + 0.5
    bell = jnp.exp2(y * y * np.float32(-LOG2E) + np.float32(-0.5 * np.log2(2.0 * np.pi)))
    return x * cdf, cdf + x * bell


def ffn_kernel(scal, w1, taps, sec, act, slope, hid_a, hid_b):
    j_first, j_last, i_first, i_last = edge_masks()

    def fill(hid, step):
        rows = pl.ds(pl.multiple_of(jnp.minimum(step, FF // 64 - 1) * 64, 64), 64)
        hid[...] = dot(w1[rows, :], sec[...])

    def group(hid, step, index):
        rows = slice(16 * index, 16 * index + 16)
        out_rows = pl.ds(pl.multiple_of(64 * step + 16 * index, 16), 16)
        k = [taps[n, out_rows, :] for n in range(10)]
        first = [k[3 * r] * j_first for r in range(3)]
        last = [k[3 * r + 2] * j_last for r in range(3)]
        quad = quads(hid, rows)
        left = [left_of(quad[a][1]) for a in range(2)]
        right = [right_of(quad[a][0]) for a in range(2)]

        def across(a, e, r):
            if e == 0:
                parts = zip(left[a], quad[a][0], quad[a][1])
                return [first[r] * x + k[3 * r + 1] * y + k[3 * r + 2] * z for x, y, z in parts]
            parts = zip(quad[a][0], quad[a][1], right[a])
            return [k[3 * r] * x + k[3 * r + 1] * y + last[r] * z for x, y, z in parts]

        for e in range(2):
            up = above(across(1, e, 0), i_first)
            down = below(across(0, e, 2), i_last)
            outs = (plus(across(0, e, 1), across(1, e, 2), up), plus(across(0, e, 0), across(1, e, 1), down))
            for a in range(2):
                for half in range(2):
                    value, grad = gelu_parts(outs[a][half] + k[9])
                    act[out_rows, tile_at(a, e, half)] = value.astype(BF16)
                    slope[out_rows, tile_at(a, e, half)] = grad.astype(BF16)

    fill(hid_a, 0)

    def two(index):
        fill(hid_b, 2 * index + 1)
        for n in range(4):
            group(hid_a, 2 * index, n)
        fill(hid_a, 2 * index + 2)
        for n in range(4):
            group(hid_b, 2 * index + 1, n)

    loop(FF // 128, two)


def ending_kernel(scal, bt, w2, act, mid, end, sect, stats, work):
    side = scal[1]
    bias, gain, shift = column(bt, B_2, 5), column(bt, G_S, 5), column(bt, C_S, 5)

    def body(tile):
        at = lanes(tile)
        mask = token_mask(tile, side)
        values = mid[:, at] + mask * (work[:, at] + bias)
        end[:, at] = values
        normed, mean, rstd = norm(values, gain, shift)
        stats[:, at] = stat_rows(mean, rstd)
        sect[:, at] = (normed.astype(BF16).astype(F32) * mask).astype(BF16)

    for quad in range(4):
        at = lanes(quad, 256)
        work[:, at] = dot(w2[...], act[:, at])
        body(2 * quad)
        body(2 * quad + 1)


def lane_sum(values):
    return jnp.sum(values, axis=1, keepdims=True)


def merge_kernel(scal, bt, c_low, c_high, sect, end, stats, cot, four, keep, send, end_grad, branch, grads, wm, patch, mg, back, work, natural):
    me, side = scal[0], scal[1]
    grads[...] = jnp.zeros_like(grads)
    for half, source in enumerate((c_low, c_high)):

        def place(c, half=half, source=source):
            block = source[:, 16 * c : 16 * c + 16, :].reshape(256, 128)
            wm[256 * half : 256 * half + 256, lanes(c)] = block

        for c in range(23):
            place(c)

    def reorder(to_owner):
        def one(slot):
            at = pl.ds(pl.multiple_of(16 * slot, 16), 16)
            owner = pl.ds(pl.multiple_of((xor_of(slot) ^ me) * 16, 16), 16)
            to_owner(at, owner)

        loop(32, one)

    j_first, j_last, i_first, i_last = edge_masks()
    quad = [[[t.astype(F32) for t in pair] for pair in row] for row in quads(sect, slice(None))]
    left = [times(left_of(quad[a][1]), j_first) for a in range(2)]
    pieces = (
        above(left[1], i_first),
        above(quad[1][0], i_first),
        above(quad[1][1], i_first),
        left[0],
        quad[0][0],
        quad[0][1],
        left[1],
        quad[1][0],
        quad[1][1],
    )
    for n, piece in enumerate(pieces):
        for half in range(2):
            patch[D * n : D * n + D, 128 * half : 128 * half + 128] = piece[half].astype(BF16)
    patch[9 * D :, :] = jnp.zeros((MERGE_PAD - 9 * D, 256), BF16)
    bias, gain, shift = column(bt, B_M, 8), column(bt, G_M, 8), column(bt, C_M, 8)
    work[...] = dot(wm[...], patch[...])

    def from_slots(at, owner):
        natural[owner, :] = work[at, :]

    reorder(from_slots)
    half_side = side >> 1
    for tile in range(2):
        at = slice(128 * tile, 128 * tile + 128)
        i, j = key_place(iota((1, 128), 1) + 128 * tile)
        mask = jnp.where((i < half_side) & (j < half_side), 1.0, 0.0)
        values = natural[:, at] + bias
        mean = jnp.mean(values, axis=0, keepdims=True)
        centred = values - mean
        rstd = lax.rsqrt(jnp.mean(centred * centred, axis=0, keepdims=True) + EPS)
        hat = centred * rstd
        four[:, at] = ((hat * gain + shift) * mask).astype(BF16)
        grad = cot[:, at].astype(F32) * mask
        low = norm_back(grad, hat, rstd, gain).astype(BF16)
        natural[:, at] = low.astype(F32)
        parts = (grad * hat, grad, low.astype(F32))
        sums = parts if tile == 0 else [s + v for s, v in zip(sums, parts)]
    put_column(grads, G_M, lane_sum(sums[0]))
    put_column(grads, C_M, lane_sum(sums[1]))
    put_column(grads, B_M, lane_sum(sums[2]))

    def to_slots(at, owner):
        mg[at, :] = natural[owner, :].astype(BF16)

    reorder(to_slots)

    def widths(body):
        loop(11, lambda c: body(pl.multiple_of(c * 256, 256), 256))
        body(11 * 256, 128)

    def patch_grad(start, width):
        back[pl.ds(start, width), :] = dot_tn(wm[:, pl.ds(start, width)], mg[...])


    def give(start, width):
        block = dot_nt(mg[...], patch[pl.ds(start, width), :]).astype(BF16)
        for c in range(width // 128):
            to = pl.ds(pl.multiple_of((start >> 3) + 16 * c, 16), 16)
            part = block[:, 128 * c : 128 * c + 128].reshape(32, 16, 128)
            keep[:, to, :] = part[0:16]
            send[:, to, :] = part[16:32]

    def both(start, width):
        patch_grad(start, width)
        give(start, width)

    widths(both)

    def piece(n):
        return [back[D * n : D * n + D, 128 * half : 128 * half + 128] for half in range(2)]

    results = (
        piece(4),
        plus(piece(5), times(right_of(piece(3)), j_last)),
        plus(piece(7), below(piece(1), i_last)),
        plus(
            piece(8),
            times(right_of(piece(6)), j_last),
            below(plus(piece(2), times(right_of(piece(0)), j_last)), i_last),
        ),
    )
    for n, values in enumerate(results):
        for half in range(2):
            end_grad[:, 256 * n + 128 * half : 256 * n + 128 * half + 128] = values[half]
    gain = column(bt, G_S, 5)
    zeros = jnp.zeros((D, 128), F32)

    def one(tile):
        at = lanes(tile)
        mask = token_mask(tile, side)
        grad = end_grad[:, at] * mask
        hat = (end[:, at] - stats[0:1, at]) * stats[1:2, at]
        result = norm_back(grad, hat, stats[1:2, at], gain)
        end_grad[:, at] = result
        low = (result * mask).astype(BF16)
        branch[:, at] = low
        return grad * hat, grad, low.astype(F32)

    sums = (zeros, zeros, zeros)
    for step in range(4):
        pairs = zip(sums, one(2 * step), one(2 * step + 1))
        sums = tuple(total + (x + y) for total, x, y in pairs)
    put_column(grads, G_S, lane_sum(sums[0]))
    put_column(grads, C_S, lane_sum(sums[1]))
    put_column(grads, B_2, lane_sum(sums[2]))


def ffn_back_kernel(first_part, count, scal, w1, w2t, taps, sec, slope, branch, hg, dkx, hid_a, hid_b, cg_a, cg_b):
    start, steps = 256 * first_part, 4 * count
    j_first, j_last, i_first, i_last = edge_masks()
    lane = iota((16, 128), 1)

    def fill(hid, cg, step):
        rows = pl.ds(pl.multiple_of(start + jnp.minimum(step, steps - 1) * 64, 64), 64)
        cg[...] = dot(w2t[rows, :], branch[...]) * slope[rows, :].astype(F32)
        hid[...] = dot(w1[rows, :], sec[...])

    def group(hid, cg, step, index):
        rows = slice(16 * index, 16 * index + 16)
        from_rows = pl.ds(pl.multiple_of(start + 64 * step + 16 * index, 16), 16)
        to_rows = pl.ds(pl.multiple_of(64 * step + 16 * index, 16), 16)
        k = [taps[n, from_rows, :] for n in range(9)]
        quad = quads(cg, rows)
        bias = functools.reduce(lambda x, y: x + y, [t for row in quad for pair in row for t in pair])
        across = [
            (
                (times(left_of(quad[a][1]), j_first), quad[a][0], quad[a][1]),
                (quad[a][0], quad[a][1], times(right_of(quad[a][0]), j_last)),
            )
            for a in range(2)
        ]
        sums = [None] * 9
        for e in range(2):
            upper = [above(tiles, i_first) for tiles in across[1][e]]
            lower = [below(tiles, i_last) for tiles in across[0][e]]
            for a, near in ((0, (upper, across[0][e], across[1][e])), (1, (across[0][e], across[1][e], lower))):
                for half in range(2):
                    value = hid[rows, tile_at(a, e, half)]
                    total = None
                    for r in range(3):
                        for c in range(3):
                            tap = 3 * (2 - r) + (2 - c)
                            term = k[tap] * near[r][c][half]
                            total = term if total is None else total + term
                            term = value * near[r][c][half]
                            sums[tap] = term if sums[tap] is None else sums[tap] + term
                    hg[to_rows, tile_at(a, e, half)] = total.astype(BF16)
        table = jnp.where(lane == 9, lane_sum(bias), 0.0)
        for n in range(9):
            table = jnp.where(lane == n, lane_sum(sums[n]), table)
        dkx[to_rows, :] = table

    fill(hid_a, cg_a, 0)

    def two(index):
        fill(hid_b, cg_b, 2 * index + 1)
        for n in range(4):
            group(hid_a, cg_a, 2 * index, n)
        fill(hid_a, cg_a, 2 * index + 2)
        for n in range(4):
            group(hid_b, cg_b, 2 * index + 1, n)

    loop(steps // 2, two)


def middle_back_kernel(scal, bt, w1t, hg0, hg1, end_grad, mid, stats, mid_grad, low_grad, grads, work):
    side = scal[1]
    grads[...] = jnp.zeros_like(grads)
    gain = column(bt, G_2, 5)
    zeros = jnp.zeros((D, 128), F32)

    def one(tile):
        at = lanes(tile)
        mask = token_mask(tile, side)
        grad = work[:, at] * mask
        hat = (mid[:, at] - stats[0:1, at]) * stats[1:2, at]
        result = end_grad[:, at] + norm_back(grad, hat, stats[1:2, at], gain)
        mid_grad[:, at] = result
        low = (result * mask).astype(BF16)
        low_grad[:, at] = low
        return grad * hat, grad, low.astype(F32)

    sums = (zeros, zeros, zeros)
    for quad in range(4):
        at = lanes(quad, 256)
        work[:, at] = sum(
            dot(w1t[:, 256 * start : 256 * (start + count)], hg[:, at]) for hg, (start, count) in zip((hg0, hg1), PARTS)
        )
        pairs = zip(sums, one(2 * quad), one(2 * quad + 1))
        sums = tuple(total + (x + y) for total, x, y in pairs)
    put_column(grads, G_2, lane_sum(sums[0]))
    put_column(grads, C_2, lane_sum(sums[1]))
    put_column(grads, B_O, lane_sum(sums[2]))


def pack_b_kernel(scal, to_tens, hg0, hg1, dk0, dk1, sec, branch, act, keep, send, grads, dw1, gather, mixed):
    me = scal[0]
    grads[...] = jnp.zeros_like(grads)
    lane = iota((256, 128), 1)
    mixed[...] = dot(to_tens[...], branch[...]).astype(BF16)
    gather[:, 0:24, :] = jnp.zeros((32, 24, 128), F32)

    def contraction(p):
        block = dot_nt(mixed[...], act[pl.ds(pl.multiple_of(256 * p, 256), 256), :])
        parts = [block[0:256, 128 * e : 128 * e + 128].reshape(32, 1, 8, 128) for e in range(2)]
        full = jnp.concatenate(parts, axis=1).reshape(32, 16, 128).astype(BF16)
        to = pl.ds(pl.multiple_of(16 * p, 16), 16)
        keep[:, to, :] = full[0:16]
        send[:, to, :] = full[16:32]
        tail = jnp.concatenate([block[256:320, 0:128], block[256:320, 128:256]], axis=0).astype(BF16)
        place = rest_row(iota((256, 1), 0)) - 128 * (p & 1)
        to = pl.ds(pl.multiple_of(8 * (p >> 1), 8), 8)
        gather[:, to, :] += dot(one_hot(iota((256, 128), 1) == place), tail).reshape(32, 8, 128)

    for hg, dkx, (at, count) in zip((hg0, hg1), (dk0, dk1), PARTS):

        def outer(n, hg=hg, dkx=dkx, at=at):
            rows = pl.ds(pl.multiple_of(256 * n, 256), 256)
            to = pl.ds(pl.multiple_of(256 * (n + at), 256), 256)
            part = dot_nt(hg[rows, :], sec[...])
            dw1[to, 0:256] = part[:, 0:256]
            turned = pltpu.roll(dkx[rows, :], 64, 1)
            dw1[to, 256:384] = jnp.where(lane < 64, part[:, 256:384], jnp.where(lane < 73, turned, 0.0))
            table = grads[...]
            for m in range(4):
                here = slice(64 * m, 64 * m + 64)
                number = 4 * (n + at) + m
                table = jnp.where(lane[here] == B_1 + number, part[here, 329:330], table)
                table = jnp.where(lane[here] == B_DW + number, dkx[rows, :][here, 9:10], table)
            grads[...] = table
            contraction(n + at)

        loop(count, outer)

    def expansion(owner):
        slot = slot_of(owner ^ me)
        rows = pl.ds(pl.multiple_of(40 * owner, 8), 40)
        for c in range(3):
            gather[slot, 24 + 40 * c : 64 + 40 * c, :] = dw1[rows, 128 * c : 128 * c + 128]

    loop(32, expansion)
    keep[:, 80:224, :] = gather[0:16].astype(BF16)
    send[:, 80:224, :] = gather[16:32].astype(BF16)


def attend_back_kernel(scal, kt, vt, qs, kv, wo, low_grad, lse, dq, dkv, og, scores_a, scores_b, grads_a, grads_b, probs_a, probs_b, back_a, back_b):
    bias = key_bias(scal[1])
    og[...] = dot_tn(wo[...], low_grad[...]).astype(BF16)

    def score(scores, grads, h, start):
        at = slice(start, start + 512)
        scores[...] = dot(kt[h], qs[head_rows(h), at])
        grads[...] = dot(vt[h], og[head_rows(h), at])

    def finish(scores, grads, probs, back, h, start):
        for tile in range(4):
            at = slice(128 * tile, 128 * tile + 128)
            to = slice(start + 128 * tile, start + 128 * tile + 128)
            weights = jnp.exp(scores[:, at] + bias - lse[h, :, to])
            grad = grads[:, at]
            mean = jnp.sum(weights * grad, axis=0, keepdims=True)
            back[:, at] = (weights * (grad - mean)).astype(BF16)
            probs[:, at] = weights.astype(BF16)
        rows, at = head_rows(h), slice(start, start + 512)
        dq[rows, at] = (dot(kv[rows, :], back[...]) * 0.125).astype(BF16)
        return dot_nt(qs[rows, at], back[...]), dot_nt(og[rows, at], probs[...])

    score(scores_a, grads_a, 0, 0)

    def head(h):
        score(scores_b, grads_b, h, 512)
        one = finish(scores_a, grads_a, probs_a, back_a, h, 0)
        score(scores_a, grads_a, jnp.minimum(h + 1, HEADS - 1), 0)
        two = finish(scores_b, grads_b, probs_b, back_b, h, 512)
        dkv[head_rows(h), :] = (one[0] + two[0]).astype(BF16)
        dkv[pl.ds(pl.multiple_of(D + 64 * h, 64), 64), :] = (one[1] + two[1]).astype(BF16)

    loop(HEADS, head)


def first_kernel(scal, bt, to_tens, to_lower, to_upper, to_rest, wq, wkv, wrs, first, red, raw, stat_r, dq, dkv, low_grad, att, entry, stats, g_one, g_two, g_three, keep, send, work, grads, wide, redin, stack_r, stack_z, tails_of):
    me = scal[0]
    grads[...] = g_one[...] + g_two[...] + g_three[...]
    for quad in range(4):
        redin[D * quad : D * quad + D, :] = first[:, 256 * quad : 256 * quad + 256]
    dred = dot_tn(wkv[...], dkv[...])
    gain = column(bt, G_R, 5)
    lows = []
    for tile in range(2):
        at = slice(128 * tile, 128 * tile + 128)
        grad = dred[:, at]
        hat = (raw[:, at] - stat_r[0:1, at]) * stat_r[1:2, at]
        low = norm_back(grad, hat, stat_r[1:2, at], gain).astype(BF16)
        lows.append(low)
        parts = (grad * hat, grad, low.astype(F32))
        sums = parts if tile == 0 else [s + v for s, v in zip(sums, parts)]
    put_column(grads, G_R, lane_sum(sums[0]))
    put_column(grads, C_R, lane_sum(sums[1]))
    put_column(grads, B_R, lane_sum(sums[2]))
    low = jnp.concatenate(lows, axis=1)
    low = dot(to_tens[...], low).astype(BF16)
    wide[...] = dot_tn(wrs[...], low)
    straight = dot_tn(wq[...], dq[...])
    for quad in range(4):
        at = slice(256 * quad, 256 * quad + 256)
        work[:, at] = straight[:, at] + wide[D * quad : D * quad + D, :]
    zeros = jnp.zeros((D, 128), F32)

    def one(tile):
        at = lanes(tile)
        grad = work[:, at]
        hat = (entry[:, at].astype(F32) - stats[0:1, at]) * stats[1:2, at]
        return grad * hat, grad, dq[:, at].astype(F32)

    sums = (zeros, zeros, zeros)
    for step in range(4):
        pairs = zip(sums, one(2 * step), one(2 * step + 1))
        sums = tuple(total + (x + y) for total, x, y in pairs)
    put_column(grads, G_1, lane_sum(sums[0]))
    put_column(grads, C_1, lane_sum(sums[1]))
    put_column(grads, B_Q, lane_sum(sums[2]))
    stack_r[...] = dot_nt(low, redin[...])

    def outer(pick, grad, value):
        return dot_nt(dot(pick[...], grad[...]).astype(BF16), value[...])

    parts = (
        outer(to_tens, dq, first),
        outer(to_lower, dkv, red),
        outer(to_upper, dkv, red),
        outer(to_tens, low_grad, att),
    )
    for part, at in zip(parts, (0, 256, 512, 1024)):
        stack_z[:, at : at + 256] = part[:, 0:256]
    stack_z[:, 768:1024] = jnp.concatenate([part[:, 256:320] for part in parts], axis=1)

    def pack(p):
        at = lanes(p, 256)
        both = stack_r[:, at], stack_z[:, at]
        for e in range(2):
            pieces = [block[0:256, 128 * e : 128 * e + 128].reshape(32, 1, 8, 128) for block in both]
            full = jnp.concatenate(pieces, axis=1).reshape(32, 16, 128).astype(BF16)
            to = pl.ds(pl.multiple_of(32 * p + 16 * e, 16), 16)
            keep[:, to, :] = full[0:16]
            send[:, to, :] = full[16:32]
        tail = jnp.concatenate(
            [block[256:320, 128 * e : 128 * e + 128] for block in both for e in range(2)], axis=0
        ).astype(BF16)
        to = pl.ds(pl.multiple_of(8 * p, 8), 8)
        tails_of[:, to, :] = dot(to_rest[...], tail).reshape(32, 8, 128)

    loop(5, pack)
    rows = jnp.transpose(jnp.concatenate([grads[...], jnp.zeros((64, 128), F32)], axis=0)).astype(BF16)
    place = iota((256, 128), 0)
    vector = iota((256, 128), 1)
    line = place & 7
    owner = xor_of(place >> 3) ^ me
    start = (7 * owner) >> 3
    straight = (
        ((line == 0) & (vector == 3 * owner))
        | ((line == 1) & (vector == 3 * owner + 2))
        | ((line == 2) & (vector == 96 + start))
    )
    turned = ((line == 0) & (vector == 3 * owner + 1)) | ((line == 2) & (vector == 97 + start))
    small = dot(one_hot(straight), rows) + pltpu.roll(dot(one_hot(turned), rows), 64, 1)
    tails_of[:, 40:48, :] = small.reshape(32, 8, 128)
    keep[:, 160:208, :] = tails_of[0:16].astype(BF16)
    send[:, 160:208, :] = tails_of[16:32].astype(BF16)


def token_kernel(scal, bt, turned, grad_in, mid_grad, entry, stats, tok, high, rest):
    side = scal[1]
    gain = column(bt, G_1, 5)

    def body(tile):
        at = lanes(tile)
        hat = (entry[:, at].astype(F32) - stats[0:1, at]) * stats[1:2, at]
        result = mid_grad[:, at] + norm_back(grad_in[:, at], hat, stats[1:2, at], gain)
        result = result * token_mask(tile, side)
        upper = result.astype(BF16)
        high[:, at] = upper
        rest[:, at] = (result - upper.astype(F32)).astype(BF16)

    for tile in range(8):
        body(tile)

    def quad(index):
        pick = turned[pl.ds(pl.multiple_of(256 * index, 256), 256), :]
        tok[:, lanes(index, 256)] = dot_nt(high[...], pick) + dot_nt(rest[...], pick)

    loop(4, quad)


def cost(micros):
    return pl.CostEstimate(flops=int(micros * 1e9), bytes_accessed=1000, transcendentals=0)


def call(kernel, args, outs, scratch=(), micros=5):
    return pl.pallas_call(
        kernel,
        in_specs=[pl.BlockSpec(memory_space=pltpu.SMEM if arg.dtype == I32 else pltpu.VMEM) for arg in args],
        out_shape=[jax.ShapeDtypeStruct(shape, dtype) for shape, dtype in outs],
        scratch_shapes=[pltpu.VMEM(shape, dtype) for shape, dtype in scratch],
        compiler_params=pltpu.CompilerParams(vmem_limit_bytes=VMEM_LIMIT),
        cost_estimate=cost(micros),
    )(*args)


def local(group, axes, *arrays):
    return step_of(group, axes, *arrays)


def step_of(group, axes, tokens, image_side, cotangent, *shards):
    index = lax.axis_index(axes[0]) * lax.axis_size(axes[1]) + lax.axis_index(axes[1])
    me = index // group
    devices = SUPER * group

    def flip(values, mask):
        pairs = [(i, ((i // group) ^ mask) * group + i % group) for i in range(devices)]
        return lax.ppermute(values, axes, pairs)

    def gather(block, split=0, direct=False):
        held = block[None]
        if direct:
            held = jnp.concatenate([held, flip(held, 2), flip(held, 4), flip(held, 6)], axis=0)
        else:
            for mask in FLIPS[:2]:
                held = jnp.concatenate([held, flip(held, mask)], axis=0)
        if split:
            one, two = held[:, :split], held[:, split:]
            one, two = (jnp.concatenate([one, flip(one, 8)], axis=0), jnp.concatenate([two, flip(two, 16)], axis=0))
            far, near = flip(one, 16), flip(two, 8)
            two = jnp.concatenate([two[:4], near[:4], two[4:], near[4:]], axis=0)
            held = jnp.concatenate([jnp.concatenate([one, far], axis=0), two], axis=1)
        else:
            for mask in FLIPS[2:]:
                held = jnp.concatenate([held, flip(held, mask)], axis=0)
        return held, flip(held, 1)

    def scatter(keep, send, split=0, direct=False):
        def step(held, mask):
            return flip(held, mask).astype(F32)

        def halve(held, mask):
            half = held.shape[0] // 2
            return held[:half].astype(F32) + step(held[half:], mask)

        held = (keep.astype(F32) + step(send, 1)).astype(BF16)
        if split:
            one, two = held[:, :split], held[:, split:].reshape(2, 2, 4, -1, 128)
            one, two = (
                halve(one, 16).astype(BF16),
                (two[:, 0].astype(F32) + step(two[:, 1], 8)).astype(BF16).reshape(8, -1, 128),
            )
            held = jnp.concatenate([halve(one, 8), halve(two, 16)], axis=1).astype(BF16)
        else:
            held = halve(held, 16).astype(BF16)
            held = halve(held, 8).astype(BF16)
        if direct:
            far = step(held[2:3], 4), step(held[3:4], 6), step(held[1:2], 2)
            return (held[0:1].astype(F32) + far[2] + far[0] + far[1])[0]
        held = halve(held, 4).astype(BF16)
        return halve(held, 2)[0]

    if group > 1:
        per = lax.axis_size(axes[1])
        start = (index % per) // group * group

        def join(shard):
            full = lax.all_gather(shard, axes[1], axis=0)
            return lax.dynamic_slice_in_dim(full, start, group, axis=0).reshape(-1)

        shards = [join(shard) for shard in shards]
    query, keyval, reduce_w, output, expand, depth, contract, merge, gains, biases = shards

    def rows(flat):
        return flat.reshape(-1, 128)

    scal = jnp.stack([me.astype(I32), image_side[0].astype(I32)])
    taps = jnp.pad(depth.reshape(40, 9), ((0, 0), (64, 55)))
    block_a = select(
        [rows(query), rows(output), rows(keyval), rows(reduce_w)],
        table_a, A_ROWS, (scal, biases[None], gains[None]),
    )
    block_b = select([rows(contract), rows(expand), taps], table_b, B_ROWS)
    block_c = select([rows(merge)], table_c, C_ROWS)
    a_low, a_high = gather(block_a, A_SPLIT, True)
    b_low, b_high = gather(block_b, B_ROWS // 2, True)
    c_low, c_high = gather(block_c, C_ROWS // 2)

    big, narrow = (D, TOKENS), (D, QUARTER)
    from_tens, to_tens, from_lower, from_upper, to_lower, to_upper, from_rest, to_rest = call(
        orders_kernel,
        (scal,),
        [((D, D), BF16)] * 2 + [((2 * D, D), BF16)] * 2 + [((D, 2 * D), BF16)] * 2 + [((256, 256), BF16)] * 2,
        micros=2,
    )
    entry, stats_1, turned = call(
        entry_kernel, (scal, tokens[0]), [(big, BF16), ((8, TOKENS), F32), ((TOKENS, TOKENS), BF16)], micros=3.5)
    wq, wkv, wr, wo, first, qs, raw, stat_r, red, kv, kt, vt, bt = call(
        project_kernel,
        (scal, from_tens, from_lower, from_upper, from_rest, a_low, a_high, entry, stats_1),
        [
            ((D, D), BF16), ((2 * D, D), BF16), ((D, 4 * D), BF16), ((D, D), BF16), (big, BF16), (big, BF16),
            (narrow, F32), ((8, QUARTER), F32), (narrow, BF16), ((2 * D, QUARTER), BF16),
            ((HEADS, QUARTER, 64), BF16), ((HEADS, QUARTER, 64), BF16), ((64, 128), F32),
        ],
        [((D, 1280), BF16), ((256, 640), BF16), ((4 * D, QUARTER), BF16)],
        micros=8,
    )
    att, lse = call(attend_kernel, (scal, kt, qs, kv), [(big, BF16), ((HEADS, 1, TOKENS), F32)],
        [((QUARTER, 512), F32)] * 2 + [((QUARTER, 512), BF16)] * 2, micros=8.5)
    mid, sec, stats_2 = call(
        middle_kernel, (scal, bt, wo, att, entry), [(big, F32), ((384, TOKENS), BF16), ((8, TOKENS), F32)], [(big, F32)],
        micros=5,
    )
    w1, w1t, w2, w2t, taps = call(
        ffn_weights_kernel,
        (scal, bt, from_tens, from_rest, b_low, b_high),
        [((FF, 384), BF16), ((D, FF), BF16), ((D, FF), BF16), ((FF, D), BF16), ((10, FF, 128), F32)],
        [((D, FF), BF16), ((256, 384), BF16), ((FF, 384), F32)],
        micros=8,
    )
    act, slope = call(
        ffn_kernel,
        (scal, w1, taps, sec),
        [((FF, TOKENS), BF16), ((FF, TOKENS), BF16)],
        [((64, TOKENS), F32), ((64, TOKENS), F32)],
        micros=17,
    )
    end, sect, stats_s = call(
        ending_kernel, (scal, bt, w2, act, mid), [(big, F32), (big, BF16), ((8, TOKENS), F32)], [(big, F32)], micros=5
    )
    four, c_keep, c_send, end_grad, branch, g_one = call(
        merge_kernel,
        (scal, bt, c_low, c_high, sect, end, stats_s, cotangent[0]),
        [
            ((OUT_D, QUARTER), BF16), ((16, C_ROWS, 128), BF16), ((16, C_ROWS, 128), BF16), (big, F32), (big, BF16),
            ((64, 128), F32),
        ],
        [
            ((OUT_D, MERGE_PAD), BF16), ((MERGE_PAD, QUARTER), BF16), ((OUT_D, QUARTER), BF16),
            ((MERGE_PAD, QUARTER), F32), ((OUT_D, QUARTER), F32), ((OUT_D, QUARTER), F32),
        ],
        micros=20,
    )
    sum_c = scatter(c_keep, c_send, C_ROWS // 2)
    hgs, dks = [], []
    for at, count in PARTS:
        hg, dk = call(
            functools.partial(ffn_back_kernel, at, count),
            (scal, w1, w2t, taps, sec, slope, branch),
            [((256 * count, TOKENS), BF16), ((256 * count, 128), F32)],
            [((64, TOKENS), F32)] * 4,
            micros=6 * count,
        )
        hgs.append(hg)
        dks.append(dk)
    b_keep, b_send, g_three = call(
        pack_b_kernel,
        (scal, to_tens, *hgs, *dks, sec, branch, act),
        [((16, B_ROWS, 128), BF16), ((16, B_ROWS, 128), BF16), ((64, 128), F32)],
        [((FF, 384), F32), ((32, 144, 128), F32), (big, BF16)],
        micros=9,
    )
    sum_b = scatter(b_keep, b_send, B_ROWS // 2, True)
    mid_grad, low_grad, g_two = call(
        middle_back_kernel,
        (scal, bt, w1t, *hgs, end_grad, mid, stats_2),
        [(big, F32), (big, BF16), ((64, 128), F32)],
        [(big, F32)],
        micros=6,
    )
    dq, dkv = call(
        attend_back_kernel,
        (scal, kt, vt, qs, kv, wo, low_grad, lse),
        [(big, BF16), ((2 * D, QUARTER), BF16)],
        [(big, BF16)] + [((QUARTER, 512), F32)] * 4 + [((QUARTER, 512), BF16)] * 4,
        micros=9,
    )
    a_keep, a_send, first_grad = call(
        first_kernel,
        (
            scal, bt, to_tens, to_lower, to_upper, to_rest, wq, wkv, wr, first, red, raw, stat_r, dq, dkv, low_grad, att, entry, stats_1, g_one, g_two, g_three,
        ),
        [((16, A_ROWS, 128), BF16), ((16, A_ROWS, 128), BF16), (big, F32)],
        [
            ((64, 128), F32), ((4 * D, QUARTER), F32), ((4 * D, QUARTER), BF16), ((D, 1280), F32), ((D, 1280), F32),
            ((32, 48, 128), F32),
        ],
        micros=11,
    )
    sum_a = scatter(a_keep, a_send, A_SPLIT, True)
    (token_grad,) = call(
        token_kernel,
        (scal, bt, turned, first_grad, mid_grad, entry, stats_1),
        [(big, F32)],
        [(big, BF16), (big, BF16)],
        micros=5,
    )
    if group > 1:

        def total(part):
            full = lax.all_gather(part, axes[1], axis=0)
            return jnp.sum(lax.dynamic_slice_in_dim(full, start, group, axis=0), axis=0)

        sum_a, sum_b, sum_c = total(sum_a), total(sum_b), total(sum_c)

    def flat(count):
        return (count, 128), F32

    query_g, output_g, keyval_g, reduce_g, biases_g, gains_g = call(
        out_a_kernel,
        (scal, sum_a),
        [flat(25), flat(25), flat(50), flat(100), ((1, 192), F32), ((1, 56), F32)],
        micros=1,
    )
    contract_g, expand_g = call(out_b_kernel, (scal, sum_b), [flat(100), flat(100)], micros=1)
    (merge_g,) = call(out_c_kernel, (scal, sum_c), [flat(360)], micros=1)
    depth_g = sum_b[184:224, 64:73]
    grads = [query_g, keyval_g, reduce_g, output_g, expand_g, depth_g, contract_g, merge_g, gains_g, biases_g]
    grads = [grad.reshape(-1) for grad in grads]
    if group > 1:
        mine = index % group
        grads = [lax.dynamic_index_in_dim(grad.reshape(group, -1), mine, keepdims=False) for grad in grads]
    return (four[None], token_grad[None], *grads)


def solution(mesh):
    axes = ("dp", "fs")
    devices = mesh.shape["dp"] * mesh.shape["fs"]
    group = devices // SUPER
    if devices != SUPER * group or mesh.shape["fs"] % group:
        raise ValueError("unsupported mesh")
    one, three = P(axes), P(axes, None, None)
    return jax.shard_map(
        functools.partial(local, group, axes),
        mesh=mesh,
        in_specs=(three, one, three) + (one,) * 10,
        out_specs=(three, three) + (one,) * 10,
        check_vma=False,
    )
```

```python
import functools

import jax
import jax.numpy as jnp
import numpy as np
from jax import lax
from jax.experimental import pallas as pl
from jax.experimental.pallas import tpu as pltpu
from jax.sharding import PartitionSpec as P


D = 320
HEADS = 5
FF = 1280
OUT_D = 512
SIDE = 32
QUARTER = 256
TOKENS = SIDE * SIDE
MERGE_PAD = 2944
SUPER = 32
FLIPS = (2, 4, 8, 16)
EPS = 1e-06
F32, BF16, I32 = jnp.float32, jnp.bfloat16, jnp.int32

B_Q, B_R, C_R, B_O, C_1, C_2, B_1, B_DW, B_2, C_S, B_M, C_M = 0, 5, 10, 15, 20, 25, 30, 50, 70, 75, 80, 88
G_R, G_1, G_2, G_S, G_M = 96, 101, 106, 111, 116

PARTS = ((0, 1), (1, 4))
A_ROWS, B_ROWS, C_ROWS = 208, 224, 368
SMALL_ROW = 200
A_SPLIT = 104
VMEM_LIMIT = 24 * 1024 * 1024
VMEM_ALL = 60 * 1024 * 1024


def slot_of(xor):
    return (xor >> 1) | ((xor & 1) << 4)


def xor_of(slot):
    return ((slot & 15) << 1) | (slot >> 4)


def dot(a, b):
    return jnp.dot(a, b, preferred_element_type=F32)


def dot_nt(a, b):
    return lax.dot_general(a, b, (((1,), (1,)), ((), ())), preferred_element_type=F32)


def dot_tn(a, b):
    return lax.dot_general(a, b, (((0,), (0,)), ((), ())), preferred_element_type=F32)


def iota(shape, axis):
    return lax.broadcasted_iota(I32, shape, axis)


def one_hot(test):
    return jnp.where(test, 1.0, 0.0).astype(BF16)


def lanes(index, width=128):
    if isinstance(index, int):
        return slice(index * width, (index + 1) * width)
    return pl.ds(pl.multiple_of(index * width, width), width)


def loop(count, body):
    def step(index, carry):
        body(index)
        return carry

    lax.fori_loop(0, count, step, 0)


def column(table, start, count):
    return jnp.concatenate(
        [jnp.broadcast_to(table[:, h : h + 1], (64, 128)) for h in range(start, start + count)], axis=0
    )


def put_column(table, start, values):
    for h in range(values.shape[0] // 64):
        table[:, start + h : start + h + 1] = values[64 * h : 64 * h + 64, 0:1]


def token_place(lane):
    quad = lane >> 8
    row = 2 * ((lane >> 4) & 15) + (quad >> 1)
    col = 2 * (lane & 15) + (quad & 1)
    return row, col


def token_mask(tile, side, width=128):
    row, col = token_place(iota((1, width), 1) + tile * width)
    return jnp.where((row < side) & (col < side), 1.0, 0.0)


def key_place(index):
    return index >> 4, index & 15


def select_kernel(count, bases, small, small_at, *refs):
    sources, refs = refs[:count], refs[count:]
    if small:
        scal, biases, gains = refs[:3]
        refs = refs[3:]
    low_ref, high_ref, out, rows_ref, sems = refs[:5]
    held = refs[5:]
    copies = [
        pltpu.make_async_copy(source, place, sems.at[n]) for n, (source, place) in enumerate(zip(sources, held))
    ]
    for copy in copies:
        copy.start()
    half = rows_ref.shape[0] // 2
    rows_ref[...] = jnp.zeros_like(rows_ref)
    place = iota((out.shape[0], 2 * half), 1)
    pick_low = one_hot(place == low_ref[...])
    pick_high = one_hot(place == high_ref[...])
    for copy in copies:
        copy.wait()
    for source, base in zip(held, bases):
        rows_ref[base : base + source.shape[0], :] = source[...].astype(F32)
    if small:
        rows_ref[small_at : small_at + 1, :] = biases[:, 0:128].astype(F32)
        rows_ref[small_at + 1 : small_at + 2, 0:64] = biases[:, 128:192].astype(F32)
        wide = jnp.concatenate([gains[...].astype(F32), jnp.zeros((1, 72), F32)], axis=1)
        wide = jnp.broadcast_to(wide, (8, 128))
        rows_ref[small_at + 2 : small_at + 3, :] = pltpu.roll(wide, (56 * scal[0]) & 63, 1)[0:1, :]
    rows_ref[half:, :] = pltpu.roll(rows_ref[0:half, :], 64, 1)
    total = rows_ref[...].astype(BF16)
    low, upper = dot(pick_low, total), dot(pick_high, total)
    out[...] = jnp.where(iota((out.shape[0], 128), 1) < 64, low, upper).astype(BF16)


def select(sources, table, rows, vectors=()):
    bases, at = [], 0
    for source in sources:
        bases.append(at)
        at += -(-source.shape[0] // 16) * 16
    small = len(vectors) > 0
    half = at + (16 if small else 0)
    low, high = table(bases + [at], half).astype(np.int32)[:, :, None]
    specs = [pl.BlockSpec(memory_space=pltpu.HBM)] * len(sources)
    if small:
        specs += [pl.BlockSpec(memory_space=pltpu.SMEM)] + [pl.BlockSpec(memory_space=pltpu.VMEM)] * 2
    specs += [pl.BlockSpec(memory_space=pltpu.VMEM)] * 2
    return pl.pallas_call(
        functools.partial(select_kernel, len(sources), tuple(bases), small, at),
        in_specs=specs,
        out_shape=jax.ShapeDtypeStruct((rows, 128), BF16),
        scratch_shapes=[pltpu.VMEM((2 * half, 128), F32), pltpu.SemaphoreType.DMA((len(sources),))]
        + [pltpu.VMEM(source.shape, source.dtype) for source in sources],
        compiler_params=pltpu.CompilerParams(vmem_limit_bytes=VMEM_ALL if small else VMEM_LIMIT),
        cost_estimate=cost(2),
    )(*sources, *vectors, low, high)


def pair(half, low_src, high_src):
    low = -1 if low_src is None else low_src[0] + low_src[1] // 2 + half * (low_src[1] % 2)
    high = -1 if high_src is None else high_src[0] + high_src[1] // 2 + half * (1 - high_src[1] % 2)
    return low, high


def chunk_sources(bases, row, c):
    q, o, kv = bases
    if c < 6 or c >= 8:
        base, first = ((q, 0), (kv, 0), (kv, 10), None, (o, 0))[c // 2]
        at = 5 * (first + row) + 2 * (c % 2)
        return (base, at), (base, at + 1)
    if c == 6:
        return (q, 5 * row + 4), (kv, 5 * row + 4)
    return (kv, 5 * (10 + row) + 4), (o, 5 * row + 4)


def a_place(kind, row, c):
    if row < 8:
        return 16 * c + 8 * kind + row
    return 160 + 8 * (c // 2) + 4 * kind + 2 * (c % 2) + row - 8


def b_place(row, c):
    if row < 8:
        return 8 * c + row
    return 80 + 8 * (c // 4) + 2 * (c % 4) + row - 8


def table_a(bases, half):
    q, o, kv, r, small = bases
    rows = [(-1, -1)] * A_ROWS
    for c in range(10):
        for row in range(10):
            at = 20 * row + 2 * c
            rows[a_place(0, row, c)] = pair(half, (r, at), (r, at + 1))
            rows[a_place(1, row, c)] = pair(half, *chunk_sources((q, o, kv), row, c))
    for row in range(3):
        rows[SMALL_ROW + row] = pair(half, (small, 2 * row), (small, 2 * row + 1))
    return np.array(rows).T


def table_b(bases, half):
    w2, w1, dw, _ = bases
    rows = [(-1, -1)] * B_ROWS
    for c in range(10):
        for row in range(10):
            at = 20 * row + 2 * c
            rows[b_place(row, c)] = pair(half, (w2, at), (w2, at + 1))
    for c in range(3):
        for row in range(40):
            at = 5 * row + 2 * c
            rows[104 + 40 * c + row] = pair(half, (w1, at), (w1, at + 1) if c < 2 else (dw, 2 * row + 1))
    return np.array(rows).T


def table_c(bases, half):
    m, _ = bases
    rows = []
    for c in range(23):
        for row in range(16):
            at = 45 * row + 2 * c
            rows.append(pair(half, (m, at), (m, at + 1) if c < 22 else None))
    return np.array(rows).T


def turn(rows):
    return pltpu.roll(rows, 64, 1)


def halves(low, high):
    return jnp.where(iota((1, 128), 1) < 64, low, high)


def put_rows(out, first, count, stride, rows):
    out[pl.ds(first, count, stride=stride), :] = rows


def put_320(out, first, count, load):
    even, odd = ([load(chunk, parity) for chunk in range(3)] for parity in range(2))
    turned = [turn(rows) for rows in odd]
    for at, rows in enumerate(
        (even[0], even[1], halves(even[2], turned[0]), halves(turned[0], turned[1]), halves(turned[1], turned[2]))
    ):
        put_rows(out, first + at, count // 2, 5, rows)


def every_other(ref, start, count):
    return ref[pl.ds(start, count, stride=2), :]


def out_a_kernel(scal, sums, q, o, kv, r, biases, gains):
    squares = (
        (q, 0, (0, 1, 6), False),
        (o, 0, (8, 9, 7), True),
        (kv, 0, (2, 3, 6), True),
        (kv, 25, (4, 5, 7), False),
    )
    for out, first, chunks, high in squares:
        for start, count, lane_row in ((0, 8, 0), (8, 2, 20)):

            def load(chunk, parity, chunks=chunks, high=high, start=start, count=count):
                rows = every_other(sums, a_place(1, start, chunks[chunk]) + parity, count // 2)
                return turn(rows) if chunk == 2 and high else rows

            put_320(out, first + lane_row, count, load)
    for c in range(10):
        for start, count in ((0, 8), (8, 2)):
            put_rows(r, 10 * start + c, count, 10, sums[pl.ds(a_place(0, start, c), count), :])
    small = sums[SMALL_ROW : SMALL_ROW + 8, :]
    biases[:, 0:128] = small[0:1]
    biases[:, 128:192] = small[1:2, 0:64]
    gains[...] = pltpu.roll(small, (128 - ((56 * scal[0]) & 63)) & 127, 1)[2:3, 0:56]


def out_b_kernel(scal, sums, w2, w1):
    for c in range(10):
        for start, count in ((0, 8), (8, 2)):
            put_rows(w2, 10 * start + c, count, 10, sums[pl.ds(b_place(start, c), count), :])
    put_320(w1, 0, 40, lambda chunk, parity: every_other(sums, 104 + 40 * chunk + parity, 20))


def out_c_kernel(scal, sums, m):
    even = [every_other(sums, 16 * c, 8) for c in range(23)]
    turned = [turn(every_other(sums, 16 * c + 1, 8)) for c in range(23)]
    for c in range(22):
        put_rows(m, c, 8, 45, even[c])
        put_rows(m, 23 + c, 8, 45, halves(turned[c], turned[c + 1]))
    put_rows(m, 22, 8, 45, halves(even[22], turned[0]))


def split_ten(row, per, magic):
    owner = (row * magic) >> 16
    return owner, row - per * owner


def tens(row, me):
    owner, rest = split_ten(row, 10, 6554)
    slot = slot_of(owner ^ me)
    return jnp.where(rest < 8, slot * 8 + rest, 248 + slot * 2 + rest)


def keyval_tens(row, me, upper):
    owner, rest = split_ten(row, 20, 3277)
    inside = (rest >= 10) if upper else (rest < 10)
    return jnp.where(inside, tens(10 * owner + rest - (10 if upper else 0), me), -1)


def rest_row(row):
    return 64 * ((row & 7) >> 1) + 2 * (row >> 3) + (row & 1)


def orders_kernel(scal, from_tens, to_tens, from_lower, from_upper, to_lower, to_upper, from_rest, to_rest):
    me = scal[0]
    from_tens[...] = one_hot(iota((D, D), 1) == tens(iota((D, 1), 0), me))
    to_tens[...] = one_hot(iota((D, D), 0) == tens(iota((1, D), 1), me))
    for upper, down, up in ((False, from_lower, to_lower), (True, from_upper, to_upper)):
        down[...] = one_hot(iota((2 * D, D), 1) == keyval_tens(iota((2 * D, 1), 0), me, upper))
        up[...] = one_hot(iota((D, 2 * D), 0) == keyval_tens(iota((1, 2 * D), 1), me, upper))
    from_rest[...] = one_hot(iota((256, 256), 0) == rest_row(iota((1, 256), 1)))
    to_rest[...] = one_hot(iota((256, 256), 1) == rest_row(iota((256, 1), 0)))


def norm(values, gain, shift):
    mean = jnp.mean(values, axis=0, keepdims=True)
    centred = values - mean
    rstd = lax.rsqrt(jnp.mean(centred * centred, axis=0, keepdims=True) + EPS)
    return centred * rstd * gain + shift, mean, rstd


def norm_back(grad, hat, rstd, gain):
    scaled = grad * gain
    return rstd * (
        scaled
        - jnp.mean(scaled, axis=0, keepdims=True)
        - hat * jnp.mean(scaled * hat, axis=0, keepdims=True)
    )


def stat_rows(mean, rstd):
    row = iota((8, mean.shape[1]), 0)
    return jnp.where(row == 0, mean, jnp.where(row == 1, rstd, 0.0))


def entry_kernel(scal, tokens, entry, stats, turned):
    side = scal[1]
    for quad in range(4):
        lane = iota((1, 256), 1) + quad * 256
        row, col = token_place(lane)
        natural = row * SIDE + col
        pick = one_hot(iota((TOKENS, 256), 0) == natural)
        turned[:, quad * 256 : quad * 256 + 256] = pick
        mask = jnp.where((row < side) & (col < side), 1.0, 0.0)
        entry[:, quad * 256 : quad * 256 + 256] = (dot(tokens[...], pick) * mask).astype(BF16)

    def body(tile):
        values = entry[:, lanes(tile)].astype(F32)
        mean = jnp.mean(values, axis=0, keepdims=True)
        centred = values - mean
        rstd = lax.rsqrt(jnp.mean(centred * centred, axis=0, keepdims=True) + EPS)
        stats[:, lanes(tile)] = stat_rows(mean, rstd)

    loop(8, body)


def small_table(me, low, high):
    gathered = jnp.concatenate(
        [half[:, SMALL_ROW : SMALL_ROW + 8, :].astype(F32).reshape(128, 128) for half in (low, high)], axis=0
    ).astype(BF16)
    vector = iota((128, 256), 0)
    place = iota((128, 256), 1)
    row = place & 7
    owner = xor_of(place >> 3) ^ me
    first = (7 * owner) >> 3
    straight = (
        ((row == 0) & (vector == 3 * owner))
        | ((row == 1) & (vector == 3 * owner + 2))
        | ((row == 2) & (vector == 96 + first))
    )
    turned = ((row == 0) & (vector == 3 * owner + 1)) | ((row == 2) & (vector == 97 + first))
    rows = dot(one_hot(straight), gathered) + pltpu.roll(dot(one_hot(turned), gathered), 64, 1)
    return jnp.transpose(rows)[0:64, :]


def project_kernel(scal, from_tens, from_lower, from_upper, from_rest, low, high, entry, stats, wq, wkv, wrs, wo, first, qs, raw, stat_r, red, kv, kt, vt, bt, square, rest, redin):
    me = scal[0]
    bt[...] = small_table(me, low, high)
    for half, source in enumerate((low, high)):

        def chunk(c, half=half, source=source):
            block = source[:, 16 * c : 16 * c + 16, :].astype(F32)
            rows = slice(128 * half, 128 * half + 128)
            wrs[rows, lanes(c)] = block[:, 0:8].reshape(128, 128).astype(BF16)
            square[rows, lanes(c)] = block[:, 8:16].reshape(128, 128).astype(BF16)

        for c in range(10):
            chunk(c)
        block = source[:, 160:208, :].astype(F32)
        for c in range(5):
            part = block[:, 8 * c : 8 * c + 8].reshape(128, 128).astype(BF16)
            rest[128 * half : 128 * half + 128, 128 * c : 128 * c + 128] = part

    def last_two(p):
        part = dot(from_rest[...], rest[:, lanes(p)]).astype(BF16)
        wrs[256:320, lanes(p, 256)] = jnp.concatenate([part[0:64], part[64:128]], axis=1)
        square[256:320, lanes(p, 256)] = jnp.concatenate([part[128:192], part[192:256]], axis=1)

    for p in range(5):
        last_two(p)
    wq[:, 0:256] = dot(from_tens[...], square[:, 0:256]).astype(BF16)
    wo[:, 0:256] = dot(from_tens[...], square[:, 1024:1280]).astype(BF16)
    tails = dot(from_tens[...], square[:, 768:1024])
    wq[:, 256:320] = tails[:, 0:64].astype(BF16)
    wo[:, 256:320] = pltpu.roll(tails, 64, 1)[:, 0:64].astype(BF16)
    wkv[:, 0:256] = (dot(from_lower[...], square[:, 256:512]) + dot(from_upper[...], square[:, 512:768])).astype(BF16)
    tail = pltpu.roll(dot(from_lower[...], square[:, 768:896]), 64, 1) + dot(from_upper[...], square[:, 896:1024])
    wkv[:, 256:320] = tail[:, 0:64].astype(BF16)

    gain, shift = column(bt, G_1, 5), column(bt, C_1, 5)

    def body(tile):
        centred = entry[:, lanes(tile)].astype(F32) - stats[0:1, lanes(tile)]
        first[:, lanes(tile)] = (centred * stats[1:2, lanes(tile)] * gain + shift).astype(BF16)

    for tile in range(8):
        body(tile)
    for quad in range(4):
        redin[D * quad : D * quad + D, :] = first[:, 256 * quad : 256 * quad + 256]
    bias = column(bt, B_Q, 5)
    bias = jnp.concatenate([bias, bias], axis=1)
    for quad in range(4):
        at = lanes(quad, 256)
        qs[:, at] = (dot(wq[...], first[:, at]) + bias).astype(BF16) * BF16(0.125)
    bias = column(bt, B_R, 5)
    bias = jnp.concatenate([bias, bias], axis=1)
    mixed = dot(wrs[...], redin[...])
    total = bias
    for part in range(3):
        piece = mixed.astype(BF16)
        total = total + dot(from_tens[...], piece)
        mixed = mixed - piece.astype(F32)
    raw[...] = total
    gain, shift = column(bt, G_R, 5), column(bt, C_R, 5)
    for tile in range(2):
        at = slice(128 * tile, 128 * tile + 128)
        values, mean, rstd = norm(raw[:, at], gain, shift)
        red[:, at] = values.astype(BF16)
        stat_r[:, at] = stat_rows(mean, rstd)
    keyval = dot(wkv[...], red[...])
    kv[...] = keyval.astype(BF16)
    turned = jnp.transpose(keyval)
    for h in range(HEADS):
        kt[h] = turned[:, 64 * h : 64 * h + 64].astype(BF16)
        vt[h] = turned[:, D + 64 * h : D + 64 * h + 64].astype(BF16)


def key_bias(side):
    i, j = key_place(iota((QUARTER, 1), 0))
    return jnp.where((i < (side >> 1)) & (j < (side >> 1)), 0.0, -10000.0)


def head_rows(h):
    return pl.ds(pl.multiple_of(64 * h, 64), 64)


def attend_kernel(scal, kt, qs, kv, att, lse, scores_a, scores_b, probs_a, probs_b):
    bias = key_bias(scal[1])

    def score(scores, h, start):
        scores[...] = dot(kt[h], qs[head_rows(h), start : start + 512])

    def finish(scores, probs, h, start):
        for tile in range(4):
            at = slice(128 * tile, 128 * tile + 128)
            to = slice(start + 128 * tile, start + 128 * tile + 128)
            part = scores[:, at] + bias
            top = jnp.max(part, axis=0, keepdims=True)
            weights = jnp.exp(part - top)
            total = jnp.sum(weights, axis=0, keepdims=True)
            lse[h, :, to] = top + jnp.log(total)
            probs[:, at] = (weights * (1.0 / total)).astype(BF16)
        values = kv[pl.ds(pl.multiple_of(D + 64 * h, 64), 64), :]
        att[head_rows(h), start : start + 512] = dot(values, probs[...]).astype(BF16)

    score(scores_a, 0, 0)

    def head(h):
        score(scores_b, h, 512)
        finish(scores_a, probs_a, h, 0)
        score(scores_a, jnp.minimum(h + 1, HEADS - 1), 0)
        finish(scores_b, probs_b, h, 512)

    loop(HEADS, head)


def middle_kernel(scal, bt, wo, att, entry, mid, sec, stats, work):
    side = scal[1]
    bias, gain, shift = column(bt, B_O, 5), column(bt, G_2, 5), column(bt, C_2, 5)

    def body(tile):
        at = lanes(tile)
        mask = token_mask(tile, side)
        values = entry[:, at].astype(F32) + mask * (work[:, at] + bias)
        mid[:, at] = values
        normed, mean, rstd = norm(values, gain, shift)
        stats[:, at] = stat_rows(mean, rstd)
        sec[0:D, at] = (normed.astype(BF16).astype(F32) * mask).astype(BF16)
        sec[D : D + 64, at] = jnp.where(iota((64, 128), 0) == 9, mask, 0.0).astype(BF16)

    for quad in range(4):
        at = lanes(quad, 256)
        work[:, at] = dot(wo[...], att[:, at])
        body(2 * quad)
        body(2 * quad + 1)


def ffn_weights_kernel(scal, bt, from_tens, from_rest, low, high, w1, w1t, w2, w2t, taps, main, rest, wide):
    me = scal[0]
    for half, source in enumerate((low, high)):
        def chunks(p, half=half, source=source):
            block = source[:, pl.ds(pl.multiple_of(16 * p, 16), 16), :].astype(F32)
            both = jnp.concatenate([block[:, 0:8].reshape(128, 128), block[:, 8:16].reshape(128, 128)], axis=1)
            main[128 * half : 128 * half + 128, lanes(p, 256)] = both.astype(BF16)

        loop(5, chunks)
        block = source[:, 80:112, :].astype(F32)
        for c in range(3):
            part = block[:, 8 * c : 8 * c + 8].reshape(128, 128).astype(BF16)
            rest[128 * half : 128 * half + 128, 128 * c : 128 * c + 128] = part

        def expansion(slot, half=half, source=source):
            owner = ((slot << 1) | half) ^ me
            block = source[slot, 80:224, :].astype(F32)
            rows = pl.ds(pl.multiple_of(40 * owner, 8), 40)
            for c in range(3):
                wide[rows, 128 * c : 128 * c + 128] = block[24 + 40 * c : 64 + 40 * c]

        loop(16, expansion)
    for j in range(3):
        part = dot(from_rest[...], rest[:, 128 * j : 128 * j + 128]).astype(BF16)
        for k in range(4 if j < 2 else 2):
            c = 4 * j + k
            main[256:320, 128 * c : 128 * c + 128] = part[64 * k : 64 * k + 64]

    def block(p):
        rows = lanes(p, 256)
        full = dot(from_tens[...], main[:, lanes(p, 256)])
        w2[:, lanes(p, 256)] = full.astype(BF16)
        w2t[rows, :] = jnp.transpose(full).astype(BF16)
        w1t[:, lanes(p, 256)] = jnp.transpose(wide[rows, :])[0:D].astype(BF16)

    for p in range(5):
        block(p)
    low_tail = wide[:, 256:384].astype(BF16)

    def spread(tap):
        taps[tap] = dot(low_tail, one_hot(iota((128, 128), 0) == 64 + tap))

    for tap in range(9):
        spread(tap)
    w1[:, 0:256] = wide[:, 0:256].astype(BF16)
    lane = iota((64, 128), 1)
    for h in range(20):
        rows = slice(64 * h, 64 * h + 64)
        taps[9, rows, :] = jnp.broadcast_to(bt[:, B_DW + h : B_DW + h + 1], (64, 128))
        beside = jnp.where(lane == 73, bt[:, B_1 + h : B_1 + h + 1], 0.0)
        w1[rows, 256:384] = jnp.where(lane < 64, wide[rows, 256:384], beside).astype(BF16)


def edge_masks():
    lane = iota((1, 128), 1)
    j = lane & 15
    return jnp.where(j != 0, 1.0, 0.0), jnp.where(j != 15, 1.0, 0.0), lane >= 16, lane < 112


def left_of(tiles):
    return [pltpu.roll(tile, 1, 1) for tile in tiles]


def right_of(tiles):
    return [pltpu.roll(tile, 127, 1) for tile in tiles]


def above(tiles, inside):
    turned = [pltpu.roll(tile, 16, 1) for tile in tiles]
    return [jnp.where(inside, turned[0], 0.0), jnp.where(inside, turned[1], turned[0])]


def below(tiles, inside):
    turned = [pltpu.roll(tile, 112, 1) for tile in tiles]
    return [jnp.where(inside, turned[0], turned[1]), jnp.where(inside, turned[1], 0.0)]


def times(tiles, factor):
    return [tile * factor for tile in tiles]


def plus(*many):
    return [functools.reduce(lambda a, b: a + b, tiles) for tiles in zip(*many)]


def tile_at(a, e, half):
    start = 256 * (2 * a + e) + 128 * half
    return slice(start, start + 128)


def quads(ref, rows):
    return [[[ref[rows, tile_at(a, e, half)] for half in range(2)] for e in range(2)] for a in range(2)]


LOG2E = float(np.log2(np.e))


def gelu_parts(x):
    y = x * np.float32(0.5**0.5)
    cdf = lax.erf(y) * 0.5 + 0.5
    bell = jnp.exp2(y * y * np.float32(-LOG2E) + np.float32(-0.5 * np.log2(2.0 * np.pi)))
    return x * cdf, cdf + x * bell


def ffn_kernel(scal, w1, taps, sec, act, slope, hid_a, hid_b):
    j_first, j_last, i_first, i_last = edge_masks()

    def fill(hid, step):
        rows = pl.ds(pl.multiple_of(jnp.minimum(step, FF // 64 - 1) * 64, 64), 64)
        hid[...] = dot(w1[rows, :], sec[...])

    def group(hid, step, index):
        rows = slice(16 * index, 16 * index + 16)
        out_rows = pl.ds(pl.multiple_of(64 * step + 16 * index, 16), 16)
        k = [taps[n, out_rows, :] for n in range(10)]
        first = [k[3 * r] * j_first for r in range(3)]
        last = [k[3 * r + 2] * j_last for r in range(3)]
        quad = quads(hid, rows)
        left = [left_of(quad[a][1]) for a in range(2)]
        right = [right_of(quad[a][0]) for a in range(2)]

        def across(a, e, r):
            if e == 0:
                parts = zip(left[a], quad[a][0], quad[a][1])
                return [first[r] * x + k[3 * r + 1] * y + k[3 * r + 2] * z for x, y, z in parts]
            parts = zip(quad[a][0], quad[a][1], right[a])
            return [k[3 * r] * x + k[3 * r + 1] * y + last[r] * z for x, y, z in parts]

        for e in range(2):
            up = above(across(1, e, 0), i_first)
            down = below(across(0, e, 2), i_last)
            outs = (plus(across(0, e, 1), across(1, e, 2), up), plus(across(0, e, 0), across(1, e, 1), down))
            for a in range(2):
                for half in range(2):
                    value, grad = gelu_parts(outs[a][half] + k[9])
                    act[out_rows, tile_at(a, e, half)] = value.astype(BF16)
                    slope[out_rows, tile_at(a, e, half)] = grad.astype(BF16)

    fill(hid_a, 0)

    def two(index):
        fill(hid_b, 2 * index + 1)
        for n in range(4):
            group(hid_a, 2 * index, n)
        fill(hid_a, 2 * index + 2)
        for n in range(4):
            group(hid_b, 2 * index + 1, n)

    loop(FF // 128, two)


def ending_kernel(scal, bt, w2, act, mid, end, sect, stats, work):
    side = scal[1]
    bias, gain, shift = column(bt, B_2, 5), column(bt, G_S, 5), column(bt, C_S, 5)

    def body(tile):
        at = lanes(tile)
        mask = token_mask(tile, side)
        values = mid[:, at] + mask * (work[:, at] + bias)
        end[:, at] = values
        normed, mean, rstd = norm(values, gain, shift)
        stats[:, at] = stat_rows(mean, rstd)
        sect[:, at] = (normed.astype(BF16).astype(F32) * mask).astype(BF16)

    for quad in range(4):
        at = lanes(quad, 256)
        work[:, at] = dot(w2[...], act[:, at])
        body(2 * quad)
        body(2 * quad + 1)


def lane_sum(values):
    return jnp.sum(values, axis=1, keepdims=True)


def merge_kernel(scal, bt, c_low, c_high, sect, end, stats, cot, four, keep, send, end_grad, branch, grads, wm, patch, mg, back, work, natural):
    me, side = scal[0], scal[1]
    grads[...] = jnp.zeros_like(grads)
    for half, source in enumerate((c_low, c_high)):

        def place(c, half=half, source=source):
            block = source[:, 16 * c : 16 * c + 16, :].reshape(256, 128)
            wm[256 * half : 256 * half + 256, lanes(c)] = block

        for c in range(23):
            place(c)

    def reorder(to_owner):
        def one(slot):
            at = pl.ds(pl.multiple_of(16 * slot, 16), 16)
            owner = pl.ds(pl.multiple_of((xor_of(slot) ^ me) * 16, 16), 16)
            to_owner(at, owner)

        loop(32, one)

    j_first, j_last, i_first, i_last = edge_masks()
    quad = [[[t.astype(F32) for t in pair] for pair in row] for row in quads(sect, slice(None))]
    left = [times(left_of(quad[a][1]), j_first) for a in range(2)]
    pieces = (
        above(left[1], i_first),
        above(quad[1][0], i_first),
        above(quad[1][1], i_first),
        left[0],
        quad[0][0],
        quad[0][1],
        left[1],
        quad[1][0],
        quad[1][1],
    )
    for n, piece in enumerate(pieces):
        for half in range(2):
            patch[D * n : D * n + D, 128 * half : 128 * half + 128] = piece[half].astype(BF16)
    patch[9 * D :, :] = jnp.zeros((MERGE_PAD - 9 * D, 256), BF16)
    bias, gain, shift = column(bt, B_M, 8), column(bt, G_M, 8), column(bt, C_M, 8)
    work[...] = dot(wm[...], patch[...])

    def from_slots(at, owner):
        natural[owner, :] = work[at, :]

    reorder(from_slots)
    half_side = side >> 1
    for tile in range(2):
        at = slice(128 * tile, 128 * tile + 128)
        i, j = key_place(iota((1, 128), 1) + 128 * tile)
        mask = jnp.where((i < half_side) & (j < half_side), 1.0, 0.0)
        values = natural[:, at] + bias
        mean = jnp.mean(values, axis=0, keepdims=True)
        centred = values - mean
        rstd = lax.rsqrt(jnp.mean(centred * centred, axis=0, keepdims=True) + EPS)
        hat = centred * rstd
        four[:, at] = ((hat * gain + shift) * mask).astype(BF16)
        grad = cot[:, at].astype(F32) * mask
        low = norm_back(grad, hat, rstd, gain).astype(BF16)
        natural[:, at] = low.astype(F32)
        parts = (grad * hat, grad, low.astype(F32))
        sums = parts if tile == 0 else [s + v for s, v in zip(sums, parts)]
    put_column(grads, G_M, lane_sum(sums[0]))
    put_column(grads, C_M, lane_sum(sums[1]))
    put_column(grads, B_M, lane_sum(sums[2]))

    def to_slots(at, owner):
        mg[at, :] = natural[owner, :].astype(BF16)

    reorder(to_slots)

    def widths(body):
        loop(5, lambda c: body(pl.multiple_of(c * 512, 512), 512))
        body(5 * 512, 384)

    def patch_grad(start, width):
        back[pl.ds(start, width), :] = dot_tn(wm[:, pl.ds(start, width)], mg[...])


    def give(start, width):
        block = dot_nt(mg[...], patch[pl.ds(start, width), :]).astype(BF16)
        for c in range(width // 128):
            to = pl.ds(pl.multiple_of((start >> 3) + 16 * c, 16), 16)
            part = block[:, 128 * c : 128 * c + 128].reshape(32, 16, 128)
            keep[:, to, :] = part[0:16]
            send[:, to, :] = part[16:32]

    def both(start, width):
        patch_grad(start, width)
        give(start, width)

    widths(both)

    def piece(n):
        return [back[D * n : D * n + D, 128 * half : 128 * half + 128] for half in range(2)]

    results = (
        piece(4),
        plus(piece(5), times(right_of(piece(3)), j_last)),
        plus(piece(7), below(piece(1), i_last)),
        plus(
            piece(8),
            times(right_of(piece(6)), j_last),
            below(plus(piece(2), times(right_of(piece(0)), j_last)), i_last),
        ),
    )
    for n, values in enumerate(results):
        for half in range(2):
            end_grad[:, 256 * n + 128 * half : 256 * n + 128 * half + 128] = values[half]
    gain = column(bt, G_S, 5)
    zeros = jnp.zeros((D, 128), F32)

    def one(tile):
        at = lanes(tile)
        mask = token_mask(tile, side)
        grad = end_grad[:, at] * mask
        hat = (end[:, at] - stats[0:1, at]) * stats[1:2, at]
        result = norm_back(grad, hat, stats[1:2, at], gain)
        end_grad[:, at] = result
        low = (result * mask).astype(BF16)
        branch[:, at] = low
        return grad * hat, grad, low.astype(F32)

    sums = (zeros, zeros, zeros)
    for step in range(4):
        pairs = zip(sums, one(2 * step), one(2 * step + 1))
        sums = tuple(total + (x + y) for total, x, y in pairs)
    put_column(grads, G_S, lane_sum(sums[0]))
    put_column(grads, C_S, lane_sum(sums[1]))
    put_column(grads, B_2, lane_sum(sums[2]))


def ffn_back_kernel(first_part, count, scal, w1, w2t, taps, sec, slope, branch, hg, dkx, hid_a, hid_b, cg_a, cg_b):
    start, steps = 256 * first_part, 4 * count
    j_first, j_last, i_first, i_last = edge_masks()
    lane = iota((16, 128), 1)

    def fill(hid, cg, step):
        rows = pl.ds(pl.multiple_of(start + jnp.minimum(step, steps - 1) * 64, 64), 64)
        cg[...] = dot(w2t[rows, :], branch[...]) * slope[rows, :].astype(F32)
        hid[...] = dot(w1[rows, :], sec[...])

    def group(hid, cg, step, index):
        rows = slice(16 * index, 16 * index + 16)
        from_rows = pl.ds(pl.multiple_of(start + 64 * step + 16 * index, 16), 16)
        to_rows = pl.ds(pl.multiple_of(64 * step + 16 * index, 16), 16)
        k = [taps[n, from_rows, :] for n in range(9)]
        quad = quads(cg, rows)
        bias = functools.reduce(lambda x, y: x + y, [t for row in quad for pair in row for t in pair])
        across = [
            (
                (times(left_of(quad[a][1]), j_first), quad[a][0], quad[a][1]),
                (quad[a][0], quad[a][1], times(right_of(quad[a][0]), j_last)),
            )
            for a in range(2)
        ]
        sums = [None] * 9
        for e in range(2):
            upper = [above(tiles, i_first) for tiles in across[1][e]]
            lower = [below(tiles, i_last) for tiles in across[0][e]]
            for a, near in ((0, (upper, across[0][e], across[1][e])), (1, (across[0][e], across[1][e], lower))):
                for half in range(2):
                    value = hid[rows, tile_at(a, e, half)]
                    total = None
                    for r in range(3):
                        for c in range(3):
                            tap = 3 * (2 - r) + (2 - c)
                            term = k[tap] * near[r][c][half]
                            total = term if total is None else total + term
                            term = value * near[r][c][half]
                            sums[tap] = term if sums[tap] is None else sums[tap] + term
                    hg[to_rows, tile_at(a, e, half)] = total.astype(BF16)
        table = jnp.where(lane == 9, lane_sum(bias), 0.0)
        for n in range(9):
            table = jnp.where(lane == n, lane_sum(sums[n]), table)
        dkx[to_rows, :] = table

    fill(hid_a, cg_a, 0)

    def two(index):
        fill(hid_b, cg_b, 2 * index + 1)
        for n in range(4):
            group(hid_a, cg_a, 2 * index, n)
        fill(hid_a, cg_a, 2 * index + 2)
        for n in range(4):
            group(hid_b, cg_b, 2 * index + 1, n)

    loop(steps // 2, two)


def middle_back_kernel(scal, bt, w1t, hg0, hg1, end_grad, mid, stats, mid_grad, low_grad, grads, work):
    side = scal[1]
    grads[...] = jnp.zeros_like(grads)
    gain = column(bt, G_2, 5)
    zeros = jnp.zeros((D, 128), F32)

    def one(tile):
        at = lanes(tile)
        mask = token_mask(tile, side)
        grad = work[:, at] * mask
        hat = (mid[:, at] - stats[0:1, at]) * stats[1:2, at]
        result = end_grad[:, at] + norm_back(grad, hat, stats[1:2, at], gain)
        mid_grad[:, at] = result
        low = (result * mask).astype(BF16)
        low_grad[:, at] = low
        return grad * hat, grad, low.astype(F32)

    sums = (zeros, zeros, zeros)
    for quad in range(4):
        at = lanes(quad, 256)
        work[:, at] = sum(
            dot(w1t[:, 256 * start : 256 * (start + count)], hg[:, at]) for hg, (start, count) in zip((hg0, hg1), PARTS)
        )
        pairs = zip(sums, one(2 * quad), one(2 * quad + 1))
        sums = tuple(total + (x + y) for total, x, y in pairs)
    put_column(grads, G_2, lane_sum(sums[0]))
    put_column(grads, C_2, lane_sum(sums[1]))
    put_column(grads, B_O, lane_sum(sums[2]))


def pack_b_kernel(scal, to_tens, hg0, hg1, dk0, dk1, sec, branch, act, keep, send, grads, dw1, gather, mixed):
    me = scal[0]
    grads[...] = jnp.zeros_like(grads)
    lane = iota((256, 128), 1)
    mixed[...] = dot(to_tens[...], branch[...]).astype(BF16)
    gather[:, 0:24, :] = jnp.zeros((32, 24, 128), F32)

    def contraction(p):
        block = dot_nt(mixed[...], act[pl.ds(pl.multiple_of(256 * p, 256), 256), :])
        parts = [block[0:256, 128 * e : 128 * e + 128].reshape(32, 1, 8, 128) for e in range(2)]
        full = jnp.concatenate(parts, axis=1).reshape(32, 16, 128).astype(BF16)
        to = pl.ds(pl.multiple_of(16 * p, 16), 16)
        keep[:, to, :] = full[0:16]
        send[:, to, :] = full[16:32]
        tail = jnp.concatenate([block[256:320, 0:128], block[256:320, 128:256]], axis=0).astype(BF16)
        place = rest_row(iota((256, 1), 0)) - 128 * (p & 1)
        to = pl.ds(pl.multiple_of(8 * (p >> 1), 8), 8)
        gather[:, to, :] += dot(one_hot(iota((256, 128), 1) == place), tail).reshape(32, 8, 128)

    for hg, dkx, (at, count) in zip((hg0, hg1), (dk0, dk1), PARTS):

        def outer(n, hg=hg, dkx=dkx, at=at):
            rows = pl.ds(pl.multiple_of(256 * n, 256), 256)
            to = pl.ds(pl.multiple_of(256 * (n + at), 256), 256)
            part = dot_nt(hg[rows, :], sec[...])
            dw1[to, 0:256] = part[:, 0:256]
            turned = pltpu.roll(dkx[rows, :], 64, 1)
            dw1[to, 256:384] = jnp.where(lane < 64, part[:, 256:384], jnp.where(lane < 73, turned, 0.0))
            table = grads[...]
            for m in range(4):
                here = slice(64 * m, 64 * m + 64)
                number = 4 * (n + at) + m
                table = jnp.where(lane[here] == B_1 + number, part[here, 329:330], table)
                table = jnp.where(lane[here] == B_DW + number, dkx[rows, :][here, 9:10], table)
            grads[...] = table
            contraction(n + at)

        loop(count, outer)

    def expansion(owner):
        slot = slot_of(owner ^ me)
        rows = slice(40 * owner, 40 * owner + 40)
        for c in range(3):
            gather[slot, 24 + 40 * c : 64 + 40 * c, :] = dw1[rows, 128 * c : 128 * c + 128]

    for owner in range(32):
        expansion(owner)
    keep[:, 80:224, :] = gather[0:16].astype(BF16)
    send[:, 80:224, :] = gather[16:32].astype(BF16)


def attend_back_kernel(scal, kt, vt, qs, kv, wo, low_grad, lse, dq, dkv, og, scores_a, scores_b, grads_a, grads_b, probs_a, probs_b, back_a, back_b):
    bias = key_bias(scal[1])
    og[...] = dot_tn(wo[...], low_grad[...]).astype(BF16)

    def score(scores, grads, h, start):
        at = slice(start, start + 512)
        scores[...] = dot(kt[h], qs[head_rows(h), at])
        grads[...] = dot(vt[h], og[head_rows(h), at])

    def finish(scores, grads, probs, back, h, start):
        for tile in range(4):
            at = slice(128 * tile, 128 * tile + 128)
            to = slice(start + 128 * tile, start + 128 * tile + 128)
            weights = jnp.exp(scores[:, at] + bias - lse[h, :, to])
            grad = grads[:, at]
            mean = jnp.sum(weights * grad, axis=0, keepdims=True)
            back[:, at] = (weights * (grad - mean)).astype(BF16)
            probs[:, at] = weights.astype(BF16)
        rows, at = head_rows(h), slice(start, start + 512)
        dq[rows, at] = (dot(kv[rows, :], back[...]) * 0.125).astype(BF16)
        return dot_nt(qs[rows, at], back[...]), dot_nt(og[rows, at], probs[...])

    score(scores_a, grads_a, 0, 0)

    def head(h):
        score(scores_b, grads_b, h, 512)
        one = finish(scores_a, grads_a, probs_a, back_a, h, 0)
        score(scores_a, grads_a, jnp.minimum(h + 1, HEADS - 1), 0)
        two = finish(scores_b, grads_b, probs_b, back_b, h, 512)
        dkv[head_rows(h), :] = (one[0] + two[0]).astype(BF16)
        dkv[pl.ds(pl.multiple_of(D + 64 * h, 64), 64), :] = (one[1] + two[1]).astype(BF16)

    loop(HEADS, head)


def first_kernel(scal, bt, to_tens, to_lower, to_upper, to_rest, wq, wkv, wrs, first, red, raw, stat_r, dq, dkv, low_grad, att, entry, stats, g_one, g_two, g_three, keep, send, work, grads, wide, redin, stack_r, stack_z, tails_of):
    me = scal[0]
    grads[...] = g_one[...] + g_two[...] + g_three[...]
    for quad in range(4):
        redin[D * quad : D * quad + D, :] = first[:, 256 * quad : 256 * quad + 256]
    dred = dot_tn(wkv[...], dkv[...])
    gain = column(bt, G_R, 5)
    lows = []
    for tile in range(2):
        at = slice(128 * tile, 128 * tile + 128)
        grad = dred[:, at]
        hat = (raw[:, at] - stat_r[0:1, at]) * stat_r[1:2, at]
        low = norm_back(grad, hat, stat_r[1:2, at], gain).astype(BF16)
        lows.append(low)
        parts = (grad * hat, grad, low.astype(F32))
        sums = parts if tile == 0 else [s + v for s, v in zip(sums, parts)]
    put_column(grads, G_R, lane_sum(sums[0]))
    put_column(grads, C_R, lane_sum(sums[1]))
    put_column(grads, B_R, lane_sum(sums[2]))
    low = jnp.concatenate(lows, axis=1)
    low = dot(to_tens[...], low).astype(BF16)
    wide[...] = dot_tn(wrs[...], low)
    straight = dot_tn(wq[...], dq[...])
    for quad in range(4):
        at = slice(256 * quad, 256 * quad + 256)
        work[:, at] = straight[:, at] + wide[D * quad : D * quad + D, :]
    zeros = jnp.zeros((D, 128), F32)

    def one(tile):
        at = lanes(tile)
        grad = work[:, at]
        hat = (entry[:, at].astype(F32) - stats[0:1, at]) * stats[1:2, at]
        return grad * hat, grad, dq[:, at].astype(F32)

    sums = (zeros, zeros, zeros)
    for step in range(4):
        pairs = zip(sums, one(2 * step), one(2 * step + 1))
        sums = tuple(total + (x + y) for total, x, y in pairs)
    put_column(grads, G_1, lane_sum(sums[0]))
    put_column(grads, C_1, lane_sum(sums[1]))
    put_column(grads, B_Q, lane_sum(sums[2]))
    stack_r[...] = dot_nt(low, redin[...])

    def outer(pick, grad, value):
        return dot_nt(dot(pick[...], grad[...]).astype(BF16), value[...])

    parts = (
        outer(to_tens, dq, first),
        outer(to_lower, dkv, red),
        outer(to_upper, dkv, red),
        outer(to_tens, low_grad, att),
    )
    for part, at in zip(parts, (0, 256, 512, 1024)):
        stack_z[:, at : at + 256] = part[:, 0:256]
    stack_z[:, 768:1024] = jnp.concatenate([part[:, 256:320] for part in parts], axis=1)

    def pack(p):
        at = lanes(p, 256)
        both = stack_r[:, at], stack_z[:, at]
        for e in range(2):
            pieces = [block[0:256, 128 * e : 128 * e + 128].reshape(32, 1, 8, 128) for block in both]
            full = jnp.concatenate(pieces, axis=1).reshape(32, 16, 128).astype(BF16)
            to = pl.ds(pl.multiple_of(32 * p + 16 * e, 16), 16)
            keep[:, to, :] = full[0:16]
            send[:, to, :] = full[16:32]
        tail = jnp.concatenate(
            [block[256:320, 128 * e : 128 * e + 128] for block in both for e in range(2)], axis=0
        ).astype(BF16)
        to = pl.ds(pl.multiple_of(8 * p, 8), 8)
        tails_of[:, to, :] = dot(to_rest[...], tail).reshape(32, 8, 128)

    loop(5, pack)
    rows = jnp.transpose(jnp.concatenate([grads[...], jnp.zeros((64, 128), F32)], axis=0)).astype(BF16)
    place = iota((256, 128), 0)
    vector = iota((256, 128), 1)
    line = place & 7
    owner = xor_of(place >> 3) ^ me
    start = (7 * owner) >> 3
    straight = (
        ((line == 0) & (vector == 3 * owner))
        | ((line == 1) & (vector == 3 * owner + 2))
        | ((line == 2) & (vector == 96 + start))
    )
    turned = ((line == 0) & (vector == 3 * owner + 1)) | ((line == 2) & (vector == 97 + start))
    small = dot(one_hot(straight), rows) + pltpu.roll(dot(one_hot(turned), rows), 64, 1)
    tails_of[:, 40:48, :] = small.reshape(32, 8, 128)
    keep[:, 160:208, :] = tails_of[0:16].astype(BF16)
    send[:, 160:208, :] = tails_of[16:32].astype(BF16)


def token_kernel(scal, bt, turned, grad_in, mid_grad, entry, stats, tok, high, rest):
    side = scal[1]
    gain = column(bt, G_1, 5)

    def body(tile):
        at = lanes(tile)
        hat = (entry[:, at].astype(F32) - stats[0:1, at]) * stats[1:2, at]
        result = mid_grad[:, at] + norm_back(grad_in[:, at], hat, stats[1:2, at], gain)
        result = result * token_mask(tile, side)
        upper = result.astype(BF16)
        high[:, at] = upper
        rest[:, at] = (result - upper.astype(F32)).astype(BF16)

    for tile in range(8):
        body(tile)

    def quad(index):
        pick = turned[pl.ds(pl.multiple_of(256 * index, 256), 256), :]
        tok[:, lanes(index, 256)] = dot_nt(high[...], pick) + dot_nt(rest[...], pick)

    loop(4, quad)


def cost(micros):
    return pl.CostEstimate(flops=int(micros * 1e9), bytes_accessed=1000, transcendentals=0)


def call(kernel, args, outs, scratch=(), micros=5):
    return pl.pallas_call(
        kernel,
        in_specs=[pl.BlockSpec(memory_space=pltpu.SMEM if arg.dtype == I32 else pltpu.VMEM) for arg in args],
        out_shape=[jax.ShapeDtypeStruct(shape, dtype) for shape, dtype in outs],
        scratch_shapes=[pltpu.VMEM(shape, dtype) for shape, dtype in scratch],
        compiler_params=pltpu.CompilerParams(vmem_limit_bytes=VMEM_LIMIT),
        cost_estimate=cost(micros),
    )(*args)


def local(group, axes, *arrays):
    return step_of(group, axes, *arrays)


def step_of(group, axes, tokens, image_side, cotangent, *shards):
    index = lax.axis_index(axes[0]) * lax.axis_size(axes[1]) + lax.axis_index(axes[1])
    me = index // group
    devices = SUPER * group

    def flip(values, mask):
        pairs = [(i, ((i // group) ^ mask) * group + i % group) for i in range(devices)]
        return lax.ppermute(values, axes, pairs)

    def gather(block, split=0, direct=False):
        held = block[None]
        if direct:
            held = jnp.concatenate([held, flip(held, 2), flip(held, 4), flip(held, 6)], axis=0)
        else:
            for mask in FLIPS[:2]:
                held = jnp.concatenate([held, flip(held, mask)], axis=0)
        if split:
            one, two = held[:, :split], held[:, split:]
            one, two = (jnp.concatenate([one, flip(one, 8)], axis=0), jnp.concatenate([two, flip(two, 16)], axis=0))
            far, near = flip(one, 16), flip(two, 8)
            two = jnp.concatenate([two[:4], near[:4], two[4:], near[4:]], axis=0)
            held = jnp.concatenate([jnp.concatenate([one, far], axis=0), two], axis=1)
        else:
            for mask in FLIPS[2:]:
                held = jnp.concatenate([held, flip(held, mask)], axis=0)
        return held, flip(held, 1)

    def scatter(keep, send, split=0, direct=False):
        def step(held, mask):
            return flip(held, mask).astype(F32)

        def halve(held, mask):
            half = held.shape[0] // 2
            return held[:half].astype(F32) + step(held[half:], mask)

        held = (keep.astype(F32) + step(send, 1)).astype(BF16)
        if split:
            one, two = held[:, :split], held[:, split:].reshape(2, 2, 4, -1, 128)
            one, two = (
                halve(one, 16).astype(BF16),
                (two[:, 0].astype(F32) + step(two[:, 1], 8)).astype(BF16).reshape(8, -1, 128),
            )
            held = jnp.concatenate([halve(one, 8), halve(two, 16)], axis=1).astype(BF16)
        else:
            held = halve(held, 16).astype(BF16)
            held = halve(held, 8).astype(BF16)
        if direct:
            far = step(held[2:3], 4), step(held[3:4], 6), step(held[1:2], 2)
            return (held[0:1].astype(F32) + far[2] + far[0] + far[1])[0]
        held = halve(held, 4).astype(BF16)
        return halve(held, 2)[0]

    if group > 1:
        per = lax.axis_size(axes[1])
        start = (index % per) // group * group

        def join(shard):
            full = lax.all_gather(shard, axes[1], axis=0)
            return lax.dynamic_slice_in_dim(full, start, group, axis=0).reshape(-1)

        shards = [join(shard) for shard in shards]
    query, keyval, reduce_w, output, expand, depth, contract, merge, gains, biases = shards

    def rows(flat):
        return flat.reshape(-1, 128)

    scal = jnp.stack([me.astype(I32), image_side[0].astype(I32)])
    taps = jnp.pad(depth.reshape(40, 9), ((0, 0), (64, 55)))
    block_a = select(
        [rows(query), rows(output), rows(keyval), rows(reduce_w)],
        table_a, A_ROWS, (scal, biases[None], gains[None]),
    )
    block_b = select([rows(contract), rows(expand), taps], table_b, B_ROWS)
    block_c = select([rows(merge)], table_c, C_ROWS)
    a_low, a_high = gather(block_a, A_SPLIT, True)
    b_low, b_high = gather(block_b, B_ROWS // 2, True)
    c_low, c_high = gather(block_c, C_ROWS // 2)

    big, narrow = (D, TOKENS), (D, QUARTER)
    from_tens, to_tens, from_lower, from_upper, to_lower, to_upper, from_rest, to_rest = call(
        orders_kernel,
        (scal,),
        [((D, D), BF16)] * 2 + [((2 * D, D), BF16)] * 2 + [((D, 2 * D), BF16)] * 2 + [((256, 256), BF16)] * 2,
        micros=2,
    )
    entry, stats_1, turned = call(
        entry_kernel, (scal, tokens[0]), [(big, BF16), ((8, TOKENS), F32), ((TOKENS, TOKENS), BF16)], micros=3.5)
    wq, wkv, wr, wo, first, qs, raw, stat_r, red, kv, kt, vt, bt = call(
        project_kernel,
        (scal, from_tens, from_lower, from_upper, from_rest, a_low, a_high, entry, stats_1),
        [
            ((D, D), BF16), ((2 * D, D), BF16), ((D, 4 * D), BF16), ((D, D), BF16), (big, BF16), (big, BF16),
            (narrow, F32), ((8, QUARTER), F32), (narrow, BF16), ((2 * D, QUARTER), BF16),
            ((HEADS, QUARTER, 64), BF16), ((HEADS, QUARTER, 64), BF16), ((64, 128), F32),
        ],
        [((D, 1280), BF16), ((256, 640), BF16), ((4 * D, QUARTER), BF16)],
        micros=8,
    )
    att, lse = call(attend_kernel, (scal, kt, qs, kv), [(big, BF16), ((HEADS, 1, TOKENS), F32)],
        [((QUARTER, 512), F32)] * 2 + [((QUARTER, 512), BF16)] * 2, micros=8.5)
    mid, sec, stats_2 = call(
        middle_kernel, (scal, bt, wo, att, entry), [(big, F32), ((384, TOKENS), BF16), ((8, TOKENS), F32)], [(big, F32)],
        micros=5,
    )
    w1, w1t, w2, w2t, taps = call(
        ffn_weights_kernel,
        (scal, bt, from_tens, from_rest, b_low, b_high),
        [((FF, 384), BF16), ((D, FF), BF16), ((D, FF), BF16), ((FF, D), BF16), ((10, FF, 128), F32)],
        [((D, FF), BF16), ((256, 384), BF16), ((FF, 384), F32)],
        micros=8,
    )
    act, slope = call(
        ffn_kernel,
        (scal, w1, taps, sec),
        [((FF, TOKENS), BF16), ((FF, TOKENS), BF16)],
        [((64, TOKENS), F32), ((64, TOKENS), F32)],
        micros=17,
    )
    end, sect, stats_s = call(
        ending_kernel, (scal, bt, w2, act, mid), [(big, F32), (big, BF16), ((8, TOKENS), F32)], [(big, F32)], micros=5
    )
    four, c_keep, c_send, end_grad, branch, g_one = call(
        merge_kernel,
        (scal, bt, c_low, c_high, sect, end, stats_s, cotangent[0]),
        [
            ((OUT_D, QUARTER), BF16), ((16, C_ROWS, 128), BF16), ((16, C_ROWS, 128), BF16), (big, F32), (big, BF16),
            ((64, 128), F32),
        ],
        [
            ((OUT_D, MERGE_PAD), BF16), ((MERGE_PAD, QUARTER), BF16), ((OUT_D, QUARTER), BF16),
            ((MERGE_PAD, QUARTER), F32), ((OUT_D, QUARTER), F32), ((OUT_D, QUARTER), F32),
        ],
        micros=20,
    )
    sum_c = scatter(c_keep, c_send, C_ROWS // 2)
    hgs, dks = [], []
    for at, count in PARTS:
        hg, dk = call(
            functools.partial(ffn_back_kernel, at, count),
            (scal, w1, w2t, taps, sec, slope, branch),
            [((256 * count, TOKENS), BF16), ((256 * count, 128), F32)],
            [((64, TOKENS), F32)] * 4,
            micros=6 * count,
        )
        hgs.append(hg)
        dks.append(dk)
    b_keep, b_send, g_three = call(
        pack_b_kernel,
        (scal, to_tens, *hgs, *dks, sec, branch, act),
        [((16, B_ROWS, 128), BF16), ((16, B_ROWS, 128), BF16), ((64, 128), F32)],
        [((FF, 384), F32), ((32, 144, 128), F32), (big, BF16)],
        micros=9,
    )
    sum_b = scatter(b_keep, b_send, B_ROWS // 2, True)
    mid_grad, low_grad, g_two = call(
        middle_back_kernel,
        (scal, bt, w1t, *hgs, end_grad, mid, stats_2),
        [(big, F32), (big, BF16), ((64, 128), F32)],
        [(big, F32)],
        micros=6,
    )
    dq, dkv = call(
        attend_back_kernel,
        (scal, kt, vt, qs, kv, wo, low_grad, lse),
        [(big, BF16), ((2 * D, QUARTER), BF16)],
        [(big, BF16)] + [((QUARTER, 512), F32)] * 4 + [((QUARTER, 512), BF16)] * 4,
        micros=9,
    )
    a_keep, a_send, first_grad = call(
        first_kernel,
        (
            scal, bt, to_tens, to_lower, to_upper, to_rest, wq, wkv, wr, first, red, raw, stat_r, dq, dkv, low_grad, att, entry, stats_1, g_one, g_two, g_three,
        ),
        [((16, A_ROWS, 128), BF16), ((16, A_ROWS, 128), BF16), (big, F32)],
        [
            ((64, 128), F32), ((4 * D, QUARTER), F32), ((4 * D, QUARTER), BF16), ((D, 1280), F32), ((D, 1280), F32),
            ((32, 48, 128), F32),
        ],
        micros=11,
    )
    sum_a = scatter(a_keep, a_send, A_SPLIT, True)
    (token_grad,) = call(
        token_kernel,
        (scal, bt, turned, first_grad, mid_grad, entry, stats_1),
        [(big, F32)],
        [(big, BF16), (big, BF16)],
        micros=5,
    )
    if group > 1:

        def total(part):
            full = lax.all_gather(part, axes[1], axis=0)
            return jnp.sum(lax.dynamic_slice_in_dim(full, start, group, axis=0), axis=0)

        sum_a, sum_b, sum_c = total(sum_a), total(sum_b), total(sum_c)

    def flat(count):
        return (count, 128), F32

    query_g, output_g, keyval_g, reduce_g, biases_g, gains_g = call(
        out_a_kernel,
        (scal, sum_a),
        [flat(25), flat(25), flat(50), flat(100), ((1, 192), F32), ((1, 56), F32)],
        micros=1,
    )
    contract_g, expand_g = call(out_b_kernel, (scal, sum_b), [flat(100), flat(100)], micros=1)
    (merge_g,) = call(out_c_kernel, (scal, sum_c), [flat(360)], micros=1)
    depth_g = sum_b[184:224, 64:73]
    grads = [query_g, keyval_g, reduce_g, output_g, expand_g, depth_g, contract_g, merge_g, gains_g, biases_g]
    grads = [grad.reshape(-1) for grad in grads]
    if group > 1:
        mine = index % group
        grads = [lax.dynamic_index_in_dim(grad.reshape(group, -1), mine, keepdims=False) for grad in grads]
    return (four[None], token_grad[None], *grads)


def solution(mesh):
    axes = ("dp", "fs")
    devices = mesh.shape["dp"] * mesh.shape["fs"]
    group = devices // SUPER
    if devices != SUPER * group or mesh.shape["fs"] % group:
        raise ValueError("unsupported mesh")
    one, three = P(axes), P(axes, None, None)
    return jax.shard_map(
        functools.partial(local, group, axes),
        mesh=mesh,
        in_specs=(three, one, three) + (one,) * 10,
        out_specs=(three, three) + (one,) * 10,
        check_vma=False,
    )
```
